32 devices in a mesh: dp: 4 (over z), seq: 4 (over x, core), fsdp: 2 (over y).
Axes of the slice: x: 2, y: 2, z: 4, core: 2. Of those that a mesh axis runs over, the one named last changes fastest.
Arguments:
- tokens: bfloat16 [4, 2560, 1024], P('dp', ('seq', 'fsdp')), may hold values from -6 to 6
- cotangent: bfloat16 [4, 2560, 1024], P('dp', ('seq', 'fsdp')), may hold values from -6 to 6
- lengths: int32 [4], P('dp'), may hold values from 640 to 2560, as said below
- order: int32 [16], replicated, may hold values from 0 to 15, each once
- routes: int32 [4, 2560, 8], P('dp', ('seq', 'fsdp')), may hold values from 0 to 15, all different within a row; in each aligned block of 320 rows (0 to 319, 320 to 639, ..., all dimensions but the last counted through in order) at most 256 rows name the same one
- norm1: bfloat16 [1024], P('fsdp'), may hold values from 0.5 to 1.5
- query_key_value_weight: bfloat16 [1024, 2048], P('fsdp'), may hold values from -0.25 to 0.25
- w_out: bfloat16 [1024, 1024], P('fsdp'), may hold values from -1.1953125 to 1.1953125
- norm2: bfloat16 [1024], P('fsdp'), may hold values from 0.5 to 1.5
- router: bfloat16 [1024, 16], P('fsdp'), may hold values from -0.09375 to 0.09375
- w_gate: bfloat16 [16, 1024, 512], P('fsdp'), may hold values from -0.1875 to 0.1875
- w_up: bfloat16 [16, 1024, 512], P('fsdp'), may hold values from -0.1875 to 0.1875
- w_down: bfloat16 [16, 512, 1024], P('fsdp'), may hold values from -1 to 1
Outputs:
- layer_out: bfloat16 [4, 2560, 1024], P('dp', ('seq', 'fsdp'))
- d_tokens: float32 [4, 2560, 1024], P('dp', ('seq', 'fsdp'))
- grad_norm1: float32 [1024], P('fsdp')
- grad_w_qkv: float32 [1024, 2048], P('fsdp')
- grad_w_out: float32 [1024, 1024], P('fsdp')
- grad_norm2: float32 [1024], P('fsdp')
- grad_router: float32 [1024, 16], P('fsdp')
- grad_w_gate: float32 [16, 1024, 512], P('fsdp')
- grad_w_up: float32 [16, 1024, 512], P('fsdp')
- grad_w_down: float32 [16, 512, 1024], P('fsdp')
The draws below stay inside these ranges and needn't reach their ends.
Inputs may be any that keep to these rules, and one draw needn't show every extreme that they name: `lengths`: one slot has exactly 2560 valid tokens and another exactly 640. `routes`: each token names 8 different experts; in each aligned block of 320 rows (the rows of one device) no expert is named by more than 256 rows, a bound that some block reaches. `order`: each span index appears once.
All inputs are finite; a program needn't handle non-finite values.
Results may differ from the reference program's by a relative error of at most 0.023.
Values may be sent and summed in bfloat16 or wider, within the bound.
A program may use at most 384 MiB of HBM per device.

```python
import math
import jax
import jax.numpy as jnp
import numpy as np
from jax import lax

MODEL_WIDTH = 1024
QUERY_HEADS = 16
KEY_VALUE_HEADS = 8
HEAD_WIDTH = 64
FF = 512
TOPK = 8
EXPERTS = 16
TOK_DEV = 320
CAP = 256
SPANS = 16
LEN = 2560
SLOTS = 4


def draw_lengths(key, part):
    first_key, second_key = jax.random.split(jax.random.fold_in(key, 11))
    drawn = jax.random.randint(first_key, (SLOTS,), LEN // 4, LEN + 1)
    shuffled = jax.random.permutation(second_key, SLOTS)
    drawn = jnp.where(shuffled == 0, LEN, drawn)
    drawn = jnp.where(shuffled == 1, LEN // 4, drawn)
    return drawn.astype(jnp.int32)


def levels(own_key, shape, cuts, least, largest):
    level, own = 1.0, jax.random.fold_in(own_key, 6)
    for dim, shards_of in cuts:
        draws = jnp.exp(jax.random.uniform(jax.random.fold_in(own, dim), (shards_of,), jnp.float32, least / len(cuts), largest / len(cuts)))
        level = level * jnp.repeat(draws, shape[dim] // shards_of).reshape([-1 if axis == dim else 1 for axis in range(len(shape))])
    return level


def routed_block(rng, own, number, rows, amount, top, bound, skew):
    ranking = jax.random.permutation(rng, amount)
    packed, common = load_shares(amount, rows * top, bound, skew, True), load_shares(amount, rows * top, bound, skew, False)
    places = jnp.arange(amount)

    def named(sizes, turn):
        used = int((sizes > 0).sum())
        fixed = max(1, used // 4)
        passed = fixed + (places - fixed + turn * (used - fixed)) % max(1, amount - fixed)
        return jnp.zeros((amount,), jnp.int32).at[ranking[jnp.where(places < fixed, places, passed)]].set(jnp.asarray(sizes, jnp.int32))

    sizes = jnp.where(number % 4 == 0, named(packed, number // 4), named(common, number - number // 4 - 1))
    mixed = jax.random.permutation(jax.random.fold_in(own, 3), amount)
    source_of, taker = mixed[0:amount // 2 * 2:2], mixed[1:amount // 2 * 2:2]
    margin = jnp.minimum(sizes[source_of] - 1, bound - sizes[taker]) // 2
    margin = jnp.where((source_of == ranking[0]) | (taker == ranking[0]) | (sizes[taker] == 0), 0, jnp.maximum(margin, 0))
    passed = jax.random.randint(jax.random.fold_in(own, 4), (amount // 2,), 0, 1 << 20) % (margin + 1)
    sizes = sizes.at[source_of].add(-passed).at[taker].add(passed)
    labels = jnp.searchsorted(jnp.cumsum(sizes), jnp.arange(rows * top), side="right").astype(jnp.int32)
    table = labels.reshape(top, rows).T
    table = table[jax.random.permutation(jax.random.fold_in(own, 1), rows)]
    turn = jax.random.randint(jax.random.fold_in(own, 2), (rows, 1), 0, top)
    return jnp.take_along_axis(table, (jnp.arange(top)[None, :] + turn) % top, axis=1)


def load_shares(number_of, total, limit, skew, full):
    loads = [(1 << 20) // math.isqrt(rank ** skew) + 1 for rank in range(1, number_of + 1)]
    largest = limit if full else min(limit, max(-(-total // number_of), total * loads[0] // sum(loads)))
    least = 1 if total - largest >= number_of - 1 else 0
    counts, rest = [largest] + [least] * (number_of - 1), total - largest - least * (number_of - 1)
    while rest > 0:
        free = [i for i in range(1, number_of) if counts[i] < largest] or [i for i in range(1, number_of) if counts[i] < limit]
        mass, remaining = sum([loads[i] for i in free]), rest
        for i in free:
            more = min(limit - counts[i], max(1, remaining * loads[i] // mass), rest)
            counts[i] = counts[i] + more
            rest = rest - more
    return np.array(counts)


def bell_draw(key, extent, width, reach, cuts=(), held_as=jnp.bfloat16):
    factor_of = levels(key, extent, cuts, -0.22, 0.18) if cuts else 1.0
    values = jax.random.normal(key, extent, jnp.float32) * width * factor_of
    return jnp.minimum(jnp.maximum(values, -reach), reach).astype(held_as)


def setup_inputs(seed: int = 0) -> dict:
    arg_keys = jax.random.split(jax.random.key(seed), 14)
    tokens = bell_draw(arg_keys[0], (SLOTS, LEN, MODEL_WIDTH), 1.0, 6.0, ((0, 4), (1, 8)))
    cotangent = bell_draw(arg_keys[1], (SLOTS, LEN, MODEL_WIDTH), 1.0, 6.0, ((0, 4), (1, 8)))
    lengths = draw_lengths(jax.random.fold_in(arg_keys[13], 71), 0)
    order = jax.random.permutation(arg_keys[3], SPANS).astype(jnp.int32)
    routes_keys = jax.random.split(jax.random.fold_in(arg_keys[4], 1), SLOTS * LEN // TOK_DEV)
    routes_turns = jax.random.permutation(jax.random.fold_in(arg_keys[4], 3), SLOTS * LEN // TOK_DEV)
    routes = jax.vmap(lambda own, number: routed_block(jax.random.fold_in(arg_keys[4], 2), own, number, TOK_DEV, EXPERTS, TOPK, CAP, 1))(routes_keys, routes_turns).reshape((SLOTS, LEN, TOPK))
    norm1 = jnp.clip(1.0 + 0.1 * jax.random.normal(arg_keys[5], (MODEL_WIDTH,), jnp.float32), 0.5, 1.5).astype(jnp.bfloat16)
    query_key_value_weight = bell_draw(arg_keys[6], (MODEL_WIDTH, (QUERY_HEADS + 2 * KEY_VALUE_HEADS) * HEAD_WIDTH), (MODEL_WIDTH // 2) ** -0.5, 0.25, ((0, 2),))
    w_out = bell_draw(arg_keys[7], (QUERY_HEADS * HEAD_WIDTH, MODEL_WIDTH), 0.2, 1.1953125, ((0, 2),))
    norm2 = jnp.clip(1.0 + 0.1 * jax.random.normal(arg_keys[8], (MODEL_WIDTH,), jnp.float32), 0.5, 1.5).astype(jnp.bfloat16)
    router = bell_draw(arg_keys[9], (MODEL_WIDTH, EXPERTS), (4 * MODEL_WIDTH) ** -0.5, 0.09375, ((0, 2),))
    w_gate = bell_draw(arg_keys[10], (EXPERTS, MODEL_WIDTH, FF), MODEL_WIDTH ** -0.5, 0.1875, ((0, 2),))
    w_up = bell_draw(arg_keys[11], (EXPERTS, MODEL_WIDTH, FF), MODEL_WIDTH ** -0.5, 0.1875, ((0, 2),))
    w_down = bell_draw(arg_keys[12], (EXPERTS, FF, MODEL_WIDTH), (FF // 16) ** -0.5, 1.0, ((0, 2),))
    return dict(tokens=tokens, cotangent=cotangent, lengths=lengths, order=order, routes=routes, norm1=norm1, query_key_value_weight=query_key_value_weight, w_out=w_out, norm2=norm2, router=router, w_gate=w_gate, w_up=w_up, w_down=w_down)


epsilon = 1e-06
rope_base = 10000.0
highest = lax.Precision.HIGHEST

@jax.custom_vjp
def low(v):
    return lax.optimization_barrier(v.astype(jnp.bfloat16)).astype(jnp.float32)

@jax.custom_vjp
def low_back(v):
    return v

def low_keep(v):
    return (low(v), None)

def low_pass(kept, grad):
    return (grad,)

def back_keep(v):
    return (v, None)

def back_low(kept, grad):
    return (low(grad),)
low.defvjp(low_keep, low_pass)
low_back.defvjp(back_keep, back_low)

def matmul(left_side, right_side):
    return jnp.dot(left_side, right_side, precision=highest, preferred_element_type=jnp.float32)

def rms_norm(inputs, gain):
    return inputs * lax.rsqrt(lax.optimization_barrier(jnp.mean(inputs * inputs, axis=-1, keepdims=True)) + epsilon) * gain

def rope_tables(positions, head_size):
    half_size = head_size // 2
    freqs = jnp.exp(jnp.arange(half_size, dtype=jnp.float32) * (-2.0 * math.log(rope_base) / head_size))
    angles = positions.astype(jnp.float32)[:, None] * freqs[None, :]
    angles = jnp.concatenate([angles, angles], axis=1)
    return (jnp.cos(angles), jnp.sin(angles))

def rotate(value_rows):
    half_size = value_rows.shape[-1] // 2
    return jnp.concatenate([-value_rows[..., half_size:], value_rows[..., :half_size]], axis=-1)

def apply_rope(value_rows, cosine_table, sine_values):
    return value_rows * cosine_table[:, None, :] + rotate(value_rows) * sine_values[:, None, :]

def layer_forward(params, inputs, positions, seq_limit, chosen):
    gain_one, weight_qkv, weight_out, gain_two, weight_router, weight_gate, weight_up, weight_down = params
    sequence_length = inputs.shape[0]
    hidden_one = low(rms_norm(inputs, gain_one))
    projected_rows = low_back(matmul(hidden_one, weight_qkv))
    queries = projected_rows[:, :QUERY_HEADS * HEAD_WIDTH].reshape(sequence_length, QUERY_HEADS, HEAD_WIDTH)
    every_key = projected_rows[:, QUERY_HEADS * HEAD_WIDTH:(QUERY_HEADS + KEY_VALUE_HEADS) * HEAD_WIDTH].reshape(sequence_length, KEY_VALUE_HEADS, HEAD_WIDTH)
    value_rows = projected_rows[:, (QUERY_HEADS + KEY_VALUE_HEADS) * HEAD_WIDTH:].reshape(sequence_length, KEY_VALUE_HEADS, HEAD_WIDTH)
    cosine_table, sine_values = rope_tables(positions, HEAD_WIDTH)
    queries = low(low_back(apply_rope(queries, cosine_table, sine_values)))
    every_key = low(low_back(apply_rope(every_key, cosine_table, sine_values)))
    value_rows = low(value_rows)
    every_key = jnp.repeat(every_key, QUERY_HEADS // KEY_VALUE_HEADS, axis=1)
    value_rows = jnp.repeat(value_rows, QUERY_HEADS // KEY_VALUE_HEADS, axis=1)
    key_valid = positions < seq_limit
    block_rows = math.gcd(sequence_length, 512)
    blocks = sequence_length // block_rows

    @jax.checkpoint
    def attend(block_item):
        query_block, query_pos = block_item
        scores = jnp.einsum('qhd,khd->hqk', query_block, every_key, precision=highest, preferred_element_type=jnp.float32) * HEAD_WIDTH ** (-0.5)
        scores = low_back(scores)
        allowed = key_valid[None, :] & (positions[None, :] <= query_pos[:, None])
        scores = jnp.where(allowed[None], scores, -1e+30)
        top_score = lax.optimization_barrier(jnp.max(scores, axis=-1, keepdims=True))
        raised = jnp.exp(scores - top_score)
        probs_all = raised / lax.optimization_barrier(jnp.sum(raised, axis=-1, keepdims=True))
        return jnp.einsum('hqk,khd->qhd', low(probs_all), value_rows, precision=highest, preferred_element_type=jnp.float32)
    attended = lax.map(attend, (queries.reshape(blocks, block_rows, QUERY_HEADS, HEAD_WIDTH), positions.reshape(blocks, block_rows)))
    attended = low(low_back(attended.reshape(sequence_length, QUERY_HEADS * HEAD_WIDTH)))
    middle = inputs + low_back(matmul(attended, weight_out))
    hidden_two = low(rms_norm(middle, gain_two))
    logits = low_back(matmul(hidden_two, weight_router))
    picked_max = lax.optimization_barrier(jnp.max(jnp.where(chosen > 0, logits, -1e+30), axis=-1, keepdims=True))
    raised_gates = jnp.where(chosen > 0, jnp.exp(logits - picked_max), 0.0)
    gates_low = low(raised_gates / lax.optimization_barrier(jnp.sum(raised_gates, axis=-1, keepdims=True)))

    @jax.checkpoint
    def expert_step(total, expert_item):
        wgate, wup, wdown, column = expert_item
        gate_pre = low_back(matmul(hidden_two, wgate))
        up_pre = low_back(matmul(hidden_two, wup))
        activated = low(jax.nn.silu(gate_pre) * up_pre)
        expert_out = low_back(matmul(activated, wdown))
        return (total + column[:, None] * expert_out, None)
    moe_out, _ = lax.scan(expert_step, jnp.zeros_like(middle), (weight_gate, weight_up, weight_down, gates_low.T))
    return middle + moe_out

def reference(tokens, cotangent, lengths, order, routes, norm1, query_key_value_weight, w_out, norm2, router, w_gate, w_up, w_down):
    params = tuple((item.astype(jnp.float32) for item in (norm1, query_key_value_weight, w_out, norm2, router, w_gate, w_up, w_down)))
    span_rows = LEN // SPANS
    positions = (order[:, None] * span_rows + jnp.arange(span_rows, dtype=jnp.int32)[None, :]).reshape(-1).astype(jnp.int32)

    def one_slot(accum, slot_item):
        slot_tokens, slot_cot, seq_limit, slot_routes = slot_item
        chosen = lax.optimization_barrier(jnp.sum((slot_routes[:, :, None] == jnp.arange(EXPERTS, dtype=jnp.int32)[None, None, :]).astype(jnp.float32), axis=1))
        valid_rows = (positions < seq_limit).astype(jnp.float32)[:, None]
        inputs = slot_tokens.astype(jnp.float32)
        masked_cot = slot_cot.astype(jnp.float32) * valid_rows
        result, pullback = jax.vjp(lambda weights, value_rows: layer_forward(weights, value_rows, positions, seq_limit, chosen), params, inputs)
        d_params, d_inputs = pullback(masked_cot)
        accum = tuple((first + second for first, second in zip(accum, d_params)))
        return (accum, (result.astype(jnp.bfloat16), d_inputs))
    zeros_init = tuple((jnp.zeros_like(item) for item in params))
    accum, (layer_out, d_tokens) = lax.scan(one_slot, zeros_init, (tokens, cotangent, lengths, routes))
    return (layer_out, d_tokens, accum[0], accum[1], accum[2], accum[3], accum[4], accum[5], accum[6], accum[7])
```

```python
import functools
import math

import jax
import jax.numpy as jnp
from jax import lax
from jax.experimental import pallas as pl
from jax.experimental.pallas import tpu as pltpu
from jax.sharding import PartitionSpec as P

QUERY_HEADS = 16
KEY_VALUE_HEADS = 8
HEAD_WIDTH = 64
TOPK = 8

EPS = 1e-06
ROPE_BASE = 10000.0
LOG2E = math.log2(math.e)
NEG = -1e30
BF = jnp.bfloat16
F32 = jnp.float32
VMEM_LIMIT = 60 * 1024 * 1024

NT_DIMS = (((1,), (1,)), ((), ()))
TN_DIMS = (((0,), (0,)), ((), ()))


def mm(a, b):
    return jnp.dot(a, b, preferred_element_type=F32)


def mm_nt(a, b):
    return lax.dot_general(a, b, NT_DIMS, preferred_element_type=F32)


def mm_tn(a, b):
    return lax.dot_general(a, b, TN_DIMS, preferred_element_type=F32)


def params(**kw):
    return pltpu.CompilerParams(vmem_limit_bytes=VMEM_LIMIT, **kw)


def whole(shape):
    return pl.BlockSpec(shape, lambda *_: (0,) * len(shape))


def rms_parts(x):
    factor = lax.rsqrt(jnp.mean(x * x, axis=-1, keepdims=True) + EPS)
    return x * factor, factor


def qkv_kernel(tok_ref, gain_ref, w_ref, cos_ref, sin_ref, h_ref, q_ref, kv_ref):
    normed, _ = rms_parts(tok_ref[...].astype(F32))
    h = (normed * gain_ref[...]).astype(BF)
    h_ref[...] = h
    proj = mm(h, w_ref[...])
    cos, sin = cos_ref[...], sin_ref[...]
    low_half = lax.broadcasted_iota(jnp.int32, cos.shape, 1) % HEAD_WIDTH < HEAD_WIDTH // 2
    half = HEAD_WIDTH // 2
    for t in range(3):
        w = proj[:, t * 128 : (t + 1) * 128]
        rot = jnp.where(low_half, -pltpu.roll(w, 128 - half, 1), pltpu.roll(w, half, 1))
        out = (w * cos + rot * sin).astype(BF)
        if t < 2:
            q_ref[:, t * 128 : (t + 1) * 128] = out
        else:
            kv_ref[:, :128] = out
    kv_ref[:, 128:] = proj[:, 384:].astype(BF)


def project(tok, gain, w, cos, sin, tile):
    rows, width = tok.shape
    return pl.pallas_call(
        qkv_kernel,
        grid=(rows // tile,),
        in_specs=[
            pl.BlockSpec((tile, width), lambda i: (i, 0)),
            whole((1, width)),
            whole(w.shape),
            pl.BlockSpec((tile, 128), lambda i: (i, 0)),
            pl.BlockSpec((tile, 128), lambda i: (i, 0)),
        ],
        out_specs=[
            pl.BlockSpec((tile, width), lambda i: (i, 0)),
            pl.BlockSpec((tile, 256), lambda i: (i, 0)),
            pl.BlockSpec((tile, 256), lambda i: (i, 0)),
        ],
        out_shape=[
            jax.ShapeDtypeStruct((rows, width), BF),
            jax.ShapeDtypeStruct((rows, 256), BF),
            jax.ShapeDtypeStruct((rows, 256), BF),
        ],
        compiler_params=params(),
        name="project",
    )(tok, gain, w, cos, sin)


def project_back_kernel(
    tok_ref, h_ref, dq_ref, dkv_ref, w_ref, cos_ref, sin_ref, dh_ref, gw_ref, gn_ref, acc
):
    step = pl.program_id(0)

    @pl.when(step == 0)
    def _():
        acc[...] = jnp.zeros_like(acc)
        gn_ref[...] = jnp.zeros_like(gn_ref)

    cos, sin = cos_ref[...], sin_ref[...]
    half = HEAD_WIDTH // 2
    low_half = lax.broadcasted_iota(jnp.int32, cos.shape, 1) % HEAD_WIDTH < half
    parts = []
    for t in range(3):
        w = dq_ref[:, t * 128 : (t + 1) * 128] if t < 2 else dkv_ref[:, :128]
        w = w.astype(F32)
        y = w * sin
        rot = jnp.where(low_half, pltpu.roll(y, 128 - half, 1), -pltpu.roll(y, half, 1))
        parts.append((w * cos + rot).astype(BF))
    parts.append(dkv_ref[:, 128:].astype(BF))
    dproj = jnp.concatenate(parts, axis=1)
    acc[...] += mm_tn(h_ref[...], dproj)
    dh = mm_nt(dproj, w_ref[...])
    dh_ref[...] = dh.astype(BF)
    normed, _ = rms_parts(tok_ref[...].astype(F32))
    gn_ref[...] += jnp.sum((dh * normed).reshape(-1, 8, dh.shape[1]), axis=0)

    @pl.when(step == pl.num_programs(0) - 1)
    def _():
        gw_ref[...] = acc[...].astype(BF)


def project_back(tok, h, dq, dkv, w, cos, sin, tile):
    rows, width = tok.shape
    row = lambda n: pl.BlockSpec((tile, n), lambda i: (i, 0))
    return pl.pallas_call(
        project_back_kernel,
        grid=(rows // tile,),
        in_specs=[row(width), row(width), row(256), row(256), whole(w.shape), row(128), row(128)],
        out_specs=[row(width), whole(w.shape), whole((8, width))],
        out_shape=[
            jax.ShapeDtypeStruct((rows, width), BF),
            jax.ShapeDtypeStruct(w.shape, BF),
            jax.ShapeDtypeStruct((8, width), F32),
        ],
        scratch_shapes=[pltpu.VMEM(w.shape, F32)],
        compiler_params=params(),
        name="project_back",
    )(tok, h, dq, dkv, w, cos, sin)


def stack_heads(a, b):
    low = lax.broadcasted_iota(jnp.int32, a.shape, 1) < HEAD_WIDTH
    zero = jnp.zeros_like(a)
    return jnp.concatenate(
        [jnp.where(low, a, zero), jnp.where(low, b, zero), jnp.where(low, zero, a), jnp.where(low, zero, b)],
        axis=0,
    )


def unstack_heads(x):
    n = x.shape[0] // 4
    low = lax.broadcasted_iota(jnp.int32, (n, 128), 1) < HEAD_WIDTH
    return (
        jnp.where(low, x[:n], x[2 * n : 3 * n]),
        jnp.where(low, x[n : 2 * n], x[3 * n :]),
    )


def block_counts(span_id, limit, span, kb):
    first = span_id * span
    seen = (first + span - 1) // kb + 1
    blocks = jnp.minimum(seen, (limit + kb - 1) // kb)
    full = jnp.minimum(first + 1, limit) // kb
    return jnp.minimum(full, blocks), blocks


def sort_spans(ktab_ref, src, dst, lanes, span, count):
    @pl.loop(0, count)
    def _(j):
        to = pl.multiple_of(ktab_ref[j] * span, span)
        dst[pl.ds(to, span), :] = src[pl.ds(pl.multiple_of(j * span, span), span), lanes]


def attend_kernel(
    qtab_ref, ktab_ref, len_ref, q_ref, kv_ref, o_ref, lse_ref, ks, vs, *, span, kb
):
    step = pl.program_id(0)
    count = ks.shape[0] // span

    @pl.when(step == 0)
    def _():
        sort_spans(ktab_ref, kv_ref, ks, slice(0, 128), span, count)
        sort_spans(ktab_ref, kv_ref, vs, slice(128, 256), span, count)

    q = stack_heads(q_ref[:, :128], q_ref[:, 128:])
    rows = 4 * span
    limit = len_ref[0]
    span_id = qtab_ref[step]
    full, blocks = block_counts(span_id, limit, span, kb)
    qpos = span_id * span + lax.broadcasted_iota(jnp.int32, (rows, kb), 0) % span
    col = lax.broadcasted_iota(jnp.int32, (rows, kb), 1)
    last = jnp.minimum(qpos, limit - 1)

    def body(masked, i, carry):
        top, total, acc = carry
        at = pl.multiple_of(i * kb, kb)
        s = mm_nt(q, ks[pl.ds(at, kb), :]) * (HEAD_WIDTH**-0.5 * LOG2E)
        if masked:
            s = jnp.where(col + i * kb <= last, s, NEG)
        new = jnp.maximum(top, jnp.max(s, axis=1, keepdims=True))
        fade = jnp.exp2(top - new)
        p = jnp.exp2(s - new)
        total = total * fade + jnp.sum(p, axis=1, keepdims=True)
        acc = acc * fade + mm(p.astype(BF), vs[pl.ds(at, kb), :])
        return new, total, acc

    carry = (
        jnp.full((rows, 1), NEG, F32),
        jnp.zeros((rows, 1), F32),
        jnp.zeros((rows, 128), F32),
    )
    carry = lax.fori_loop(0, full, functools.partial(body, False), carry)
    top, total, acc = lax.fori_loop(full, blocks, functools.partial(body, True), carry)
    a, b = unstack_heads(acc / total)
    o_ref[:, :128] = a
    o_ref[:, 128:] = b
    lse = jnp.broadcast_to(top + jnp.log2(total), (rows, 128))
    lse_ref[0] = jnp.transpose(lse)[:8]


def attend(qtab, ktab, limit, q, kv, span, kb):
    steps, keys = q.shape[0] // span, kv.shape[0]
    return pl.pallas_call(
        functools.partial(attend_kernel, span=span, kb=kb),
        grid_spec=pltpu.PrefetchScalarGridSpec(
            num_scalar_prefetch=3,
            grid=(steps,),
            in_specs=[pl.BlockSpec((span, 256), lambda i, *_: (i, 0)), whole(kv.shape)],
            out_specs=[
                pl.BlockSpec((span, 256), lambda i, *_: (i, 0)),
                pl.BlockSpec((1, 8, 4 * span), lambda i, *_: (i, 0, 0)),
            ],
            scratch_shapes=[pltpu.VMEM((keys, 128), BF), pltpu.VMEM((keys, 128), BF)],
        ),
        out_shape=[
            jax.ShapeDtypeStruct((q.shape[0], 256), F32),
            jax.ShapeDtypeStruct((steps, 8, 4 * span), F32),
        ],
        compiler_params=params(),
        name="attend",
    )(qtab, ktab, limit, q, kv)


def attend_back_kernel(
    qtab_ref, ktab_ref, len_ref, q_ref, kv_ref, do_ref, o_ref, lse_ref, dq_ref, dkv_ref,
    ks, vs, dk, dv, *, span, kb,
):
    step = pl.program_id(0)
    count = ks.shape[0] // span
    scale = HEAD_WIDTH**-0.5

    @pl.when(step == 0)
    def _():
        sort_spans(ktab_ref, kv_ref, ks, slice(0, 128), span, count)
        sort_spans(ktab_ref, kv_ref, vs, slice(128, 256), span, count)
        dk[...] = jnp.zeros_like(dk)
        dv[...] = jnp.zeros_like(dv)

    q = stack_heads(q_ref[:, :128], q_ref[:, 128:])
    do = stack_heads(do_ref[:, :128], do_ref[:, 128:])
    rows = 4 * span
    inner = do.astype(F32) * stack_heads(o_ref[:, :128], o_ref[:, 128:])
    delta = jnp.sum(jnp.transpose(inner), axis=0, keepdims=True)
    lse = lse_ref[0, :1]
    limit = len_ref[0]
    span_id = qtab_ref[step]
    full, blocks = block_counts(span_id, limit, span, kb)
    blocks = jnp.where(span_id * span < limit, blocks, 0)
    full = jnp.minimum(full, blocks)
    qpos = span_id * span + lax.broadcasted_iota(jnp.int32, (kb, rows), 1) % span
    key = lax.broadcasted_iota(jnp.int32, (kb, rows), 0)
    last = jnp.minimum(qpos, limit - 1)

    def body(masked, i, dq):
        at = pl.ds(pl.multiple_of(i * kb, kb), kb)
        k, v = ks[at, :], vs[at, :]
        s = mm_nt(k, q) * (scale * LOG2E)
        p = jnp.exp2(s - lse)
        if masked:
            p = jnp.where(key + i * kb <= last, p, 0.0)
        dp = mm_nt(v, do)
        ds = (p * (dp - delta)).astype(BF)
        dk[at, :] += mm(ds, q)
        dv[at, :] += mm(p.astype(BF), do)
        return dq + mm_tn(ds, k)

    dq = jnp.zeros((rows, 128), F32)
    dq = lax.fori_loop(0, full, functools.partial(body, False), dq)
    dq = lax.fori_loop(full, blocks, functools.partial(body, True), dq)
    a, b = unstack_heads(dq * scale)
    dq_ref[:, :128] = a.astype(BF)
    dq_ref[:, 128:] = b.astype(BF)

    @pl.when(step == pl.num_programs(0) - 1)
    def _():
        @pl.loop(0, count)
        def _(j):
            at = pl.ds(pl.multiple_of(ktab_ref[j] * span, span), span)
            to = pl.ds(pl.multiple_of(j * span, span), span)
            dkv_ref[to, :128] = (dk[at, :] * scale).astype(BF)
            dkv_ref[to, 128:] = dv[at, :].astype(BF)


def attend_back(qtab, ktab, limit, q, kv, do, o, lse, span, kb):
    steps, keys = q.shape[0] // span, kv.shape[0]
    row = pl.BlockSpec((span, 256), lambda i, *_: (i, 0))
    return pl.pallas_call(
        functools.partial(attend_back_kernel, span=span, kb=kb),
        grid_spec=pltpu.PrefetchScalarGridSpec(
            num_scalar_prefetch=3,
            grid=(steps,),
            in_specs=[
                row, whole(kv.shape), row, row,
                pl.BlockSpec((1, 8, 4 * span), lambda i, *_: (i, 0, 0)),
            ],
            out_specs=[row, whole(kv.shape)],
            scratch_shapes=[
                pltpu.VMEM((keys, 128), BF), pltpu.VMEM((keys, 128), BF),
                pltpu.VMEM((keys, 128), F32), pltpu.VMEM((keys, 128), F32),
            ],
        ),
        out_shape=[
            jax.ShapeDtypeStruct((q.shape[0], 256), BF),
            jax.ShapeDtypeStruct(kv.shape, BF),
        ],
        compiler_params=params(),
        name="attend_back",
    )(qtab, ktab, limit, q, kv, do, o, lse)


def experts_kernel(
    base_ref, h_ref, c_ref, wg_ref, wu_ref, wd_ref, moe_ref, dh_ref, gg_ref, gu_ref, gd_ref,
    moe, dh, dgates, s_act, s_gate, s_up, *, tile,
):
    step = pl.program_id(0)
    width = c_ref.shape[1]
    expert = base_ref[1] + step
    wg, wu, wd = wg_ref[0], wu_ref[0], wd_ref[0]

    @pl.when(step == 0)
    def _():
        moe[...] = jnp.zeros_like(moe)
        dh[...] = jnp.zeros_like(dh)
        dgates[...] = jnp.zeros_like(dgates)

    @pl.loop(0, moe.shape[0] // tile)
    def _(t):
        at = pl.ds(pl.multiple_of(t * tile, tile), tile)
        h, c = h_ref[at, :width], c_ref[at, :]
        lane = lax.broadcasted_iota(jnp.int32, (tile, 128), 1)
        mine = lane == expert
        gate = jnp.sum(
            jnp.where(mine, h_ref[at, width:].astype(F32), 0.0), axis=1, keepdims=True
        )
        g, u, z = mm(h, wg), mm(h, wu), mm_nt(c, wd)
        sig = jax.nn.sigmoid(g)
        silu = g * sig
        act = silu * u
        dgates[at, :] += jnp.where(mine, jnp.sum(act * z, axis=1, keepdims=True), 0.0)
        act = (act * gate).astype(BF)
        dact = z * gate
        dgate = (dact * u * sig * (1.0 + g * (1.0 - sig))).astype(BF)
        dup = (dact * silu).astype(BF)
        s_act[at, :] = act
        s_gate[at, :] = dgate
        s_up[at, :] = dup
        moe[at, :] += mm(act, wd)
        dh[at, :] += mm_nt(dgate, wg) + mm_nt(dup, wu)

    for i in range(4):
        n = width // 4
        gg_ref[0, i * n : (i + 1) * n, :] = mm_tn(h_ref[:, i * n : (i + 1) * n], s_gate[...]).astype(BF)
        gu_ref[0, i * n : (i + 1) * n, :] = mm_tn(h_ref[:, i * n : (i + 1) * n], s_up[...]).astype(BF)
    for i in range(2):
        n = wd.shape[0] // 2
        gd_ref[0, i * n : (i + 1) * n, :] = mm_tn(s_act[:, i * n : (i + 1) * n], c_ref[...]).astype(BF)

    @pl.when(step == pl.num_programs(0) - 1)
    def _():
        moe_ref[...] = moe[...].astype(BF)
        dh_ref[:, :width] = dh[...].astype(BF)
        dh_ref[:, width:] = dgates[...].astype(BF)


def experts(base, count, h, c, wg, wu, wd, tile):
    rows, width = c.shape
    ff = wg.shape[2]
    pick = lambda shape: pl.BlockSpec((1,) + shape, lambda e, s: (s[0] + e, 0, 0))
    put = lambda shape: pl.BlockSpec((1,) + shape, lambda e, s: (e, 0, 0))
    return pl.pallas_call(
        functools.partial(experts_kernel, tile=tile),
        grid_spec=pltpu.PrefetchScalarGridSpec(
            num_scalar_prefetch=1,
            grid=(count,),
            in_specs=[
                whole(h.shape), whole(c.shape),
                pick((width, ff)), pick((width, ff)), pick((ff, width)),
            ],
            out_specs=[
                whole(c.shape), whole(h.shape),
                put((width, ff)), put((width, ff)), put((ff, width)),
            ],
            scratch_shapes=[
                pltpu.VMEM((rows, width), F32), pltpu.VMEM((rows, width), F32),
                pltpu.VMEM((rows, 128), F32),
                pltpu.VMEM((rows, ff), BF), pltpu.VMEM((rows, ff), BF), pltpu.VMEM((rows, ff), BF),
            ],
        ),
        out_shape=[
            jax.ShapeDtypeStruct(c.shape, BF),
            jax.ShapeDtypeStruct(h.shape, BF),
            jax.ShapeDtypeStruct((count, width, ff), BF),
            jax.ShapeDtypeStruct((count, width, ff), BF),
            jax.ShapeDtypeStruct((count, ff, width), BF),
        ],
        compiler_params=params(),
        name="experts",
    )(base, h, c, wg, wu, wd)


def flip_core(x):
    return lax.ppermute(x, "seq", [(0, 1), (1, 0), (2, 3), (3, 2)])


def flip_x(x):
    return lax.ppermute(x, "seq", [(0, 2), (2, 0), (1, 3), (3, 1)])


def flip_both(x):
    return lax.ppermute(x, "seq", [(0, 3), (3, 0), (1, 2), (2, 1)])


def gather_seq(x):
    own = jnp.stack([x, flip_core(x)])
    far = flip_x(x)
    return jnp.concatenate([own, far[None], flip_core(far)[None]])


def swap_seq(blocks):
    return [blocks[0], flip_core(blocks[1]), flip_x(blocks[2]), flip_both(blocks[3])]


def gather_fsdp(x, axis=0):
    if lax.axis_size("fsdp") == 2:
        return jnp.concatenate([x, lax.ppermute(x, "fsdp", [(0, 1), (1, 0)])], axis=axis)
    return lax.all_gather(x, "fsdp", axis=axis, tiled=True)


def scatter_fsdp(x):
    if lax.axis_size("fsdp") == 2:
        n = x.shape[0] // 2
        other = lax.ppermute(x[n:], "fsdp", [(0, 1), (1, 0)])
        return x[:n].astype(F32) + other.astype(F32)
    return lax.psum_scatter(x, "fsdp", scatter_dimension=0, tiled=True).astype(F32)


def gather_rows(x):
    return lax.all_gather(x, "fsdp", axis=0, tiled=True)


def local(
    tokens, cotangent, lengths, order, routes, norm1, query_key_value_weight, w_out, norm2, router,
    w_gate, w_up, w_down,
):
    groups = lax.axis_size("seq")
    shards = lax.axis_size("fsdp")
    slots = lax.axis_size("dp")
    assert groups == 4
    seq, fsdp = lax.axis_index("seq"), lax.axis_index("fsdp")
    core = seq % 2
    rows, width = tokens.shape[1:]
    span = rows // 2
    x = tokens[0]
    limit = lengths[:1]
    n_experts = router.shape[1]
    owned = w_gate.shape[0]
    count = owned // 2

    table = order.reshape(groups, shards, 2)
    relative = jnp.arange(groups, dtype=jnp.int32) ^ seq
    table = jnp.take(table, relative, axis=0)
    qtab = jnp.take(table, fsdp, axis=1).reshape(-1)
    if shards == 2:
        held = jnp.stack([fsdp, 1 - fsdp])
    else:
        held = jnp.arange(shards)
    ktab = jnp.transpose(jnp.take(table, held, axis=1), (1, 0, 2)).reshape(-1)
    qpos = (qtab[:, None] * span + jnp.arange(span, dtype=jnp.int32)[None, :]).reshape(-1)
    half = HEAD_WIDTH // 2
    freqs = jnp.exp(jnp.arange(half, dtype=F32) * (-2.0 * math.log(ROPE_BASE) / HEAD_WIDTH))
    angles = qpos.astype(F32)[:, None] * freqs[None, :]
    cos = jnp.tile(jnp.cos(angles), (1, 4))
    sin = jnp.tile(jnp.sin(angles), (1, 4))

    heads = QUERY_HEADS // groups
    qw, kw = heads * HEAD_WIDTH, KEY_VALUE_HEADS // groups * HEAD_WIDTH
    w3 = query_key_value_weight
    wq = lax.dynamic_slice_in_dim(w3, seq * qw, qw, 1).reshape(-1, 2, 2, HEAD_WIDTH)
    wq = jnp.swapaxes(wq, 1, 2).reshape(-1, qw)
    wk = lax.dynamic_slice_in_dim(w3, QUERY_HEADS * HEAD_WIDTH + seq * kw, kw, 1)
    wv = lax.dynamic_slice_in_dim(w3, (QUERY_HEADS + KEY_VALUE_HEADS) * HEAD_WIDTH + seq * kw, kw, 1)
    wcols = gather_rows(jnp.concatenate([wq, wk, wv], axis=1))
    small = jnp.concatenate([norm1[:, None], norm2[:, None], router], axis=1)
    small = gather_rows(small)
    gain_one = small[:, 0].astype(F32)
    gain_two = small[:, 1].astype(F32)
    route_full = small[:, 2:]
    out_full = gather_rows(w_out)

    tok = gather_seq(x).reshape(groups * rows, width)
    hidden_one, q, kv_own = project(tok, gain_one[None], wcols, cos, sin, rows)
    kv = gather_fsdp(kv_own)
    kb = 4 * span
    attended, lse = attend(qtab, ktab, limit, q, kv, span, kb)
    sent = attended.astype(BF).reshape(groups, rows, qw)
    got = jnp.stack(swap_seq([sent[m] for m in range(groups)]))
    got = jnp.take(got, relative, axis=0).reshape(groups, rows, 2, 2, HEAD_WIDTH)
    token_out = jnp.transpose(got, (1, 0, 3, 2, 4)).reshape(rows, groups * qw)

    own_valid = (qpos[:rows] < limit[0])[:, None]
    inputs = x.astype(F32)
    middle = inputs + mm(token_out, out_full)
    normed_two, factor_two = rms_parts(middle)
    hidden_two = (normed_two * gain_two).astype(BF)
    logits = mm(hidden_two, route_full)
    chosen = jnp.any(
        routes[0][:, :, None] == jnp.arange(n_experts, dtype=jnp.int32)[None, None, :], axis=1
    )
    top = jnp.max(jnp.where(chosen, logits, NEG), axis=-1, keepdims=True)
    raised = jnp.where(chosen, jnp.exp(logits - top), 0.0)
    gates = raised / jnp.sum(raised, axis=-1, keepdims=True)
    masked_cot = jnp.where(own_valid, cotangent[0], jnp.zeros_like(cotangent[0]))

    def share(v):
        near = gather_fsdp(v)
        return jnp.concatenate([near, flip_core(near)])

    cot_all = share(masked_cot)
    extended = jnp.concatenate(
        [hidden_two, gates.astype(BF), jnp.zeros((rows, 128 - n_experts), BF)], axis=1
    )
    hid_all = share(extended)
    base = jnp.stack([core * count, fsdp * owned + core * count]).astype(jnp.int32)
    part = rows * 4
    moe_parts, dh_parts, weight_grads = [], [], None
    for i in range(hid_all.shape[0] // part):
        got = experts(
            base, count, hid_all[i * part : (i + 1) * part], cot_all[i * part : (i + 1) * part],
            w_gate, w_up, w_down, rows,
        )
        moe_parts.append(got[0])
        dh_parts.append(got[1])
        if weight_grads is None:
            weight_grads = list(got[2:])
        else:
            weight_grads = [a.astype(F32) + b.astype(F32) for a, b in zip(weight_grads, got[2:])]
            weight_grads = [a.astype(BF) for a in weight_grads]

    def give_back(parts):
        v = jnp.concatenate(parts) if len(parts) > 1 else parts[0]
        n = v.shape[0] // 2
        near = v[:n].astype(F32) + flip_core(v[n:]).astype(F32)
        return scatter_fsdp(near.astype(BF))

    d_ext = give_back(dh_parts)
    d_gates = d_ext[:, width : width + n_experts]
    d_logits = (gates * (d_gates - jnp.sum(gates * d_gates, axis=-1, keepdims=True))).astype(BF)
    grad_router = mm_tn(hidden_two, d_logits)
    d_hidden = d_ext[:, :width] + mm_nt(d_logits, route_full)
    grad_norm2 = jnp.sum(d_hidden * normed_two, axis=0)
    d_n = d_hidden * gain_two
    d_middle = masked_cot.astype(F32) + factor_two * (
        d_n - normed_two * jnp.mean(d_n * normed_two, axis=-1, keepdims=True)
    )
    d_attn = d_middle.astype(BF)
    grad_out = mm_tn(token_out, d_attn).astype(BF)
    d_token_out = mm_nt(d_attn, out_full).astype(BF)
    d_heads = d_token_out.reshape(rows, groups, 2, 2, HEAD_WIDTH)
    d_heads = jnp.transpose(d_heads, (1, 0, 3, 2, 4)).reshape(groups, rows, qw)
    d_heads = jnp.take(d_heads, relative, axis=0)
    d_heads = jnp.concatenate(swap_seq([d_heads[m] for m in range(groups)]))
    dq, dkv = attend_back(qtab, ktab, limit, q, kv, d_heads, attended, lse, span, kb)
    dkv = scatter_fsdp(dkv)
    dh_one, grad_cols, grad_norm1 = project_back(
        tok, hidden_one, dq, dkv, wcols, cos, sin, rows
    )
    dh_one = dh_one.reshape(groups, rows, width)
    near = dh_one[0::2].astype(F32) + flip_core(dh_one[1::2]).astype(F32)
    d_hidden_one = near[0] + flip_x(near[1].astype(BF)).astype(F32)
    normed_one, factor_one = rms_parts(inputs)
    d_n = d_hidden_one * gain_one
    d_inputs = d_middle + factor_one * (
        d_n - normed_one * jnp.mean(d_n * normed_one, axis=-1, keepdims=True)
    )

    every = ("dp", "seq")
    fold = [[d * groups + 2 * i + c for d in range(slots) for i in range(groups // 2)] for c in range(2)]

    def reduce_experts(g):
        part = lax.psum_scatter(
            g, every, scatter_dimension=1, tiled=True, axis_index_groups=fold
        )
        full = lax.all_gather(part, every, axis=0)
        n, r, m = part.shape
        full = full.reshape(slots, groups // 2, 2, n, r, m)
        full = jnp.transpose(full, (2, 3, 0, 1, 4, 5))
        return full.reshape(2 * n, slots * groups // 2 * r, m).astype(F32)

    grad_gate, grad_up, grad_down = [reduce_experts(g) for g in weight_grads]
    shard_out = lax.psum(
        lax.psum_scatter(grad_out, "fsdp", scatter_dimension=0, tiled=True), every
    ).astype(F32)
    shard_cols = lax.psum(
        lax.psum_scatter(grad_cols, "fsdp", scatter_dimension=0, tiled=True), "dp"
    )
    cols = lax.all_gather(shard_cols, "seq", axis=0)
    gq = cols[:, :, :qw].reshape(groups, -1, 2, 2, HEAD_WIDTH)
    gq = jnp.transpose(gq, (1, 0, 3, 2, 4)).reshape(-1, groups * qw)
    gk = jnp.transpose(cols[:, :, qw : qw + kw], (1, 0, 2)).reshape(-1, groups * kw)
    gv = jnp.transpose(cols[:, :, qw + kw :], (1, 0, 2)).reshape(-1, groups * kw)
    shard_qkv = jnp.concatenate([gq, gk, gv], axis=1).astype(F32)
    tiny = jnp.concatenate(
        [jnp.sum(grad_norm1, axis=0)[:, None], grad_norm2[:, None], grad_router], axis=1
    )
    tiny = lax.psum(lax.psum_scatter(tiny, "fsdp", scatter_dimension=0, tiled=True), every)
    layer_out = (middle + give_back(moe_parts)).astype(BF)
    return (
        layer_out[None], d_inputs[None], tiny[:, 0], shard_qkv, shard_out, tiny[:, 1], tiny[:, 2:],
        grad_gate, grad_up, grad_down,
    )


def solution(mesh):
    placed = (
        P("dp", ("seq", "fsdp"), None),
        P("dp", ("seq", "fsdp"), None),
        P("dp"),
        P(),
        P("dp", ("seq", "fsdp"), None),
        P("fsdp"),
        P("fsdp", None),
        P("fsdp", None),
        P("fsdp"),
        P("fsdp", None),
        P("fsdp", None, None),
        P("fsdp", None, None),
        P("fsdp", None, None),
    )
    return jax.shard_map(
        local,
        mesh=mesh,
        in_specs=placed,
        out_specs=(
            P("dp", ("seq", "fsdp"), None),
            P("dp", ("seq", "fsdp"), None),
            P("fsdp"),
            P("fsdp", None),
            P("fsdp", None),
            P("fsdp"),
            P("fsdp", None),
            P("fsdp", None, None),
            P("fsdp", None, None),
            P("fsdp", None, None),
        ),
        check_vma=False,
    )
```

```python
import functools
import math

import jax
import jax.numpy as jnp
from jax import lax
from jax.experimental import pallas as pl
from jax.experimental.pallas import tpu as pltpu
from jax.sharding import PartitionSpec as P

QUERY_HEADS = 16
KEY_VALUE_HEADS = 8
HEAD_WIDTH = 64
TOPK = 8

EPS = 1e-06
ROPE_BASE = 10000.0
LOG2E = math.log2(math.e)
NEG = -1e30
BF = jnp.bfloat16
F32 = jnp.float32
VMEM_LIMIT = 60 * 1024 * 1024

NT_DIMS = (((1,), (1,)), ((), ()))
TN_DIMS = (((0,), (0,)), ((), ()))


def mm(a, b):
    return jnp.dot(a, b, preferred_element_type=F32)


def mm_nt(a, b):
    return lax.dot_general(a, b, NT_DIMS, preferred_element_type=F32)


def mm_tn(a, b):
    return lax.dot_general(a, b, TN_DIMS, preferred_element_type=F32)


def params(**kw):
    return pltpu.CompilerParams(vmem_limit_bytes=VMEM_LIMIT, **kw)


def whole(shape):
    return pl.BlockSpec(shape, lambda *_: (0,) * len(shape))


def rms_parts(x):
    factor = lax.rsqrt(jnp.mean(x * x, axis=-1, keepdims=True) + EPS)
    return x * factor, factor


def qkv_kernel(tok_ref, gain_ref, w_ref, cos_ref, sin_ref, h_ref, q_ref, kv_ref):
    normed, _ = rms_parts(tok_ref[...].astype(F32))
    h = (normed * gain_ref[...]).astype(BF)
    h_ref[...] = h
    proj = mm(h, w_ref[...])
    cos, sin = cos_ref[...], sin_ref[...]
    low_half = lax.broadcasted_iota(jnp.int32, cos.shape, 1) % HEAD_WIDTH < HEAD_WIDTH // 2
    half = HEAD_WIDTH // 2
    for t in range(3):
        w = proj[:, t * 128 : (t + 1) * 128]
        rot = jnp.where(low_half, -pltpu.roll(w, 128 - half, 1), pltpu.roll(w, half, 1))
        out = (w * cos + rot * sin).astype(BF)
        if t < 2:
            q_ref[:, t * 128 : (t + 1) * 128] = out
        else:
            kv_ref[:, :128] = out
    kv_ref[:, 128:] = proj[:, 384:].astype(BF)


def project(tok, gain, w, cos, sin, tile):
    rows, width = tok.shape
    return pl.pallas_call(
        qkv_kernel,
        grid=(rows // tile,),
        in_specs=[
            pl.BlockSpec((tile, width), lambda i: (i, 0)),
            whole((1, width)),
            whole(w.shape),
            pl.BlockSpec((tile, 128), lambda i: (i, 0)),
            pl.BlockSpec((tile, 128), lambda i: (i, 0)),
        ],
        out_specs=[
            pl.BlockSpec((tile, width), lambda i: (i, 0)),
            pl.BlockSpec((tile, 256), lambda i: (i, 0)),
            pl.BlockSpec((tile, 256), lambda i: (i, 0)),
        ],
        out_shape=[
            jax.ShapeDtypeStruct((rows, width), BF),
            jax.ShapeDtypeStruct((rows, 256), BF),
            jax.ShapeDtypeStruct((rows, 256), BF),
        ],
        compiler_params=params(),
        name="project",
    )(tok, gain, w, cos, sin)


def project_back_kernel(
    tok_ref, h_ref, dq_ref, dkv_ref, w_ref, cos_ref, sin_ref, dh_ref, gw_ref, gn_ref, acc
):
    step = pl.program_id(0)

    @pl.when(step == 0)
    def _():
        acc[...] = jnp.zeros_like(acc)
        gn_ref[...] = jnp.zeros_like(gn_ref)

    cos, sin = cos_ref[...], sin_ref[...]
    half = HEAD_WIDTH // 2
    low_half = lax.broadcasted_iota(jnp.int32, cos.shape, 1) % HEAD_WIDTH < half
    parts = []
    for t in range(3):
        w = dq_ref[:, t * 128 : (t + 1) * 128] if t < 2 else dkv_ref[:, :128]
        w = w.astype(F32)
        y = w * sin
        rot = jnp.where(low_half, pltpu.roll(y, 128 - half, 1), -pltpu.roll(y, half, 1))
        parts.append((w * cos + rot).astype(BF))
    parts.append(dkv_ref[:, 128:].astype(BF))
    dproj = jnp.concatenate(parts, axis=1)
    acc[...] += mm_tn(h_ref[...], dproj)
    dh = mm_nt(dproj, w_ref[...])
    dh_ref[...] = dh.astype(BF)
    normed, _ = rms_parts(tok_ref[...].astype(F32))
    gn_ref[...] += jnp.sum((dh * normed).reshape(-1, 8, dh.shape[1]), axis=0)

    @pl.when(step == pl.num_programs(0) - 1)
    def _():
        gw_ref[...] = acc[...].astype(BF)


def project_back(tok, h, dq, dkv, w, cos, sin, tile):
    rows, width = tok.shape
    row = lambda n: pl.BlockSpec((tile, n), lambda i: (i, 0))
    return pl.pallas_call(
        project_back_kernel,
        grid=(rows // tile,),
        in_specs=[row(width), row(width), row(256), row(256), whole(w.shape), row(128), row(128)],
        out_specs=[row(width), whole(w.shape), whole((8, width))],
        out_shape=[
            jax.ShapeDtypeStruct((rows, width), BF),
            jax.ShapeDtypeStruct(w.shape, BF),
            jax.ShapeDtypeStruct((8, width), F32),
        ],
        scratch_shapes=[pltpu.VMEM(w.shape, F32)],
        compiler_params=params(),
        name="project_back",
    )(tok, h, dq, dkv, w, cos, sin)


def stack_heads(a, b):
    low = lax.broadcasted_iota(jnp.int32, a.shape, 1) < HEAD_WIDTH
    zero = jnp.zeros_like(a)
    return jnp.concatenate(
        [jnp.where(low, a, zero), jnp.where(low, b, zero), jnp.where(low, zero, a), jnp.where(low, zero, b)],
        axis=0,
    )


def unstack_heads(x):
    n = x.shape[0] // 4
    low = lax.broadcasted_iota(jnp.int32, (n, 128), 1) < HEAD_WIDTH
    return (
        jnp.where(low, x[:n], x[2 * n : 3 * n]),
        jnp.where(low, x[n : 2 * n], x[3 * n :]),
    )


def block_counts(span_id, limit, span, kb):
    first = span_id * span
    seen = (first + span - 1) // kb + 1
    blocks = jnp.minimum(seen, (limit + kb - 1) // kb)
    full = jnp.minimum(first + 1, limit) // kb
    return jnp.minimum(full, blocks), blocks


def sort_spans(ktab_ref, src, dst, lanes, span, count):
    @pl.loop(0, count)
    def _(j):
        to = pl.multiple_of(ktab_ref[j] * span, span)
        dst[pl.ds(to, span), :] = src[pl.ds(pl.multiple_of(j * span, span), span), lanes]


def attend_kernel(
    qtab_ref, ktab_ref, len_ref, q_ref, kv_ref, o_ref, lse_ref, ks, vs, *, span, kb
):
    step = pl.program_id(0)
    count = ks.shape[0] // span

    @pl.when(step == 0)
    def _():
        sort_spans(ktab_ref, kv_ref, ks, slice(0, 128), span, count)
        sort_spans(ktab_ref, kv_ref, vs, slice(128, 256), span, count)

    q = stack_heads(q_ref[:, :128], q_ref[:, 128:])
    rows = 4 * span
    limit = len_ref[0]
    span_id = qtab_ref[step]
    full, blocks = block_counts(span_id, limit, span, kb)
    qpos = span_id * span + lax.broadcasted_iota(jnp.int32, (rows, kb), 0) % span
    col = lax.broadcasted_iota(jnp.int32, (rows, kb), 1)
    last = jnp.minimum(qpos, limit - 1)

    def body(masked, i, carry):
        top, total, acc = carry
        at = pl.multiple_of(i * kb, kb)
        s = mm_nt(q, ks[pl.ds(at, kb), :]) * (HEAD_WIDTH**-0.5 * LOG2E)
        if masked:
            s = jnp.where(col + i * kb <= last, s, NEG)
        new = jnp.maximum(top, jnp.max(s, axis=1, keepdims=True))
        fade = jnp.exp2(top - new)
        p = jnp.exp2(s - new)
        total = total * fade + jnp.sum(p, axis=1, keepdims=True)
        acc = acc * fade + mm(p.astype(BF), vs[pl.ds(at, kb), :])
        return new, total, acc

    carry = (
        jnp.full((rows, 1), NEG, F32),
        jnp.zeros((rows, 1), F32),
        jnp.zeros((rows, 128), F32),
    )
    carry = lax.fori_loop(0, full, functools.partial(body, False), carry)
    top, total, acc = lax.fori_loop(full, blocks, functools.partial(body, True), carry)
    a, b = unstack_heads(acc / total)
    o_ref[:, :128] = a
    o_ref[:, 128:] = b
    lse = jnp.broadcast_to(top + jnp.log2(total), (rows, 128))
    lse_ref[0] = jnp.transpose(lse)[:8]


def attend(qtab, ktab, limit, q, kv, span, kb):
    steps, keys = q.shape[0] // span, kv.shape[0]
    return pl.pallas_call(
        functools.partial(attend_kernel, span=span, kb=kb),
        grid_spec=pltpu.PrefetchScalarGridSpec(
            num_scalar_prefetch=3,
            grid=(steps,),
            in_specs=[pl.BlockSpec((span, 256), lambda i, *_: (i, 0)), whole(kv.shape)],
            out_specs=[
                pl.BlockSpec((span, 256), lambda i, *_: (i, 0)),
                pl.BlockSpec((1, 8, 4 * span), lambda i, *_: (i, 0, 0)),
            ],
            scratch_shapes=[pltpu.VMEM((keys, 128), BF), pltpu.VMEM((keys, 128), BF)],
        ),
        out_shape=[
            jax.ShapeDtypeStruct((q.shape[0], 256), F32),
            jax.ShapeDtypeStruct((steps, 8, 4 * span), F32),
        ],
        compiler_params=params(),
        name="attend",
    )(qtab, ktab, limit, q, kv)


def attend_back_kernel(
    qtab_ref, ktab_ref, len_ref, q_ref, kv_ref, do_ref, o_ref, lse_ref, dq_ref, dkv_ref,
    ks, vs, dk, dv, *, span, kb,
):
    step = pl.program_id(0)
    count = ks.shape[0] // span
    scale = HEAD_WIDTH**-0.5

    @pl.when(step == 0)
    def _():
        sort_spans(ktab_ref, kv_ref, ks, slice(0, 128), span, count)
        sort_spans(ktab_ref, kv_ref, vs, slice(128, 256), span, count)
        dk[...] = jnp.zeros_like(dk)
        dv[...] = jnp.zeros_like(dv)

    q = stack_heads(q_ref[:, :128], q_ref[:, 128:])
    do = stack_heads(do_ref[:, :128], do_ref[:, 128:])
    rows = 4 * span
    inner = do.astype(F32) * stack_heads(o_ref[:, :128], o_ref[:, 128:])
    delta = jnp.sum(jnp.transpose(inner), axis=0, keepdims=True)
    lse = lse_ref[0, :1]
    limit = len_ref[0]
    span_id = qtab_ref[step]
    full, blocks = block_counts(span_id, limit, span, kb)
    blocks = jnp.where(span_id * span < limit, blocks, 0)
    full = jnp.minimum(full, blocks)
    qpos = span_id * span + lax.broadcasted_iota(jnp.int32, (kb, rows), 1) % span
    key = lax.broadcasted_iota(jnp.int32, (kb, rows), 0)
    last = jnp.minimum(qpos, limit - 1)

    def body(masked, i, dq):
        at = pl.ds(pl.multiple_of(i * kb, kb), kb)
        k, v = ks[at, :], vs[at, :]
        s = mm_nt(k, q) * (scale * LOG2E)
        p = jnp.exp2(s - lse)
        if masked:
            p = jnp.where(key + i * kb <= last, p, 0.0)
        dp = mm_nt(v, do)
        ds = (p * (dp - delta)).astype(BF)
        dk[at, :] += mm(ds, q)
        dv[at, :] += mm(p.astype(BF), do)
        return dq + mm_tn(ds, k)

    dq = jnp.zeros((rows, 128), F32)
    dq = lax.fori_loop(0, full, functools.partial(body, False), dq)
    dq = lax.fori_loop(full, blocks, functools.partial(body, True), dq)
    a, b = unstack_heads(dq * scale)
    dq_ref[:, :128] = a.astype(BF)
    dq_ref[:, 128:] = b.astype(BF)

    @pl.when(step == pl.num_programs(0) - 1)
    def _():
        @pl.loop(0, count)
        def _(j):
            at = pl.ds(pl.multiple_of(ktab_ref[j] * span, span), span)
            to = pl.ds(pl.multiple_of(j * span, span), span)
            dkv_ref[to, :128] = (dk[at, :] * scale).astype(BF)
            dkv_ref[to, 128:] = dv[at, :].astype(BF)


def attend_back(qtab, ktab, limit, q, kv, do, o, lse, span, kb):
    steps, keys = q.shape[0] // span, kv.shape[0]
    row = pl.BlockSpec((span, 256), lambda i, *_: (i, 0))
    return pl.pallas_call(
        functools.partial(attend_back_kernel, span=span, kb=kb),
        grid_spec=pltpu.PrefetchScalarGridSpec(
            num_scalar_prefetch=3,
            grid=(steps,),
            in_specs=[
                row, whole(kv.shape), row, row,
                pl.BlockSpec((1, 8, 4 * span), lambda i, *_: (i, 0, 0)),
            ],
            out_specs=[row, whole(kv.shape)],
            scratch_shapes=[
                pltpu.VMEM((keys, 128), BF), pltpu.VMEM((keys, 128), BF),
                pltpu.VMEM((keys, 128), F32), pltpu.VMEM((keys, 128), F32),
            ],
        ),
        out_shape=[
            jax.ShapeDtypeStruct((q.shape[0], 256), BF),
            jax.ShapeDtypeStruct(kv.shape, BF),
        ],
        compiler_params=params(),
        name="attend_back",
    )(qtab, ktab, limit, q, kv, do, o, lse)


def experts_kernel(
    base_ref, h_ref, c_ref, wg_ref, wu_ref, wd_ref, moe_ref, dh_ref, grad_ref,
    moe, dh, dgates, s_act, s_gate, s_up, *, tile,
):
    step = pl.program_id(0)
    width = c_ref.shape[1]
    expert = base_ref[1] + step
    wg, wu, wd = wg_ref[0], wu_ref[0], wd_ref[0]

    @pl.when(step == 0)
    def _():
        moe[...] = jnp.zeros_like(moe)
        dh[...] = jnp.zeros_like(dh)
        dgates[...] = jnp.zeros_like(dgates)

    @pl.loop(0, moe.shape[0] // tile)
    def _(t):
        at = pl.ds(pl.multiple_of(t * tile, tile), tile)
        h, c = h_ref[at, :width], c_ref[at, :]
        lane = lax.broadcasted_iota(jnp.int32, (tile, 128), 1)
        mine = lane == expert
        gate = jnp.sum(
            jnp.where(mine, h_ref[at, width:].astype(F32), 0.0), axis=1, keepdims=True
        )
        g, u, z = mm(h, wg), mm(h, wu), mm_nt(c, wd)
        sig = jax.nn.sigmoid(g)
        silu = g * sig
        act = silu * u
        dgates[at, :] += jnp.where(mine, jnp.sum(act * z, axis=1, keepdims=True), 0.0)
        act = (act * gate).astype(BF)
        dact = z * gate
        dgate = (dact * u * sig * (1.0 + g * (1.0 - sig))).astype(BF)
        dup = (dact * silu).astype(BF)
        s_act[at, :] = act
        s_gate[at, :] = dgate
        s_up[at, :] = dup
        moe[at, :] += mm(act, wd)
        dh[at, :] += mm_nt(dgate, wg) + mm_nt(dup, wu)

    block = grad_ref.shape[2]
    for i in range(2):
        at = slice(i * block, (i + 1) * block)
        grad_ref[0, i] = mm_tn(h_ref[:, at], s_gate[...]).astype(BF)
        grad_ref[0, 2 + i] = mm_tn(h_ref[:, at], s_up[...]).astype(BF)
        grad_ref[0, 4 + i] = mm_tn(s_act[...], c_ref[:, at]).astype(BF)

    @pl.when(step == pl.num_programs(0) - 1)
    def _():
        moe_ref[...] = moe[...].astype(BF)
        dh_ref[:, :width] = dh[...].astype(BF)
        dh_ref[:, width:] = dgates[...].astype(BF)


def experts(base, count, h, c, wg, wu, wd, tile):
    rows, width = c.shape
    ff = wg.shape[2]
    pick = lambda shape: pl.BlockSpec((1,) + shape, lambda e, s: (s[0] + e, 0, 0))
    return pl.pallas_call(
        functools.partial(experts_kernel, tile=tile),
        grid_spec=pltpu.PrefetchScalarGridSpec(
            num_scalar_prefetch=1,
            grid=(count,),
            in_specs=[
                whole(h.shape), whole(c.shape),
                pick((width, ff)), pick((width, ff)), pick((ff, width)),
            ],
            out_specs=[
                whole(c.shape), whole(h.shape),
                pl.BlockSpec((1, 6, ff, ff), lambda e, s: (e, 0, 0, 0)),
            ],
            scratch_shapes=[
                pltpu.VMEM((rows, width), F32), pltpu.VMEM((rows, width), F32),
                pltpu.VMEM((rows, 128), F32),
                pltpu.VMEM((rows, ff), BF), pltpu.VMEM((rows, ff), BF), pltpu.VMEM((rows, ff), BF),
            ],
        ),
        out_shape=[
            jax.ShapeDtypeStruct(c.shape, BF),
            jax.ShapeDtypeStruct(h.shape, BF),
            jax.ShapeDtypeStruct((count, 6, ff, ff), BF),
        ],
        compiler_params=params(),
        name="experts",
    )(base, h, c, wg, wu, wd)


def flip_core(x):
    return lax.ppermute(x, "seq", [(0, 1), (1, 0), (2, 3), (3, 2)])


def flip_x(x):
    return lax.ppermute(x, "seq", [(0, 2), (2, 0), (1, 3), (3, 1)])


def flip_both(x):
    return lax.ppermute(x, "seq", [(0, 3), (3, 0), (1, 2), (2, 1)])


def flip_y(x):
    return lax.ppermute(x, "fsdp", [(0, 1), (1, 0)])


def gather_seq(x):
    own = jnp.stack([x, flip_core(x)])
    far = flip_x(x)
    return jnp.concatenate([own, far[None], flip_core(far)[None]])


def swap_seq(blocks):
    return [blocks[0], flip_core(blocks[1]), flip_x(blocks[2]), flip_both(blocks[3])]


def gather_fsdp(x, axis=0):
    if lax.axis_size("fsdp") == 2:
        return jnp.concatenate([x, lax.ppermute(x, "fsdp", [(0, 1), (1, 0)])], axis=axis)
    return lax.all_gather(x, "fsdp", axis=axis, tiled=True)


def scatter_fsdp(x):
    if lax.axis_size("fsdp") == 2:
        n = x.shape[0] // 2
        other = lax.ppermute(x[n:], "fsdp", [(0, 1), (1, 0)])
        return x[:n].astype(F32) + other.astype(F32)
    return lax.psum_scatter(x, "fsdp", scatter_dimension=0, tiled=True).astype(F32)


MESH = pl.DeviceIdType.MESH


def reduce_kernel(
    gm, eo, cols, tiny, gate, up, down, out, qkv, tiny_out,
    mine, rc, pre, suf, oth, far, faro, stage, trecv,
    s_mine, s_rc, s_pre, s_suf, s_oth, s_far, s_faro, s_out, s_tiny,
    *, slots, groups, shards,
):
    z, s, f = lax.axis_index("dp"), lax.axis_index("seq"), lax.axis_index("fsdp")
    core, x = s % 2, s // 2
    peer_core = (z, s + 1 - 2 * core, f)
    peer_x = (z, (s + 2) % 4, f)
    right, left = (z + 1, s, f), (z - 1, s, f)
    nb = gm.shape[0]
    items = nb + 3
    count = nb // 6
    half = mine.shape[1]
    ndev = slots * groups * shards
    me = (z * groups + s) * shards + f

    barrier = pltpu.get_barrier_semaphore()

    def other(k):
        q = (me + k) % ndev
        return q // (groups * shards), (q // shards) % groups, q % shards

    @pl.loop(1, ndev)
    def _(k):
        pl.semaphore_signal(barrier, inc=1, device_id=other(k), device_id_type=MESH)

    def remote(src, dst, sems, b, dev):
        return pltpu.make_async_remote_copy(
            src_ref=src, dst_ref=dst, send_sem=sems.at[0, b], recv_sem=sems.at[1, b],
            device_id=dev, device_id_type=MESH,
        )

    def load(src, b):
        return pltpu.make_async_copy(src, mine.at[b], s_mine.at[b])

    @pl.loop(0, nb)
    def _(b):
        load(gm.at[b, core], b).start()

    load(eo.at[core], nb).start()
    load(cols.at[0], nb + 1).start()
    load(cols.at[1], nb + 2).start()
    pl.semaphore_wait(barrier, ndev - 1)

    @pl.loop(0, nb)
    def _(b):
        remote(gm.at[b, 1 - core], rc.at[b], s_rc, b, peer_core).start()

    remote(eo.at[1 - core], rc.at[nb], s_rc, nb, peer_core).start()

    def tiny_copy(k):
        dev = other(k)
        return remote(tiny.at[dev[2]], trecv.at[k], s_tiny, k, dev)

    @pl.loop(1, ndev)
    def _(k):
        tiny_copy(k).start()

    def emit(kind, b, ref):
        slot = kind * 2 + b % 2
        drained = pltpu.make_async_copy(
            stage.at[slot], gate.at[0, pl.ds(0, half), :], s_out.at[slot]
        )

        @pl.when(b >= 2)
        def _():
            drained.wait()

        which = x if kind < 2 else 1 - x
        part = core if kind % 2 == 0 else 1 - core
        rows = pl.ds(pl.multiple_of(part * half, half), half)
        e, j = which * count + b // 6, b % 6
        jj = j % 2

        def put(src, dst):
            pltpu.make_async_copy(src, dst, s_out.at[slot]).start()

        @pl.when(b <= nb)
        def _():
            stage[slot] = ref[b].astype(F32)

        for m, o in enumerate((gate, up)):
            @pl.when((b < nb) & (j // 2 == m))
            def _():
                at = pl.multiple_of(jj * 2 * half + part * half, half)
                put(stage.at[slot], o.at[e, pl.ds(at, half), :])

        wide = pl.ds(pl.multiple_of(jj * 2 * half, 2 * half), 2 * half)

        @pl.when((b < nb) & (j // 2 == 2))
        def _():
            put(stage.at[slot], down.at[e, rows, wide])

        @pl.when(b == nb)
        def _():
            put(stage.at[slot], out.at[rows, pl.ds(pl.multiple_of(which * 2 * half, 2 * half), 2 * half)])

        @pl.when(b > nb)
        def _():
            v = ref[b].astype(F32)
            mid = v[:, 64:192]
            low = lax.broadcasted_iota(jnp.int32, (half, 128), 1) < 64
            stage[slot, :, :128] = jnp.where(low, v[:, :128], mid)
            stage[slot, :, 128:256] = jnp.where(low, mid, v[:, 128:256])
            stage[slot, :, 256:] = v[:, 256:]
            owner = 2 * which + part
            at = pl.ds(pl.multiple_of((b - nb - 1) * half, half), half)
            put(stage.at[slot, :, pl.ds(0, 256)], qkv.at[at, pl.ds(pl.multiple_of(owner * 256, 256), 256)])
            put(stage.at[slot, :, pl.ds(256, 128)], qkv.at[at, pl.ds(pl.multiple_of(1024 + owner * 128, 128), 128)])
            put(stage.at[slot, :, pl.ds(384, 128)], qkv.at[at, pl.ds(pl.multiple_of(1536 + owner * 128, 128), 128)])

    def add(a, b):
        return a.astype(F32) + b.astype(F32)

    def hop(buf, sems, b, dev):
        return remote(buf.at[b], buf.at[b], sems, b, dev)

    def spread(b):
        remote(rc.at[b], oth.at[b], s_oth, b, peer_core).start()
        remote(rc.at[b], far.at[b], s_far, b, peer_x).start()
        emit(0, b, rc)

    last = slots - 1
    lag = 2

    def begin(b):
        load(gm.at[0, 0], b).wait()

        @pl.when(b <= nb)
        def _():
            remote(gm.at[0, 0], rc.at[b], s_rc, b, peer_core).wait_recv()
            mine[b] = add(mine[b], rc[b]).astype(BF)

        @pl.when(z == 0)
        def _():
            remote(mine.at[b], pre.at[b], s_pre, b, right).start()

        @pl.when(z == last)
        def _():
            remote(mine.at[b], suf.at[b], s_suf, b, left).start()

    def prefix(b):
        hop(pre, s_pre, b, peer_x).wait_recv()
        got = pre[b].astype(F32)
        own = got + mine[b].astype(F32)

        @pl.when(z == last)
        def _():
            rc[b] = own.astype(BF)

        @pl.when(z < last)
        def _():
            @pl.when(2 * z >= slots)
            def _():
                rc[b] = (got + suf[b].astype(F32)).astype(BF)

            pre[b] = own.astype(BF)
            hop(pre, s_pre, b, right).start()

        @pl.when(2 * z >= slots)
        def _():
            spread(b)

    def suffix(b):
        hop(suf, s_suf, b, peer_x).wait_recv()
        got = suf[b].astype(F32)
        own = got + mine[b].astype(F32)

        @pl.when(z == 0)
        def _():
            rc[b] = own.astype(BF)

        @pl.when(z > 0)
        def _():
            @pl.when(2 * z < slots)
            def _():
                rc[b] = (got + pre[b].astype(F32)).astype(BF)

            suf[b] = own.astype(BF)
            hop(suf, s_suf, b, left).start()

        @pl.when(2 * z < slots)
        def _():
            spread(b)

    def forward(b):
        hop(far, s_far, b, peer_x).wait_recv()
        remote(far.at[b], faro.at[b], s_faro, b, peer_core).start()
        emit(2, b, far)

    def finish(b):
        hop(oth, s_oth, b, peer_core).wait_recv()
        emit(1, b, oth)
        hop(faro, s_faro, b, peer_core).wait_recv()
        emit(3, b, faro)

    def within(b, cond=True):
        return (b >= 0) & (b < items) & cond

    @pl.loop(0, items + (last + 2) * lag)
    def _(i):
        for fn, b, cond in (
            (begin, i, True),
            (prefix, i - lag * z, z > 0),
            (suffix, i - lag * (last - z), z < last),
            (forward, i - lag * (last + 1), True),
            (finish, i - lag * (last + 2), True),
        ):
            @pl.when(within(b, cond))
            def _():
                fn(b)

    own = tiny[f].astype(F32)
    trecv[0] = tiny[f]

    @pl.loop(1, ndev)
    def _(k):
        tiny_copy(k).wait()

    tiny_out[...] = lax.fori_loop(
        1, ndev, lambda k, t: t + trecv[k].astype(F32), own
    )

    @pl.loop(0, items)
    def _(b):
        @pl.when(b <= nb)
        def _():
            remote(rc.at[b], rc.at[b], s_rc, b, peer_core).wait_send()

        @pl.when(z < last)
        def _():
            hop(pre, s_pre, b, peer_x).wait_send()

        @pl.when(z > 0)
        def _():
            hop(suf, s_suf, b, peer_x).wait_send()

        hop(oth, s_oth, b, peer_core).wait_send()
        hop(far, s_far, b, peer_x).wait_send()
        hop(faro, s_faro, b, peer_core).wait_send()

    @pl.loop(0, 8)
    def _(slot):
        pltpu.make_async_copy(
            stage.at[slot], gate.at[0, pl.ds(0, half), :], s_out.at[slot]
        ).wait()


def reduce_grads(gm, eo, cols, tiny, slots, groups, shards):
    count, _, ff, _ = gm.shape
    width = 2 * ff
    nb = 6 * count
    half = ff // 2
    items = nb + 3
    ndev = slots * groups * shards
    buf = lambda: pltpu.VMEM((items, half, ff), BF)
    sems = lambda n: pltpu.SemaphoreType.DMA((2, n))
    hbm = pl.BlockSpec(memory_space=pl.ANY)
    vmem = pl.BlockSpec(memory_space=pltpu.VMEM)
    return pl.pallas_call(
        functools.partial(reduce_kernel, slots=slots, groups=groups, shards=shards),
        in_specs=[hbm, hbm, hbm, vmem],
        out_specs=[hbm] * 5 + [vmem],
        out_shape=[
            jax.ShapeDtypeStruct((2 * count, width, ff), F32),
            jax.ShapeDtypeStruct((2 * count, width, ff), F32),
            jax.ShapeDtypeStruct((2 * count, ff, width), F32),
            jax.ShapeDtypeStruct((ff, width), F32),
            jax.ShapeDtypeStruct((ff, 2 * width), F32),
            jax.ShapeDtypeStruct(tiny.shape[1:], F32),
        ],
        scratch_shapes=[
            buf(), buf(), buf(), buf(), buf(), buf(), buf(),
            pltpu.VMEM((8, half, ff), F32),
            pltpu.VMEM((ndev,) + tiny.shape[1:], BF),
            pltpu.SemaphoreType.DMA((items,)),
            sems(items), sems(items), sems(items), sems(items), sems(items), sems(items),
            pltpu.SemaphoreType.DMA((8,)),
            sems(ndev),
        ],
        compiler_params=params(collective_id=1, has_side_effects=True),
        name="reduce_grads",
    )(gm.reshape(nb, 2, half, ff), eo.reshape(2, half, ff), cols.reshape(2, half, ff), tiny)


def gather_rows(x):
    return lax.all_gather(x, "fsdp", axis=0, tiled=True)


def local(
    tokens, cotangent, lengths, order, routes, norm1, query_key_value_weight, w_out, norm2, router,
    w_gate, w_up, w_down,
):
    groups = lax.axis_size("seq")
    shards = lax.axis_size("fsdp")
    slots = lax.axis_size("dp")
    assert groups == 4
    seq, fsdp = lax.axis_index("seq"), lax.axis_index("fsdp")
    core, far = seq % 2, seq // 2
    rows, width = tokens.shape[1:]
    span = rows // 2
    x = tokens[0]
    limit = lengths[:1]
    n_experts = router.shape[1]
    owned = w_gate.shape[0]
    count = owned // 2

    table = order.reshape(groups, shards, 2)
    relative = jnp.arange(groups, dtype=jnp.int32) ^ seq
    table = jnp.take(table, relative, axis=0)
    qtab = jnp.take(table, fsdp, axis=1).reshape(-1)
    if shards == 2:
        held = jnp.stack([fsdp, 1 - fsdp])
    else:
        held = jnp.arange(shards)
    ktab = jnp.transpose(jnp.take(table, held, axis=1), (1, 0, 2)).reshape(-1)
    qpos = (qtab[:, None] * span + jnp.arange(span, dtype=jnp.int32)[None, :]).reshape(-1)
    half = HEAD_WIDTH // 2
    freqs = jnp.exp(jnp.arange(half, dtype=F32) * (-2.0 * math.log(ROPE_BASE) / HEAD_WIDTH))
    angles = qpos.astype(F32)[:, None] * freqs[None, :]
    cos = jnp.tile(jnp.cos(angles), (1, 4))
    sin = jnp.tile(jnp.sin(angles), (1, 4))

    heads = QUERY_HEADS // groups
    qw, kw = heads * HEAD_WIDTH, KEY_VALUE_HEADS // groups * HEAD_WIDTH
    w3 = query_key_value_weight
    wq = lax.dynamic_slice_in_dim(w3, seq * qw, qw, 1).reshape(-1, 2, 2, HEAD_WIDTH)
    wq = jnp.swapaxes(wq, 1, 2).reshape(-1, qw)
    wk = lax.dynamic_slice_in_dim(w3, QUERY_HEADS * HEAD_WIDTH + seq * kw, kw, 1)
    wv = lax.dynamic_slice_in_dim(w3, (QUERY_HEADS + KEY_VALUE_HEADS) * HEAD_WIDTH + seq * kw, kw, 1)
    wcols = gather_rows(jnp.concatenate([wq, wk, wv], axis=1))
    small = jnp.concatenate([norm1[:, None], norm2[:, None], router], axis=1)
    small = gather_rows(small)
    gain_one = small[:, 0].astype(F32)
    gain_two = small[:, 1].astype(F32)
    route_full = small[:, 2:]
    out_full = gather_rows(w_out)

    tok = gather_seq(x).reshape(groups * rows, width)
    hidden_one, q, kv_own = project(tok, gain_one[None], wcols, cos, sin, rows)
    kv = gather_fsdp(kv_own)
    kb = 4 * span
    attended, lse = attend(qtab, ktab, limit, q, kv, span, kb)
    sent = attended.astype(BF).reshape(groups, rows, qw)
    got = jnp.stack(swap_seq([sent[m] for m in range(groups)]))
    got = jnp.take(got, relative, axis=0).reshape(groups, rows, 2, 2, HEAD_WIDTH)
    token_out = jnp.transpose(got, (1, 0, 3, 2, 4)).reshape(rows, groups * qw)

    own_valid = (qpos[:rows] < limit[0])[:, None]
    inputs = x.astype(F32)
    middle = inputs + mm(token_out, out_full)
    normed_two, factor_two = rms_parts(middle)
    hidden_two = (normed_two * gain_two).astype(BF)
    logits = mm(hidden_two, route_full)
    chosen = jnp.any(
        routes[0][:, :, None] == jnp.arange(n_experts, dtype=jnp.int32)[None, None, :], axis=1
    )
    top = jnp.max(jnp.where(chosen, logits, NEG), axis=-1, keepdims=True)
    raised = jnp.where(chosen, jnp.exp(logits - top), 0.0)
    gates = raised / jnp.sum(raised, axis=-1, keepdims=True)
    masked_cot = jnp.where(own_valid, cotangent[0], jnp.zeros_like(cotangent[0]))

    def share(v):
        if shards != 2:
            near = gather_fsdp(v)
            return jnp.concatenate([near, flip_x(near)])
        n = rows // 2
        up, over = flip_y(v), flip_x(v)
        return jnp.concatenate([v, up, over, flip_y(over[:n]), flip_x(up[n:])])

    cot_all = share(masked_cot)
    extended = jnp.concatenate(
        [hidden_two, gates.astype(BF), jnp.zeros((rows, 128 - n_experts), BF)], axis=1
    )
    hid_all = share(extended)
    base = jnp.stack([far * count, fsdp * owned + far * count]).astype(jnp.int32)
    part = rows * 4
    moe_parts, dh_parts, weight_grads = [], [], None
    for i in range(hid_all.shape[0] // part):
        got = experts(
            base, count, hid_all[i * part : (i + 1) * part], cot_all[i * part : (i + 1) * part],
            w_gate, w_up, w_down, rows,
        )
        moe_parts.append(got[0])
        dh_parts.append(got[1])
        if weight_grads is None:
            weight_grads = got[2]
        else:
            weight_grads = (weight_grads.astype(F32) + got[2].astype(F32)).astype(BF)

    def give_back(parts):
        v = jnp.concatenate(parts) if len(parts) > 1 else parts[0]
        if shards != 2:
            n = v.shape[0] // 2
            near = v[:n].astype(F32) + flip_x(v[n:]).astype(F32)
            return scatter_fsdp(near.astype(BF))
        v = v.reshape(4, 2, rows // 2, v.shape[1])
        first = v[:2, 0].astype(F32) + flip_x(v[2:, 0]).astype(F32)
        second = v[0::2, 1].astype(F32) + flip_y(v[1::2, 1]).astype(F32)
        first = first[0] + flip_y(first[1].astype(BF)).astype(F32)
        second = second[0] + flip_x(second[1].astype(BF)).astype(F32)
        return jnp.concatenate([first, second])

    d_ext = give_back(dh_parts)
    d_gates = d_ext[:, width : width + n_experts]
    d_logits = (gates * (d_gates - jnp.sum(gates * d_gates, axis=-1, keepdims=True))).astype(BF)
    grad_router = mm_tn(hidden_two, d_logits)
    d_hidden = d_ext[:, :width] + mm_nt(d_logits, route_full)
    grad_norm2 = jnp.sum(d_hidden * normed_two, axis=0)
    d_n = d_hidden * gain_two
    d_middle = masked_cot.astype(F32) + factor_two * (
        d_n - normed_two * jnp.mean(d_n * normed_two, axis=-1, keepdims=True)
    )
    d_attn = d_middle.astype(BF)
    grad_out = mm_tn(token_out, d_attn).astype(BF)
    d_token_out = mm_nt(d_attn, out_full).astype(BF)
    d_heads = d_token_out.reshape(rows, groups, 2, 2, HEAD_WIDTH)
    d_heads = jnp.transpose(d_heads, (1, 0, 3, 2, 4)).reshape(groups, rows, qw)
    d_heads = jnp.take(d_heads, relative, axis=0)
    d_heads = jnp.concatenate(swap_seq([d_heads[m] for m in range(groups)]))
    dq, dkv = attend_back(qtab, ktab, limit, q, kv, d_heads, attended, lse, span, kb)
    dkv = scatter_fsdp(dkv)
    dh_one, grad_cols, grad_norm1 = project_back(
        tok, hidden_one, dq, dkv, wcols, cos, sin, rows
    )
    dh_one = dh_one.reshape(groups, rows, width)
    near = dh_one[0::2].astype(F32) + flip_core(dh_one[1::2]).astype(F32)
    d_hidden_one = near[0] + flip_x(near[1].astype(BF)).astype(F32)
    normed_one, factor_one = rms_parts(inputs)
    d_n = d_hidden_one * gain_one
    d_inputs = d_middle + factor_one * (
        d_n - normed_one * jnp.mean(d_n * normed_one, axis=-1, keepdims=True)
    )

    block = w_gate.shape[2]

    def to_owner(g):
        if shards == 2:
            half = g.reshape(2, -1, g.shape[1])
            kept = lax.dynamic_index_in_dim(half, fsdp, 0, keepdims=False)
            sent = lax.dynamic_index_in_dim(half, 1 - fsdp, 0, keepdims=False)
            return (kept.astype(F32) + flip_y(sent).astype(F32)).astype(BF)
        part = lax.psum_scatter(g, "fsdp", scatter_dimension=0, tiled=True)
        return jnp.pad(part, ((0, block - part.shape[0]), (0, 0)))

    shard_rows = width // shards
    cols = to_owner(grad_cols)
    mine = to_owner(grad_out).reshape(block, 2, block)
    kept = lax.dynamic_index_in_dim(mine, far, 1, keepdims=False)
    sent = lax.dynamic_index_in_dim(mine, 1 - far, 1, keepdims=False)
    outs = (kept.astype(F32) + flip_x(sent).astype(F32)).astype(BF)
    tiny = jnp.concatenate(
        [jnp.sum(grad_norm1, axis=0)[None], grad_norm2[None], jnp.transpose(grad_router),
         jnp.zeros((14, width), F32)]
    )
    tiny = jnp.transpose(tiny.reshape(32, shards, shard_rows), (1, 0, 2)).astype(BF)
    grad_gate, grad_up, grad_down, shard_out, shard_qkv, tiny = reduce_grads(
        weight_grads, outs, cols, tiny, slots, groups, shards
    )
    shard_out, shard_qkv = shard_out[:shard_rows], shard_qkv[:shard_rows]
    tiny = jnp.transpose(tiny)
    layer_out = (middle + give_back(moe_parts)).astype(BF)
    return (
        layer_out[None], d_inputs[None], tiny[:, 0], shard_qkv, shard_out, tiny[:, 1], tiny[:, 2 : 2 + n_experts],
        grad_gate, grad_up, grad_down,
    )


def solution(mesh):
    placed = (
        P("dp", ("seq", "fsdp"), None),
        P("dp", ("seq", "fsdp"), None),
        P("dp"),
        P(),
        P("dp", ("seq", "fsdp"), None),
        P("fsdp"),
        P("fsdp", None),
        P("fsdp", None),
        P("fsdp"),
        P("fsdp", None),
        P("fsdp", None, None),
        P("fsdp", None, None),
        P("fsdp", None, None),
    )
    return jax.shard_map(
        local,
        mesh=mesh,
        in_specs=placed,
        out_specs=(
            P("dp", ("seq", "fsdp"), None),
            P("dp", ("seq", "fsdp"), None),
            P("fsdp"),
            P("fsdp", None),
            P("fsdp", None),
            P("fsdp"),
            P("fsdp", None),
            P("fsdp", None, None),
            P("fsdp", None, None),
            P("fsdp", None, None),
        ),
        check_vma=False,
    )
```

```python
import functools
import math
import types

import jax
import jax.numpy as jnp
import numpy as np
from jax import lax
from jax.experimental import pallas as pl
from jax.experimental.pallas import tpu as pltpu
from jax.sharding import PartitionSpec as P

QUERY_HEADS = 16
KEY_VALUE_HEADS = 8
HEAD_WIDTH = 64
TOPK = 8

EPS = 1e-06
ROPE_BASE = 10000.0
LOG2E = math.log2(math.e)
NEG = -1e30
BF = jnp.bfloat16
F32 = jnp.float32
VMEM_LIMIT = 60 * 1024 * 1024

NT_DIMS = (((1,), (1,)), ((), ()))
TN_DIMS = (((0,), (0,)), ((), ()))


def mm(a, b):
    return jnp.dot(a, b, preferred_element_type=F32)


def mm_nt(a, b):
    return lax.dot_general(a, b, NT_DIMS, preferred_element_type=F32)


def mm_tn(a, b):
    return lax.dot_general(a, b, TN_DIMS, preferred_element_type=F32)


def params(**kw):
    return pltpu.CompilerParams(vmem_limit_bytes=VMEM_LIMIT, **kw)


def whole(shape):
    return pl.BlockSpec(shape, lambda *_: (0,) * len(shape))


def rms_parts(x):
    factor = lax.rsqrt(jnp.mean(x * x, axis=-1, keepdims=True) + EPS)
    return x * factor, factor


def qkv_kernel(tok_ref, gain_ref, w_ref, cos_ref, sin_ref, h_ref, q_ref, kv_ref):
    normed, _ = rms_parts(tok_ref[...].astype(F32))
    h = (normed * gain_ref[...]).astype(BF)
    h_ref[...] = h
    proj = mm(h, w_ref[...])
    cos, sin = cos_ref[...], sin_ref[...]
    low_half = lax.broadcasted_iota(jnp.int32, cos.shape, 1) % HEAD_WIDTH < HEAD_WIDTH // 2
    half = HEAD_WIDTH // 2
    for t in range(3):
        w = proj[:, t * 128 : (t + 1) * 128]
        rot = jnp.where(low_half, -pltpu.roll(w, 128 - half, 1), pltpu.roll(w, half, 1))
        out = (w * cos + rot * sin).astype(BF)
        if t < 2:
            q_ref[:, t * 128 : (t + 1) * 128] = out
        else:
            kv_ref[:, :128] = out
    kv_ref[:, 128:] = proj[:, 384:].astype(BF)


def project(tok, gain, w, cos, sin, tile):
    rows, width = tok.shape
    return pl.pallas_call(
        qkv_kernel,
        grid=(rows // tile,),
        in_specs=[
            pl.BlockSpec((tile, width), lambda i: (i, 0)),
            whole((1, width)),
            whole(w.shape),
            pl.BlockSpec((tile, 128), lambda i: (i, 0)),
            pl.BlockSpec((tile, 128), lambda i: (i, 0)),
        ],
        out_specs=[
            pl.BlockSpec((tile, width), lambda i: (i, 0)),
            pl.BlockSpec((tile, 256), lambda i: (i, 0)),
            pl.BlockSpec((tile, 256), lambda i: (i, 0)),
        ],
        out_shape=[
            jax.ShapeDtypeStruct((rows, width), BF),
            jax.ShapeDtypeStruct((rows, 256), BF),
            jax.ShapeDtypeStruct((rows, 256), BF),
        ],
        compiler_params=params(),
        name="project",
    )(tok, gain, w, cos, sin)


MESH = pl.DeviceIdType.MESH


def rope_rows(w, cos, sin):
    half = HEAD_WIDTH // 2
    low_half = lax.broadcasted_iota(jnp.int32, w.shape, 1) % HEAD_WIDTH < half
    rot = jnp.where(low_half, -pltpu.roll(w, 128 - half, 1), pltpu.roll(w, half, 1))
    return w * cos + rot * sin


def front_kernel(
    spans, tok, w3, small, rtab, stab, tok_out, wc_out, small_all, h_out, q, kv, cos_out, sin_out,
    tok_all, wc, h, cos, sin, s_tok, s_w, s_own, s_kv, s_end
):
    z, s, f = lax.axis_index("dp"), lax.axis_index("seq"), lax.axis_index("fsdp")
    core = s % 2
    peer_core = (z, s + 1 - 2 * core, f)
    peer_x = (z, (s + 2) % 4, f)
    peer_y = (z, s, 1 - f)
    rows, width = tok.shape
    part = small.shape[1]

    barrier = pltpu.get_barrier_semaphore()
    for dev in (peer_core, peer_x, peer_y):
        pl.semaphore_signal(barrier, inc=1, device_id=dev, device_id_type=MESH)

    def remote(src, dst, sems, b, dev):
        return pltpu.make_async_remote_copy(
            src_ref=src, dst_ref=dst, send_sem=sems.at[0, b], recv_sem=sems.at[1, b],
            device_id=dev, device_id_type=MESH,
        )

    own_rows = pl.ds(pl.multiple_of(f * part, part), part)
    pieces = []
    for first, n, to in ((0, 256, 0), (width, 128, 256), (width + width // 2, 128, 384)):
        src = w3.at[:, pl.ds(pl.multiple_of(first + s * n, 128), n)]
        pieces.append((src, wc.at[own_rows, pl.ds(to, n)]))
    local = [pltpu.make_async_copy(a, b, s_own.at[i]) for i, (a, b) in enumerate(pieces)]
    for copy in local:
        copy.start()
    small_all[:, own_rows] = small[...]
    tok_all[0] = tok[...]
    pl.semaphore_wait(barrier, 3)
    over = remote(tok, tok_all.at[2], s_tok, 1, peer_x)
    near = remote(tok, tok_all.at[1], s_tok, 0, peer_core)
    onward = remote(tok_all.at[2], tok_all.at[3], s_tok, 2, peer_core)
    weights = [remote(a, b, s_w, i, peer_y) for i, (a, b) in enumerate(pieces)]
    weights.append(remote(small, small_all.at[:, own_rows], s_w, 3, peer_y))
    over.start()
    for copy in weights:
        copy.start()
    near.start()
    for copy in local:
        copy.wait()
    for copy in weights:
        copy.wait_recv()
    gain = small_all[16:17, :].astype(F32)

    def kv_copy(t):
        at = pl.ds(t * rows, rows)
        return remote(kv.at[0, at], kv.at[1, at], s_kv, t, peer_y)

    ends = [pltpu.make_async_copy(wc, wc_out, s_end.at[0])]
    ends[0].start()
    span = rows // 2
    for k in range(8):
        at = pl.ds(k * span, span)
        row = pl.ds(spans[k], 1)
        c, n = stab[0, row, :], stab[1, row, :]
        cos[at, :] = rtab[0] * c - rtab[1] * n
        sin[at, :] = rtab[1] * c + rtab[0] * n
    for i, (src, dst) in enumerate(((cos, cos_out), (sin, sin_out))):
        ends.append(pltpu.make_async_copy(src, dst, s_end.at[1 + i]))
        ends[-1].start()

    for t in range(4):
        if t == 1:
            near.wait_recv()
        if t == 2:
            over.wait_recv()
            onward.start()
        if t == 3:
            onward.wait_recv()
        at = pl.ds(t * rows, rows)
        ends.append(pltpu.make_async_copy(tok_all.at[t], tok_out.at[t], s_end.at[3 + t]))
        ends[-1].start()
        normed, _ = rms_parts(tok_all[t].astype(F32))
        hidden = (normed * gain).astype(BF)
        h[at, :] = hidden
        proj = mm(hidden, wc[...])
        c, n = cos[at, :], sin[at, :]
        kv[0, at, :128] = rope_rows(proj[:, 256:384], c, n).astype(BF)
        kv[0, at, 128:] = proj[:, 384:].astype(BF)
        kv_copy(t).start()
        for k in range(2):
            q[at, k * 128 : (k + 1) * 128] = rope_rows(proj[:, k * 128 : (k + 1) * 128], c, n).astype(BF)
        ends.append(pltpu.make_async_copy(h.at[at], h_out.at[at], s_end.at[7 + t]))
        ends[-1].start()
    for t in range(4):
        kv_copy(t).wait()
    for copy in ends:
        copy.wait()
    for copy in (over, near, onward, *weights):
        copy.wait_send()


def front(spans, n_spans, tok, w3, small):
    rows, width = tok.shape
    span, half = rows // 2, HEAD_WIDTH // 2
    freqs = np.exp(np.arange(half) * (-2.0 * math.log(ROPE_BASE) / HEAD_WIDTH)).astype(np.float32)

    def table(positions):
        angles = np.tile(positions[:, None].astype(np.float64) * freqs[None, :], (1, 4))
        return jnp.asarray(np.stack([np.cos(angles), np.sin(angles)]), F32)

    rtab, stab = table(np.arange(span)), table(np.arange(n_spans) * span)
    vmem = pl.BlockSpec(memory_space=pltpu.VMEM)
    hbm = pl.BlockSpec(memory_space=pl.ANY)
    dma = pltpu.SemaphoreType.DMA
    shape = jax.ShapeDtypeStruct
    return pl.pallas_call(
        front_kernel,
        in_specs=[pl.BlockSpec(memory_space=pltpu.SMEM), vmem, hbm, vmem, vmem, vmem],
        out_specs=[hbm, hbm, vmem, hbm, vmem, vmem, hbm, hbm],
        out_shape=[
            shape((4, rows, width), BF),
            shape((width, 512), BF),
            shape((small.shape[0], width), BF),
            shape((4 * rows, width), BF),
            shape((4 * rows, 256), BF),
            shape((2, 4 * rows, 256), BF),
            shape((4 * rows, 128), F32),
            shape((4 * rows, 128), F32),
        ],
        scratch_shapes=[
            pltpu.VMEM((4, rows, width), BF), pltpu.VMEM((width, 512), BF),
            pltpu.VMEM((4 * rows, width), BF),
            pltpu.VMEM((4 * rows, 128), F32), pltpu.VMEM((4 * rows, 128), F32),
            dma((2, 3)), dma((2, 4)), dma((3,)), dma((2, 4)), dma((11,)),
        ],
        compiler_params=params(collective_id=2, has_side_effects=True),
        name="front",
    )(spans, tok, w3, small, rtab, stab)


def widen_kernel(*refs):
    n = (len(refs) - 4) // 2
    ins, outs = refs[:n], refs[n + 1 : 2 * n + 1]
    for a, b in zip(ins, outs):
        b[...] = a[...].astype(F32)
    tiny, (one, two, router) = refs[n], refs[2 * n + 1 :]

    @pl.when(pl.program_id(0) == 0)
    def _():
        one[...] = tiny[16:17, :]
        two[...] = tiny[17:18, :]
        router[...] = jnp.transpose(tiny[...])[:, : router.shape[1]]


def widen(arrays, tiny, n_experts):
    flat = [a.reshape(-1, a.shape[-1]) for a in arrays]
    steps = 16
    wide = tiny.shape[1]
    specs = [pl.BlockSpec((a.shape[0] // steps, a.shape[1]), lambda i: (i, 0)) for a in flat]
    shape = jax.ShapeDtypeStruct
    got = pl.pallas_call(
        widen_kernel,
        grid=(steps,),
        in_specs=specs + [whole(tiny.shape)],
        out_specs=specs + [whole((1, wide)), whole((1, wide)), whole((wide, n_experts))],
        out_shape=[shape(a.shape, F32) for a in flat]
        + [shape((1, wide), F32), shape((1, wide), F32), shape((wide, n_experts), F32)],
        compiler_params=params(),
        name="widen",
    )(*flat, tiny)
    n = len(arrays)
    return [g.reshape(a.shape) for g, a in zip(got, arrays)] + [got[n][0], got[n + 1][0], got[n + 2]]


def project_back_kernel(
    tok_ref, h_ref, dq_ref, dkv_ref, w_ref, cos_ref, sin_ref, dh_ref, gw_ref, gn_ref, acc
):
    step = pl.program_id(0)

    @pl.when(step == 0)
    def _():
        acc[...] = jnp.zeros_like(acc)
        gn_ref[...] = jnp.zeros_like(gn_ref)

    cos, sin = cos_ref[...], sin_ref[...]
    half = HEAD_WIDTH // 2
    low_half = lax.broadcasted_iota(jnp.int32, cos.shape, 1) % HEAD_WIDTH < half
    parts = []
    for t in range(3):
        w = dq_ref[:, t * 128 : (t + 1) * 128] if t < 2 else dkv_ref[:, :128]
        w = w.astype(F32)
        y = w * sin
        rot = jnp.where(low_half, pltpu.roll(y, 128 - half, 1), -pltpu.roll(y, half, 1))
        parts.append((w * cos + rot).astype(BF))
    parts.append(dkv_ref[:, 128:].astype(BF))
    dproj = jnp.concatenate(parts, axis=1)
    acc[...] += mm_tn(h_ref[...], dproj)
    dh = mm_nt(dproj, w_ref[...])
    dh_ref[...] = dh.astype(BF)
    normed, _ = rms_parts(tok_ref[...].astype(F32))
    gn_ref[...] += jnp.sum((dh * normed).reshape(-1, 8, dh.shape[1]), axis=0)

    @pl.when(step == pl.num_programs(0) - 1)
    def _():
        gw_ref[...] = acc[...].astype(BF)


def project_back(tok, h, dq, dkv, w, cos, sin, tile):
    rows, width = tok.shape
    row = lambda n: pl.BlockSpec((tile, n), lambda i: (i, 0))
    return pl.pallas_call(
        project_back_kernel,
        grid=(rows // tile,),
        in_specs=[row(width), row(width), row(256), row(256), whole(w.shape), row(128), row(128)],
        out_specs=[row(width), whole(w.shape), whole((8, width))],
        out_shape=[
            jax.ShapeDtypeStruct((rows, width), BF),
            jax.ShapeDtypeStruct(w.shape, BF),
            jax.ShapeDtypeStruct((8, width), F32),
        ],
        scratch_shapes=[pltpu.VMEM(w.shape, F32)],
        compiler_params=params(),
        name="project_back",
    )(tok, h, dq, dkv, w, cos, sin)


def stack_heads(a, b, dtype=BF):
    a, b = a.astype(F32), b.astype(F32)
    low = lax.broadcasted_iota(jnp.int32, a.shape, 1) < HEAD_WIDTH
    turn = lambda v: pltpu.roll(v, HEAD_WIDTH, 1)
    rows = [
        jnp.where(low, a, 0.0), jnp.where(low, turn(a), 0.0),
        jnp.where(low, 0.0, turn(b)), jnp.where(low, 0.0, b),
    ]
    return jnp.concatenate(rows, axis=0).astype(dtype)


def unstack_heads(x):
    n = x.shape[0] // 4
    low = lax.broadcasted_iota(jnp.int32, (n, 128), 1) < HEAD_WIDTH
    turn = lambda v: pltpu.roll(v, HEAD_WIDTH, 1)
    return (
        jnp.where(low, x[:n], turn(x[n : 2 * n])),
        jnp.where(low, turn(x[2 * n : 3 * n]), x[3 * n :]),
    )


def block_counts(span_id, limit, span, kb):
    first = span_id * span
    seen = (first + span - 1) // kb + 1
    blocks = jnp.minimum(seen, (limit + kb - 1) // kb)
    full = jnp.minimum(first + 1, limit) // kb
    return jnp.minimum(full, blocks), blocks


def sort_spans(ktab_ref, src, dst, lanes, span, count):
    @pl.loop(0, count)
    def _(j):
        to = pl.multiple_of(ktab_ref[j] * span, span)
        dst[pl.ds(to, span), :] = src[pl.ds(pl.multiple_of(j * span, span), span), lanes]


def attend_kernel(
    qtab_ref, ktab_ref, len_ref, q_ref, kv_ref, o_ref, low_ref, lse_ref, ks, vs, *, span, kb
):
    step = pl.program_id(0)
    count = ks.shape[0] // span

    @pl.when(step == 0)
    def _():
        sort_spans(ktab_ref, kv_ref, ks, slice(0, 128), span, count)
        sort_spans(ktab_ref, kv_ref, vs, slice(128, 256), span, count)

    q = stack_heads(q_ref[:, :128], q_ref[:, 128:])
    rows = 4 * span
    limit = len_ref[0]
    span_id = qtab_ref[step]
    full, blocks = block_counts(span_id, limit, span, kb)
    qpos = span_id * span + lax.broadcasted_iota(jnp.int32, (rows, kb), 0) % span
    col = lax.broadcasted_iota(jnp.int32, (rows, kb), 1)
    last = jnp.minimum(qpos, limit - 1)

    def body(masked, i, carry):
        top, total, acc = carry
        at = pl.multiple_of(i * kb, kb)
        s = mm_nt(q, ks[pl.ds(at, kb), :]) * (HEAD_WIDTH**-0.5 * LOG2E)
        if masked:
            s = jnp.where(col + i * kb <= last, s, NEG)
        new = jnp.maximum(top, jnp.max(s, axis=1, keepdims=True))
        fade = jnp.exp2(top - new)
        p = jnp.exp2(s - new)
        total = total * fade + jnp.sum(p, axis=1, keepdims=True)
        acc = acc * fade + mm(p.astype(BF), vs[pl.ds(at, kb), :])
        return new, total, acc

    carry = (
        jnp.full((rows, 1), NEG, F32),
        jnp.zeros((rows, 1), F32),
        jnp.zeros((rows, 128), F32),
    )
    carry = lax.fori_loop(0, full, functools.partial(body, False), carry)
    top, total, acc = lax.fori_loop(full, blocks, functools.partial(body, True), carry)
    a, b = unstack_heads(acc / total)
    o_ref[:, :128] = a
    o_ref[:, 128:] = b
    low_ref[:, :128] = a.astype(BF)
    low_ref[:, 128:] = b.astype(BF)
    lse = jnp.broadcast_to(top + jnp.log2(total), (rows, 128))
    lse_ref[0] = jnp.transpose(lse)[:8]


def attend(qtab, ktab, limit, q, kv, span, kb):
    steps, keys = q.shape[0] // span, kv.shape[0]
    return pl.pallas_call(
        functools.partial(attend_kernel, span=span, kb=kb),
        grid_spec=pltpu.PrefetchScalarGridSpec(
            num_scalar_prefetch=3,
            grid=(steps,),
            in_specs=[pl.BlockSpec((span, 256), lambda i, *_: (i, 0)), whole(kv.shape)],
            out_specs=[
                pl.BlockSpec((span, 256), lambda i, *_: (i, 0)),
                pl.BlockSpec((span, 256), lambda i, *_: (i, 0)),
                pl.BlockSpec((1, 8, 4 * span), lambda i, *_: (i, 0, 0)),
            ],
            scratch_shapes=[pltpu.VMEM((keys, 128), BF), pltpu.VMEM((keys, 128), BF)],
        ),
        out_shape=[
            jax.ShapeDtypeStruct((q.shape[0], 256), F32),
            jax.ShapeDtypeStruct((q.shape[0], 256), BF),
            jax.ShapeDtypeStruct((steps, 8, 4 * span), F32),
        ],
        compiler_params=params(),
        name="attend",
    )(qtab, ktab, limit, q, kv)


def attend_back_kernel(
    qtab_ref, ktab_ref, len_ref, q_ref, kv_ref, do_ref, o_ref, lse_ref, dq_ref, dkv_ref,
    ks, vs, dk, dv, *, span, kb,
):
    step = pl.program_id(0)
    count = ks.shape[0] // span
    scale = HEAD_WIDTH**-0.5

    @pl.when(step == 0)
    def _():
        sort_spans(ktab_ref, kv_ref, ks, slice(0, 128), span, count)
        sort_spans(ktab_ref, kv_ref, vs, slice(128, 256), span, count)
        dk[...] = jnp.zeros_like(dk)
        dv[...] = jnp.zeros_like(dv)

    q = stack_heads(q_ref[:, :128], q_ref[:, 128:])
    do = stack_heads(do_ref[:, :128], do_ref[:, 128:])
    rows = 4 * span
    inner = do.astype(F32) * stack_heads(o_ref[:, :128], o_ref[:, 128:], F32)
    delta = jnp.sum(jnp.transpose(inner), axis=0, keepdims=True)
    lse = lse_ref[0, :1]
    limit = len_ref[0]
    span_id = qtab_ref[step]
    full, blocks = block_counts(span_id, limit, span, kb)
    blocks = jnp.where(span_id * span < limit, blocks, 0)
    full = jnp.minimum(full, blocks)
    qpos = span_id * span + lax.broadcasted_iota(jnp.int32, (kb, rows), 1) % span
    key = lax.broadcasted_iota(jnp.int32, (kb, rows), 0)
    last = jnp.minimum(qpos, limit - 1)

    def body(masked, i, dq):
        at = pl.ds(pl.multiple_of(i * kb, kb), kb)
        k, v = ks[at, :], vs[at, :]
        s = mm_nt(k, q) * (scale * LOG2E)
        p = jnp.exp2(s - lse)
        if masked:
            p = jnp.where(key + i * kb <= last, p, 0.0)
        dp = mm_nt(v, do)
        ds = (p * (dp - delta)).astype(BF)
        dk[at, :] += mm(ds, q)
        dv[at, :] += mm(p.astype(BF), do)
        return dq + mm_tn(ds, k)

    dq = jnp.zeros((rows, 128), F32)
    dq = lax.fori_loop(0, full, functools.partial(body, False), dq)
    dq = lax.fori_loop(full, blocks, functools.partial(body, True), dq)
    a, b = unstack_heads(dq * scale)
    dq_ref[:, :128] = a.astype(BF)
    dq_ref[:, 128:] = b.astype(BF)

    @pl.when(step == pl.num_programs(0) - 1)
    def _():
        @pl.loop(0, count)
        def _(j):
            at = pl.ds(pl.multiple_of(ktab_ref[j] * span, span), span)
            to = pl.ds(pl.multiple_of(j * span, span), span)
            dkv_ref[to, :128] = (dk[at, :] * scale).astype(BF)
            dkv_ref[to, 128:] = dv[at, :].astype(BF)


def attend_back(qtab, ktab, limit, q, kv, do, o, lse, span, kb):
    steps, keys = q.shape[0] // span, kv.shape[0]
    row = pl.BlockSpec((span, 256), lambda i, *_: (i, 0))
    return pl.pallas_call(
        functools.partial(attend_back_kernel, span=span, kb=kb),
        grid_spec=pltpu.PrefetchScalarGridSpec(
            num_scalar_prefetch=3,
            grid=(steps,),
            in_specs=[
                row, whole(kv.shape), row, row,
                pl.BlockSpec((1, 8, 4 * span), lambda i, *_: (i, 0, 0)),
            ],
            out_specs=[row, whole(kv.shape)],
            scratch_shapes=[
                pltpu.VMEM((keys, 128), BF), pltpu.VMEM((keys, 128), BF),
                pltpu.VMEM((keys, 128), F32), pltpu.VMEM((keys, 128), F32),
            ],
        ),
        out_shape=[
            jax.ShapeDtypeStruct((q.shape[0], 256), BF),
            jax.ShapeDtypeStruct(kv.shape, BF),
        ],
        compiler_params=params(),
        name="attend_back",
    )(qtab, ktab, limit, q, kv, do, o, lse)


def experts_kernel(
    base_ref, h_ref, c_ref, wg_ref, wu_ref, wd_ref, moe_ref, dh_ref, grad_ref,
    moe, dh, dgates, s_act, s_gate, s_up, *, tile,
):
    step = pl.program_id(0)
    width = c_ref.shape[1]
    expert = base_ref[1] + step
    wg, wu, wd = wg_ref[0], wu_ref[0], wd_ref[0]

    @pl.when(step == 0)
    def _():
        moe[...] = jnp.zeros_like(moe)
        dh[...] = jnp.zeros_like(dh)
        dgates[...] = jnp.zeros_like(dgates)

    @pl.loop(0, moe.shape[0] // tile)
    def _(t):
        at = pl.ds(pl.multiple_of(t * tile, tile), tile)
        h, c = h_ref[at, :width], c_ref[at, :]
        lane = lax.broadcasted_iota(jnp.int32, (tile, 128), 1)
        mine = lane == expert
        gate = jnp.sum(
            jnp.where(mine, h_ref[at, width:].astype(F32), 0.0), axis=1, keepdims=True
        )
        g, u, z = mm(h, wg), mm(h, wu), mm_nt(c, wd)
        sig = jax.nn.sigmoid(g)
        silu = g * sig
        act = silu * u
        dgates[at, :] += jnp.where(mine, jnp.sum(act * z, axis=1, keepdims=True), 0.0)
        act = (act * gate).astype(BF)
        dact = z * gate
        dgate = (dact * u * sig * (1.0 + g * (1.0 - sig))).astype(BF)
        dup = (dact * silu).astype(BF)
        s_act[at, :] = act
        s_gate[at, :] = dgate
        s_up[at, :] = dup
        moe[at, :] += mm(act, wd)
        dh[at, :] += mm_nt(dgate, wg) + mm_nt(dup, wu)

    block = grad_ref.shape[2]
    for i in range(2):
        at = slice(i * block, (i + 1) * block)
        grad_ref[0, i] = mm_tn(h_ref[:, at], s_gate[...]).astype(BF)
        grad_ref[0, 2 + i] = mm_tn(h_ref[:, at], s_up[...]).astype(BF)
        grad_ref[0, 4 + i] = mm_tn(s_act[...], c_ref[:, at]).astype(BF)

    @pl.when(step == pl.num_programs(0) - 1)
    def _():
        moe_ref[...] = moe[...].astype(BF)
        dh_ref[:, :width] = dh[...].astype(BF)
        dh_ref[:, width:] = dgates[...].astype(BF)


def experts(base, count, h, c, wg, wu, wd, tile):
    rows, width = c.shape
    ff = wg.shape[2]
    pick = lambda shape: pl.BlockSpec((1,) + shape, lambda e, s: (s[0] + e, 0, 0))
    return pl.pallas_call(
        functools.partial(experts_kernel, tile=tile),
        grid_spec=pltpu.PrefetchScalarGridSpec(
            num_scalar_prefetch=1,
            grid=(count,),
            in_specs=[
                whole(h.shape), whole(c.shape),
                pick((width, ff)), pick((width, ff)), pick((ff, width)),
            ],
            out_specs=[
                whole(c.shape), whole(h.shape),
                pl.BlockSpec((1, 6, ff, ff), lambda e, s: (e, 0, 0, 0)),
            ],
            scratch_shapes=[
                pltpu.VMEM((rows, width), F32), pltpu.VMEM((rows, width), F32),
                pltpu.VMEM((rows, 128), F32),
                pltpu.VMEM((rows, ff), BF), pltpu.VMEM((rows, ff), BF), pltpu.VMEM((rows, ff), BF),
            ],
        ),
        out_shape=[
            jax.ShapeDtypeStruct(c.shape, BF),
            jax.ShapeDtypeStruct(h.shape, BF),
            jax.ShapeDtypeStruct((count, 6, ff, ff), BF),
        ],
        compiler_params=params(),
        name="experts",
    )(base, h, c, wg, wu, wd)


def moe_kernel(*refs, names, topk, count):
    r = types.SimpleNamespace(**dict(zip(names, refs)))
    z, s, f = lax.axis_index("dp"), lax.axis_index("seq"), lax.axis_index("fsdp")
    core, x = s % 2, s // 2
    flip = 1 - 2 * core
    seqs = (s, s + flip, (s + 2) % 4, (s + 2) % 4 + flip)
    peers = [(z, q, f) for q in seqs]
    peer_x, peer_y = peers[2], (z, s, 1 - f)
    att, att_in, tout, hx, cots = r.att, r.att_in, r.tout, r.hx, r.cots
    rows, width = tout.shape
    n = rows // 2
    ext = hx.shape[1]
    ff = r.wgs.shape[2]
    owned = r.wg.shape[0]

    barrier = pltpu.get_barrier_semaphore()
    for dev in (*peers[1:], peer_y):
        pl.semaphore_signal(barrier, inc=1, device_id=dev, device_id_type=MESH)

    def remote(src, dst, sems, b, dev):
        return pltpu.make_async_remote_copy(
            src_ref=src, dst_ref=dst, send_sem=sems.at[0, b], recv_sem=sems.at[1, b],
            device_id=dev, device_id_type=MESH,
        )

    def block(t):
        return pl.ds(pl.multiple_of(t * rows, rows), rows)

    load_cots = [
        pltpu.make_async_copy(v, cots.at[block(i)], r.s_cot.at[i])
        for i, v in enumerate((r.cot, r.cot_y, r.cot_x))
    ]
    for copy in load_cots:
        copy.start()

    def load_weights(e, act):
        for i, (src, dst) in enumerate(((r.wg, r.wgs), (r.wu, r.wus), (r.wd, r.wds))):
            act(pltpu.make_async_copy(src.at[x * count + e], dst.at[e], r.s_w.at[i, e]))

    @pl.loop(0, count)
    def _(e):
        load_weights(e, lambda copy: copy.start())

    pl.semaphore_wait(barrier, 4)
    heads = [remote(att.at[m], att_in.at[m], r.s_att, m, peers[m]) for m in range(1, 4)]
    for copy in heads:
        copy.start()
    diag = [
        remote(r.cot_x.at[pl.ds(0, n)], cots.at[pl.ds(3 * rows, n)], r.s_diag, 0, peer_y),
        remote(r.cot_y.at[pl.ds(n, n)], cots.at[pl.ds(3 * rows + n, n)], r.s_diag, 1, peer_x),
    ]
    for copy in diag:
        copy.start()

    small = r.small
    table = r.table
    table[...] = jnp.zeros_like(table)
    table[: small.shape[0], :] = small[...]
    n_exp = r.gates.shape[1]
    gain = small[17:18, :].astype(F32)
    own_cols = pl.ds(pl.multiple_of(f * ff, ff), ff)
    away_cols = pl.ds(pl.multiple_of((1 - f) * ff, ff), ff)

    def head_cols(m):
        return pl.ds(pl.multiple_of(seqs[m] * 256, 256), 256)

    tout[:, head_cols(0)] = att[0]
    for m in range(1, 4):
        heads[m - 1].wait_recv()
        tout[:, head_cols(m)] = att_in[m]

    shares = []
    for i in range(2):
        at = pl.ds(i * n, n)
        middle = (
            r.tok[at, :].astype(F32)
            + mm(tout[at, own_cols], r.wo_own[...])
            + mm(tout[at, away_cols], r.wo_there[...])
        )
        r.middle[at, :] = middle
        normed, _ = rms_parts(middle)
        hidden = (normed * gain).astype(BF)
        logits = mm_nt(hidden, table[...])
        lane = lax.broadcasted_iota(jnp.int32, logits.shape, 1)
        chosen = lane == r.routes[at, 0:1]
        for k in range(1, topk):
            chosen = chosen | (lane == r.routes[at, k : k + 1])
        top = jnp.max(jnp.where(chosen, logits, NEG), axis=-1, keepdims=True)
        raised = jnp.where(chosen, jnp.exp(logits - top), 0.0)
        gates = raised / jnp.sum(raised, axis=-1, keepdims=True)
        r.gates[at, :] = gates
        hx[at, :width] = hidden
        hx[at, width:] = gates.astype(BF)
        for j, dev in ((0, peer_y), (1, peer_x)):
            to = pl.ds((j + 1) * rows + i * n, n)
            copy = remote(hx.at[at], hx.at[to], r.s_h, 2 * j + i, dev)
            copy.start()
            shares.append(copy)
    second = remote(
        hx.at[pl.ds(rows + n, n)], hx.at[pl.ds(3 * rows + n, n)], r.s_h, 4, peer_x
    )
    first = remote(hx.at[pl.ds(2 * rows, n)], hx.at[pl.ds(3 * rows, n)], r.s_h, 5, peer_y)

    dhs, moe, dh, dgates = r.dhs, r.moe_acc, r.dh_acc, r.dg_acc
    back_y = remote(dhs.at[block(1)], r.rdh.at[0], r.s_d, 0, peer_y)
    back_x = remote(dhs.at[block(2)], r.rdh.at[1], r.s_d, 1, peer_x)
    hop_x = remote(dhs.at[pl.ds(3 * rows, n)], r.via.at[0], r.s_d, 2, peer_x)
    hop_y = remote(dhs.at[pl.ds(3 * rows + n, n)], r.via.at[1], r.s_d, 3, peer_y)
    end_y = remote(r.via.at[0], r.rdd.at[pl.ds(0, n)], r.s_d, 4, peer_y)
    end_x = remote(r.via.at[1], r.rdd.at[pl.ds(n, n)], r.s_d, 5, peer_x)

    moes = (r.moe0, r.moe1, r.moe2, r.moe3)

    def moe_out(t):
        return pltpu.make_async_copy(r.mstage.at[t % 2], moes[t], r.s_m.at[t])

    @pl.loop(0, 4 * count)
    def _(k):
        t, e = k // count, k % count

        @pl.when(k < count)
        def _():
            load_weights(e, lambda copy: copy.wait())

        @pl.when(k == 0)
        def _():
            load_cots[0].wait()

        @pl.when(k == count)
        def _():
            for copy in shares:
                copy.wait_recv()
            second.start()
            first.start()
            load_cots[1].wait()
            load_cots[2].wait()

        @pl.when(k == 3 * count)
        def _():
            first.wait_recv()
            second.wait_recv()
            for copy in diag:
                copy.wait_recv()

        at = block(t)
        h, c = hx[at, :width], cots[at, :]
        wg, wu, wd = r.wgs[e], r.wus[e], r.wds[e]
        expert = f * owned + x * count + e
        mine = lax.broadcasted_iota(jnp.int32, (rows, ext - width), 1) == expert
        gate = jnp.sum(jnp.where(mine, hx[at, width:].astype(F32), 0.0), axis=1, keepdims=True)
        g, u, zz = mm(h, wg), mm(h, wu), mm_nt(c, wd)
        sig = jax.nn.sigmoid(g)
        silu = g * sig
        act = silu * u
        dgate_col = jnp.where(mine, jnp.sum(act * zz, axis=1, keepdims=True), 0.0)
        act = (act * gate).astype(BF)
        dact = zz * gate
        dgate = (dact * u * sig * (1.0 + g * (1.0 - sig))).astype(BF)
        dup = (dact * silu).astype(BF)
        r.s_act[e, at, :] = act
        r.s_gate[e, at, :] = dgate
        r.s_up[e, at, :] = dup

        @pl.when(e == 0)
        def _():
            moe[...] = mm(act, wd)
            dh[...] = mm_nt(dgate, wg) + mm_nt(dup, wu)
            dgates[...] = dgate_col

        @pl.when(e > 0)
        def _():
            moe[...] += mm(act, wd)
            dh[...] += mm_nt(dgate, wg) + mm_nt(dup, wu)
            dgates[...] += dgate_col

        @pl.when(e == count - 1)
        def _():
            for k in range(4):
                @pl.when(t == k)
                def _():
                    if k >= 2:
                        moe_out(k - 2).wait()
                    r.mstage[k % 2] = moe[...].astype(BF)
                    moe_out(k).start()

            dhs[at, :width] = dh[...].astype(BF)
            dhs[at, width:] = dgates[...].astype(BF)

            @pl.when(t == 1)
            def _():
                back_y.start()

            @pl.when(t == 2)
            def _():
                back_x.start()

            @pl.when(t == 3)
            def _():
                hop_x.start()
                hop_y.start()

    stage = r.stage

    def grad_copy(b, slot):
        return pltpu.make_async_copy(stage.at[slot], r.grads.at[b], r.s_g.at[slot])

    dattn, dto, dsend = r.dattn, r.dto, r.dsend
    returns = [remote(dsend.at[m], r.do.at[m], r.s_back, m, peers[m]) for m in range(1, 4)]

    def middle_back():
        for copy in (back_y, back_x, end_y, end_x):
            copy.wait_recv()
        gn = jnp.zeros((1, width), F32)
        rg = jnp.zeros((table.shape[0], width), F32)
        for i in range(2):
            at = pl.ds(i * n, n)
            total = (
                dhs[at, :].astype(F32) + r.rdh[0, at, :].astype(F32)
                + r.rdh[1, at, :].astype(F32) + r.rdd[at, :].astype(F32)
            )
            dg, gates = total[:, width:], r.gates[at, :]
            dl = (gates * (dg - jnp.sum(gates * dg, axis=-1, keepdims=True))).astype(BF)
            rg += mm_tn(dl, hx[at, :width])
            d_hidden = total[:, :width] + mm(dl, table[...])
            normed, factor = rms_parts(r.middle[at, :])
            gn += jnp.sum(d_hidden * normed, axis=0, keepdims=True)
            d_n = d_hidden * gain
            d_mid = cots[at, :].astype(F32) + factor * (
                d_n - normed * jnp.mean(d_n * normed, axis=-1, keepdims=True)
            )
            r.dmid[at, :] = d_mid
            low = d_mid.astype(BF)
            dattn[at, :] = low
            dto[at, own_cols] = mm_nt(low, r.wo_own[...]).astype(BF)
            dto[at, away_cols] = mm_nt(low, r.wo_there[...]).astype(BF)
        for m in range(1, 4):
            dsend[m] = dto[:, head_cols(m)]
            returns[m - 1].start()
        r.do[0] = dto[:, head_cols(0)]
        top = rg[:32]
        row = lax.broadcasted_iota(jnp.int32, top.shape, 0)
        top = jnp.where(row == 17, gn, jnp.where(row < 16, top, 0.0))
        r.tiny[0] = top[:, : width // 2]
        r.tiny[1] = top[:, width // 2 :]
        for i in range(4):
            at = slice(i * 256, (i + 1) * 256)
            r.gout[at, :] = mm_tn(tout[:, at], dattn[...]).astype(BF)

    def forward():
        hop_x.wait_recv()
        end_y.start()
        hop_y.wait_recv()
        end_x.start()

    @pl.loop(0, 3 * count)
    def _(k):
        e, j = k // 3, k % 3
        pl.when(k == 5)(forward)
        pl.when(k == 3 * count - 2)(middle_back)

        @pl.when(k > 0)
        def _():
            grad_copy(0, 0).wait()
            grad_copy(0, 1).wait()

        for which, left, right in ((0, hx, r.s_gate), (1, hx, r.s_up), (2, cots, r.s_act)):
            @pl.when(j == which)
            def _():
                for i in range(2):
                    at = slice(i * ff, (i + 1) * ff)
                    if which < 2:
                        v = mm_tn(left[:, at], right[e])
                    else:
                        v = mm_tn(right[e], left[:, at])
                    stage[i] = v.astype(BF)

        for i in range(2):
            grad_copy(6 * e + 2 * j + i, i).start()

    grad_copy(0, 0).wait()
    grad_copy(0, 1).wait()
    moe_out(2).wait()
    moe_out(3).wait()
    for copy in returns:
        copy.wait()
    for copy in (*heads, *diag, *shares, first, second, back_y, back_x, hop_x, hop_y, end_y, end_x):
        copy.wait_send()


def moe_layer(att, tok, wo_own, wo_there, small, routes, cot, cot_y, cot_x, wg, wu, wd):
    rows, width = tok.shape
    owned, _, ff = wg.shape
    count = owned // 2
    ext = width + 128
    hbm = pl.BlockSpec(memory_space=pl.ANY)
    vmem = pl.BlockSpec(memory_space=pltpu.VMEM)
    dma = pltpu.SemaphoreType.DMA
    args = dict(
        att=(att.reshape(4, rows, 256), vmem), tok=(tok, vmem), wo_own=(wo_own, vmem),
        wo_there=(wo_there, vmem), small=(small, vmem), routes=(routes, vmem),
        cot=(cot, hbm), cot_y=(cot_y, hbm), cot_x=(cot_x, hbm),
        wg=(wg, hbm), wu=(wu, hbm), wd=(wd, hbm),
    )
    shape = jax.ShapeDtypeStruct
    outs = dict(
        middle=(shape((rows, width), F32), vmem),
        moe0=(shape((rows, width), BF), hbm), moe1=(shape((rows, width), BF), hbm),
        moe2=(shape((rows, width), BF), hbm), moe3=(shape((rows, width), BF), hbm),
        dmid=(shape((rows, width), F32), vmem),
        do=(shape((4, rows, 256), BF), vmem),
        grads=(shape((6 * count, ff, ff), BF), hbm),
        gout=(shape((width, width), BF), vmem),
        tiny=(shape((2, 32, width // 2), F32), vmem),
    )
    stash = pltpu.VMEM((count, 4 * rows, ff), BF)
    scratch = dict(
        att_in=pltpu.VMEM((4, rows, 256), BF), tout=pltpu.VMEM((rows, width), BF),
        hx=pltpu.VMEM((4 * rows, ext), BF), cots=pltpu.VMEM((4 * rows, width), BF),
        table=pltpu.VMEM((128, width), BF), gates=pltpu.VMEM((rows, 128), F32),
        wgs=pltpu.VMEM((count, width, ff), BF), wus=pltpu.VMEM((count, width, ff), BF),
        wds=pltpu.VMEM((count, ff, width), BF),
        s_act=stash, s_gate=stash, s_up=stash,
        moe_acc=pltpu.VMEM((rows, width), F32), dh_acc=pltpu.VMEM((rows, width), F32),
        dg_acc=pltpu.VMEM((rows, 128), F32), mstage=pltpu.VMEM((2, rows, width), BF),
        dhs=pltpu.VMEM((4 * rows, ext), BF), rdh=pltpu.VMEM((2, rows, ext), BF),
        via=pltpu.VMEM((2, rows // 2, ext), BF), rdd=pltpu.VMEM((rows, ext), BF),
        dattn=pltpu.VMEM((rows, width), BF), dto=pltpu.VMEM((rows, width), BF),
        dsend=pltpu.VMEM((4, rows, 256), BF), stage=pltpu.VMEM((2, ff, ff), BF),
        s_att=dma((2, 4)), s_diag=dma((2, 2)), s_h=dma((2, 6)), s_d=dma((2, 6)), s_back=dma((2, 4)),
        s_cot=dma((3,)), s_w=dma((3, count)), s_m=dma((4,)), s_g=dma((2,)),
    )
    names = tuple(args) + tuple(outs) + tuple(scratch)
    got = pl.pallas_call(
        functools.partial(moe_kernel, names=names, topk=routes.shape[1], count=count),
        in_specs=[v[1] for v in args.values()],
        out_specs=[v[1] for v in outs.values()],
        out_shape=[v[0] for v in outs.values()],
        scratch_shapes=list(scratch.values()),
        compiler_params=pltpu.CompilerParams(
            vmem_limit_bytes=67043328, collective_id=3, has_side_effects=True
        ),
        name="moe_layer",
    )(*[v[0] for v in args.values()])
    return types.SimpleNamespace(**dict(zip(outs, got)))


def flip_core(x):
    return lax.ppermute(x, "seq", [(0, 1), (1, 0), (2, 3), (3, 2)])


def flip_x(x):
    return lax.ppermute(x, "seq", [(0, 2), (2, 0), (1, 3), (3, 1)])


def flip_both(x):
    return lax.ppermute(x, "seq", [(0, 3), (3, 0), (1, 2), (2, 1)])


def flip_y(x):
    return lax.ppermute(x, "fsdp", [(0, 1), (1, 0)])


def flip_xy(x):
    perm = [(2 * q + f, 2 * ((q + 2) % 4) + 1 - f) for q in range(4) for f in range(2)]
    return lax.ppermute(x, ("seq", "fsdp"), perm)


def gather_seq(x):
    own = jnp.stack([x, flip_core(x)])
    far = flip_x(x)
    return jnp.concatenate([own, far[None], flip_core(far)[None]])


def swap_seq(blocks):
    return [blocks[0], flip_core(blocks[1]), flip_x(blocks[2]), flip_both(blocks[3])]


def gather_fsdp(x, axis=0):
    if lax.axis_size("fsdp") == 2:
        return jnp.concatenate([x, lax.ppermute(x, "fsdp", [(0, 1), (1, 0)])], axis=axis)
    return lax.all_gather(x, "fsdp", axis=axis, tiled=True)


def scatter_fsdp(x):
    if lax.axis_size("fsdp") == 2:
        n = x.shape[0] // 2
        other = lax.ppermute(x[n:], "fsdp", [(0, 1), (1, 0)])
        return x[:n].astype(F32) + other.astype(F32)
    return lax.psum_scatter(x, "fsdp", scatter_dimension=0, tiled=True).astype(F32)


def rope_back(w, cos, sin, low_half):
    half = HEAD_WIDTH // 2
    y = w * sin
    return w * cos + jnp.where(low_half, pltpu.roll(y, 128 - half, 1), -pltpu.roll(y, half, 1))


def reduce_kernel(*refs, names, slots, shards, fused):
    r = types.SimpleNamespace(**dict(zip(names, refs)))
    gm, mine, rc, pre, suf = r.gm, r.mine, r.rc, r.pre, r.suf
    gate, up, down, out, qkv = r.gate, r.up, r.down, r.out, r.qkv
    z, s, f = lax.axis_index("dp"), lax.axis_index("seq"), lax.axis_index("fsdp")
    core, x = s % 2, s // 2
    peer_core = (z, s + 1 - 2 * core, f)
    peer_x = (z, (s + 2) % 4, f)
    peer_y = (z, s, 1 - f)
    right, left = (z + 1, s, f), (z - 1, s, f)
    nb = gm.shape[0]
    n_moe, n_out, items = 2 * nb, 2 * nb + 2, 2 * nb + 6
    count = nb // 6
    piece = mine.shape[1]
    half, block = 2 * piece, 4 * piece
    last = slots - 1

    def other_z(k):
        return ((z + k) % slots, s, f)

    barrier = pltpu.get_barrier_semaphore()
    peers = [other_z(k) for k in range(1, slots)] + [peer_core, peer_x] + [peer_y] * fused
    for dev in peers:
        pl.semaphore_signal(barrier, inc=1, device_id=dev, device_id_type=MESH)

    def remote(src, dst, sems, b, dev):
        return pltpu.make_async_remote_copy(
            src_ref=src, dst_ref=dst, send_sem=sems.at[0, b], recv_sem=sems.at[1, b],
            device_id=dev, device_id_type=MESH,
        )

    def load(src, b):
        return pltpu.make_async_copy(src, mine.at[b], r.s_mine.at[b])

    @pl.loop(0, n_moe)
    def _(b):
        load(gm.at[b // 2, core, b % 2], b).start()

    if fused:
        loads = [
            pltpu.make_async_copy(a, b, r.s_in.at[i])
            for i, (a, b) in enumerate((
                (r.dkv.at[pl.ds(0, r.dkvs.shape[0])], r.dkvs), (r.dq, r.dq_in), (r.wc, r.wc_in),
                (r.cos, r.cos_in), (r.sin, r.sin_in), (r.h, r.h_in), (r.tok, r.tok_in),
                (r.gout, r.gout_in), (r.dmid, r.dmid_in),
            ))
        ]
        for copy in loads:
            copy.start()
    else:
        for i in range(2):
            load(r.eo.at[core, i], n_moe + i).start()
        for i in range(4):
            load(r.cols.at[i], n_out + i).start()
    pl.semaphore_wait(barrier, len(peers))

    @pl.loop(0, n_moe)
    def _(b):
        remote(gm.at[b // 2, 1 - core, b % 2], rc.at[b], r.s_rc, b, peer_core).start()

    if not fused:
        for i in range(2):
            remote(r.eo.at[1 - core, i], rc.at[n_moe + i], r.s_rc, n_moe + i, peer_core).start()

    def place(b, which, part, act):
        first_row = part * half + b % 2 * piece
        rows = pl.ds(pl.multiple_of(first_row, piece), piece)
        e, j = which * count + b // 12, b // 2 % 6
        jj = j % 2
        wide = pl.ds(pl.multiple_of(jj * block, block), block)
        at = pl.ds(pl.multiple_of(jj * block + first_row, piece), piece)
        for m, o in enumerate((gate, up)):
            @pl.when((b < n_moe) & (j // 2 == m))
            def _():
                act(o.at[e, at, :])

        @pl.when((b < n_moe) & (j // 2 == 2))
        def _():
            act(down.at[e, rows, wide])

        @pl.when((b >= n_moe) & (b < n_out))
        def _():
            act(out.at[rows, pl.ds(pl.multiple_of(which * block, block), block)])

        @pl.when(b >= n_out)
        def _():
            at = pl.ds(pl.multiple_of((b - n_out) * piece, piece), piece)
            wide = 2 * block
            for first, n, to in ((0, 256, 0), (wide, 128, 256), (wide + wide // 2, 128, 384)):
                col = pl.multiple_of(first + (2 * which + part) * n, 128)
                act(qkv.at[at, pl.ds(col, n)], pl.ds(to, n))

    def add(a, b):
        return a.astype(F32) + b.astype(F32)

    def hop(buf, sems, b, dev):
        return remote(buf.at[b], buf.at[b], sems, b, dev)

    def spread(b):
        def act(dst, cut=None):
            src = rc.at[b] if cut is None else rc.at[b, :, cut]
            remote(src, dst, r.s_oth, 0, peer_core).start()
            pltpu.make_async_copy(src, dst, r.s_out.at[0]).start()
            remote(src, dst, r.s_far, b, peer_x).start()

        place(b, x, core, act)

    lag = 2
    ahead = 16

    def begin(b):
        @pl.when(b < (n_moe if fused else items))
        def _():
            load(gm.at[0, 0, 0], b).wait()

        @pl.when(b < n_out)
        def _():
            remote(gm.at[0, 0, 0], rc.at[b], r.s_rc, b, peer_core).wait_recv()
            mine[b] = add(mine[b], rc[b]).astype(BF)

        @pl.when(z == 0)
        def _():
            remote(mine.at[b], pre.at[b], r.s_pre, b, right).start()

        @pl.when(z == last)
        def _():
            remote(mine.at[b], suf.at[b], r.s_suf, b, left).start()

    def prefix(b):
        hop(pre, r.s_pre, b, peer_x).wait_recv()
        got = pre[b].astype(F32)
        own = got + mine[b].astype(F32)

        @pl.when(z == last)
        def _():
            rc[b] = own.astype(BF)

        @pl.when(z < last)
        def _():
            @pl.when(2 * z >= slots)
            def _():
                rc[b] = (got + suf[b].astype(F32)).astype(BF)

            pre[b] = own.astype(BF)
            hop(pre, r.s_pre, b, right).start()

        @pl.when(2 * z >= slots)
        def _():
            spread(b)

    def suffix(b):
        hop(suf, r.s_suf, b, peer_x).wait_recv()
        got = suf[b].astype(F32)
        own = got + mine[b].astype(F32)

        @pl.when(z == 0)
        def _():
            rc[b] = own.astype(BF)

        @pl.when(z > 0)
        def _():
            @pl.when(2 * z < slots)
            def _():
                rc[b] = (got + pre[b].astype(F32)).astype(BF)

            suf[b] = own.astype(BF)
            hop(suf, r.s_suf, b, left).start()

        @pl.when(2 * z < slots)
        def _():
            spread(b)

    def forward(b):
        remote(rc.at[b], rc.at[b], r.s_far, b, peer_x).wait_recv()

        def act(dst, cut=None):
            remote(dst, dst, r.s_faro, 0, peer_core).start()

        place(b, 1 - x, core, act)

    def within(b, cond=True):
        return (b >= 0) & (b < items) & cond

    tsum, trecv, s_tiny = r.tsum, r.trecv, r.s_tiny

    def tiny_swap(k, dev):
        return remote(tsum.at[k], trecv.at[k], s_tiny, k, dev)

    def tiny_add(k):
        tiny_swap(k, peer_x).wait_recv()
        tsum[k + 1] = add(tsum[k], trecv[k]).astype(BF)

    def tiny_x():
        tiny_swap(0, peer_x).start()

    def tiny_core():
        tiny_add(0)
        tiny_swap(1, peer_core).start()

    def tiny_spread():
        tiny_add(1)
        for k in range(1, slots):
            remote(tsum.at[2], trecv.at[1 + k], s_tiny, 1 + k, other_z(k)).start()

    def tiny_end():
        total = tsum[2].astype(F32)
        for k in range(1, slots):
            remote(tsum.at[2], trecv.at[1 + k], s_tiny, 1 + k, other_z(k)).wait_recv()
            total = total + trecv[1 + k].astype(F32)
        r.tiny_out[...] = total

    steps = {}
    if fused:
        s_fg = r.s_fg
        dh, osum = r.dh, r.osum
        keys = r.dkvs.shape[0]
        tile = dh.shape[1]
        owner = pl.multiple_of(f * block, block)
        away = pl.multiple_of((1 - f) * block, block)
        mine_rows, away_rows = pl.ds(owner, block), pl.ds(away, block)
        near_cols = pl.ds(pl.multiple_of(x * block, block), block)
        far_cols = pl.ds(pl.multiple_of((1 - x) * block, block), block)

        send_dkv = remote(r.dkv.at[pl.ds(keys, keys)], r.rdkv, s_fg, 0, peer_y)
        send_out = remote(r.gout.at[away_rows], r.rout, s_fg, 1, peer_y)
        send_dh3 = remote(dh.at[3], r.rdh.at[1], s_fg, 2, peer_core)
        send_dh1 = remote(dh.at[1], r.rdh.at[0], s_fg, 3, peer_core)
        send_dhx = remote(r.dhx, r.rdx, s_fg, 4, peer_x)
        send_cols = remote(r.cbuf.at[away_rows], r.rcol, s_fg, 5, peer_y)
        send_outx = remote(r.osend, r.rox, s_fg, 6, peer_x)
        send_tiny = remote(r.tbuf.at[1 - f], r.rtiny, s_fg, 7, peer_y)
        eo_core = [
            remote(r.eo.at[1 - core, i], rc.at[n_moe + i], r.s_rc, n_moe + i, peer_core)
            for i in range(2)
        ]
        send_dkv.start()
        send_out.start()

        def sum_dkv():
            for copy in loads:
                copy.wait()
            send_dkv.wait_recv()
            r.dkvs[...] = add(r.dkvs[...], r.rdkv[...]).astype(BF)

        def back_tile(t, first=False):
            at = pl.ds(t * tile, tile)
            cos, sin = r.cos_in[at, :], r.sin_in[at, :]
            low_half = lax.broadcasted_iota(jnp.int32, cos.shape, 1) % HEAD_WIDTH < HEAD_WIDTH // 2
            parts = []
            for k in range(3):
                w = r.dq_in[at, k * 128 : (k + 1) * 128] if k < 2 else r.dkvs[at, :128]
                parts.append(rope_back(w.astype(F32), cos, sin, low_half).astype(BF))
            parts.append(r.dkvs[at, 128:])
            dproj = jnp.concatenate(parts, axis=1)
            grad = mm_tn(r.h_in[at, :], dproj)
            back = mm_nt(dproj, r.wc_in[...])
            dh[t] = back.astype(BF)
            normed, _ = rms_parts(r.tok_in[at, :].astype(F32))
            gain = jnp.sum((back * normed).reshape(-1, 8, back.shape[1]), axis=0)
            if first:
                r.acc[...] = grad
                r.gn[...] = gain
            else:
                r.acc[...] += grad
                r.gn[...] += gain

        def tile3():
            back_tile(3, True)
            send_dh3.start()

        def tile1():
            back_tile(1)
            send_dh1.start()

        def tile2():
            back_tile(2)
            send_dh3.wait_recv()
            r.dhx[...] = add(dh[2], r.rdh[1]).astype(BF)
            send_dhx.start()

        def tile0():
            back_tile(0)
            r.cbuf[...] = r.acc[...].astype(BF)
            send_cols.start()
            total = jnp.sum(r.gn[...], axis=0, keepdims=True)
            wide = tsum.shape[2]
            row = lax.broadcasted_iota(jnp.int32, (tsum.shape[1], wide), 0) == 16
            for k in range(2):
                part = total[:, k * wide : (k + 1) * wide]
                r.tbuf[k] = jnp.where(row, part, r.tiny[k]).astype(BF)
            send_tiny.start()

        def sum_out():
            send_out.wait_recv()
            osum[...] = add(r.gout_in[mine_rows, :], r.rout[...]).astype(BF)
            r.osend[...] = osum[:, far_cols]
            send_outx.start()

        def tiny_y():
            send_tiny.wait_recv()
            tsum[0] = add(r.tbuf[f], r.rtiny[...]).astype(BF)
            tiny_x()

        def sum_cols():
            send_cols.wait_recv()
            v = add(r.cbuf[mine_rows, :], r.rcol[...]).astype(BF)
            for i in range(4):
                mine[n_out + i] = v[i * piece : (i + 1) * piece]

        def sum_outx():
            send_outx.wait_recv()
            v = add(osum[:, near_cols], r.rox[...]).astype(BF)
            for i in range(4):
                r.eo[i // 2, i % 2] = v[i * piece : (i + 1) * piece]
            for i in range(2):
                eo_core[i].start()
                mine[n_moe + i] = r.eo[core, i]

        def inputs_back():
            send_dh1.wait_recv()
            send_dhx.wait_recv()
            up_grad = add(dh[0], r.rdh[0]) + r.rdx[...].astype(F32)
            normed, factor = rms_parts(r.tok_in[:tile].astype(F32))
            d_n = up_grad * r.small[16:17, :].astype(F32)
            r.dtok[...] = r.dmid_in[...] + factor * (
                d_n - normed * jnp.mean(d_n * normed, axis=-1, keepdims=True)
            )

        order = [
            None, sum_dkv, tile3, tile1, tile2, tile0, sum_out, tiny_y, sum_cols, tiny_core,
            sum_outx, inputs_back, tiny_spread,
        ]
        steps = {2 * i + ahead - 2: fn for i, fn in enumerate(order) if fn is not None}
    else:
        tsum[0] = r.tiny[...].astype(BF)
        tiny_x()
        steps = {1: tiny_core, 2: tiny_spread}

    @pl.loop(0, items + ahead + (last + 1) * lag)
    def _(i):
        for fn, b, cond in (
            (begin, i, True),
            (prefix, i - ahead - lag * z, z > 0),
            (suffix, i - ahead - lag * (last - z), z < last),
            (forward, i - ahead - lag * (last + 1), True),
        ):
            @pl.when(within(b, cond))
            def _():
                fn(b)

        for k, fn in steps.items():
            pl.when(i == k)(fn)

    tiny_end()

    @pl.loop(0, items)
    def _(b):
        one = rc.at[b]

        @pl.when(b < n_out)
        def _():
            remote(one, one, r.s_rc, b, peer_core).wait_send()

        @pl.when(z < last)
        def _():
            hop(pre, r.s_pre, b, peer_x).wait_send()

        @pl.when(z > 0)
        def _():
            hop(suf, r.s_suf, b, peer_x).wait_send()

        remote(one, one, r.s_far, b, peer_x).wait_send()

    remote(rc, rc, r.s_oth, 0, peer_core).wait()
    remote(rc, rc, r.s_faro, 0, peer_core).wait()
    pltpu.make_async_copy(rc, rc, r.s_out.at[0]).wait()
    tiny_swap(0, peer_x).wait_send()
    tiny_swap(1, peer_core).wait_send()
    for k in range(1, slots):
        remote(tsum.at[2], trecv.at[1 + k], s_tiny, 1 + k, other_z(k)).wait_send()
    if fused:
        for copy in (send_dkv, send_out, send_dh3, send_dh1, send_dhx, send_cols, send_outx, send_tiny):
            copy.wait_send()


def reduce_grads(gm, tiny, slots, shards, eo=None, cols=None, fused=None):
    count, _, ff, _ = gm.shape
    width = 2 * ff
    nb = 6 * count
    piece = ff // 4
    items = 2 * nb + 6
    hbm = pl.BlockSpec(memory_space=pl.ANY)
    vmem = pl.BlockSpec(memory_space=pltpu.VMEM)
    dma = pltpu.SemaphoreType.DMA
    args = dict(gm=(gm.reshape(nb, 2, 2, piece, ff), hbm), tiny=(tiny, vmem))
    outs = dict(
        gate=(jax.ShapeDtypeStruct((2 * count, width, ff), BF), hbm),
        up=(jax.ShapeDtypeStruct((2 * count, width, ff), BF), hbm),
        down=(jax.ShapeDtypeStruct((2 * count, ff, width), BF), hbm),
        out=(jax.ShapeDtypeStruct((ff, width), BF), hbm),
        qkv=(jax.ShapeDtypeStruct((ff, 2 * width), BF), hbm),
        tiny_out=(jax.ShapeDtypeStruct(tiny.shape[-2:], F32), vmem),
    )
    buf = pltpu.VMEM((items, piece, ff), BF)
    scratch = dict(
        mine=buf, rc=buf, pre=buf, suf=buf,
        tsum=pltpu.VMEM((3,) + tiny.shape[-2:], BF),
        trecv=pltpu.VMEM((slots + 1,) + tiny.shape[-2:], BF),
        s_tiny=dma((2, slots + 1)), s_mine=dma((items,)), s_out=dma((1,)),
    )
    each = dma((2, items))
    scratch.update(s_rc=each, s_pre=each, s_suf=each, s_far=each)
    scratch.update(s_oth=dma((2, 1)), s_faro=dma((2, 1)))
    if fused is None:
        args.update(
            eo=(eo.reshape(2, 2, piece, ff), hbm), cols=(cols.reshape(4, piece, ff), hbm)
        )
    else:
        inner = {}
        for k, v in fused.items():
            args[k] = (v, hbm)
            inner[k] = pltpu.VMEM(v.shape, v.dtype)
        args.update(small=(fused.pop("small"), vmem))
        rows = args["dmid"][0].shape[0]
        keys = args["dkv"][0].shape[0] // 2
        outs.update(dtok=(jax.ShapeDtypeStruct((rows, width), F32), vmem))
        scratch.update(
            rdkv=pltpu.VMEM((keys, 256), BF), dkvs=pltpu.VMEM((keys, 256), BF),
            rout=pltpu.VMEM((ff, width), BF), osum=pltpu.VMEM((ff, width), BF),
            osend=pltpu.VMEM((ff, ff), BF), rox=pltpu.VMEM((ff, ff), BF),
            eo=pltpu.VMEM((2, 2, piece, ff), BF),
            dq_in=inner["dq"], wc_in=inner["wc"], cos_in=inner["cos"], sin_in=inner["sin"],
            h_in=inner["h"], tok_in=inner["tok"], gout_in=inner["gout"], dmid_in=inner["dmid"],
            s_in=dma((9,)),
            dh=pltpu.VMEM((4, rows, width), BF), rdh=pltpu.VMEM((2, rows, width), BF),
            dhx=pltpu.VMEM((rows, width), BF), rdx=pltpu.VMEM((rows, width), BF),
            acc=pltpu.VMEM((width, ff), F32), gn=pltpu.VMEM((8, width), F32),
            cbuf=pltpu.VMEM((width, ff), BF), rcol=pltpu.VMEM((ff, ff), BF),
            tbuf=pltpu.VMEM(tiny.shape, BF), rtiny=pltpu.VMEM(tiny.shape[-2:], BF),
            s_fg=dma((2, 8)),
        )
    names = tuple(args) + tuple(outs) + tuple(scratch)
    got = pl.pallas_call(
        functools.partial(
            reduce_kernel, names=names, slots=slots, shards=shards, fused=fused is not None
        ),
        in_specs=[v[1] for v in args.values()],
        out_specs=[v[1] for v in outs.values()],
        out_shape=[v[0] for v in outs.values()],
        scratch_shapes=list(scratch.values()),
        compiler_params=params(collective_id=1, has_side_effects=True),
        name="reduce_grads",
    )(*[v[0] for v in args.values()])
    return types.SimpleNamespace(**dict(zip(outs, got)))


def gather_rows(x):
    return lax.all_gather(x, "fsdp", axis=0, tiled=True)


def local(
    tokens, cotangent, lengths, order, routes, norm1, query_key_value_weight, w_out, norm2, router,
    w_gate, w_up, w_down,
):
    groups = lax.axis_size("seq")
    shards = lax.axis_size("fsdp")
    slots = lax.axis_size("dp")
    assert groups == 4
    seq, fsdp = lax.axis_index("seq"), lax.axis_index("fsdp")
    core, far = seq % 2, seq // 2
    rows, width = tokens.shape[1:]
    span = rows // 2
    x = tokens[0]
    limit = lengths[:1]
    n_experts = router.shape[1]
    owned = w_gate.shape[0]
    count = owned // 2

    table = order.reshape(groups, shards, 2)
    relative = jnp.arange(groups, dtype=jnp.int32) ^ seq
    table = jnp.take(table, relative, axis=0)
    qtab = jnp.take(table, fsdp, axis=1).reshape(-1)
    if shards == 2:
        held = jnp.stack([fsdp, 1 - fsdp])
    else:
        held = jnp.arange(shards)
    ktab = jnp.transpose(jnp.take(table, held, axis=1), (1, 0, 2)).reshape(-1)
    qpos = (qtab[:, None] * span + jnp.arange(span, dtype=jnp.int32)[None, :]).reshape(-1)

    heads = QUERY_HEADS // groups
    qw, kw = heads * HEAD_WIDTH, KEY_VALUE_HEADS // groups * HEAD_WIDTH
    w3 = query_key_value_weight
    small = jnp.concatenate(
        [jnp.transpose(router), norm1[None], norm2[None], jnp.zeros((14, norm1.shape[0]), BF)]
    )
    if shards == 2:
        tok, wcols, small, hidden_one, q, kv, cos, sin = front(qtab, order.shape[0], x, w3, small)
        tok, kv = tok.reshape(groups * rows, width), kv.reshape(-1, 256)
        w_out, cotangent, kv = lax.optimization_barrier((w_out, cotangent, kv))
    else:
        half = HEAD_WIDTH // 2
        freqs = jnp.exp(jnp.arange(half, dtype=F32) * (-2.0 * math.log(ROPE_BASE) / HEAD_WIDTH))
        angles = qpos.astype(F32)[:, None] * freqs[None, :]
        cos, sin = jnp.tile(jnp.cos(angles), (1, 4)), jnp.tile(jnp.sin(angles), (1, 4))
        wq = lax.dynamic_slice_in_dim(w3, seq * qw, qw, 1)
        wk = lax.dynamic_slice_in_dim(w3, QUERY_HEADS * HEAD_WIDTH + seq * kw, kw, 1)
        wv = lax.dynamic_slice_in_dim(
            w3, (QUERY_HEADS + KEY_VALUE_HEADS) * HEAD_WIDTH + seq * kw, kw, 1
        )
        wcols = gather_rows(jnp.concatenate([wq, wk, wv], axis=1))
        small = lax.all_gather(small, "fsdp", axis=1, tiled=True)
        tok = gather_seq(x).reshape(groups * rows, width)
        hidden_one, q, kv_own = project(tok, small[16:17].astype(F32), wcols, cos, sin, rows)
        kv = gather_fsdp(kv_own)
    gain_one, gain_two = small[16].astype(F32), small[17].astype(F32)
    route_rows = small[:n_experts]

    kb = 4 * span
    own_valid = (qpos[:rows] < limit[0])[:, None]
    masked_cot = jnp.where(own_valid, cotangent[0], jnp.zeros_like(cotangent[0]))
    if shards == 2:
        wo_there, cot_y, cot_x = flip_y(w_out), flip_y(masked_cot), flip_x(masked_cot)
    attended, low, lse = attend(qtab, ktab, limit, q, kv, span, kb)
    inputs = x.astype(F32)
    if shards == 2:
        out = moe_layer(
            low, x, w_out, wo_there, small, routes[0], masked_cot, cot_y, cot_x, w_gate, w_up, w_down
        )
        parts = [out.moe0, flip_y(out.moe1), flip_x(out.moe2), flip_xy(out.moe3)]
        d_heads = out.do.reshape(groups * rows, qw)
        middle, d_middle, grad_out, tiny = out.middle, out.dmid, out.gout, out.tiny
        weight_grads = out.grads.reshape(count, 6, w_gate.shape[2], -1)
    else:
        sent = low.reshape(groups, rows, qw)
        got = jnp.stack(swap_seq([sent[m] for m in range(groups)]))
        got = jnp.take(got, relative, axis=0)
        token_out = jnp.transpose(got, (1, 0, 2)).reshape(rows, groups * qw)
        out_full = gather_rows(w_out)

        middle = inputs + mm(token_out, out_full)
        normed_two, factor_two = rms_parts(middle)
        hidden_two = (normed_two * gain_two).astype(BF)
        logits = mm_nt(hidden_two, route_rows)
        chosen = jnp.any(
            routes[0][:, :, None] == jnp.arange(n_experts, dtype=jnp.int32)[None, None, :], axis=1
        )
        top = jnp.max(jnp.where(chosen, logits, NEG), axis=-1, keepdims=True)
        raised = jnp.where(chosen, jnp.exp(logits - top), 0.0)
        gates = raised / jnp.sum(raised, axis=-1, keepdims=True)

        def share(v):
            near = gather_rows(v)
            return jnp.concatenate([near, flip_x(near)])

        cot_all = share(masked_cot)
        extended = jnp.concatenate(
            [hidden_two, gates.astype(BF), jnp.zeros((rows, 128 - n_experts), BF)], axis=1
        )
        hid_all = share(extended)
        base = jnp.stack([far * count, fsdp * owned + far * count]).astype(jnp.int32)
        part = rows * 4
        moe_parts, dh_parts, weight_grads = [], [], None
        for i in range(hid_all.shape[0] // part):
            got = experts(
                base, count, hid_all[i * part : (i + 1) * part], cot_all[i * part : (i + 1) * part],
                w_gate, w_up, w_down, rows,
            )
            moe_parts.append(got[0])
            dh_parts.append(got[1])
            if weight_grads is None:
                weight_grads = got[2]
            else:
                weight_grads = (weight_grads.astype(F32) + got[2].astype(F32)).astype(BF)

        def give_back(parts):
            v = jnp.concatenate(parts) if len(parts) > 1 else parts[0]
            n = v.shape[0] // 2
            near = v[:n].astype(F32) + flip_x(v[n:]).astype(F32)
            return lax.psum_scatter(near.astype(BF), "fsdp", scatter_dimension=0, tiled=True).astype(F32)

        d_ext = give_back(dh_parts)
        d_gates = d_ext[:, width : width + n_experts]
        d_logits = (gates * (d_gates - jnp.sum(gates * d_gates, axis=-1, keepdims=True))).astype(BF)
        grad_router = mm_tn(hidden_two, d_logits)
        d_hidden = d_ext[:, :width] + mm(d_logits, route_rows)
        grad_norm2 = jnp.sum(d_hidden * normed_two, axis=0)
        d_n = d_hidden * gain_two
        d_middle = masked_cot.astype(F32) + factor_two * (
            d_n - normed_two * jnp.mean(d_n * normed_two, axis=-1, keepdims=True)
        )
        d_attn = d_middle.astype(BF)
        grad_out = mm_tn(token_out, d_attn).astype(BF)
        d_token_out = mm_nt(d_attn, out_full).astype(BF)
        d_heads = jnp.transpose(d_token_out.reshape(rows, groups, qw), (1, 0, 2))
        d_heads = jnp.take(d_heads, relative, axis=0)
        d_heads = jnp.concatenate(swap_seq([d_heads[m] for m in range(groups)]))
    dq, dkv = attend_back(qtab, ktab, limit, q, kv, d_heads, attended, lse, span, kb)

    block = w_gate.shape[2]
    shard_rows = width // shards

    def tiny_rows(first):
        return jnp.concatenate(
            [jnp.transpose(grad_router), first[None], grad_norm2[None], jnp.zeros((14, width), F32)]
        ).reshape(32, shards, shard_rows).transpose(1, 0, 2)

    if shards == 2:
        got = reduce_grads(
            weight_grads, tiny, slots, shards,
            fused=dict(
                dkv=dkv, dq=dq, tok=tok, h=hidden_one, wc=wcols, cos=cos, sin=sin,
                small=small, dmid=d_middle, gout=grad_out,
            ),
        )
        d_inputs = got.dtok
    else:
        dh_one, grad_cols, grad_norm1 = project_back(
            tok, hidden_one, dq, scatter_fsdp(dkv), wcols, cos, sin, rows
        )
        dh_one = dh_one.reshape(groups, rows, width)
        near = dh_one[0::2].astype(F32) + flip_core(dh_one[1::2]).astype(F32)
        d_hidden_one = near[0] + flip_x(near[1].astype(BF)).astype(F32)
        normed_one, factor_one = rms_parts(inputs)
        d_n = d_hidden_one * gain_one
        d_inputs = d_middle + factor_one * (
            d_n - normed_one * jnp.mean(d_n * normed_one, axis=-1, keepdims=True)
        )

        def to_owner(g):
            part = lax.psum_scatter(g, "fsdp", scatter_dimension=0, tiled=True)
            return jnp.pad(part, ((0, block - part.shape[0]), (0, 0)))

        cols = to_owner(grad_cols)
        mine = to_owner(grad_out).reshape(block, 2, block)
        kept = lax.dynamic_index_in_dim(mine, far, 1, keepdims=False)
        sent = lax.dynamic_index_in_dim(mine, 1 - far, 1, keepdims=False)
        outs = (kept.astype(F32) + flip_x(sent).astype(F32)).astype(BF)
        tiny = tiny_rows(jnp.sum(grad_norm1, axis=0))
        tiny = lax.psum_scatter(tiny, "fsdp", scatter_dimension=0, tiled=True)[0]
        got = reduce_grads(weight_grads, tiny, slots, shards, eo=outs, cols=cols)
    grad_gate, grad_up, grad_down, shard_out, shard_qkv, *tiny = widen(
        [got.gate, got.up, got.down, got.out, got.qkv], got.tiny_out, n_experts
    )
    shard_out, shard_qkv = shard_out[:shard_rows], shard_qkv[:shard_rows]
    if shards == 2:
        layer_out = (middle + sum(p.astype(F32) for p in parts)).astype(BF)
    else:
        layer_out = (middle + give_back(moe_parts)).astype(BF)
    return (
        layer_out[None], d_inputs[None], tiny[0], shard_qkv, shard_out, tiny[1], tiny[2],
        grad_gate, grad_up, grad_down,
    )


def solution(mesh):
    placed = (
        P("dp", ("seq", "fsdp"), None),
        P("dp", ("seq", "fsdp"), None),
        P("dp"),
        P(),
        P("dp", ("seq", "fsdp"), None),
        P("fsdp"),
        P("fsdp", None),
        P("fsdp", None),
        P("fsdp"),
        P("fsdp", None),
        P("fsdp", None, None),
        P("fsdp", None, None),
        P("fsdp", None, None),
    )
    return jax.shard_map(
        local,
        mesh=mesh,
        in_specs=placed,
        out_specs=(
            P("dp", ("seq", "fsdp"), None),
            P("dp", ("seq", "fsdp"), None),
            P("fsdp"),
            P("fsdp", None),
            P("fsdp", None),
            P("fsdp"),
            P("fsdp", None),
            P("fsdp", None, None),
            P("fsdp", None, None),
            P("fsdp", None, None),
        ),
        check_vma=False,
    )
```

```python
import functools
import math
import types

import jax
import jax.numpy as jnp
import numpy as np
from jax import lax
from jax.experimental import pallas as pl
from jax.experimental.pallas import tpu as pltpu
from jax.sharding import PartitionSpec as P

QUERY_HEADS = 16
KEY_VALUE_HEADS = 8
HEAD_WIDTH = 64
TOPK = 8

EPS = 1e-06
ROPE_BASE = 10000.0
LOG2E = math.log2(math.e)
NEG = -1e30
BF = jnp.bfloat16
F32 = jnp.float32
VMEM_LIMIT = 60 * 1024 * 1024
OUT_STEP = 6

NT_DIMS = (((1,), (1,)), ((), ()))
TN_DIMS = (((0,), (0,)), ((), ()))


def mm(a, b):
    return jnp.dot(a, b, preferred_element_type=F32)


def mm_nt(a, b):
    return lax.dot_general(a, b, NT_DIMS, preferred_element_type=F32)


def mm_tn(a, b):
    return lax.dot_general(a, b, TN_DIMS, preferred_element_type=F32)


def params(**kw):
    return pltpu.CompilerParams(vmem_limit_bytes=VMEM_LIMIT, **kw)


def whole(shape):
    return pl.BlockSpec(shape, lambda *_: (0,) * len(shape))


def rms_parts(x):
    factor = lax.rsqrt(jnp.mean(x * x, axis=-1, keepdims=True) + EPS)
    return x * factor, factor


def qkv_kernel(tok_ref, gain_ref, w_ref, cos_ref, sin_ref, h_ref, q_ref, kv_ref):
    normed, _ = rms_parts(tok_ref[...].astype(F32))
    h = (normed * gain_ref[...]).astype(BF)
    h_ref[...] = h
    proj = mm(h, w_ref[...])
    cos, sin = cos_ref[...], sin_ref[...]
    low_half = lax.broadcasted_iota(jnp.int32, cos.shape, 1) % HEAD_WIDTH < HEAD_WIDTH // 2
    half = HEAD_WIDTH // 2
    for t in range(3):
        w = proj[:, t * 128 : (t + 1) * 128]
        rot = jnp.where(low_half, -pltpu.roll(w, 128 - half, 1), pltpu.roll(w, half, 1))
        out = (w * cos + rot * sin).astype(BF)
        if t < 2:
            q_ref[:, t * 128 : (t + 1) * 128] = out
        else:
            kv_ref[:, :128] = out
    kv_ref[:, 128:] = proj[:, 384:].astype(BF)


def project(tok, gain, w, cos, sin, tile):
    rows, width = tok.shape
    return pl.pallas_call(
        qkv_kernel,
        grid=(rows // tile,),
        in_specs=[
            pl.BlockSpec((tile, width), lambda i: (i, 0)),
            whole((1, width)),
            whole(w.shape),
            pl.BlockSpec((tile, 128), lambda i: (i, 0)),
            pl.BlockSpec((tile, 128), lambda i: (i, 0)),
        ],
        out_specs=[
            pl.BlockSpec((tile, width), lambda i: (i, 0)),
            pl.BlockSpec((tile, 256), lambda i: (i, 0)),
            pl.BlockSpec((tile, 256), lambda i: (i, 0)),
        ],
        out_shape=[
            jax.ShapeDtypeStruct((rows, width), BF),
            jax.ShapeDtypeStruct((rows, 256), BF),
            jax.ShapeDtypeStruct((rows, 256), BF),
        ],
        compiler_params=params(),
        name="project",
    )(tok, gain, w, cos, sin)


MESH = pl.DeviceIdType.MESH


def rope_rows(w, cos, sin):
    half = HEAD_WIDTH // 2
    low_half = lax.broadcasted_iota(jnp.int32, w.shape, 1) % HEAD_WIDTH < half
    rot = jnp.where(low_half, -pltpu.roll(w, 128 - half, 1), pltpu.roll(w, half, 1))
    return w * cos + rot * sin


def front_kernel(
    spans, tok, w3, small, rtab, stab, tok_out, wc_out, small_all, h_out, q, kv, cos_out, sin_out,
    tok_all, wc, h, cos, sin, s_tok, s_w, s_own, s_kv, s_end
):
    z, s, f = lax.axis_index("dp"), lax.axis_index("seq"), lax.axis_index("fsdp")
    core = s % 2
    peer_core = (z, s + 1 - 2 * core, f)
    peer_x = (z, (s + 2) % 4, f)
    peer_y = (z, s, 1 - f)
    rows, width = tok.shape
    part = small.shape[1]

    barrier = pltpu.get_barrier_semaphore()
    for dev in (peer_core, peer_x, peer_y):
        pl.semaphore_signal(barrier, inc=1, device_id=dev, device_id_type=MESH)

    def remote(src, dst, sems, b, dev):
        return pltpu.make_async_remote_copy(
            src_ref=src, dst_ref=dst, send_sem=sems.at[0, b], recv_sem=sems.at[1, b],
            device_id=dev, device_id_type=MESH,
        )

    own_rows = pl.ds(pl.multiple_of(f * part, part), part)
    pieces = []
    for first, n, to in ((0, 256, 0), (width, 128, 256), (width + width // 2, 128, 384)):
        src = w3.at[:, pl.ds(pl.multiple_of(first + s * n, 128), n)]
        pieces.append((src, wc.at[own_rows, pl.ds(to, n)]))
    local = [pltpu.make_async_copy(a, b, s_own.at[i]) for i, (a, b) in enumerate(pieces)]
    for copy in local:
        copy.start()
    small_all[:, own_rows] = small[...]
    tok_all[0] = tok[...]
    pl.semaphore_wait(barrier, 3)
    over = remote(tok, tok_all.at[2], s_tok, 1, peer_x)
    near = remote(tok, tok_all.at[1], s_tok, 0, peer_core)
    onward = remote(tok_all.at[2], tok_all.at[3], s_tok, 2, peer_core)
    weights = [remote(a, b, s_w, i, peer_y) for i, (a, b) in enumerate(pieces)]
    weights.append(remote(small, small_all.at[:, own_rows], s_w, 3, peer_y))
    over.start()
    for copy in weights:
        copy.start()
    near.start()
    for copy in local:
        copy.wait()
    for copy in weights:
        copy.wait_recv()
    gain = small_all[16:17, :].astype(F32)

    def kv_copy(t):
        at = pl.ds(pl.multiple_of(t * rows, rows), rows)
        return remote(kv.at[0, at], kv.at[1, at], s_kv, t, peer_y)

    ends = [pltpu.make_async_copy(wc, wc_out, s_end.at[0])]
    ends[0].start()
    span = rows // 2
    for k in range(8):
        at = pl.ds(k * span, span)
        row = pl.ds(spans[k], 1)
        c, n = stab[0, row, :], stab[1, row, :]
        cos[at, :] = rtab[0] * c - rtab[1] * n
        sin[at, :] = rtab[1] * c + rtab[0] * n
    for i, (src, dst) in enumerate(((cos, cos_out), (sin, sin_out))):
        ends.append(pltpu.make_async_copy(src, dst, s_end.at[1 + i]))
        ends[-1].start()

    def end(t):
        at = pl.ds(pl.multiple_of(t * rows, rows), rows)
        return [
            pltpu.make_async_copy(tok_all.at[t], tok_out.at[t], s_end.at[3 + t]),
            pltpu.make_async_copy(h.at[at], h_out.at[at], s_end.at[7 + t]),
        ]

    @pl.loop(0, 4)
    def _(t):
        pl.when(t == 1)(near.wait_recv)

        @pl.when(t == 2)
        def _():
            over.wait_recv()
            onward.start()

        pl.when(t == 3)(onward.wait_recv)
        at = pl.ds(pl.multiple_of(t * rows, rows), rows)
        normed, _ = rms_parts(tok_all[t].astype(F32))
        hidden = (normed * gain).astype(BF)
        h[at, :] = hidden
        proj = mm(hidden, wc[...])
        c, n = cos[at, :], sin[at, :]
        kv[0, at, :128] = rope_rows(proj[:, 256:384], c, n).astype(BF)
        kv[0, at, 128:] = proj[:, 384:].astype(BF)
        kv_copy(t).start()
        for k in range(2):
            q[at, k * 128 : (k + 1) * 128] = rope_rows(proj[:, k * 128 : (k + 1) * 128], c, n).astype(BF)
        for copy in end(t):
            copy.start()

    for t in range(4):
        ends.extend(end(t))
    for t in range(4):
        kv_copy(t).wait()
    for copy in ends:
        copy.wait()
    for copy in (over, near, onward, *weights):
        copy.wait_send()


def front(spans, n_spans, tok, w3, small):
    rows, width = tok.shape
    span, half = rows // 2, HEAD_WIDTH // 2
    freqs = np.exp(np.arange(half) * (-2.0 * math.log(ROPE_BASE) / HEAD_WIDTH)).astype(np.float32)

    def table(positions):
        angles = np.tile(positions[:, None].astype(np.float64) * freqs[None, :], (1, 4))
        return jnp.asarray(np.stack([np.cos(angles), np.sin(angles)]), F32)

    rtab, stab = table(np.arange(span)), table(np.arange(n_spans) * span)
    vmem = pl.BlockSpec(memory_space=pltpu.VMEM)
    hbm = pl.BlockSpec(memory_space=pl.ANY)
    dma = pltpu.SemaphoreType.DMA
    shape = jax.ShapeDtypeStruct
    return pl.pallas_call(
        front_kernel,
        in_specs=[pl.BlockSpec(memory_space=pltpu.SMEM), vmem, hbm, vmem, vmem, vmem],
        out_specs=[hbm, hbm, vmem, hbm, vmem, vmem, hbm, hbm],
        out_shape=[
            shape((4, rows, width), BF),
            shape((width, 512), BF),
            shape((small.shape[0], width), BF),
            shape((4 * rows, width), BF),
            shape((4 * rows, 256), BF),
            shape((2, 4 * rows, 256), BF),
            shape((4 * rows, 128), F32),
            shape((4 * rows, 128), F32),
        ],
        scratch_shapes=[
            pltpu.VMEM((4, rows, width), BF), pltpu.VMEM((width, 512), BF),
            pltpu.VMEM((4 * rows, width), BF),
            pltpu.VMEM((4 * rows, 128), F32), pltpu.VMEM((4 * rows, 128), F32),
            dma((2, 3)), dma((2, 4)), dma((3,)), dma((2, 4)), dma((11,)),
        ],
        compiler_params=params(collective_id=2, has_side_effects=True),
        name="front",
    )(spans, tok, w3, small, rtab, stab)


def widen_kernel(*refs):
    n = (len(refs) - 4) // 2
    ins, outs = refs[:n], refs[n + 1 : 2 * n + 1]
    for a, b in zip(ins, outs):
        b[...] = a[...].astype(F32)
    tiny, (one, two, router) = refs[n], refs[2 * n + 1 :]

    @pl.when(pl.program_id(0) == 0)
    def _():
        one[...] = tiny[16:17, :]
        two[...] = tiny[17:18, :]
        router[...] = jnp.transpose(tiny[...])[:, : router.shape[1]]


def widen(arrays, tiny, n_experts):
    flat = [a.reshape(-1, a.shape[-1]) for a in arrays]
    steps = 8
    wide = tiny.shape[1]
    specs = [pl.BlockSpec((a.shape[0] // steps, a.shape[1]), lambda i: (i, 0)) for a in flat]
    shape = jax.ShapeDtypeStruct
    got = pl.pallas_call(
        widen_kernel,
        grid=(steps,),
        in_specs=specs + [whole(tiny.shape)],
        out_specs=specs + [whole((1, wide)), whole((1, wide)), whole((wide, n_experts))],
        out_shape=[shape(a.shape, F32) for a in flat]
        + [shape((1, wide), F32), shape((1, wide), F32), shape((wide, n_experts), F32)],
        compiler_params=params(),
        name="widen",
    )(*flat, tiny)
    n = len(arrays)
    return [g.reshape(a.shape) for g, a in zip(got, arrays)] + [got[n][0], got[n + 1][0], got[n + 2]]


def project_back_kernel(
    tok_ref, h_ref, dq_ref, dkv_ref, w_ref, cos_ref, sin_ref, dh_ref, gw_ref, gn_ref, acc
):
    step = pl.program_id(0)

    @pl.when(step == 0)
    def _():
        acc[...] = jnp.zeros_like(acc)
        gn_ref[...] = jnp.zeros_like(gn_ref)

    cos, sin = cos_ref[...], sin_ref[...]
    half = HEAD_WIDTH // 2
    low_half = lax.broadcasted_iota(jnp.int32, cos.shape, 1) % HEAD_WIDTH < half
    parts = []
    for t in range(3):
        w = dq_ref[:, t * 128 : (t + 1) * 128] if t < 2 else dkv_ref[:, :128]
        w = w.astype(F32)
        y = w * sin
        rot = jnp.where(low_half, pltpu.roll(y, 128 - half, 1), -pltpu.roll(y, half, 1))
        parts.append((w * cos + rot).astype(BF))
    parts.append(dkv_ref[:, 128:].astype(BF))
    dproj = jnp.concatenate(parts, axis=1)
    acc[...] += mm_tn(h_ref[...], dproj)
    dh = mm_nt(dproj, w_ref[...])
    dh_ref[...] = dh.astype(BF)
    normed, _ = rms_parts(tok_ref[...].astype(F32))
    gn_ref[...] += jnp.sum((dh * normed).reshape(-1, 8, dh.shape[1]), axis=0)

    @pl.when(step == pl.num_programs(0) - 1)
    def _():
        gw_ref[...] = acc[...].astype(BF)


def project_back(tok, h, dq, dkv, w, cos, sin, tile):
    rows, width = tok.shape
    row = lambda n: pl.BlockSpec((tile, n), lambda i: (i, 0))
    return pl.pallas_call(
        project_back_kernel,
        grid=(rows // tile,),
        in_specs=[row(width), row(width), row(256), row(256), whole(w.shape), row(128), row(128)],
        out_specs=[row(width), whole(w.shape), whole((8, width))],
        out_shape=[
            jax.ShapeDtypeStruct((rows, width), BF),
            jax.ShapeDtypeStruct(w.shape, BF),
            jax.ShapeDtypeStruct((8, width), F32),
        ],
        scratch_shapes=[pltpu.VMEM(w.shape, F32)],
        compiler_params=params(),
        name="project_back",
    )(tok, h, dq, dkv, w, cos, sin)


def stack_heads(a, b, dtype=BF):
    a, b = a.astype(F32), b.astype(F32)
    low = lax.broadcasted_iota(jnp.int32, a.shape, 1) < HEAD_WIDTH
    turn = lambda v: pltpu.roll(v, HEAD_WIDTH, 1)
    rows = [
        jnp.where(low, a, 0.0), jnp.where(low, turn(a), 0.0),
        jnp.where(low, 0.0, turn(b)), jnp.where(low, 0.0, b),
    ]
    return jnp.concatenate(rows, axis=0).astype(dtype)


def unstack_heads(x):
    n = x.shape[0] // 4
    low = lax.broadcasted_iota(jnp.int32, (n, 128), 1) < HEAD_WIDTH
    turn = lambda v: pltpu.roll(v, HEAD_WIDTH, 1)
    return (
        jnp.where(low, x[:n], turn(x[n : 2 * n])),
        jnp.where(low, turn(x[2 * n : 3 * n]), x[3 * n :]),
    )


def block_counts(span_id, limit, span, kb):
    first = span_id * span
    seen = (first + span - 1) // kb + 1
    blocks = jnp.minimum(seen, (limit + kb - 1) // kb)
    full = jnp.minimum(first + 1, limit) // kb
    return jnp.minimum(full, blocks), blocks


def sort_spans(ktab_ref, src, dst, lanes, span, count):
    @pl.loop(0, count)
    def _(j):
        to = pl.multiple_of(ktab_ref[j] * span, span)
        dst[pl.ds(to, span), :] = src[pl.ds(pl.multiple_of(j * span, span), span), lanes]


def attend_kernel(
    qtab_ref, ktab_ref, len_ref, q_ref, kv_ref, o_ref, low_ref, lse_ref, ks, vs, *, span, kb
):
    step = pl.program_id(0)
    count = ks.shape[0] // span

    @pl.when(step == 0)
    def _():
        sort_spans(ktab_ref, kv_ref, ks, slice(0, 128), span, count)
        sort_spans(ktab_ref, kv_ref, vs, slice(128, 256), span, count)

    q = stack_heads(q_ref[:, :128], q_ref[:, 128:])
    rows = 4 * span
    limit = len_ref[0]
    span_id = qtab_ref[step]
    full, blocks = block_counts(span_id, limit, span, kb)
    qpos = span_id * span + lax.broadcasted_iota(jnp.int32, (rows, kb), 0) % span
    col = lax.broadcasted_iota(jnp.int32, (rows, kb), 1)
    last = jnp.minimum(qpos, limit - 1)

    def body(masked, i, carry):
        top, total, acc = carry
        at = pl.multiple_of(i * kb, kb)
        s = mm_nt(q, ks[pl.ds(at, kb), :]) * (HEAD_WIDTH**-0.5 * LOG2E)
        if masked:
            s = jnp.where(col + i * kb <= last, s, NEG)
        new = jnp.maximum(top, jnp.max(s, axis=1, keepdims=True))
        fade = jnp.exp2(top - new)
        p = jnp.exp2(s - new)
        total = total * fade + jnp.sum(p, axis=1, keepdims=True)
        acc = acc * fade + mm(p.astype(BF), vs[pl.ds(at, kb), :])
        return new, total, acc

    carry = (
        jnp.full((rows, 1), NEG, F32),
        jnp.zeros((rows, 1), F32),
        jnp.zeros((rows, 128), F32),
    )
    carry = lax.fori_loop(0, full, functools.partial(body, False), carry)
    top, total, acc = lax.fori_loop(full, blocks, functools.partial(body, True), carry)
    a, b = unstack_heads(acc / total)
    o_ref[:, :128] = a
    o_ref[:, 128:] = b
    low_ref[:, :128] = a.astype(BF)
    low_ref[:, 128:] = b.astype(BF)
    lse = jnp.broadcast_to(top + jnp.log2(total), (rows, 128))
    lse_ref[0] = jnp.transpose(lse)[:8]


def attend_short_kernel(
    qtab_ref, ktab_ref, len_ref, q_ref, kv_ref, o_ref, low_ref, lse_ref, ks, vs, *, span, kb
):
    step = pl.program_id(0)
    count = ks.shape[0] // span

    @pl.when(step == 0)
    def _():
        sort_spans(ktab_ref, kv_ref, ks, slice(0, 128), span, count)
        sort_spans(ktab_ref, kv_ref, vs, slice(128, 256), span, count)

    q = stack_heads(q_ref[:, :128], q_ref[:, 128:])
    rows = 2 * span
    limit = len_ref[0]
    span_id = qtab_ref[step]
    _, blocks = block_counts(span_id, limit, span, kb)
    qpos = span_id * span + lax.broadcasted_iota(jnp.int32, (rows, kb), 0) % span
    last = jnp.minimum(qpos, limit - 1)
    col = lax.broadcasted_iota(jnp.int32, (rows, kb), 1)

    def run(n):
        outs, sums = [], []
        for g in range(2):
            part = q[g * rows : (g + 1) * rows]
            scores = []
            for i in range(n):
                v = mm_nt(part, ks[i * kb : (i + 1) * kb, :]) * (HEAD_WIDTH**-0.5 * LOG2E)
                if i == n - 1:
                    v = jnp.where(col + i * kb <= last, v, NEG)
                scores.append(v)
            tops = [jnp.max(v, axis=1, keepdims=True) for v in scores]
            top = functools.reduce(jnp.maximum, tops)
            total = jnp.zeros((rows, 1), F32)
            acc = jnp.zeros((rows, 128), F32)
            for i in range(n):
                p = jnp.exp2(scores[i] - top)
                total = total + jnp.sum(p, axis=1, keepdims=True)
                acc = acc + mm(p.astype(BF), vs[i * kb : (i + 1) * kb, :])
            outs.append(acc / total)
            sums.append(top + jnp.log2(total))
        a, b = unstack_heads(jnp.concatenate(outs, axis=0))
        o_ref[:, :128] = a
        o_ref[:, 128:] = b
        low_ref[:, :128] = a.astype(BF)
        low_ref[:, 128:] = b.astype(BF)
        lse = jnp.broadcast_to(jnp.concatenate(sums, axis=0), (2 * rows, 128))
        lse_ref[0] = jnp.transpose(lse)[:8]

    for n in range(1, ks.shape[0] // kb + 1):
        pl.when(blocks == n)(functools.partial(run, n))


def attend(qtab, ktab, limit, q, kv, span, kb):
    steps, keys = q.shape[0] // span, kv.shape[0]
    body = attend_short_kernel if keys <= 4 * kb else attend_kernel
    return pl.pallas_call(
        functools.partial(body, span=span, kb=kb),
        grid_spec=pltpu.PrefetchScalarGridSpec(
            num_scalar_prefetch=3,
            grid=(steps,),
            in_specs=[pl.BlockSpec((span, 256), lambda i, *_: (i, 0)), whole(kv.shape)],
            out_specs=[
                pl.BlockSpec((span, 256), lambda i, *_: (i, 0)),
                pl.BlockSpec((span, 256), lambda i, *_: (i, 0)),
                pl.BlockSpec((1, 8, 4 * span), lambda i, *_: (i, 0, 0)),
            ],
            scratch_shapes=[pltpu.VMEM((keys, 128), BF), pltpu.VMEM((keys, 128), BF)],
        ),
        out_shape=[
            jax.ShapeDtypeStruct((q.shape[0], 256), F32),
            jax.ShapeDtypeStruct((q.shape[0], 256), BF),
            jax.ShapeDtypeStruct((steps, 8, 4 * span), F32),
        ],
        compiler_params=params(),
        name="attend",
    )(qtab, ktab, limit, q, kv)


def attend_back_kernel(
    qtab_ref, ktab_ref, len_ref, q_ref, kv_ref, do_ref, o_ref, lse_ref, dq_ref, dkv_ref,
    ks, vs, dk, dv, *, span, kb,
):
    step = pl.program_id(0)
    count = ks.shape[0] // span
    scale = HEAD_WIDTH**-0.5

    @pl.when(step == 0)
    def _():
        sort_spans(ktab_ref, kv_ref, ks, slice(0, 128), span, count)
        sort_spans(ktab_ref, kv_ref, vs, slice(128, 256), span, count)
        dk[...] = jnp.zeros_like(dk)
        dv[...] = jnp.zeros_like(dv)

    q = stack_heads(q_ref[:, :128], q_ref[:, 128:])
    do = stack_heads(do_ref[:, :128], do_ref[:, 128:])
    rows = 4 * span
    inner = do.astype(F32) * stack_heads(o_ref[:, :128], o_ref[:, 128:], F32)
    delta = jnp.sum(jnp.transpose(inner), axis=0, keepdims=True)
    lse = lse_ref[0, :1]
    limit = len_ref[0]
    span_id = qtab_ref[step]
    full, blocks = block_counts(span_id, limit, span, kb)
    blocks = jnp.where(span_id * span < limit, blocks, 0)
    full = jnp.minimum(full, blocks)
    qpos = span_id * span + lax.broadcasted_iota(jnp.int32, (kb, rows), 1) % span
    key = lax.broadcasted_iota(jnp.int32, (kb, rows), 0)
    last = jnp.minimum(qpos, limit - 1)

    def body(masked, i, dq):
        at = pl.ds(pl.multiple_of(i * kb, kb), kb)
        k, v = ks[at, :], vs[at, :]
        s = mm_nt(k, q) * (scale * LOG2E)
        p = jnp.exp2(s - lse)
        if masked:
            p = jnp.where(key + i * kb <= last, p, 0.0)
        dp = mm_nt(v, do)
        ds = (p * (dp - delta)).astype(BF)
        dk[at, :] += mm(ds, q)
        dv[at, :] += mm(p.astype(BF), do)
        return dq + mm_tn(ds, k)

    dq = jnp.zeros((rows, 128), F32)
    dq = lax.fori_loop(0, full, functools.partial(body, False), dq)
    dq = lax.fori_loop(full, blocks, functools.partial(body, True), dq)
    a, b = unstack_heads(dq * scale)
    dq_ref[:, :128] = a.astype(BF)
    dq_ref[:, 128:] = b.astype(BF)

    @pl.when(step == pl.num_programs(0) - 1)
    def _():
        @pl.loop(0, count)
        def _(j):
            at = pl.ds(pl.multiple_of(ktab_ref[j] * span, span), span)
            to = pl.ds(pl.multiple_of(j * span, span), span)
            dkv_ref[to, :128] = (dk[at, :] * scale).astype(BF)
            dkv_ref[to, 128:] = dv[at, :].astype(BF)


def attend_back(qtab, ktab, limit, q, kv, do, o, lse, span, kb):
    steps, keys = q.shape[0] // span, kv.shape[0]
    row = pl.BlockSpec((span, 256), lambda i, *_: (i, 0))
    return pl.pallas_call(
        functools.partial(attend_back_kernel, span=span, kb=kb),
        grid_spec=pltpu.PrefetchScalarGridSpec(
            num_scalar_prefetch=3,
            grid=(steps,),
            in_specs=[
                row, whole(kv.shape), row, row,
                pl.BlockSpec((1, 8, 4 * span), lambda i, *_: (i, 0, 0)),
            ],
            out_specs=[row, whole(kv.shape)],
            scratch_shapes=[
                pltpu.VMEM((keys, 128), BF), pltpu.VMEM((keys, 128), BF),
                pltpu.VMEM((keys, 128), F32), pltpu.VMEM((keys, 128), F32),
            ],
        ),
        out_shape=[
            jax.ShapeDtypeStruct((q.shape[0], 256), BF),
            jax.ShapeDtypeStruct(kv.shape, BF),
        ],
        compiler_params=params(),
        name="attend_back",
    )(qtab, ktab, limit, q, kv, do, o, lse)


def experts_kernel(
    base_ref, h_ref, c_ref, wg_ref, wu_ref, wd_ref, moe_ref, dh_ref, grad_ref,
    moe, dh, dgates, s_act, s_gate, s_up, *, tile,
):
    step = pl.program_id(0)
    width = c_ref.shape[1]
    expert = base_ref[1] + step
    wg, wu, wd = wg_ref[0], wu_ref[0], wd_ref[0]

    @pl.when(step == 0)
    def _():
        moe[...] = jnp.zeros_like(moe)
        dh[...] = jnp.zeros_like(dh)
        dgates[...] = jnp.zeros_like(dgates)

    @pl.loop(0, moe.shape[0] // tile)
    def _(t):
        at = pl.ds(pl.multiple_of(t * tile, tile), tile)
        h, c = h_ref[at, :width], c_ref[at, :]
        lane = lax.broadcasted_iota(jnp.int32, (tile, 128), 1)
        mine = lane == expert
        gate = jnp.sum(
            jnp.where(mine, h_ref[at, width:].astype(F32), 0.0), axis=1, keepdims=True
        )
        g, u, z = mm(h, wg), mm(h, wu), mm_nt(c, wd)
        sig = jax.nn.sigmoid(g)
        silu = g * sig
        act = silu * u
        dgates[at, :] += jnp.where(mine, jnp.sum(act * z, axis=1, keepdims=True), 0.0)
        act = (act * gate).astype(BF)
        dact = z * gate
        dgate = (dact * u * sig * (1.0 + g * (1.0 - sig))).astype(BF)
        dup = (dact * silu).astype(BF)
        s_act[at, :] = act
        s_gate[at, :] = dgate
        s_up[at, :] = dup
        moe[at, :] += mm(act, wd)
        dh[at, :] += mm_nt(dgate, wg) + mm_nt(dup, wu)

    block = grad_ref.shape[2]
    for i in range(2):
        at = slice(i * block, (i + 1) * block)
        grad_ref[0, i] = mm_tn(h_ref[:, at], s_gate[...]).astype(BF)
        grad_ref[0, 2 + i] = mm_tn(h_ref[:, at], s_up[...]).astype(BF)
        grad_ref[0, 4 + i] = mm_tn(s_act[...], c_ref[:, at]).astype(BF)

    @pl.when(step == pl.num_programs(0) - 1)
    def _():
        moe_ref[...] = moe[...].astype(BF)
        dh_ref[:, :width] = dh[...].astype(BF)
        dh_ref[:, width:] = dgates[...].astype(BF)


def experts(base, count, h, c, wg, wu, wd, tile):
    rows, width = c.shape
    ff = wg.shape[2]
    pick = lambda shape: pl.BlockSpec((1,) + shape, lambda e, s: (s[0] + e, 0, 0))
    return pl.pallas_call(
        functools.partial(experts_kernel, tile=tile),
        grid_spec=pltpu.PrefetchScalarGridSpec(
            num_scalar_prefetch=1,
            grid=(count,),
            in_specs=[
                whole(h.shape), whole(c.shape),
                pick((width, ff)), pick((width, ff)), pick((ff, width)),
            ],
            out_specs=[
                whole(c.shape), whole(h.shape),
                pl.BlockSpec((1, 6, ff, ff), lambda e, s: (e, 0, 0, 0)),
            ],
            scratch_shapes=[
                pltpu.VMEM((rows, width), F32), pltpu.VMEM((rows, width), F32),
                pltpu.VMEM((rows, 128), F32),
                pltpu.VMEM((rows, ff), BF), pltpu.VMEM((rows, ff), BF), pltpu.VMEM((rows, ff), BF),
            ],
        ),
        out_shape=[
            jax.ShapeDtypeStruct(c.shape, BF),
            jax.ShapeDtypeStruct(h.shape, BF),
            jax.ShapeDtypeStruct((count, 6, ff, ff), BF),
        ],
        compiler_params=params(),
        name="experts",
    )(base, h, c, wg, wu, wd)


def moe_kernel(*refs, names, topk, count):
    r = types.SimpleNamespace(**dict(zip(names, refs)))
    z, s, f = lax.axis_index("dp"), lax.axis_index("seq"), lax.axis_index("fsdp")
    core, x = s % 2, s // 2
    flip = 1 - 2 * core
    seqs = (s, s + flip, (s + 2) % 4, (s + 2) % 4 + flip)
    peers = [(z, q, f) for q in seqs]
    peer_x, peer_y = peers[2], (z, s, 1 - f)
    att, att_in, tout, hx, cots = r.att, r.att_in, r.tout, r.hx, r.cots
    rows, width = tout.shape
    n = rows // 2
    ext = hx.shape[1]
    ff = r.wgs.shape[2]
    owned = r.wg.shape[0]

    barrier = pltpu.get_barrier_semaphore()
    for dev in (*peers[1:], peer_y):
        pl.semaphore_signal(barrier, inc=1, device_id=dev, device_id_type=MESH)

    def remote(src, dst, sems, b, dev):
        return pltpu.make_async_remote_copy(
            src_ref=src, dst_ref=dst, send_sem=sems.at[0, b], recv_sem=sems.at[1, b],
            device_id=dev, device_id_type=MESH,
        )

    def block(t):
        return pl.ds(pl.multiple_of(t * rows, rows), rows)

    load_cots = [
        pltpu.make_async_copy(v, cots.at[block(i)], r.s_cot.at[i])
        for i, v in enumerate((r.cot, r.cot_y, r.cot_x))
    ]
    for copy in load_cots:
        copy.start()

    def load_weights(e, act):
        for i, (src, dst) in enumerate(((r.wg, r.wgs), (r.wu, r.wus), (r.wd, r.wds))):
            act(pltpu.make_async_copy(src.at[x * count + e], dst.at[e], r.s_w.at[i, e]))

    @pl.loop(0, count)
    def _(e):
        load_weights(e, lambda copy: copy.start())

    pl.semaphore_wait(barrier, 4)
    def head(m, i):
        at = pl.ds(pl.multiple_of(i * n, n), n)
        return remote(att.at[m, at], att_in.at[m, at], r.s_att, 2 * m + i, peers[m])

    heads = [head(m, i) for i in range(2) for m in (3, 2, 1)]
    for copy in heads:
        copy.start()
    diag = [
        remote(r.cot_x.at[pl.ds(0, n)], cots.at[pl.ds(3 * rows, n)], r.s_diag, 0, peer_y),
        remote(r.cot_y.at[pl.ds(n, n)], cots.at[pl.ds(3 * rows + n, n)], r.s_diag, 1, peer_x),
    ]
    wo_rows = pl.ds(pl.multiple_of(core * (ff // 2), ff // 2), ff // 2)
    wo_there = r.wo_there
    wo_copy = pltpu.make_async_copy(r.wo_near, wo_there.at[wo_rows], r.s_wo.at[0])
    wo_share = remote(r.wo_near, wo_there.at[wo_rows], r.s_diag, 2, peers[1])
    wo_copy.start()
    wo_share.start()
    for copy in diag:
        copy.start()

    small = r.small
    table = r.table
    table[...] = jnp.zeros_like(table)
    table[: small.shape[0], :] = small[...]
    n_exp = r.gates.shape[1]
    gain = small[17:18, :].astype(F32)
    own_cols = pl.ds(pl.multiple_of(f * ff, ff), ff)
    away_cols = pl.ds(pl.multiple_of((1 - f) * ff, ff), ff)

    def head_cols(m):
        return pl.ds(pl.multiple_of(seqs[m] * 256, 256), 256)

    wo_copy.wait()
    wo_share.wait_recv()
    def share(i, j, dev):
        at = pl.multiple_of(i * n, n)
        return remote(
            hx.at[pl.ds(at, n)], hx.at[pl.ds((j + 1) * rows + at, n)], r.s_h, 2 * j + i, dev
        )

    @pl.loop(0, 2)
    def _(i):
        at = pl.ds(pl.multiple_of(i * n, n), n)
        tout[at, head_cols(0)] = att[0, at, :]
        for m in range(1, 4):
            head(m, i).wait_recv()
            tout[at, head_cols(m)] = att_in[m, at, :]
        middle = (
            r.tok[at, :].astype(F32)
            + mm(tout[at, own_cols], r.wo_own[...])
            + mm(tout[at, away_cols], wo_there[...])
        )
        r.middle[at, :] = middle
        normed, _ = rms_parts(middle)
        hidden = (normed * gain).astype(BF)
        logits = mm_nt(hidden, table[...])
        lane = lax.broadcasted_iota(jnp.int32, logits.shape, 1)
        chosen = lane == r.routes[at, 0:1]
        for k in range(1, topk):
            chosen = chosen | (lane == r.routes[at, k : k + 1])
        top = jnp.max(jnp.where(chosen, logits, NEG), axis=-1, keepdims=True)
        raised = jnp.where(chosen, jnp.exp(logits - top), 0.0)
        gates = raised / jnp.sum(raised, axis=-1, keepdims=True)
        r.gates[at, :] = gates
        hx[at, :width] = hidden
        hx[at, width:] = gates.astype(BF)
        share(i, 0, peer_y).start()
        share(i, 1, peer_x).start()

    shares = [share(i, j, dev) for i in range(2) for j, dev in ((0, peer_y), (1, peer_x))]
    second = remote(
        hx.at[pl.ds(rows + n, n)], hx.at[pl.ds(3 * rows + n, n)], r.s_h, 4, peer_x
    )
    first = remote(hx.at[pl.ds(2 * rows, n)], hx.at[pl.ds(3 * rows, n)], r.s_h, 5, peer_y)

    dhs, moe, dh, dgates = r.dhs, r.moe_acc, r.dh_acc, r.dg_acc
    few = 3 * rows // 4
    half_rows = [(0, n), (n, n)]
    back_y = [
        remote(dhs.at[pl.ds(rows + a, k)], r.rdh.at[0, pl.ds(a, k)], r.s_d, i, peer_y)
        for i, (a, k) in enumerate(half_rows)
    ]
    back_x = remote(dhs.at[block(2)], r.rdh.at[1], r.s_d, 2, peer_x)

    def two_hops(a, k, sem, first_dev, second_dev):
        via = r.via.at[pl.ds(a, k)]
        return (
            remote(dhs.at[pl.ds(3 * rows + a, k)], via, r.s_d, sem, first_dev),
            remote(via, r.rdd.at[pl.ds(a, k)], r.s_d, sem + 1, second_dev),
        )

    hop_y0, end_x0 = two_hops(0, n, 3, peer_y, peer_x)
    hop_y1, end_x1 = two_hops(n, few - n, 5, peer_y, peer_x)
    hop_x, end_y = two_hops(few, rows - few, 7, peer_x, peer_y)
    moe_x = remote(r.moe2, r.got2, r.s_d, 9, peer_x)

    moes = (r.moe0, r.moe1, r.moe2, r.moe3)

    def moe_out(t):
        return pltpu.make_async_copy(r.mstage.at[(0, 1, 1, 0)[t]], moes[t], r.s_m.at[t])

    @pl.loop(0, 4 * count)
    def _(k):
        turn, e = k // count, k % count
        t = 2 * turn - turn // 2 - 4 * (turn // 3)

        @pl.when(k < count)
        def _():
            load_weights(e, lambda copy: copy.wait())

        @pl.when(k == 0)
        def _():
            load_cots[0].wait()

        @pl.when(k == count)
        def _():
            for copy in shares:
                copy.wait_recv()
            second.start()
            first.start()
            load_cots[1].wait()
            load_cots[2].wait()

        @pl.when(k == 2 * count)
        def _():
            first.wait_recv()
            second.wait_recv()
            for copy in diag:
                copy.wait_recv()

        at = block(t)
        h, c = hx[at, :width], cots[at, :]
        wg, wu, wd = r.wgs[e], r.wus[e], r.wds[e]
        expert = f * owned + x * count + e
        mine = lax.broadcasted_iota(jnp.int32, (rows, ext - width), 1) == expert
        gate = jnp.sum(jnp.where(mine, hx[at, width:].astype(F32), 0.0), axis=1, keepdims=True)
        g, u, zz = mm(h, wg), mm(h, wu), mm_nt(c, wd)
        sig = jax.nn.sigmoid(g)
        silu = g * sig
        act = silu * u
        dgate_col = jnp.where(mine, jnp.sum(act * zz, axis=1, keepdims=True), 0.0)
        act = (act * gate).astype(BF)
        dact = zz * gate
        dgate = (dact * u * sig * (1.0 + g * (1.0 - sig))).astype(BF)
        dup = (dact * silu).astype(BF)
        r.s_act[e, at, :] = act
        r.s_gate[e, at, :] = dgate
        r.s_up[e, at, :] = dup

        @pl.when(e == 0)
        def _():
            moe[...] = mm(act, wd)
            dh[...] = mm_nt(dgate, wg) + mm_nt(dup, wu)
            dgates[...] = dgate_col

        @pl.when(e > 0)
        def _():
            moe[...] += mm(act, wd)
            dh[...] += mm_nt(dgate, wg) + mm_nt(dup, wu)
            dgates[...] += dgate_col

        @pl.when(e == count - 1)
        def _():
            for i, k in enumerate((0, 2, 3, 1)):
                @pl.when(t == k)
                def _():
                    if i >= 2:
                        moe_out((0, 2)[i - 2]).wait()
                    r.mstage[i % 2] = moe[...].astype(BF)
                    moe_out(k).start()

            dhs[at, :width] = dh[...].astype(BF)
            dhs[at, width:] = dgates[...].astype(BF)

            @pl.when(t == 1)
            def _():
                for copy in back_y:
                    copy.start()

            @pl.when(t == 2)
            def _():
                back_x.start()

            @pl.when(t == 3)
            def _():
                hop_y0.start()
                hop_x.start()
                hop_y1.start()

    stage = r.stage

    def grad_copy(b, slot):
        return pltpu.make_async_copy(stage.at[slot], r.grads.at[b], r.s_g.at[slot])

    dattn, dto, dsend = r.dattn, r.dto, r.dsend
    returns = [
        [
            remote(dsend.at[m, pl.ds(i * n, n)], r.do.at[m, pl.ds(i * n, n)], r.s_back, 2 * m + i, peers[m])
            for m in (3, 2, 1)
        ]
        for i in range(2)
    ]

    def middle_back(i):
        at = pl.ds(i * n, n)
        total = (
            dhs[at, :].astype(F32) + r.rdh[0, at, :].astype(F32)
            + r.rdh[1, at, :].astype(F32) + r.rdd[at, :].astype(F32)
        )
        dg, gates = total[:, width:], r.gates[at, :]
        dl = (gates * (dg - jnp.sum(gates * dg, axis=-1, keepdims=True))).astype(BF)
        rg = mm_tn(dl, hx[at, :width])[:32]
        d_hidden = total[:, :width] + mm(dl, table[...])
        normed, factor = rms_parts(r.middle[at, :])
        gn = jnp.sum(d_hidden * normed, axis=0, keepdims=True)
        d_n = d_hidden * gain
        d_mid = cots[at, :].astype(F32) + factor * (
            d_n - normed * jnp.mean(d_n * normed, axis=-1, keepdims=True)
        )
        r.dmid[at, :] = d_mid
        low = d_mid.astype(BF)
        dattn[at, :] = low
        dto[at, own_cols] = mm_nt(low, r.wo_own[...]).astype(BF)
        dto[at, away_cols] = mm_nt(low, wo_there[...]).astype(BF)
        for m in range(1, 4):
            dsend[m, at, :] = dto[at, head_cols(m)]
        for copy in returns[i]:
            copy.start()
        r.do[0, at, :] = dto[at, head_cols(0)]
        if i == 0:
            r.rg[...] = rg
            r.gn[:1, :] = gn
            return
        rg, gn = r.rg[...] + rg, r.gn[:1, :] + gn
        row = lax.broadcasted_iota(jnp.int32, rg.shape, 0)
        top = jnp.where(row == 17, gn, jnp.where(row < 16, rg, 0.0))
        r.tiny[0] = top[:, : width // 2]
        r.tiny[1] = top[:, width // 2 :]
        for k in range(4):
            cols = slice(k * 256, (k + 1) * 256)
            r.gout[cols, :] = mm_tn(tout[:, cols], dattn[...]).astype(BF)

    def forward0():
        hop_y0.wait_recv()
        end_x0.start()

    def forward1():
        hop_y1.wait_recv()
        end_x1.start()
        hop_x.wait_recv()
        end_y.start()
        moe_x.start()

    def back0():
        for copy in (back_y[0], back_x, end_x0):
            copy.wait_recv()
        middle_back(0)

    def back1():
        for copy in (back_y[1], end_x1, end_y):
            copy.wait_recv()
        middle_back(1)

    @pl.loop(0, 3 * count)
    def _(k):
        e, j = k // 3, k % 3
        pl.when(k == 0)(forward0)
        pl.when(k == 2)(forward1)
        pl.when(k == 3 * count - 6)(back0)
        pl.when(k == 3 * count - 1)(back1)

        @pl.when(k > 0)
        def _():
            grad_copy(0, 0).wait()
            grad_copy(0, 1).wait()

        for which, left, right in ((0, hx, r.s_gate), (1, hx, r.s_up), (2, cots, r.s_act)):
            @pl.when(j == which)
            def _():
                for i in range(2):
                    at = slice(i * ff, (i + 1) * ff)
                    if which < 2:
                        v = mm_tn(left[:, at], right[e])
                    else:
                        v = mm_tn(right[e], left[:, at])
                    stage[i] = v.astype(BF)

        for i in range(2):
            grad_copy(6 * e + 2 * j + i, i).start()

    grad_copy(0, 0).wait()
    grad_copy(0, 1).wait()
    moe_out(3).wait()
    moe_out(1).wait()
    for copy in (*returns[0], *returns[1], moe_x):
        copy.wait()
    for copy in (*heads, *diag, wo_share, *shares, first, second, *back_y, back_x, hop_x, hop_y0, hop_y1, end_y, end_x0, end_x1):
        copy.wait_send()


def moe_layer(att, tok, wo_own, wo_near, small, routes, cot, cot_y, cot_x, wg, wu, wd):
    rows, width = tok.shape
    owned, _, ff = wg.shape
    count = owned // 2
    ext = width + 128
    hbm = pl.BlockSpec(memory_space=pl.ANY)
    vmem = pl.BlockSpec(memory_space=pltpu.VMEM)
    dma = pltpu.SemaphoreType.DMA
    args = dict(
        att=(att.reshape(4, rows, 256), vmem), tok=(tok, vmem), wo_own=(wo_own, vmem),
        wo_near=(wo_near, hbm), small=(small, vmem), routes=(routes, vmem),
        cot=(cot, hbm), cot_y=(cot_y, hbm), cot_x=(cot_x, hbm),
        wg=(wg, hbm), wu=(wu, hbm), wd=(wd, hbm),
    )
    shape = jax.ShapeDtypeStruct
    outs = dict(
        middle=(shape((rows, width), F32), vmem),
        moe0=(shape((rows, width), BF), hbm), moe1=(shape((rows, width), BF), hbm),
        moe2=(shape((rows, width), BF), hbm), moe3=(shape((rows, width), BF), hbm),
        got2=(shape((rows, width), BF), hbm),
        dmid=(shape((rows, width), F32), vmem),
        do=(shape((4, rows, 256), BF), vmem),
        grads=(shape((6 * count, ff, ff), BF), hbm),
        gout=(shape((width, width), BF), vmem),
        tiny=(shape((2, 32, width // 2), F32), vmem),
    )
    stash = pltpu.VMEM((count, 4 * rows, ff), BF)
    scratch = dict(
        att_in=pltpu.VMEM((4, rows, 256), BF), tout=pltpu.VMEM((rows, width), BF),
        hx=pltpu.VMEM((4 * rows, ext), BF), cots=pltpu.VMEM((4 * rows, width), BF),
        wo_there=pltpu.VMEM((ff, width), BF), rg=pltpu.VMEM((32, width), F32),
        gn=pltpu.VMEM((8, width), F32), table=pltpu.VMEM((128, width), BF), gates=pltpu.VMEM((rows, 128), F32),
        wgs=pltpu.VMEM((count, width, ff), BF), wus=pltpu.VMEM((count, width, ff), BF),
        wds=pltpu.VMEM((count, ff, width), BF),
        s_act=stash, s_gate=stash, s_up=stash,
        moe_acc=pltpu.VMEM((rows, width), F32), dh_acc=pltpu.VMEM((rows, width), F32),
        dg_acc=pltpu.VMEM((rows, 128), F32), mstage=pltpu.VMEM((2, rows, width), BF),
        dhs=pltpu.VMEM((4 * rows, ext), BF), rdh=pltpu.VMEM((2, rows, ext), BF),
        via=pltpu.VMEM((rows, ext), BF), rdd=pltpu.VMEM((rows, ext), BF),
        dattn=pltpu.VMEM((rows, width), BF), dto=pltpu.VMEM((rows, width), BF),
        dsend=pltpu.VMEM((4, rows, 256), BF), stage=pltpu.VMEM((2, ff, ff), BF),
        s_att=dma((2, 8)), s_diag=dma((2, 3)), s_h=dma((2, 6)), s_d=dma((2, 10)), s_back=dma((2, 8)),
        s_cot=dma((3,)), s_wo=dma((1,)), s_w=dma((3, count)), s_m=dma((4,)), s_g=dma((2,)),
    )
    names = tuple(args) + tuple(outs) + tuple(scratch)
    got = pl.pallas_call(
        functools.partial(moe_kernel, names=names, topk=routes.shape[1], count=count),
        in_specs=[v[1] for v in args.values()],
        out_specs=[v[1] for v in outs.values()],
        out_shape=[v[0] for v in outs.values()],
        scratch_shapes=list(scratch.values()),
        compiler_params=pltpu.CompilerParams(
            vmem_limit_bytes=67043328, collective_id=3, has_side_effects=True
        ),
        name="moe_layer",
    )(*[v[0] for v in args.values()])
    return types.SimpleNamespace(**dict(zip(outs, got)))


def flip_core(x):
    return lax.ppermute(x, "seq", [(0, 1), (1, 0), (2, 3), (3, 2)])


def flip_x(x):
    return lax.ppermute(x, "seq", [(0, 2), (2, 0), (1, 3), (3, 1)])


def flip_both(x):
    return lax.ppermute(x, "seq", [(0, 3), (3, 0), (1, 2), (2, 1)])


def flip_y(x):
    return lax.ppermute(x, "fsdp", [(0, 1), (1, 0)])


def gather_seq(x):
    own = jnp.stack([x, flip_core(x)])
    far = flip_x(x)
    return jnp.concatenate([own, far[None], flip_core(far)[None]])


def swap_seq(blocks):
    return [blocks[0], flip_core(blocks[1]), flip_x(blocks[2]), flip_both(blocks[3])]


def gather_fsdp(x, axis=0):
    if lax.axis_size("fsdp") == 2:
        return jnp.concatenate([x, lax.ppermute(x, "fsdp", [(0, 1), (1, 0)])], axis=axis)
    return lax.all_gather(x, "fsdp", axis=axis, tiled=True)


def scatter_fsdp(x):
    if lax.axis_size("fsdp") == 2:
        n = x.shape[0] // 2
        other = lax.ppermute(x[n:], "fsdp", [(0, 1), (1, 0)])
        return x[:n].astype(F32) + other.astype(F32)
    return lax.psum_scatter(x, "fsdp", scatter_dimension=0, tiled=True).astype(F32)


def rope_back(w, cos, sin, low_half):
    half = HEAD_WIDTH // 2
    y = w * sin
    return w * cos + jnp.where(low_half, pltpu.roll(y, 128 - half, 1), -pltpu.roll(y, half, 1))


def reduce_kernel(*refs, names, slots, shards, fused):
    r = types.SimpleNamespace(**dict(zip(names, refs)))
    gm, mine, rc, pre, suf = r.gm, r.mine, r.rc, r.pre, r.suf
    gate, up, down, out, qkv = r.gate, r.up, r.down, r.out, r.qkv
    z, s, f = lax.axis_index("dp"), lax.axis_index("seq"), lax.axis_index("fsdp")
    core, x = s % 2, s // 2
    peer_core = (z, s + 1 - 2 * core, f)
    peer_x = (z, (s + 2) % 4, f)
    peer_y = (z, s, 1 - f)
    right, left = (z + 1, s, f), (z - 1, s, f)
    nb = gm.shape[0]
    n_moe, n_out, items = 2 * nb, 2 * nb + 2, 2 * nb + 6
    count = nb // 6
    piece = mine.shape[1]
    half, block = 2 * piece, 4 * piece
    last = slots - 1

    def other_z(k):
        return ((z + k) % slots, s, f)

    barrier = pltpu.get_barrier_semaphore()
    peer_xy = (z, (s + 2) % 4, 1 - f)
    peers = [other_z(k) for k in range(1, slots)] + [peer_core, peer_x] + [peer_y, peer_xy] * fused
    for dev in peers:
        pl.semaphore_signal(barrier, inc=1, device_id=dev, device_id_type=MESH)

    def remote(src, dst, sems, b, dev):
        return pltpu.make_async_remote_copy(
            src_ref=src, dst_ref=dst, send_sem=sems.at[0, b], recv_sem=sems.at[1, b],
            device_id=dev, device_id_type=MESH,
        )

    def load(src, b):
        return pltpu.make_async_copy(src, mine.at[b], r.s_mine.at[b])

    @pl.loop(0, n_moe)
    def _(b):
        load(gm.at[b // 2, core, b % 2], b).start()

    if fused:
        loads = [
            pltpu.make_async_copy(a, b, r.s_in.at[i])
            for i, (a, b) in enumerate((
                (r.q, r.q_in), (r.kv, r.kv_in), (r.do, r.do_in), (r.o, r.o_in), (r.lse, r.lse_in),
                (r.wc, r.wc_in),
                (r.cos, r.cos_in), (r.sin, r.sin_in), (r.h, r.h_in), (r.tok, r.tok_in),
                (r.gout.at[pl.ds(pl.multiple_of(f * block, block), block)], r.gout_in),
                (r.dmid, r.dmid_in),
            ))
        ]
        for copy in loads:
            copy.start()
    else:
        for i in range(2):
            load(r.eo.at[core, i], n_moe + i).start()
        for i in range(4):
            load(r.cols.at[i], n_out + i).start()
    pl.semaphore_wait(barrier, len(peers))

    @pl.loop(0, n_moe)
    def _(b):
        remote(gm.at[b // 2, 1 - core, b % 2], rc.at[b], r.s_rc, b, peer_core).start()

    if not fused:
        for i in range(2):
            remote(r.eo.at[1 - core, i], rc.at[n_moe + i], r.s_rc, n_moe + i, peer_core).start()

    def place(b, which, part, act):
        first_row = part * half + b % 2 * piece
        rows = pl.ds(pl.multiple_of(first_row, piece), piece)
        e, j = which * count + b // 12, b // 2 % 6
        jj = j % 2
        wide = pl.ds(pl.multiple_of(jj * block, block), block)
        at = pl.ds(pl.multiple_of(jj * block + first_row, piece), piece)
        for m, o in enumerate((gate, up)):
            @pl.when((b < n_moe) & (j // 2 == m))
            def _():
                act(o.at[e, at, :])

        @pl.when((b < n_moe) & (j // 2 == 2))
        def _():
            act(down.at[e, rows, wide])

        @pl.when((b >= n_moe) & (b < n_out))
        def _():
            act(out.at[rows, pl.ds(pl.multiple_of(which * block, block), block)])

        @pl.when(b >= n_out)
        def _():
            at = pl.ds(pl.multiple_of((b - n_out) * piece, piece), piece)
            wide = 2 * block
            for first, n, to in ((0, 256, 0), (wide, 128, 256), (wide + wide // 2, 128, 384)):
                col = pl.multiple_of(first + (2 * which + part) * n, 128)
                act(qkv.at[at, pl.ds(col, n)], pl.ds(to, n))

    def add(a, b):
        return a.astype(F32) + b.astype(F32)

    def hop(buf, sems, b, dev):
        return remote(buf.at[b], buf.at[b], sems, b, dev)

    def spread(b):
        def act(dst, cut=None):
            src = rc.at[b] if cut is None else rc.at[b, :, cut]
            remote(src, dst, r.s_oth, 0, peer_core).start()
            pltpu.make_async_copy(src, dst, r.s_out.at[0]).start()
            remote(src, dst, r.s_far, b, peer_x).start()

        place(b, x, core, act)

    lag = 2
    ahead = 4

    def begin(b):
        @pl.when(b < (n_moe if fused else items))
        def _():
            load(gm.at[0, 0, 0], b).wait()

        @pl.when(b < n_out)
        def _():
            remote(gm.at[0, 0, 0], rc.at[b], r.s_rc, b, peer_core).wait_recv()
            mine[b] = add(mine[b], rc[b]).astype(BF)

        @pl.when(z == 0)
        def _():
            remote(mine.at[b], pre.at[b], r.s_pre, b, right).start()

        @pl.when(z == last)
        def _():
            remote(mine.at[b], suf.at[b], r.s_suf, b, left).start()

    def prefix(b):
        hop(pre, r.s_pre, b, peer_x).wait_recv()
        got = pre[b].astype(F32)
        own = got + mine[b].astype(F32)

        @pl.when(z == last)
        def _():
            rc[b] = own.astype(BF)

        @pl.when(z < last)
        def _():
            @pl.when(2 * z >= slots)
            def _():
                rc[b] = (got + suf[b].astype(F32)).astype(BF)

            pre[b] = own.astype(BF)
            hop(pre, r.s_pre, b, right).start()

        @pl.when(2 * z >= slots)
        def _():
            spread(b)

    def suffix(b):
        hop(suf, r.s_suf, b, peer_x).wait_recv()
        got = suf[b].astype(F32)
        own = got + mine[b].astype(F32)

        @pl.when(z == 0)
        def _():
            rc[b] = own.astype(BF)

        @pl.when(z > 0)
        def _():
            @pl.when(2 * z < slots)
            def _():
                rc[b] = (got + pre[b].astype(F32)).astype(BF)

            suf[b] = own.astype(BF)
            hop(suf, r.s_suf, b, left).start()

        @pl.when(2 * z < slots)
        def _():
            spread(b)

    def forward(b):
        remote(rc.at[b], rc.at[b], r.s_far, b, peer_x).wait_recv()

        def act(dst, cut=None):
            remote(dst, dst, r.s_faro, 0, peer_core).start()

        place(b, 1 - x, core, act)

    def within(b, cond=True):
        return (b >= 0) & (b < items) & cond

    tsum, trecv, s_tiny = r.tsum, r.trecv, r.s_tiny

    def tiny_swap(k, dev):
        return remote(tsum.at[k], trecv.at[k], s_tiny, k, dev)

    def tiny_add(k):
        tiny_swap(k, peer_x).wait_recv()
        tsum[k + 1] = add(tsum[k], trecv[k]).astype(BF)

    def tiny_x():
        tiny_swap(0, peer_x).start()

    def tiny_core():
        tiny_add(0)
        tiny_swap(1, peer_core).start()

    def tiny_spread():
        tiny_add(1)
        for k in range(1, slots):
            remote(tsum.at[2], trecv.at[1 + k], s_tiny, 1 + k, other_z(k)).start()

    def tiny_end():
        total = tsum[2].astype(F32)
        for k in range(1, slots):
            remote(tsum.at[2], trecv.at[1 + k], s_tiny, 1 + k, other_z(k)).wait_recv()
            total = total + trecv[1 + k].astype(F32)
        r.tiny_out[...] = total

    steps = {}
    if fused:
        s_fg = r.s_fg
        keys = r.dkvs.shape[0]
        tile = r.dhx.shape[0]
        dh = [r.h_in.at[pl.ds(t * tile, tile)] for t in range(4)]
        owner = pl.multiple_of(f * block, block)
        away = pl.multiple_of((1 - f) * block, block)
        mine_rows, away_rows = pl.ds(owner, block), pl.ds(away, block)
        near_cols = pl.ds(pl.multiple_of(x * block, block), block)
        far_cols = pl.ds(pl.multiple_of((1 - x) * block, block), block)

        send_dkv = remote(r.kv_in.at[pl.ds(keys, keys)], r.rdkv, s_fg, 0, peer_y)
        send_out = [
            remote(r.gout.at[away_rows, cols], r.rout.at[i], s_fg, (1, 8)[i], peer_y)
            for i, cols in enumerate((far_cols, near_cols))
        ]
        send_dh3 = remote(dh[3], r.rdh.at[1], s_fg, 2, peer_core)
        send_dh1 = remote(dh[1], r.rdh.at[0], s_fg, 3, peer_core)
        send_dhx = remote(r.dhx, r.rdx, s_fg, 4, peer_x)
        send_cols = remote(r.cbuf.at[away_rows], r.rcol, s_fg, 5, peer_y)
        send_outx = remote(r.osend, r.rox, s_fg, 6, peer_x)
        send_tiny = remote(r.tbuf.at[1 - f], r.rtiny, s_fg, 7, peer_y)
        eo_core = [
            remote(r.eo.at[1 - core, i], rc.at[n_moe + i], r.s_rc, n_moe + i, peer_core)
            for i in range(2)
        ]
        moe_back = [
            remote(r.moe3, r.got3, r.s_moe, 1, peer_xy), remote(r.moe1, r.got1, r.s_moe, 0, peer_y),
        ]
        moe_back[0].start()
        for copy in send_out:
            copy.start()
        moe_back[1].start()

        span, kb = tile // 2, 2 * tile
        parts = 2 * keys // kb
        n_steps = 8 * parts
        scale = HEAD_WIDTH**-0.5

        def attention(n):
            j, m = n // parts, n % parts
            at = pl.ds(pl.multiple_of(j * span, span), span)

            @pl.when(n == 0)
            def _():
                r.dk[...] = jnp.zeros_like(r.dk)
                r.dv[...] = jnp.zeros_like(r.dv)
                inside = lax.broadcasted_iota(jnp.int32, (span, 1), 0)
                for k in range(2 * keys // span):
                    r.kpos[k * span : (k + 1) * span, :] = r.ktab[k] * span + inside
                across = lax.broadcasted_iota(jnp.int32, (8, 4 * span), 1) % span
                for k in range(8):
                    r.last[k] = jnp.minimum(r.qtab[k] * span + across, r.limit[0] - 1)

            @pl.when(m == 0)
            def _():
                r.qs[...] = stack_heads(r.q_in[at, :128], r.q_in[at, 128:])
                do = stack_heads(r.do_in[at, :128], r.do_in[at, 128:])
                r.dos[...] = do
                inner = do.astype(F32) * stack_heads(r.o_in[at, :128], r.o_in[at, 128:], F32)
                delta = jnp.sum(jnp.transpose(inner), axis=0, keepdims=True)
                r.delta[...] = jnp.broadcast_to(delta, r.delta.shape)

            key = pl.ds(pl.multiple_of(m * kb, kb), kb)
            k, v = r.kv_in[key, :128], r.kv_in[key, 128:]
            q, do = r.qs[...], r.dos[...]
            p = jnp.exp2(mm_nt(k, q) * (scale * LOG2E) - r.lse_in[j, :1])
            p = jnp.where(r.kpos[key, :] <= r.last[j, :1], p, 0.0)
            ds = (p * (mm_nt(v, do) - r.delta[:1])).astype(BF)
            r.dk[key, :] += mm(ds, q)
            r.dv[key, :] += mm(p.astype(BF), do)
            dq = mm_tn(ds, k)

            @pl.when(m == 0)
            def _():
                r.dqa[...] = dq

            @pl.when(m > 0)
            def _():
                r.dqa[...] += dq

            @pl.when(m == parts - 1)
            def _():
                a, b = unstack_heads(r.dqa[...] * scale)
                r.dq_in[at, :128] = a.astype(BF)
                r.dq_in[at, 128:] = b.astype(BF)

        def send_keys():
            r.kv_in[:, :128] = (r.dk[...] * scale).astype(BF)
            r.kv_in[:, 128:] = r.dv[...].astype(BF)
            send_dkv.start()

        def sum_dkv():
            send_dkv.wait_recv()
            r.dkvs[...] = add(r.kv_in[:keys], r.rdkv[...]).astype(BF)

        def back_tile(t, first=False):
            at = pl.ds(t * tile, tile)
            cos, sin = r.cos_in[at, :], r.sin_in[at, :]
            low_half = lax.broadcasted_iota(jnp.int32, cos.shape, 1) % HEAD_WIDTH < HEAD_WIDTH // 2
            parts = []
            for k in range(3):
                w = r.dq_in[at, k * 128 : (k + 1) * 128] if k < 2 else r.dkvs[at, :128]
                parts.append(rope_back(w.astype(F32), cos, sin, low_half).astype(BF))
            parts.append(r.dkvs[at, 128:])
            dproj = jnp.concatenate(parts, axis=1)
            grad = mm_tn(r.h_in[at, :], dproj)
            back = mm_nt(dproj, r.wc_in[...])
            dh[t][...] = back.astype(BF)
            normed, _ = rms_parts(r.tok_in[at, :].astype(F32))
            gain = jnp.sum((back * normed).reshape(-1, 8, back.shape[1]), axis=0)
            if first:
                r.acc[...] = grad
                r.gn[...] = gain
            else:
                r.acc[...] += grad
                r.gn[...] += gain

        def tile3():
            back_tile(3, True)
            send_dh3.start()

        def tile1():
            back_tile(1)
            send_dh1.start()

        def tile2():
            back_tile(2)
            send_dh3.wait_recv()
            r.dhx[...] = add(dh[2][...], r.rdh[1]).astype(BF)
            send_dhx.start()

        def tile0():
            back_tile(0)
            r.cbuf[...] = r.acc[...].astype(BF)
            send_cols.start()
            total = jnp.sum(r.gn[...], axis=0, keepdims=True)
            wide = tsum.shape[2]
            row = lax.broadcasted_iota(jnp.int32, (tsum.shape[1], wide), 0) == 16
            for k in range(2):
                part = total[:, k * wide : (k + 1) * wide]
                r.tbuf[k] = jnp.where(row, part, r.tiny[k]).astype(BF)
            send_tiny.start()

        def sum_out():
            send_out[0].wait_recv()
            r.osend[...] = add(r.gout_in[:, far_cols], r.rout[0]).astype(BF)
            send_outx.start()

        def tiny_y():
            send_tiny.wait_recv()
            tsum[0] = add(r.tbuf[f], r.rtiny[...]).astype(BF)
            tiny_x()

        def sum_cols():
            send_cols.wait_recv()
            v = add(r.cbuf[mine_rows, :], r.rcol[...]).astype(BF)
            for i in range(4):
                mine[n_out + i] = v[i * piece : (i + 1) * piece]

        def sum_outx():
            send_out[1].wait_recv()
            send_outx.wait_recv()
            v = add(r.gout_in[:, near_cols], r.rout[1]) + r.rox[...].astype(F32)
            v = v.astype(BF)
            for i in range(4):
                r.eo[i // 2, i % 2] = v[i * piece : (i + 1) * piece]
            for i in range(2):
                eo_core[i].start()
                mine[n_moe + i] = r.eo[core, i]

        def inputs_back():
            send_dh1.wait_recv()
            send_dhx.wait_recv()
            up_grad = add(dh[0][...], r.rdh[0]) + r.rdx[...].astype(F32)
            normed, factor = rms_parts(r.tok_in[:tile].astype(F32))
            d_n = up_grad * r.small[16:17, :].astype(F32)
            r.dtok[...] = r.dmid_in[...] + factor * (
                d_n - normed * jnp.mean(d_n * normed, axis=-1, keepdims=True)
            )

        def arrive():
            for copy in loads:
                copy.wait()

        first_step = 1
        done = first_step + n_steps
        order = [
            send_keys, None, None, sum_outx, None, sum_dkv, tile3, tile1, tile2, tile0, None, None,
            tiny_y, sum_cols, None, inputs_back, tiny_core, None, tiny_spread,
        ]
        steps = {done + i: fn for i, fn in enumerate(order) if fn is not None}
        steps.update({0: arrive, OUT_STEP: sum_out})
    else:
        tsum[0] = r.tiny[...].astype(BF)
        tiny_x()
        steps = {1: tiny_core, 2: tiny_spread}

    @pl.loop(0, items + ahead + (last + 1) * lag)
    def _(i):
        for fn, b, cond in (
            (begin, i, True),
            (prefix, i - ahead - lag * z, z > 0),
            (suffix, i - ahead - lag * (last - z), z < last),
            (forward, i - ahead - lag * (last + 1), True),
        ):
            @pl.when(within(b, cond))
            def _():
                fn(b)

        if fused:
            @pl.when((i >= first_step) & (i < done))
            def _():
                attention(i - first_step)

        for k, fn in steps.items():
            pl.when(i == k)(fn)

    tiny_end()

    @pl.loop(0, items)
    def _(b):
        one = rc.at[b]

        @pl.when(b < n_out)
        def _():
            remote(one, one, r.s_rc, b, peer_core).wait_send()

        @pl.when(z < last)
        def _():
            hop(pre, r.s_pre, b, peer_x).wait_send()

        @pl.when(z > 0)
        def _():
            hop(suf, r.s_suf, b, peer_x).wait_send()

        remote(one, one, r.s_far, b, peer_x).wait_send()

    remote(rc, rc, r.s_oth, 0, peer_core).wait()
    remote(rc, rc, r.s_faro, 0, peer_core).wait()
    pltpu.make_async_copy(rc, rc, r.s_out.at[0]).wait()
    tiny_swap(0, peer_x).wait_send()
    tiny_swap(1, peer_core).wait_send()
    for k in range(1, slots):
        remote(tsum.at[2], trecv.at[1 + k], s_tiny, 1 + k, other_z(k)).wait_send()
    if fused:
        for copy in (send_dkv, *send_out, send_dh3, send_dh1, send_dhx, send_cols, send_outx, send_tiny):
            copy.wait_send()
        for copy in moe_back:
            copy.wait()


def reduce_grads(gm, tiny, slots, shards, eo=None, cols=None, fused=None, small=None, tables=None, moes=None):
    count, _, ff, _ = gm.shape
    width = 2 * ff
    nb = 6 * count
    piece = ff // 4
    items = 2 * nb + 6
    hbm = pl.BlockSpec(memory_space=pl.ANY)
    vmem = pl.BlockSpec(memory_space=pltpu.VMEM)
    dma = pltpu.SemaphoreType.DMA
    args = dict(gm=(gm.reshape(nb, 2, 2, piece, ff), hbm), tiny=(tiny, vmem))
    outs = dict(
        gate=(jax.ShapeDtypeStruct((2 * count, width, ff), BF), hbm),
        up=(jax.ShapeDtypeStruct((2 * count, width, ff), BF), hbm),
        down=(jax.ShapeDtypeStruct((2 * count, ff, width), BF), hbm),
        out=(jax.ShapeDtypeStruct((ff, width), BF), hbm),
        qkv=(jax.ShapeDtypeStruct((ff, 2 * width), BF), hbm),
        tiny_out=(jax.ShapeDtypeStruct(tiny.shape[-2:], F32), vmem),
    )
    buf = pltpu.VMEM((items, piece, ff), BF)
    scratch = dict(
        mine=buf, rc=buf, pre=buf, suf=buf,
        tsum=pltpu.VMEM((3,) + tiny.shape[-2:], BF),
        trecv=pltpu.VMEM((slots + 1,) + tiny.shape[-2:], BF),
        s_tiny=dma((2, slots + 1)), s_mine=dma((items,)), s_out=dma((1,)),
    )
    each = dma((2, items))
    scratch.update(s_rc=each, s_pre=each, s_suf=each, s_far=each)
    scratch.update(s_oth=dma((2, 1)), s_faro=dma((2, 1)))
    if fused is None:
        args.update(
            eo=(eo.reshape(2, 2, piece, ff), hbm), cols=(cols.reshape(4, piece, ff), hbm)
        )
    else:
        inner = {}
        for k, v in fused.items():
            args[k] = (v, hbm)
            inner[k + "_in"] = pltpu.VMEM(v.shape, v.dtype)
        smem = pl.BlockSpec(memory_space=pltpu.SMEM)
        qtab, ktab, limit = tables
        args.update(
            small=(small, vmem), qtab=(qtab, smem), ktab=(ktab, smem), limit=(limit, smem),
            moe1=(moes[0], hbm), moe3=(moes[1], hbm),
        )
        outs.update({k: (jax.ShapeDtypeStruct(moes[0].shape, BF), hbm) for k in ("got1", "got3")})
        rows = args["dmid"][0].shape[0]
        keys = args["kv"][0].shape[0] // 2
        inner.update(gout_in=pltpu.VMEM((ff, width), BF))
        scratch.update(inner)
        outs.update(dtok=(jax.ShapeDtypeStruct((rows, width), F32), vmem))
        scratch.update(
            rdkv=pltpu.VMEM((keys, 256), BF), dkvs=pltpu.VMEM((keys, 256), BF),
            rout=pltpu.VMEM((2, ff, ff), BF),
            osend=pltpu.VMEM((ff, ff), BF), rox=pltpu.VMEM((ff, ff), BF),
            eo=pltpu.VMEM((2, 2, piece, ff), BF),
            dq_in=pltpu.VMEM((keys, 256), BF),
            dk=pltpu.VMEM((2 * keys, 128), F32), dv=pltpu.VMEM((2 * keys, 128), F32),
            qs=pltpu.VMEM((2 * rows, 128), BF), dos=pltpu.VMEM((2 * rows, 128), BF),
            delta=pltpu.VMEM((8, 2 * rows), F32), dqa=pltpu.VMEM((2 * rows, 128), F32),
            kpos=pltpu.VMEM((2 * keys, 1), jnp.int32), last=pltpu.VMEM((8, 8, 2 * rows), jnp.int32),
            s_in=dma((len(fused),)), s_moe=dma((2, 2)),
            rdh=pltpu.VMEM((2, rows, width), BF),
            dhx=pltpu.VMEM((rows, width), BF), rdx=pltpu.VMEM((rows, width), BF),
            acc=pltpu.VMEM((width, ff), F32), gn=pltpu.VMEM((8, width), F32),
            cbuf=pltpu.VMEM((width, ff), BF), rcol=pltpu.VMEM((ff, ff), BF),
            tbuf=pltpu.VMEM(tiny.shape, BF), rtiny=pltpu.VMEM(tiny.shape[-2:], BF),
            s_fg=dma((2, 9)),
        )
    names = tuple(args) + tuple(outs) + tuple(scratch)
    got = pl.pallas_call(
        functools.partial(
            reduce_kernel, names=names, slots=slots, shards=shards, fused=fused is not None
        ),
        in_specs=[v[1] for v in args.values()],
        out_specs=[v[1] for v in outs.values()],
        out_shape=[v[0] for v in outs.values()],
        scratch_shapes=list(scratch.values()),
        compiler_params=pltpu.CompilerParams(
            vmem_limit_bytes=67043328, collective_id=1, has_side_effects=True
        ),
        name="reduce_grads",
    )(*[v[0] for v in args.values()])
    return types.SimpleNamespace(**dict(zip(outs, got)))


def gather_rows(x):
    return lax.all_gather(x, "fsdp", axis=0, tiled=True)


def local(
    tokens, cotangent, lengths, order, routes, norm1, query_key_value_weight, w_out, norm2, router,
    w_gate, w_up, w_down,
):
    groups = lax.axis_size("seq")
    shards = lax.axis_size("fsdp")
    slots = lax.axis_size("dp")
    assert groups == 4
    seq, fsdp = lax.axis_index("seq"), lax.axis_index("fsdp")
    core, far = seq % 2, seq // 2
    rows, width = tokens.shape[1:]
    span = rows // 2
    x = tokens[0]
    limit = lengths[:1]
    n_experts = router.shape[1]
    owned = w_gate.shape[0]
    count = owned // 2

    table = order.reshape(groups, shards, 2)
    relative = jnp.arange(groups, dtype=jnp.int32) ^ seq
    table = jnp.take(table, relative, axis=0)
    qtab = jnp.take(table, fsdp, axis=1).reshape(-1)
    if shards == 2:
        held = jnp.stack([fsdp, 1 - fsdp])
    else:
        held = jnp.arange(shards)
    ktab = jnp.transpose(jnp.take(table, held, axis=1), (1, 0, 2)).reshape(-1)
    qpos = (qtab[:, None] * span + jnp.arange(span, dtype=jnp.int32)[None, :]).reshape(-1)

    heads = QUERY_HEADS // groups
    qw, kw = heads * HEAD_WIDTH, KEY_VALUE_HEADS // groups * HEAD_WIDTH
    w3 = query_key_value_weight
    small = jnp.concatenate(
        [jnp.transpose(router), norm1[None], norm2[None], jnp.zeros((14, norm1.shape[0]), BF)]
    )
    if shards == 2:
        tok, wcols, small, hidden_one, q, kv, cos, sin = front(qtab, order.shape[0], x, w3, small)
        tok, kv = tok.reshape(groups * rows, width), kv.reshape(-1, 256)
        w_out, cotangent, kv = lax.optimization_barrier((w_out, cotangent, kv))
    else:
        half = HEAD_WIDTH // 2
        freqs = jnp.exp(jnp.arange(half, dtype=F32) * (-2.0 * math.log(ROPE_BASE) / HEAD_WIDTH))
        angles = qpos.astype(F32)[:, None] * freqs[None, :]
        cos, sin = jnp.tile(jnp.cos(angles), (1, 4)), jnp.tile(jnp.sin(angles), (1, 4))
        wq = lax.dynamic_slice_in_dim(w3, seq * qw, qw, 1)
        wk = lax.dynamic_slice_in_dim(w3, QUERY_HEADS * HEAD_WIDTH + seq * kw, kw, 1)
        wv = lax.dynamic_slice_in_dim(
            w3, (QUERY_HEADS + KEY_VALUE_HEADS) * HEAD_WIDTH + seq * kw, kw, 1
        )
        wcols = gather_rows(jnp.concatenate([wq, wk, wv], axis=1))
        small = lax.all_gather(small, "fsdp", axis=1, tiled=True)
        tok = gather_seq(x).reshape(groups * rows, width)
        hidden_one, q, kv_own = project(tok, small[16:17].astype(F32), wcols, cos, sin, rows)
        kv = gather_fsdp(kv_own)
    gain_one, gain_two = small[16].astype(F32), small[17].astype(F32)
    route_rows = small[:n_experts]

    kb = 4 * span
    own_valid = (qpos[:rows] < limit[0])[:, None]
    masked_cot = jnp.where(own_valid, cotangent[0], jnp.zeros_like(cotangent[0]))
    if shards == 2:
        shared = w_out.shape[0] // 2
        wo_near = flip_y(lax.dynamic_slice_in_dim(w_out, core * shared, shared, 0))
        cot_y, cot_x = flip_y(masked_cot), flip_x(masked_cot)
    attended, low, lse = attend(qtab, ktab, limit, q, kv, span, kb)
    inputs = x.astype(F32)
    if shards == 2:
        out = moe_layer(
            low, x, w_out, wo_near, small, routes[0], masked_cot, cot_y, cot_x, w_gate, w_up, w_down
        )
        moes = (out.moe1, out.moe3)
        d_heads = out.do.reshape(groups * rows, qw)
        middle, d_middle, grad_out, tiny = out.middle, out.dmid, out.gout, out.tiny
        weight_grads = out.grads.reshape(count, 6, w_gate.shape[2], -1)
    else:
        sent = low.reshape(groups, rows, qw)
        got = jnp.stack(swap_seq([sent[m] for m in range(groups)]))
        got = jnp.take(got, relative, axis=0)
        token_out = jnp.transpose(got, (1, 0, 2)).reshape(rows, groups * qw)
        out_full = gather_rows(w_out)

        middle = inputs + mm(token_out, out_full)
        normed_two, factor_two = rms_parts(middle)
        hidden_two = (normed_two * gain_two).astype(BF)
        logits = mm_nt(hidden_two, route_rows)
        chosen = jnp.any(
            routes[0][:, :, None] == jnp.arange(n_experts, dtype=jnp.int32)[None, None, :], axis=1
        )
        top = jnp.max(jnp.where(chosen, logits, NEG), axis=-1, keepdims=True)
        raised = jnp.where(chosen, jnp.exp(logits - top), 0.0)
        gates = raised / jnp.sum(raised, axis=-1, keepdims=True)

        def share(v):
            near = gather_rows(v)
            return jnp.concatenate([near, flip_x(near)])

        cot_all = share(masked_cot)
        extended = jnp.concatenate(
            [hidden_two, gates.astype(BF), jnp.zeros((rows, 128 - n_experts), BF)], axis=1
        )
        hid_all = share(extended)
        base = jnp.stack([far * count, fsdp * owned + far * count]).astype(jnp.int32)
        part = rows * 4
        moe_parts, dh_parts, weight_grads = [], [], None
        for i in range(hid_all.shape[0] // part):
            got = experts(
                base, count, hid_all[i * part : (i + 1) * part], cot_all[i * part : (i + 1) * part],
                w_gate, w_up, w_down, rows,
            )
            moe_parts.append(got[0])
            dh_parts.append(got[1])
            if weight_grads is None:
                weight_grads = got[2]
            else:
                weight_grads = (weight_grads.astype(F32) + got[2].astype(F32)).astype(BF)

        def give_back(parts):
            v = jnp.concatenate(parts) if len(parts) > 1 else parts[0]
            n = v.shape[0] // 2
            near = v[:n].astype(F32) + flip_x(v[n:]).astype(F32)
            return lax.psum_scatter(near.astype(BF), "fsdp", scatter_dimension=0, tiled=True).astype(F32)

        d_ext = give_back(dh_parts)
        d_gates = d_ext[:, width : width + n_experts]
        d_logits = (gates * (d_gates - jnp.sum(gates * d_gates, axis=-1, keepdims=True))).astype(BF)
        grad_router = mm_tn(hidden_two, d_logits)
        d_hidden = d_ext[:, :width] + mm(d_logits, route_rows)
        grad_norm2 = jnp.sum(d_hidden * normed_two, axis=0)
        d_n = d_hidden * gain_two
        d_middle = masked_cot.astype(F32) + factor_two * (
            d_n - normed_two * jnp.mean(d_n * normed_two, axis=-1, keepdims=True)
        )
        d_attn = d_middle.astype(BF)
        grad_out = mm_tn(token_out, d_attn).astype(BF)
        d_token_out = mm_nt(d_attn, out_full).astype(BF)
        d_heads = jnp.transpose(d_token_out.reshape(rows, groups, qw), (1, 0, 2))
        d_heads = jnp.take(d_heads, relative, axis=0)
        d_heads = jnp.concatenate(swap_seq([d_heads[m] for m in range(groups)]))
    block = w_gate.shape[2]
    shard_rows = width // shards

    def tiny_rows(first):
        return jnp.concatenate(
            [jnp.transpose(grad_router), first[None], grad_norm2[None], jnp.zeros((14, width), F32)]
        ).reshape(32, shards, shard_rows).transpose(1, 0, 2)

    if shards == 2:
        got = reduce_grads(
            weight_grads, tiny, slots, shards,
            fused=dict(
                q=q, kv=kv, do=d_heads, o=attended, lse=lse,
                tok=tok, h=hidden_one, wc=wcols, cos=cos, sin=sin, dmid=d_middle, gout=grad_out,
            ),
            small=small, tables=(qtab, ktab, limit), moes=moes,
        )
        d_inputs = got.dtok
    else:
        dq, dkv = attend_back(qtab, ktab, limit, q, kv, d_heads, attended, lse, span, kb)
        dh_one, grad_cols, grad_norm1 = project_back(
            tok, hidden_one, dq, scatter_fsdp(dkv), wcols, cos, sin, rows
        )
        dh_one = dh_one.reshape(groups, rows, width)
        near = dh_one[0::2].astype(F32) + flip_core(dh_one[1::2]).astype(F32)
        d_hidden_one = near[0] + flip_x(near[1].astype(BF)).astype(F32)
        normed_one, factor_one = rms_parts(inputs)
        d_n = d_hidden_one * gain_one
        d_inputs = d_middle + factor_one * (
            d_n - normed_one * jnp.mean(d_n * normed_one, axis=-1, keepdims=True)
        )

        def to_owner(g):
            part = lax.psum_scatter(g, "fsdp", scatter_dimension=0, tiled=True)
            return jnp.pad(part, ((0, block - part.shape[0]), (0, 0)))

        cols = to_owner(grad_cols)
        mine = to_owner(grad_out).reshape(block, 2, block)
        kept = lax.dynamic_index_in_dim(mine, far, 1, keepdims=False)
        sent = lax.dynamic_index_in_dim(mine, 1 - far, 1, keepdims=False)
        outs = (kept.astype(F32) + flip_x(sent).astype(F32)).astype(BF)
        tiny = tiny_rows(jnp.sum(grad_norm1, axis=0))
        tiny = lax.psum_scatter(tiny, "fsdp", scatter_dimension=0, tiled=True)[0]
        got = reduce_grads(weight_grads, tiny, slots, shards, eo=outs, cols=cols)
    grad_gate, grad_up, grad_down, shard_out, shard_qkv, *tiny = widen(
        [got.gate, got.up, got.down, got.out, got.qkv], got.tiny_out, n_experts
    )
    shard_out, shard_qkv = shard_out[:shard_rows], shard_qkv[:shard_rows]
    if shards == 2:
        parts = (out.moe0, got.got1, out.got2, got.got3)
        layer_out = (middle + sum(p.astype(F32) for p in parts)).astype(BF)
    else:
        layer_out = (middle + give_back(moe_parts)).astype(BF)
    return (
        layer_out[None], d_inputs[None], tiny[0], shard_qkv, shard_out, tiny[1], tiny[2],
        grad_gate, grad_up, grad_down,
    )


def solution(mesh):
    placed = (
        P("dp", ("seq", "fsdp"), None),
        P("dp", ("seq", "fsdp"), None),
        P("dp"),
        P(),
        P("dp", ("seq", "fsdp"), None),
        P("fsdp"),
        P("fsdp", None),
        P("fsdp", None),
        P("fsdp"),
        P("fsdp", None),
        P("fsdp", None, None),
        P("fsdp", None, None),
        P("fsdp", None, None),
    )
    return jax.shard_map(
        local,
        mesh=mesh,
        in_specs=placed,
        out_specs=(
            P("dp", ("seq", "fsdp"), None),
            P("dp", ("seq", "fsdp"), None),
            P("fsdp"),
            P("fsdp", None),
            P("fsdp", None),
            P("fsdp"),
            P("fsdp", None),
            P("fsdp", None, None),
            P("fsdp", None, None),
            P("fsdp", None, None),
        ),
        check_vma=False,
    )
```

```python
import functools
import math
import types

import jax
import jax.numpy as jnp
import numpy as np
from jax import lax
from jax.experimental import pallas as pl
from jax.experimental.pallas import tpu as pltpu
from jax.sharding import PartitionSpec as P

QUERY_HEADS = 16
KEY_VALUE_HEADS = 8
HEAD_WIDTH = 64
TOPK = 8

EPS = 1e-06
ROPE_BASE = 10000.0
LOG2E = math.log2(math.e)
NEG = -1e30
BF = jnp.bfloat16
F32 = jnp.float32
VMEM_LIMIT = 60 * 1024 * 1024
OUT_STEP = 6

NT_DIMS = (((1,), (1,)), ((), ()))
TN_DIMS = (((0,), (0,)), ((), ()))


def mm(a, b):
    return jnp.dot(a, b, preferred_element_type=F32)


def mm_nt(a, b):
    return lax.dot_general(a, b, NT_DIMS, preferred_element_type=F32)


def mm_tn(a, b):
    return lax.dot_general(a, b, TN_DIMS, preferred_element_type=F32)


def params(**kw):
    return pltpu.CompilerParams(vmem_limit_bytes=VMEM_LIMIT, **kw)


def whole(shape):
    return pl.BlockSpec(shape, lambda *_: (0,) * len(shape))


def rms_parts(x):
    factor = lax.rsqrt(jnp.mean(x * x, axis=-1, keepdims=True) + EPS)
    return x * factor, factor


def qkv_kernel(tok_ref, gain_ref, w_ref, cos_ref, sin_ref, h_ref, q_ref, kv_ref):
    normed, _ = rms_parts(tok_ref[...].astype(F32))
    h = (normed * gain_ref[...]).astype(BF)
    h_ref[...] = h
    proj = mm(h, w_ref[...])
    cos, sin = cos_ref[...], sin_ref[...]
    low_half = lax.broadcasted_iota(jnp.int32, cos.shape, 1) % HEAD_WIDTH < HEAD_WIDTH // 2
    half = HEAD_WIDTH // 2
    for t in range(3):
        w = proj[:, t * 128 : (t + 1) * 128]
        rot = jnp.where(low_half, -pltpu.roll(w, 128 - half, 1), pltpu.roll(w, half, 1))
        out = (w * cos + rot * sin).astype(BF)
        if t < 2:
            q_ref[:, t * 128 : (t + 1) * 128] = out
        else:
            kv_ref[:, :128] = out
    kv_ref[:, 128:] = proj[:, 384:].astype(BF)


def project(tok, gain, w, cos, sin, tile):
    rows, width = tok.shape
    return pl.pallas_call(
        qkv_kernel,
        grid=(rows // tile,),
        in_specs=[
            pl.BlockSpec((tile, width), lambda i: (i, 0)),
            whole((1, width)),
            whole(w.shape),
            pl.BlockSpec((tile, 128), lambda i: (i, 0)),
            pl.BlockSpec((tile, 128), lambda i: (i, 0)),
        ],
        out_specs=[
            pl.BlockSpec((tile, width), lambda i: (i, 0)),
            pl.BlockSpec((tile, 256), lambda i: (i, 0)),
            pl.BlockSpec((tile, 256), lambda i: (i, 0)),
        ],
        out_shape=[
            jax.ShapeDtypeStruct((rows, width), BF),
            jax.ShapeDtypeStruct((rows, 256), BF),
            jax.ShapeDtypeStruct((rows, 256), BF),
        ],
        compiler_params=params(),
        name="project",
    )(tok, gain, w, cos, sin)


MESH = pl.DeviceIdType.MESH


def rope_rows(w, cos, sin):
    half = HEAD_WIDTH // 2
    low_half = lax.broadcasted_iota(jnp.int32, w.shape, 1) % HEAD_WIDTH < half
    rot = jnp.where(low_half, -pltpu.roll(w, 128 - half, 1), pltpu.roll(w, half, 1))
    return w * cos + rot * sin


def span_at(order, j):
    s, f = lax.axis_index("seq"), lax.axis_index("fsdp")
    x, c = s // 2, s % 2
    a, b, away = j % 8 // 4, j % 4 // 2, j // 8
    q = (x + a - 2 * x * a) * 2 + c + b - 2 * c * b
    return order[(q * 2 + f + away - 2 * f * away) * 2 + j % 2]


def front_kernel(
    order, tok, w3, norm1, norm2, router, rtab, stab, tok_out, wc_out, small_all, h_out, q, kv, cos_out, sin_out,
    small, tok_all, wc, h, cos, sin, s_tok, s_w, s_own, s_kv, s_end
):
    z, s, f = lax.axis_index("dp"), lax.axis_index("seq"), lax.axis_index("fsdp")
    core = s % 2
    peer_core = (z, s + 1 - 2 * core, f)
    peer_x = (z, (s + 2) % 4, f)
    peer_y = (z, s, 1 - f)
    rows, width = tok.shape
    part = small.shape[1]

    barrier = pltpu.get_barrier_semaphore()
    for dev in (peer_core, peer_x, peer_y):
        pl.semaphore_signal(barrier, inc=1, device_id=dev, device_id_type=MESH)

    def remote(src, dst, sems, b, dev):
        return pltpu.make_async_remote_copy(
            src_ref=src, dst_ref=dst, send_sem=sems.at[0, b], recv_sem=sems.at[1, b],
            device_id=dev, device_id_type=MESH,
        )

    own_rows = pl.ds(pl.multiple_of(f * part, part), part)
    pieces = []
    for first, n, to in ((width, 128, 256), (width + width // 2, 128, 384), (0, 256, 0)):
        src = w3.at[:, pl.ds(pl.multiple_of(first + s * n, 128), n)]
        pieces.append((src, wc.at[own_rows, pl.ds(to, n)]))
    local = [pltpu.make_async_copy(a, b, s_own.at[i]) for i, (a, b) in enumerate(pieces)]
    for copy in local:
        copy.start()
    n_exp = router.shape[1]
    row = lax.broadcasted_iota(jnp.int32, (small.shape[0] - n_exp, part), 0)
    gains = [v[...].astype(F32).reshape(1, part) for v in (norm1, norm2)]
    small[:n_exp, :] = jnp.transpose(router[...].astype(F32)).astype(BF)
    small[n_exp:, :] = jnp.where(row == 0, gains[0], jnp.where(row == 1, gains[1], 0.0)).astype(BF)
    small_all[:, own_rows] = small[...]
    tok_all[0] = tok[...]
    pl.semaphore_wait(barrier, 3)
    over = remote(tok, tok_all.at[2], s_tok, 1, peer_x)
    near = remote(tok, tok_all.at[1], s_tok, 0, peer_core)
    onward = remote(tok_all.at[2], tok_all.at[3], s_tok, 2, peer_core)
    weights = [remote(a, b, s_w, i, peer_y) for i, (a, b) in enumerate(pieces)]
    weights.insert(0, remote(small, small_all.at[:, own_rows], s_w, 3, peer_y))
    over.start()
    for copy in weights:
        copy.start()
    near.start()
    for copy in local:
        copy.wait()
    for copy in weights[:3]:
        copy.wait_recv()
    gain = small_all[16:17, :].astype(F32)

    def kv_copy(t):
        at = pl.ds(pl.multiple_of(t * rows, rows), rows)
        return remote(kv.at[0, at], kv.at[1, at], s_kv, t, peer_y)

    ends = []
    span = rows // 2
    for k in range(8):
        at = pl.ds(k * span, span)
        row = pl.ds(span_at(order, k), 1)
        c, n = stab[0, row, :], stab[1, row, :]
        cos[at, :] = rtab[0] * c - rtab[1] * n
        sin[at, :] = rtab[1] * c + rtab[0] * n
    for i, (src, dst) in enumerate(((cos, cos_out), (sin, sin_out))):
        ends.append(pltpu.make_async_copy(src, dst, s_end.at[1 + i]))
        ends[-1].start()

    def end(t):
        at = pl.ds(pl.multiple_of(t * rows, rows), rows)
        return [
            pltpu.make_async_copy(tok_all.at[t], tok_out.at[t], s_end.at[3 + t]),
            pltpu.make_async_copy(h.at[at], h_out.at[at], s_end.at[7 + t]),
        ]

    @pl.loop(0, 4)
    def _(t):
        pl.when(t == 1)(near.wait_recv)

        @pl.when(t == 2)
        def _():
            over.wait_recv()
            onward.start()

        pl.when(t == 3)(onward.wait_recv)
        at = pl.ds(pl.multiple_of(t * rows, rows), rows)
        normed, _ = rms_parts(tok_all[t].astype(F32))
        hidden = (normed * gain).astype(BF)
        h[at, :] = hidden
        proj = mm(hidden, wc[:, 256:])
        kv[0, at, :128] = rope_rows(proj[:, :128], cos[at, :], sin[at, :]).astype(BF)
        kv[0, at, 128:] = proj[:, 128:].astype(BF)
        kv_copy(t).start()
        for copy in end(t):
            copy.start()

    weights[3].wait_recv()
    ends.append(pltpu.make_async_copy(wc, wc_out, s_end.at[0]))
    ends[-1].start()

    @pl.loop(0, 4)
    def _(t):
        at = pl.ds(pl.multiple_of(t * rows, rows), rows)
        proj = mm(h[at, :], wc[:, :256])
        for k in range(2):
            w = proj[:, k * 128 : (k + 1) * 128]
            q[at, k * 128 : (k + 1) * 128] = rope_rows(w, cos[at, :], sin[at, :]).astype(BF)

    for t in range(4):
        ends.extend(end(t))
    for t in range(4):
        kv_copy(t).wait()
    for copy in ends:
        copy.wait()
    for copy in (over, near, onward, *weights):
        copy.wait_send()


def front(order, tok, w3, norm1, norm2, router):
    rows, width = tok.shape
    n_spans = order.shape[0]
    span, half = rows // 2, HEAD_WIDTH // 2
    freqs = np.exp(np.arange(half) * (-2.0 * math.log(ROPE_BASE) / HEAD_WIDTH)).astype(np.float32)

    def table(positions):
        angles = np.tile(positions[:, None].astype(np.float64) * freqs[None, :], (1, 4))
        return jnp.asarray(np.stack([np.cos(angles), np.sin(angles)]), F32)

    rtab, stab = table(np.arange(span)), table(np.arange(n_spans) * span)
    vmem = pl.BlockSpec(memory_space=pltpu.VMEM)
    hbm = pl.BlockSpec(memory_space=pl.ANY)
    dma = pltpu.SemaphoreType.DMA
    shape = jax.ShapeDtypeStruct
    return pl.pallas_call(
        front_kernel,
        in_specs=[pl.BlockSpec(memory_space=pltpu.SMEM), vmem, hbm, vmem, vmem, vmem, vmem, vmem],
        out_specs=[hbm, hbm, vmem, hbm, vmem, vmem, hbm, hbm],
        out_shape=[
            shape((4, rows, width), BF),
            shape((width, 512), BF),
            shape((32, width), BF),
            shape((4 * rows, width), BF),
            shape((4 * rows, 256), BF),
            shape((2, 4 * rows, 256), BF),
            shape((4 * rows, 128), F32),
            shape((4 * rows, 128), F32),
        ],
        scratch_shapes=[
            pltpu.VMEM((32, norm1.shape[0]), BF),
            pltpu.VMEM((4, rows, width), BF), pltpu.VMEM((width, 512), BF),
            pltpu.VMEM((4 * rows, width), BF),
            pltpu.VMEM((4 * rows, 128), F32), pltpu.VMEM((4 * rows, 128), F32),
            dma((2, 3)), dma((2, 4)), dma((3,)), dma((2, 4)), dma((11,)),
        ],
        compiler_params=params(collective_id=2, has_side_effects=True),
        name="front",
    )(order, tok, w3, norm1, norm2, router, rtab, stab)


def widen_kernel(*refs, wide, parts):
    n = wide + parts + 1
    ins, outs = refs[:n], refs[n:]
    for a, b in zip(ins[:wide], outs[:wide]):
        b[...] = a[...].astype(F32)
    if parts:
        total = ins[wide][...].astype(F32)
        for part in ins[wide + 1 : wide + parts]:
            total = total + part[...].astype(F32)
        outs[wide][...] = total.astype(BF)
    tiny, (one, two, router) = ins[-1], outs[-3:]

    @pl.when(pl.program_id(0) == 0)
    def _():
        one[...] = tiny[16:17, :]
        two[...] = tiny[17:18, :]
        router[...] = jnp.transpose(tiny[...])[:, : router.shape[1]]


def widen(arrays, parts, tiny, n_experts):
    flat = [a.reshape(-1, a.shape[-1]) for a in arrays]
    steps = 4
    cols = tiny.shape[1]
    block = lambda a: pl.BlockSpec((a.shape[0] // steps, a.shape[1]), lambda i: (i, 0))
    shape = jax.ShapeDtypeStruct
    smalls = [(1, cols), (1, cols), (cols, n_experts)]
    sums = [shape(p.shape, BF) for p in parts[:1]]
    got = pl.pallas_call(
        functools.partial(widen_kernel, wide=len(flat), parts=len(parts)),
        grid=(steps,),
        in_specs=[block(a) for a in (*flat, *parts)] + [whole(tiny.shape)],
        out_specs=[block(a) for a in (*flat, *sums)] + [whole(v) for v in smalls],
        out_shape=[shape(a.shape, F32) for a in flat] + sums + [shape(v, F32) for v in smalls],
        compiler_params=params(),
        name="widen",
    )(*flat, *parts, tiny)
    n = len(arrays)
    wide = [g.reshape(a.shape) for g, a in zip(got, arrays)]
    return wide, got[n : n + len(sums)], [got[-3][0], got[-2][0], got[-1]]


def project_back_kernel(
    tok_ref, h_ref, dq_ref, dkv_ref, w_ref, cos_ref, sin_ref, dh_ref, gw_ref, gn_ref, acc
):
    step = pl.program_id(0)

    @pl.when(step == 0)
    def _():
        acc[...] = jnp.zeros_like(acc)
        gn_ref[...] = jnp.zeros_like(gn_ref)

    cos, sin = cos_ref[...], sin_ref[...]
    half = HEAD_WIDTH // 2
    low_half = lax.broadcasted_iota(jnp.int32, cos.shape, 1) % HEAD_WIDTH < half
    parts = []
    for t in range(3):
        w = dq_ref[:, t * 128 : (t + 1) * 128] if t < 2 else dkv_ref[:, :128]
        w = w.astype(F32)
        y = w * sin
        rot = jnp.where(low_half, pltpu.roll(y, 128 - half, 1), -pltpu.roll(y, half, 1))
        parts.append((w * cos + rot).astype(BF))
    parts.append(dkv_ref[:, 128:].astype(BF))
    dproj = jnp.concatenate(parts, axis=1)
    acc[...] += mm_tn(h_ref[...], dproj)
    dh = mm_nt(dproj, w_ref[...])
    dh_ref[...] = dh.astype(BF)
    normed, _ = rms_parts(tok_ref[...].astype(F32))
    gn_ref[...] += jnp.sum((dh * normed).reshape(-1, 8, dh.shape[1]), axis=0)

    @pl.when(step == pl.num_programs(0) - 1)
    def _():
        gw_ref[...] = acc[...].astype(BF)


def project_back(tok, h, dq, dkv, w, cos, sin, tile):
    rows, width = tok.shape
    row = lambda n: pl.BlockSpec((tile, n), lambda i: (i, 0))
    return pl.pallas_call(
        project_back_kernel,
        grid=(rows // tile,),
        in_specs=[row(width), row(width), row(256), row(256), whole(w.shape), row(128), row(128)],
        out_specs=[row(width), whole(w.shape), whole((8, width))],
        out_shape=[
            jax.ShapeDtypeStruct((rows, width), BF),
            jax.ShapeDtypeStruct(w.shape, BF),
            jax.ShapeDtypeStruct((8, width), F32),
        ],
        scratch_shapes=[pltpu.VMEM(w.shape, F32)],
        compiler_params=params(),
        name="project_back",
    )(tok, h, dq, dkv, w, cos, sin)


def stack_heads(a, b, dtype=BF):
    a, b = a.astype(F32), b.astype(F32)
    low = lax.broadcasted_iota(jnp.int32, a.shape, 1) < HEAD_WIDTH
    turn = lambda v: pltpu.roll(v, HEAD_WIDTH, 1)
    rows = [
        jnp.where(low, a, 0.0), jnp.where(low, turn(a), 0.0),
        jnp.where(low, 0.0, turn(b)), jnp.where(low, 0.0, b),
    ]
    return jnp.concatenate(rows, axis=0).astype(dtype)


def unstack_heads(x):
    n = x.shape[0] // 4
    low = lax.broadcasted_iota(jnp.int32, (n, 128), 1) < HEAD_WIDTH
    turn = lambda v: pltpu.roll(v, HEAD_WIDTH, 1)
    return (
        jnp.where(low, x[:n], turn(x[n : 2 * n])),
        jnp.where(low, turn(x[2 * n : 3 * n]), x[3 * n :]),
    )


def block_counts(span_id, limit, span, kb):
    first = span_id * span
    seen = (first + span - 1) // kb + 1
    blocks = jnp.minimum(seen, (limit + kb - 1) // kb)
    full = jnp.minimum(first + 1, limit) // kb
    return jnp.minimum(full, blocks), blocks


def sort_spans(ktab_ref, src, dst, lanes, span, count):
    @pl.loop(0, count)
    def _(j):
        to = pl.multiple_of(ktab_ref[j] * span, span)
        dst[pl.ds(to, span), :] = src[pl.ds(pl.multiple_of(j * span, span), span), lanes]


def attend_kernel(
    qtab_ref, ktab_ref, len_ref, q_ref, kv_ref, o_ref, low_ref, lse_ref, ks, vs, *, span, kb
):
    step = pl.program_id(0)
    count = ks.shape[0] // span

    @pl.when(step == 0)
    def _():
        sort_spans(ktab_ref, kv_ref, ks, slice(0, 128), span, count)
        sort_spans(ktab_ref, kv_ref, vs, slice(128, 256), span, count)

    q = stack_heads(q_ref[:, :128], q_ref[:, 128:])
    rows = 4 * span
    limit = len_ref[0]
    span_id = qtab_ref[step]
    full, blocks = block_counts(span_id, limit, span, kb)
    qpos = span_id * span + lax.broadcasted_iota(jnp.int32, (rows, kb), 0) % span
    col = lax.broadcasted_iota(jnp.int32, (rows, kb), 1)
    last = jnp.minimum(qpos, limit - 1)

    def body(masked, i, carry):
        top, total, acc = carry
        at = pl.multiple_of(i * kb, kb)
        s = mm_nt(q, ks[pl.ds(at, kb), :]) * (HEAD_WIDTH**-0.5 * LOG2E)
        if masked:
            s = jnp.where(col + i * kb <= last, s, NEG)
        new = jnp.maximum(top, jnp.max(s, axis=1, keepdims=True))
        fade = jnp.exp2(top - new)
        p = jnp.exp2(s - new)
        total = total * fade + jnp.sum(p, axis=1, keepdims=True)
        acc = acc * fade + mm(p.astype(BF), vs[pl.ds(at, kb), :])
        return new, total, acc

    carry = (
        jnp.full((rows, 1), NEG, F32),
        jnp.zeros((rows, 1), F32),
        jnp.zeros((rows, 128), F32),
    )
    carry = lax.fori_loop(0, full, functools.partial(body, False), carry)
    top, total, acc = lax.fori_loop(full, blocks, functools.partial(body, True), carry)
    a, b = unstack_heads(acc / total)
    o_ref[:, :128] = a
    o_ref[:, 128:] = b
    low_ref[:, :128] = a.astype(BF)
    low_ref[:, 128:] = b.astype(BF)
    lse = jnp.broadcast_to(top + jnp.log2(total), (rows, 128))
    lse_ref[0] = jnp.transpose(lse)[:8]


def attend_short_kernel(
    order_ref, len_ref, q_ref, kv_ref, o_ref, low_ref, lse_ref, ks, vs, *, span, kb
):
    step = pl.program_id(0)
    count = ks.shape[0] // span

    @pl.when(step == 0)
    def _():
        @pl.loop(0, count)
        def _(j):
            to = pl.ds(pl.multiple_of(span_at(order_ref, j) * span, span), span)
            at = pl.ds(pl.multiple_of(j * span, span), span)
            ks[to, :] = kv_ref[at, :128]
            vs[to, :] = kv_ref[at, 128:]

    q = stack_heads(q_ref[:, :128], q_ref[:, 128:])
    rows = 2 * span
    limit = len_ref[0]
    span_id = span_at(order_ref, step)
    _, blocks = block_counts(span_id, limit, span, kb)
    qpos = span_id * span + lax.broadcasted_iota(jnp.int32, (rows, kb), 0) % span
    last = jnp.minimum(qpos, limit - 1)
    col = lax.broadcasted_iota(jnp.int32, (rows, kb), 1)

    def run(n):
        outs, sums = [], []
        for g in range(2):
            part = q[g * rows : (g + 1) * rows]
            scores = []
            for i in range(n):
                v = mm_nt(part, ks[i * kb : (i + 1) * kb, :]) * (HEAD_WIDTH**-0.5 * LOG2E)
                if i == n - 1:
                    v = jnp.where(col + i * kb <= last, v, NEG)
                scores.append(v)
            tops = [jnp.max(v, axis=1, keepdims=True) for v in scores]
            top = functools.reduce(jnp.maximum, tops)
            total = jnp.zeros((rows, 1), F32)
            acc = jnp.zeros((rows, 128), F32)
            for i in range(n):
                p = jnp.exp2(scores[i] - top)
                total = total + jnp.sum(p, axis=1, keepdims=True)
                acc = acc + mm(p.astype(BF), vs[i * kb : (i + 1) * kb, :])
            outs.append(acc / total)
            sums.append(top + jnp.log2(total))
        a, b = unstack_heads(jnp.concatenate(outs, axis=0))
        o_ref[:, :128] = a
        o_ref[:, 128:] = b
        low_ref[:, :128] = a.astype(BF)
        low_ref[:, 128:] = b.astype(BF)
        lse = jnp.broadcast_to(jnp.concatenate(sums, axis=0), (2 * rows, 128))
        lse_ref[0] = jnp.transpose(lse)[:8]

    for n in range(1, ks.shape[0] // kb + 1):
        pl.when(blocks == n)(functools.partial(run, n))


def attend(body, tables, q, kv, span, kb):
    steps, keys = q.shape[0] // span, kv.shape[0]
    return pl.pallas_call(
        functools.partial(body, span=span, kb=kb),
        grid_spec=pltpu.PrefetchScalarGridSpec(
            num_scalar_prefetch=len(tables),
            grid=(steps,),
            in_specs=[pl.BlockSpec((span, 256), lambda i, *_: (i, 0)), whole(kv.shape)],
            out_specs=[
                pl.BlockSpec((span, 256), lambda i, *_: (i, 0)),
                pl.BlockSpec((span, 256), lambda i, *_: (i, 0)),
                pl.BlockSpec((1, 8, 4 * span), lambda i, *_: (i, 0, 0)),
            ],
            scratch_shapes=[pltpu.VMEM((keys, 128), BF), pltpu.VMEM((keys, 128), BF)],
        ),
        out_shape=[
            jax.ShapeDtypeStruct((q.shape[0], 256), F32),
            jax.ShapeDtypeStruct((q.shape[0], 256), BF),
            jax.ShapeDtypeStruct((steps, 8, 4 * span), F32),
        ],
        compiler_params=params(),
        name="attend",
    )(*tables, q, kv)


def attend_back_kernel(
    qtab_ref, ktab_ref, len_ref, q_ref, kv_ref, do_ref, o_ref, lse_ref, dq_ref, dkv_ref,
    ks, vs, dk, dv, *, span, kb,
):
    step = pl.program_id(0)
    count = ks.shape[0] // span
    scale = HEAD_WIDTH**-0.5

    @pl.when(step == 0)
    def _():
        sort_spans(ktab_ref, kv_ref, ks, slice(0, 128), span, count)
        sort_spans(ktab_ref, kv_ref, vs, slice(128, 256), span, count)
        dk[...] = jnp.zeros_like(dk)
        dv[...] = jnp.zeros_like(dv)

    q = stack_heads(q_ref[:, :128], q_ref[:, 128:])
    do = stack_heads(do_ref[:, :128], do_ref[:, 128:])
    rows = 4 * span
    inner = do.astype(F32) * stack_heads(o_ref[:, :128], o_ref[:, 128:], F32)
    delta = jnp.sum(jnp.transpose(inner), axis=0, keepdims=True)
    lse = lse_ref[0, :1]
    limit = len_ref[0]
    span_id = qtab_ref[step]
    full, blocks = block_counts(span_id, limit, span, kb)
    blocks = jnp.where(span_id * span < limit, blocks, 0)
    full = jnp.minimum(full, blocks)
    qpos = span_id * span + lax.broadcasted_iota(jnp.int32, (kb, rows), 1) % span
    key = lax.broadcasted_iota(jnp.int32, (kb, rows), 0)
    last = jnp.minimum(qpos, limit - 1)

    def body(masked, i, dq):
        at = pl.ds(pl.multiple_of(i * kb, kb), kb)
        k, v = ks[at, :], vs[at, :]
        s = mm_nt(k, q) * (scale * LOG2E)
        p = jnp.exp2(s - lse)
        if masked:
            p = jnp.where(key + i * kb <= last, p, 0.0)
        dp = mm_nt(v, do)
        ds = (p * (dp - delta)).astype(BF)
        dk[at, :] += mm(ds, q)
        dv[at, :] += mm(p.astype(BF), do)
        return dq + mm_tn(ds, k)

    dq = jnp.zeros((rows, 128), F32)
    dq = lax.fori_loop(0, full, functools.partial(body, False), dq)
    dq = lax.fori_loop(full, blocks, functools.partial(body, True), dq)
    a, b = unstack_heads(dq * scale)
    dq_ref[:, :128] = a.astype(BF)
    dq_ref[:, 128:] = b.astype(BF)

    @pl.when(step == pl.num_programs(0) - 1)
    def _():
        @pl.loop(0, count)
        def _(j):
            at = pl.ds(pl.multiple_of(ktab_ref[j] * span, span), span)
            to = pl.ds(pl.multiple_of(j * span, span), span)
            dkv_ref[to, :128] = (dk[at, :] * scale).astype(BF)
            dkv_ref[to, 128:] = dv[at, :].astype(BF)


def attend_back(qtab, ktab, limit, q, kv, do, o, lse, span, kb):
    steps, keys = q.shape[0] // span, kv.shape[0]
    row = pl.BlockSpec((span, 256), lambda i, *_: (i, 0))
    return pl.pallas_call(
        functools.partial(attend_back_kernel, span=span, kb=kb),
        grid_spec=pltpu.PrefetchScalarGridSpec(
            num_scalar_prefetch=3,
            grid=(steps,),
            in_specs=[
                row, whole(kv.shape), row, row,
                pl.BlockSpec((1, 8, 4 * span), lambda i, *_: (i, 0, 0)),
            ],
            out_specs=[row, whole(kv.shape)],
            scratch_shapes=[
                pltpu.VMEM((keys, 128), BF), pltpu.VMEM((keys, 128), BF),
                pltpu.VMEM((keys, 128), F32), pltpu.VMEM((keys, 128), F32),
            ],
        ),
        out_shape=[
            jax.ShapeDtypeStruct((q.shape[0], 256), BF),
            jax.ShapeDtypeStruct(kv.shape, BF),
        ],
        compiler_params=params(),
        name="attend_back",
    )(qtab, ktab, limit, q, kv, do, o, lse)


def experts_kernel(
    base_ref, h_ref, c_ref, wg_ref, wu_ref, wd_ref, moe_ref, dh_ref, grad_ref,
    moe, dh, dgates, s_act, s_gate, s_up, *, tile,
):
    step = pl.program_id(0)
    width = c_ref.shape[1]
    expert = base_ref[1] + step
    wg, wu, wd = wg_ref[0], wu_ref[0], wd_ref[0]

    @pl.when(step == 0)
    def _():
        moe[...] = jnp.zeros_like(moe)
        dh[...] = jnp.zeros_like(dh)
        dgates[...] = jnp.zeros_like(dgates)

    @pl.loop(0, moe.shape[0] // tile)
    def _(t):
        at = pl.ds(pl.multiple_of(t * tile, tile), tile)
        h, c = h_ref[at, :width], c_ref[at, :]
        lane = lax.broadcasted_iota(jnp.int32, (tile, 128), 1)
        mine = lane == expert
        gate = jnp.sum(
            jnp.where(mine, h_ref[at, width:].astype(F32), 0.0), axis=1, keepdims=True
        )
        g, u, z = mm(h, wg), mm(h, wu), mm_nt(c, wd)
        sig = jax.nn.sigmoid(g)
        silu = g * sig
        act = silu * u
        dgates[at, :] += jnp.where(mine, jnp.sum(act * z, axis=1, keepdims=True), 0.0)
        act = (act * gate).astype(BF)
        dact = z * gate
        dgate = (dact * u * sig * (1.0 + g * (1.0 - sig))).astype(BF)
        dup = (dact * silu).astype(BF)
        s_act[at, :] = act
        s_gate[at, :] = dgate
        s_up[at, :] = dup
        moe[at, :] += mm(act, wd)
        dh[at, :] += mm_nt(dgate, wg) + mm_nt(dup, wu)

    block = grad_ref.shape[2]
    for i in range(2):
        at = slice(i * block, (i + 1) * block)
        grad_ref[0, i] = mm_tn(h_ref[:, at], s_gate[...]).astype(BF)
        grad_ref[0, 2 + i] = mm_tn(h_ref[:, at], s_up[...]).astype(BF)
        grad_ref[0, 4 + i] = mm_tn(s_act[...], c_ref[:, at]).astype(BF)

    @pl.when(step == pl.num_programs(0) - 1)
    def _():
        moe_ref[...] = moe[...].astype(BF)
        dh_ref[:, :width] = dh[...].astype(BF)
        dh_ref[:, width:] = dgates[...].astype(BF)


def experts(base, count, h, c, wg, wu, wd, tile):
    rows, width = c.shape
    ff = wg.shape[2]
    pick = lambda shape: pl.BlockSpec((1,) + shape, lambda e, s: (s[0] + e, 0, 0))
    return pl.pallas_call(
        functools.partial(experts_kernel, tile=tile),
        grid_spec=pltpu.PrefetchScalarGridSpec(
            num_scalar_prefetch=1,
            grid=(count,),
            in_specs=[
                whole(h.shape), whole(c.shape),
                pick((width, ff)), pick((width, ff)), pick((ff, width)),
            ],
            out_specs=[
                whole(c.shape), whole(h.shape),
                pl.BlockSpec((1, 6, ff, ff), lambda e, s: (e, 0, 0, 0)),
            ],
            scratch_shapes=[
                pltpu.VMEM((rows, width), F32), pltpu.VMEM((rows, width), F32),
                pltpu.VMEM((rows, 128), F32),
                pltpu.VMEM((rows, ff), BF), pltpu.VMEM((rows, ff), BF), pltpu.VMEM((rows, ff), BF),
            ],
        ),
        out_shape=[
            jax.ShapeDtypeStruct(c.shape, BF),
            jax.ShapeDtypeStruct(h.shape, BF),
            jax.ShapeDtypeStruct((count, 6, ff, ff), BF),
        ],
        compiler_params=params(),
        name="experts",
    )(base, h, c, wg, wu, wd)


def moe_kernel(*refs, names, topk, count):
    r = types.SimpleNamespace(**dict(zip(names, refs)))
    z, s, f = lax.axis_index("dp"), lax.axis_index("seq"), lax.axis_index("fsdp")
    core, x = s % 2, s // 2
    flip = 1 - 2 * core
    seqs = (s, s + flip, (s + 2) % 4, (s + 2) % 4 + flip)
    peers = [(z, q, f) for q in seqs]
    peer_x, peer_y = peers[2], (z, s, 1 - f)
    att, att_in, tout, hx, cots = r.att, r.att_in, r.tout, r.hx, r.cots
    rows, width = tout.shape
    n = rows // 2
    ext = hx.shape[1]
    ff = r.wgs.shape[2]
    owned = r.wg.shape[0]

    barrier = pltpu.get_barrier_semaphore()
    for dev in (*peers[1:], peer_y):
        pl.semaphore_signal(barrier, inc=1, device_id=dev, device_id_type=MESH)

    def remote(src, dst, sems, b, dev):
        return pltpu.make_async_remote_copy(
            src_ref=src, dst_ref=dst, send_sem=sems.at[0, b], recv_sem=sems.at[1, b],
            device_id=dev, device_id_type=MESH,
        )

    def block(t):
        return pl.ds(pl.multiple_of(t * rows, rows), rows)

    load_cots = [
        pltpu.make_async_copy(v, cots.at[block(i)], r.s_cot.at[i])
        for i, v in enumerate((r.cot, r.cot_y, r.cot_x))
    ]
    for copy in load_cots:
        copy.start()

    def load_weights(e, act):
        for i, (src, dst) in enumerate(((r.wg, r.wgs), (r.wu, r.wus), (r.wd, r.wds))):
            act(pltpu.make_async_copy(src.at[x * count + e], dst.at[e], r.s_w.at[i, e]))

    @pl.loop(0, count)
    def _(e):
        load_weights(e, lambda copy: copy.start())

    pl.semaphore_wait(barrier, 4)
    def head(m, i):
        at = pl.ds(pl.multiple_of(i * n, n), n)
        return remote(att.at[m, at], att_in.at[m, at], r.s_att, 2 * m + i, peers[m])

    heads = [head(m, i) for i in range(2) for m in (3, 2, 1)]
    for copy in heads:
        copy.start()
    diag = [
        remote(r.cot_x.at[pl.ds(0, n)], cots.at[pl.ds(3 * rows, n)], r.s_diag, 0, peer_y),
        remote(r.cot_y.at[pl.ds(n, n)], cots.at[pl.ds(3 * rows + n, n)], r.s_diag, 1, peer_x),
    ]
    wo_rows = pl.ds(pl.multiple_of(core * (ff // 2), ff // 2), ff // 2)
    wo_there = r.wo_there
    wo_copy = pltpu.make_async_copy(r.wo_near, wo_there.at[wo_rows], r.s_wo.at[0])
    wo_share = remote(r.wo_near, wo_there.at[wo_rows], r.s_diag, 2, peers[1])
    wo_copy.start()
    wo_share.start()
    for copy in diag:
        copy.start()

    small = r.small
    table = r.table
    table[...] = jnp.zeros_like(table)
    table[: small.shape[0], :] = small[...]
    n_exp = r.gates.shape[1]
    gain = small[17:18, :].astype(F32)
    own_cols = pl.ds(pl.multiple_of(f * ff, ff), ff)
    away_cols = pl.ds(pl.multiple_of((1 - f) * ff, ff), ff)

    def head_cols(m):
        return pl.ds(pl.multiple_of(seqs[m] * 256, 256), 256)

    wo_copy.wait()
    wo_share.wait_recv()
    def share(i, j, dev):
        at = pl.multiple_of(i * n, n)
        return remote(
            hx.at[pl.ds(at, n)], hx.at[pl.ds((j + 1) * rows + at, n)], r.s_h, 2 * j + i, dev
        )

    @pl.loop(0, 2)
    def _(i):
        at = pl.ds(pl.multiple_of(i * n, n), n)
        tout[at, head_cols(0)] = att[0, at, :]
        for m in range(1, 4):
            head(m, i).wait_recv()
            tout[at, head_cols(m)] = att_in[m, at, :]
        middle = (
            r.tok[at, :].astype(F32)
            + mm(tout[at, own_cols], r.wo_own[...])
            + mm(tout[at, away_cols], wo_there[...])
        )
        r.middle[at, :] = middle
        normed, _ = rms_parts(middle)
        hidden = (normed * gain).astype(BF)
        logits = mm_nt(hidden, table[...])
        lane = lax.broadcasted_iota(jnp.int32, logits.shape, 1)
        chosen = lane == r.routes[at, 0:1]
        for k in range(1, topk):
            chosen = chosen | (lane == r.routes[at, k : k + 1])
        top = jnp.max(jnp.where(chosen, logits, NEG), axis=-1, keepdims=True)
        raised = jnp.where(chosen, jnp.exp(logits - top), 0.0)
        gates = raised / jnp.sum(raised, axis=-1, keepdims=True)
        r.gates[at, :] = gates
        hx[at, :width] = hidden
        hx[at, width:] = gates.astype(BF)
        share(i, 0, peer_y).start()
        share(i, 1, peer_x).start()

    shares = [share(i, j, dev) for i in range(2) for j, dev in ((0, peer_y), (1, peer_x))]
    second = remote(
        hx.at[pl.ds(rows + n, n)], hx.at[pl.ds(3 * rows + n, n)], r.s_h, 4, peer_x
    )
    first = remote(hx.at[pl.ds(2 * rows, n)], hx.at[pl.ds(3 * rows, n)], r.s_h, 5, peer_y)

    dhs, moe, dh, dgates = r.dhs, r.moe_acc, r.dh_acc, r.dg_acc
    few = 3 * rows // 4
    half_rows = [(0, n), (n, n)]
    back_y = [
        remote(dhs.at[pl.ds(rows + a, k)], r.rdh.at[0, pl.ds(a, k)], r.s_d, i, peer_y)
        for i, (a, k) in enumerate(half_rows)
    ]
    back_x = remote(dhs.at[block(2)], r.rdh.at[1], r.s_d, 2, peer_x)

    def two_hops(a, k, sem, first_dev, second_dev):
        via = r.via.at[pl.ds(a, k)]
        return (
            remote(dhs.at[pl.ds(3 * rows + a, k)], via, r.s_d, sem, first_dev),
            remote(via, r.rdd.at[pl.ds(a, k)], r.s_d, sem + 1, second_dev),
        )

    hop_y0, end_x0 = two_hops(0, n, 3, peer_y, peer_x)
    hop_y1, end_x1 = two_hops(n, few - n, 5, peer_y, peer_x)
    hop_x, end_y = two_hops(few, rows - few, 7, peer_x, peer_y)
    moe_x = remote(r.moe2, r.got2, r.s_d, 9, peer_x)

    moes = (r.moe0, r.moe1, r.moe2, r.moe3)

    def moe_out(t):
        return pltpu.make_async_copy(r.mstage.at[(0, 1, 1, 0)[t]], moes[t], r.s_m.at[t])

    @pl.loop(0, 4 * count)
    def _(k):
        turn, e = k // count, k % count
        t = 2 * turn - turn // 2 - 4 * (turn // 3)

        @pl.when(k < count)
        def _():
            load_weights(e, lambda copy: copy.wait())

        @pl.when(k == 0)
        def _():
            load_cots[0].wait()

        @pl.when(k == count)
        def _():
            for copy in shares:
                copy.wait_recv()
            second.start()
            first.start()
            load_cots[1].wait()
            load_cots[2].wait()

        @pl.when(k == 2 * count)
        def _():
            first.wait_recv()
            second.wait_recv()
            for copy in diag:
                copy.wait_recv()

        at = block(t)
        h, c = hx[at, :width], cots[at, :]
        wg, wu, wd = r.wgs[e], r.wus[e], r.wds[e]
        expert = f * owned + x * count + e
        mine = lax.broadcasted_iota(jnp.int32, (rows, ext - width), 1) == expert
        gate = jnp.sum(jnp.where(mine, hx[at, width:].astype(F32), 0.0), axis=1, keepdims=True)
        g, u, zz = mm(h, wg), mm(h, wu), mm_nt(c, wd)
        sig = jax.nn.sigmoid(g)
        silu = g * sig
        act = silu * u
        dgate_col = jnp.where(mine, jnp.sum(act * zz, axis=1, keepdims=True), 0.0)
        act = (act * gate).astype(BF)
        dact = zz * gate
        dgate = (dact * u * sig * (1.0 + g * (1.0 - sig))).astype(BF)
        dup = (dact * silu).astype(BF)
        r.s_act[e, at, :] = act
        r.s_gate[e, at, :] = dgate
        r.s_up[e, at, :] = dup

        @pl.when(e == 0)
        def _():
            moe[...] = mm(act, wd)
            dh[...] = mm_nt(dgate, wg) + mm_nt(dup, wu)
            dgates[...] = dgate_col

        @pl.when(e > 0)
        def _():
            moe[...] += mm(act, wd)
            dh[...] += mm_nt(dgate, wg) + mm_nt(dup, wu)
            dgates[...] += dgate_col

        @pl.when(e == count - 1)
        def _():
            for i, k in enumerate((0, 2, 3, 1)):
                @pl.when(t == k)
                def _():
                    if i >= 2:
                        moe_out((0, 2)[i - 2]).wait()
                    r.mstage[i % 2] = moe[...].astype(BF)
                    moe_out(k).start()

            dhs[at, :width] = dh[...].astype(BF)
            dhs[at, width:] = dgates[...].astype(BF)

            @pl.when(t == 1)
            def _():
                for copy in back_y:
                    copy.start()

            @pl.when(t == 2)
            def _():
                back_x.start()

            @pl.when(t == 3)
            def _():
                hop_y0.start()
                hop_x.start()
                hop_y1.start()

    stage = r.stage

    def grad_copy(b, slot):
        return pltpu.make_async_copy(stage.at[slot], r.grads.at[b], r.s_g.at[slot])

    dattn, dto, dsend = r.dattn, r.dto, r.dsend
    returns = [
        [
            remote(dsend.at[m, pl.ds(i * n, n)], r.do.at[m, pl.ds(i * n, n)], r.s_back, 2 * m + i, peers[m])
            for m in (3, 2, 1)
        ]
        for i in range(2)
    ]

    def middle_back(i):
        at = pl.ds(i * n, n)
        total = (
            dhs[at, :].astype(F32) + r.rdh[0, at, :].astype(F32)
            + r.rdh[1, at, :].astype(F32) + r.rdd[at, :].astype(F32)
        )
        dg, gates = total[:, width:], r.gates[at, :]
        dl = (gates * (dg - jnp.sum(gates * dg, axis=-1, keepdims=True))).astype(BF)
        rg = mm_tn(dl, hx[at, :width])[:32]
        d_hidden = total[:, :width] + mm(dl, table[...])
        normed, factor = rms_parts(r.middle[at, :])
        gn = jnp.sum(d_hidden * normed, axis=0, keepdims=True)
        d_n = d_hidden * gain
        d_mid = cots[at, :].astype(F32) + factor * (
            d_n - normed * jnp.mean(d_n * normed, axis=-1, keepdims=True)
        )
        r.dmid[at, :] = d_mid
        low = d_mid.astype(BF)
        dattn[at, :] = low
        dto[at, own_cols] = mm_nt(low, r.wo_own[...]).astype(BF)
        dto[at, away_cols] = mm_nt(low, wo_there[...]).astype(BF)
        for m in range(1, 4):
            dsend[m, at, :] = dto[at, head_cols(m)]
        for copy in returns[i]:
            copy.start()
        r.do[0, at, :] = dto[at, head_cols(0)]
        if i == 0:
            r.rg[...] = rg
            r.gn[:1, :] = gn
            return
        rg, gn = r.rg[...] + rg, r.gn[:1, :] + gn
        row = lax.broadcasted_iota(jnp.int32, rg.shape, 0)
        top = jnp.where(row == 17, gn, jnp.where(row < 16, rg, 0.0))
        r.tiny[0] = top[:, : width // 2]
        r.tiny[1] = top[:, width // 2 :]
        for k in range(4):
            cols = slice(k * 256, (k + 1) * 256)
            r.gout[cols, :] = mm_tn(tout[:, cols], dattn[...]).astype(BF)

    def forward0():
        hop_y0.wait_recv()
        end_x0.start()

    def forward1():
        hop_y1.wait_recv()
        end_x1.start()
        hop_x.wait_recv()
        end_y.start()
        moe_x.start()

    def back0():
        for copy in (back_y[0], back_x, end_x0):
            copy.wait_recv()
        middle_back(0)

    def back1():
        for copy in (back_y[1], end_x1, end_y):
            copy.wait_recv()
        middle_back(1)

    @pl.loop(0, 3 * count)
    def _(k):
        e, j = k // 3, k % 3
        pl.when(k == 0)(forward0)
        pl.when(k == 2)(forward1)
        pl.when(k == 3 * count - 6)(back0)
        pl.when(k == 3 * count - 1)(back1)

        @pl.when(k > 0)
        def _():
            grad_copy(0, 0).wait()
            grad_copy(0, 1).wait()

        for which, left, right in ((0, hx, r.s_gate), (1, hx, r.s_up), (2, cots, r.s_act)):
            @pl.when(j == which)
            def _():
                for i in range(2):
                    at = slice(i * ff, (i + 1) * ff)
                    if which < 2:
                        v = mm_tn(left[:, at], right[e])
                    else:
                        v = mm_tn(right[e], left[:, at])
                    stage[i] = v.astype(BF)

        for i in range(2):
            grad_copy(6 * e + 2 * j + i, i).start()

    grad_copy(0, 0).wait()
    grad_copy(0, 1).wait()
    moe_out(3).wait()
    moe_out(1).wait()
    for copy in (*returns[0], *returns[1], moe_x):
        copy.wait()
    for copy in (*heads, *diag, wo_share, *shares, first, second, *back_y, back_x, hop_x, hop_y0, hop_y1, end_y, end_x0, end_x1):
        copy.wait_send()


def moe_layer(att, tok, wo_own, wo_near, small, routes, cot, cot_y, cot_x, wg, wu, wd):
    rows, width = tok.shape
    owned, _, ff = wg.shape
    count = owned // 2
    ext = width + 128
    hbm = pl.BlockSpec(memory_space=pl.ANY)
    vmem = pl.BlockSpec(memory_space=pltpu.VMEM)
    dma = pltpu.SemaphoreType.DMA
    args = dict(
        att=(att.reshape(4, rows, 256), vmem), tok=(tok, vmem), wo_own=(wo_own, vmem),
        wo_near=(wo_near, hbm), small=(small, vmem), routes=(routes, vmem),
        cot=(cot, hbm), cot_y=(cot_y, hbm), cot_x=(cot_x, hbm),
        wg=(wg, hbm), wu=(wu, hbm), wd=(wd, hbm),
    )
    shape = jax.ShapeDtypeStruct
    outs = dict(
        middle=(shape((rows, width), F32), vmem),
        moe0=(shape((rows, width), BF), hbm), moe1=(shape((rows, width), BF), hbm),
        moe2=(shape((rows, width), BF), hbm), moe3=(shape((rows, width), BF), hbm),
        got2=(shape((rows, width), BF), hbm),
        dmid=(shape((rows, width), F32), vmem),
        do=(shape((4, rows, 256), BF), vmem),
        grads=(shape((6 * count, ff, ff), BF), hbm),
        gout=(shape((width, width), BF), vmem),
        tiny=(shape((2, 32, width // 2), F32), vmem),
    )
    stash = pltpu.VMEM((count, 4 * rows, ff), BF)
    scratch = dict(
        att_in=pltpu.VMEM((4, rows, 256), BF), tout=pltpu.VMEM((rows, width), BF),
        hx=pltpu.VMEM((4 * rows, ext), BF), cots=pltpu.VMEM((4 * rows, width), BF),
        wo_there=pltpu.VMEM((ff, width), BF), rg=pltpu.VMEM((32, width), F32),
        gn=pltpu.VMEM((8, width), F32), table=pltpu.VMEM((128, width), BF), gates=pltpu.VMEM((rows, 128), F32),
        wgs=pltpu.VMEM((count, width, ff), BF), wus=pltpu.VMEM((count, width, ff), BF),
        wds=pltpu.VMEM((count, ff, width), BF),
        s_act=stash, s_gate=stash, s_up=stash,
        moe_acc=pltpu.VMEM((rows, width), F32), dh_acc=pltpu.VMEM((rows, width), F32),
        dg_acc=pltpu.VMEM((rows, 128), F32), mstage=pltpu.VMEM((2, rows, width), BF),
        dhs=pltpu.VMEM((4 * rows, ext), BF), rdh=pltpu.VMEM((2, rows, ext), BF),
        via=pltpu.VMEM((rows, ext), BF), rdd=pltpu.VMEM((rows, ext), BF),
        dattn=pltpu.VMEM((rows, width), BF), dto=pltpu.VMEM((rows, width), BF),
        dsend=pltpu.VMEM((4, rows, 256), BF), stage=pltpu.VMEM((2, ff, ff), BF),
        s_att=dma((2, 8)), s_diag=dma((2, 3)), s_h=dma((2, 6)), s_d=dma((2, 10)), s_back=dma((2, 8)),
        s_cot=dma((3,)), s_wo=dma((1,)), s_w=dma((3, count)), s_m=dma((4,)), s_g=dma((2,)),
    )
    names = tuple(args) + tuple(outs) + tuple(scratch)
    got = pl.pallas_call(
        functools.partial(moe_kernel, names=names, topk=routes.shape[1], count=count),
        in_specs=[v[1] for v in args.values()],
        out_specs=[v[1] for v in outs.values()],
        out_shape=[v[0] for v in outs.values()],
        scratch_shapes=list(scratch.values()),
        compiler_params=pltpu.CompilerParams(
            vmem_limit_bytes=67043328, collective_id=3, has_side_effects=True
        ),
        name="moe_layer",
    )(*[v[0] for v in args.values()])
    return types.SimpleNamespace(**dict(zip(outs, got)))


def flip_core(x):
    return lax.ppermute(x, "seq", [(0, 1), (1, 0), (2, 3), (3, 2)])


def flip_x(x):
    return lax.ppermute(x, "seq", [(0, 2), (2, 0), (1, 3), (3, 1)])


def flip_both(x):
    return lax.ppermute(x, "seq", [(0, 3), (3, 0), (1, 2), (2, 1)])


def flip_y(x):
    return lax.ppermute(x, "fsdp", [(0, 1), (1, 0)])


def gather_seq(x):
    own = jnp.stack([x, flip_core(x)])
    far = flip_x(x)
    return jnp.concatenate([own, far[None], flip_core(far)[None]])


def swap_seq(blocks):
    return [blocks[0], flip_core(blocks[1]), flip_x(blocks[2]), flip_both(blocks[3])]


def gather_fsdp(x, axis=0):
    if lax.axis_size("fsdp") == 2:
        return jnp.concatenate([x, lax.ppermute(x, "fsdp", [(0, 1), (1, 0)])], axis=axis)
    return lax.all_gather(x, "fsdp", axis=axis, tiled=True)


def scatter_fsdp(x):
    if lax.axis_size("fsdp") == 2:
        n = x.shape[0] // 2
        other = lax.ppermute(x[n:], "fsdp", [(0, 1), (1, 0)])
        return x[:n].astype(F32) + other.astype(F32)
    return lax.psum_scatter(x, "fsdp", scatter_dimension=0, tiled=True).astype(F32)


def rope_back(w, cos, sin, low_half):
    half = HEAD_WIDTH // 2
    y = w * sin
    return w * cos + jnp.where(low_half, pltpu.roll(y, 128 - half, 1), -pltpu.roll(y, half, 1))


def reduce_kernel(*refs, names, slots, shards, fused):
    r = types.SimpleNamespace(**dict(zip(names, refs)))
    gm, mine, rc, pre, suf = r.gm, r.mine, r.rc, r.pre, r.suf
    gate, up, down, out, qkv = r.gate, r.up, r.down, r.out, r.qkv
    z, s, f = lax.axis_index("dp"), lax.axis_index("seq"), lax.axis_index("fsdp")
    core, x = s % 2, s // 2
    peer_core = (z, s + 1 - 2 * core, f)
    peer_x = (z, (s + 2) % 4, f)
    peer_y = (z, s, 1 - f)
    right, left = (z + 1, s, f), (z - 1, s, f)
    nb = gm.shape[0]
    n_moe, n_out, items = 2 * nb, 2 * nb + 2, 2 * nb + 6
    count = nb // 6
    piece = mine.shape[1]
    half, block = 2 * piece, 4 * piece
    last = slots - 1

    def other_z(k):
        return ((z + k) % slots, s, f)

    barrier = pltpu.get_barrier_semaphore()
    peer_xy = (z, (s + 2) % 4, 1 - f)
    peers = [other_z(k) for k in range(1, slots)] + [peer_core, peer_x] + [peer_y, peer_xy] * fused
    for dev in peers:
        pl.semaphore_signal(barrier, inc=1, device_id=dev, device_id_type=MESH)

    def remote(src, dst, sems, b, dev):
        return pltpu.make_async_remote_copy(
            src_ref=src, dst_ref=dst, send_sem=sems.at[0, b], recv_sem=sems.at[1, b],
            device_id=dev, device_id_type=MESH,
        )

    def load(src, b):
        return pltpu.make_async_copy(src, mine.at[b], r.s_mine.at[b])

    @pl.loop(0, n_moe)
    def _(b):
        load(gm.at[b // 2, core, b % 2], b).start()

    if fused:
        loads = [
            pltpu.make_async_copy(a, b, r.s_in.at[i])
            for i, (a, b) in enumerate((
                (r.q, r.q_in), (r.kv, r.kv_in), (r.do, r.do_in), (r.o, r.o_in), (r.lse, r.lse_in),
                (r.wc, r.wc_in),
                (r.cos, r.cos_in), (r.sin, r.sin_in), (r.h, r.h_in), (r.tok, r.tok_in),
                (r.gout.at[pl.ds(pl.multiple_of(f * block, block), block)], r.gout_in),
                (r.dmid, r.dmid_in),
            ))
        ]
        for copy in loads:
            copy.start()
    else:
        for i in range(2):
            load(r.eo.at[core, i], n_moe + i).start()
        for i in range(4):
            load(r.cols.at[i], n_out + i).start()
    pl.semaphore_wait(barrier, len(peers))

    @pl.loop(0, n_moe)
    def _(b):
        remote(gm.at[b // 2, 1 - core, b % 2], rc.at[b], r.s_rc, b, peer_core).start()

    if not fused:
        for i in range(2):
            remote(r.eo.at[1 - core, i], rc.at[n_moe + i], r.s_rc, n_moe + i, peer_core).start()

    def place(b, which, part, act):
        first_row = part * half + b % 2 * piece
        rows = pl.ds(pl.multiple_of(first_row, piece), piece)
        e, j = which * count + b // 12, b // 2 % 6
        jj = j % 2
        wide = pl.ds(pl.multiple_of(jj * block, block), block)
        at = pl.ds(pl.multiple_of(jj * block + first_row, piece), piece)
        for m, o in enumerate((gate, up)):
            @pl.when((b < n_moe) & (j // 2 == m))
            def _():
                act(o.at[e, at, :])

        @pl.when((b < n_moe) & (j // 2 == 2))
        def _():
            act(down.at[e, rows, wide])

        @pl.when((b >= n_moe) & (b < n_out))
        def _():
            act(out.at[rows, pl.ds(pl.multiple_of(which * block, block), block)])

        @pl.when(b >= n_out)
        def _():
            at = pl.ds(pl.multiple_of((b - n_out) * piece, piece), piece)
            wide = 2 * block
            for first, n, to in ((0, 256, 0), (wide, 128, 256), (wide + wide // 2, 128, 384)):
                col = pl.multiple_of(first + (2 * which + part) * n, 128)
                act(qkv.at[at, pl.ds(col, n)], pl.ds(to, n))

    def add(a, b):
        return a.astype(F32) + b.astype(F32)

    def hop(buf, sems, b, dev):
        return remote(buf.at[b], buf.at[b], sems, b, dev)

    def spread(b):
        def act(dst, cut=None):
            src = rc.at[b] if cut is None else rc.at[b, :, cut]
            remote(src, dst, r.s_oth, 0, peer_core).start()
            pltpu.make_async_copy(src, dst, r.s_out.at[0]).start()
            remote(src, dst, r.s_far, b, peer_x).start()

        place(b, x, core, act)

    lag = 2
    ahead = 4

    def begin(b):
        @pl.when(b < (n_moe if fused else items))
        def _():
            load(gm.at[0, 0, 0], b).wait()

        @pl.when(b < n_out)
        def _():
            remote(gm.at[0, 0, 0], rc.at[b], r.s_rc, b, peer_core).wait_recv()
            mine[b] = add(mine[b], rc[b]).astype(BF)

        @pl.when(z == 0)
        def _():
            remote(mine.at[b], pre.at[b], r.s_pre, b, right).start()

        @pl.when(z == last)
        def _():
            remote(mine.at[b], suf.at[b], r.s_suf, b, left).start()

    def prefix(b):
        hop(pre, r.s_pre, b, peer_x).wait_recv()
        got = pre[b].astype(F32)
        own = got + mine[b].astype(F32)

        @pl.when(z == last)
        def _():
            rc[b] = own.astype(BF)

        @pl.when(z < last)
        def _():
            @pl.when(2 * z >= slots)
            def _():
                rc[b] = (got + suf[b].astype(F32)).astype(BF)

            pre[b] = own.astype(BF)
            hop(pre, r.s_pre, b, right).start()

        @pl.when(2 * z >= slots)
        def _():
            spread(b)

    def suffix(b):
        hop(suf, r.s_suf, b, peer_x).wait_recv()
        got = suf[b].astype(F32)
        own = got + mine[b].astype(F32)

        @pl.when(z == 0)
        def _():
            rc[b] = own.astype(BF)

        @pl.when(z > 0)
        def _():
            @pl.when(2 * z < slots)
            def _():
                rc[b] = (got + pre[b].astype(F32)).astype(BF)

            suf[b] = own.astype(BF)
            hop(suf, r.s_suf, b, left).start()

        @pl.when(2 * z < slots)
        def _():
            spread(b)

    def forward(b):
        remote(rc.at[b], rc.at[b], r.s_far, b, peer_x).wait_recv()

        def act(dst, cut=None):
            remote(dst, dst, r.s_faro, 0, peer_core).start()

        place(b, 1 - x, core, act)

    def within(b, cond=True):
        return (b >= 0) & (b < items) & cond

    tsum, trecv, s_tiny = r.tsum, r.trecv, r.s_tiny

    def tiny_swap(k, dev):
        return remote(tsum.at[k], trecv.at[k], s_tiny, k, dev)

    def tiny_add(k):
        tiny_swap(k, peer_x).wait_recv()
        tsum[k + 1] = add(tsum[k], trecv[k]).astype(BF)

    def tiny_x():
        tiny_swap(0, peer_x).start()

    def tiny_core():
        tiny_add(0)
        tiny_swap(1, peer_core).start()

    def tiny_spread():
        tiny_add(1)
        for k in range(1, slots):
            remote(tsum.at[2], trecv.at[1 + k], s_tiny, 1 + k, other_z(k)).start()

    def tiny_end():
        total = tsum[2].astype(F32)
        for k in range(1, slots):
            remote(tsum.at[2], trecv.at[1 + k], s_tiny, 1 + k, other_z(k)).wait_recv()
            total = total + trecv[1 + k].astype(F32)
        r.tiny_out[...] = total

    steps = {}
    if fused:
        s_fg = r.s_fg
        keys = r.dkvs.shape[0]
        tile = r.dhx.shape[0]
        dh = [r.h_in.at[pl.ds(t * tile, tile)] for t in range(4)]
        owner = pl.multiple_of(f * block, block)
        away = pl.multiple_of((1 - f) * block, block)
        mine_rows, away_rows = pl.ds(owner, block), pl.ds(away, block)
        near_cols = pl.ds(pl.multiple_of(x * block, block), block)
        far_cols = pl.ds(pl.multiple_of((1 - x) * block, block), block)

        send_dkv = remote(r.kv_in.at[pl.ds(keys, keys)], r.rdkv, s_fg, 0, peer_y)
        send_out = [
            remote(r.gout.at[away_rows, cols], r.rout.at[i], s_fg, (1, 8)[i], peer_y)
            for i, cols in enumerate((far_cols, near_cols))
        ]
        send_dh3 = remote(dh[3], r.rdh.at[1], s_fg, 2, peer_core)
        send_dh1 = remote(dh[1], r.rdh.at[0], s_fg, 3, peer_core)
        send_dhx = remote(r.dhx, r.rdx, s_fg, 4, peer_x)
        send_cols = remote(r.cbuf.at[away_rows], r.rcol, s_fg, 5, peer_y)
        send_outx = remote(r.osend, r.rox, s_fg, 6, peer_x)
        send_tiny = remote(r.tbuf.at[1 - f], r.rtiny, s_fg, 7, peer_y)
        eo_core = [
            remote(r.eo.at[1 - core, i], rc.at[n_moe + i], r.s_rc, n_moe + i, peer_core)
            for i in range(2)
        ]
        moe_back = [
            remote(r.moe3, r.got3, r.s_moe, 1, peer_xy), remote(r.moe1, r.got1, r.s_moe, 0, peer_y),
        ]
        moe_back[0].start()
        for copy in send_out:
            copy.start()
        moe_back[1].start()

        span, kb = tile // 2, 2 * tile
        parts = 2 * keys // kb
        n_steps = 8 * parts
        scale = HEAD_WIDTH**-0.5

        def attention(n):
            j, m = n // parts, n % parts
            at = pl.ds(pl.multiple_of(j * span, span), span)

            @pl.when(n == 0)
            def _():
                r.dk[...] = jnp.zeros_like(r.dk)
                r.dv[...] = jnp.zeros_like(r.dv)
                inside = lax.broadcasted_iota(jnp.int32, (span, 1), 0)
                for k in range(2 * keys // span):
                    r.kpos[k * span : (k + 1) * span, :] = span_at(r.order, k) * span + inside
                across = lax.broadcasted_iota(jnp.int32, (8, 4 * span), 1) % span
                for k in range(8):
                    r.last[k] = jnp.minimum(span_at(r.order, k) * span + across, r.limit[0] - 1)

            @pl.when(m == 0)
            def _():
                r.qs[...] = stack_heads(r.q_in[at, :128], r.q_in[at, 128:])
                do = stack_heads(r.do_in[at, :128], r.do_in[at, 128:])
                r.dos[...] = do
                inner = do.astype(F32) * stack_heads(r.o_in[at, :128], r.o_in[at, 128:], F32)
                delta = jnp.sum(jnp.transpose(inner), axis=0, keepdims=True)
                r.delta[...] = jnp.broadcast_to(delta, r.delta.shape)

            key = pl.ds(pl.multiple_of(m * kb, kb), kb)
            k, v = r.kv_in[key, :128], r.kv_in[key, 128:]
            q, do = r.qs[...], r.dos[...]
            p = jnp.exp2(mm_nt(k, q) * (scale * LOG2E) - r.lse_in[j, :1])
            p = jnp.where(r.kpos[key, :] <= r.last[j, :1], p, 0.0)
            ds = (p * (mm_nt(v, do) - r.delta[:1])).astype(BF)
            r.dk[key, :] += mm(ds, q)
            r.dv[key, :] += mm(p.astype(BF), do)
            dq = mm_tn(ds, k)

            @pl.when(m == 0)
            def _():
                r.dqa[...] = dq

            @pl.when(m > 0)
            def _():
                r.dqa[...] += dq

            @pl.when(m == parts - 1)
            def _():
                a, b = unstack_heads(r.dqa[...] * scale)
                r.dq_in[at, :128] = a.astype(BF)
                r.dq_in[at, 128:] = b.astype(BF)

        def send_keys():
            r.kv_in[:, :128] = (r.dk[...] * scale).astype(BF)
            r.kv_in[:, 128:] = r.dv[...].astype(BF)
            send_dkv.start()

        def sum_dkv():
            send_dkv.wait_recv()
            r.dkvs[...] = add(r.kv_in[:keys], r.rdkv[...]).astype(BF)

        def back_tile(t, first=False):
            at = pl.ds(t * tile, tile)
            cos, sin = r.cos_in[at, :], r.sin_in[at, :]
            low_half = lax.broadcasted_iota(jnp.int32, cos.shape, 1) % HEAD_WIDTH < HEAD_WIDTH // 2
            parts = []
            for k in range(3):
                w = r.dq_in[at, k * 128 : (k + 1) * 128] if k < 2 else r.dkvs[at, :128]
                parts.append(rope_back(w.astype(F32), cos, sin, low_half).astype(BF))
            parts.append(r.dkvs[at, 128:])
            dproj = jnp.concatenate(parts, axis=1)
            grad = mm_tn(r.h_in[at, :], dproj)
            back = mm_nt(dproj, r.wc_in[...])
            dh[t][...] = back.astype(BF)
            normed, _ = rms_parts(r.tok_in[at, :].astype(F32))
            gain = jnp.sum((back * normed).reshape(-1, 8, back.shape[1]), axis=0)
            if first:
                r.acc[...] = grad
                r.gn[...] = gain
            else:
                r.acc[...] += grad
                r.gn[...] += gain

        def tile3():
            back_tile(3, True)
            send_dh3.start()

        def tile1():
            back_tile(1)
            send_dh1.start()

        def tile2():
            back_tile(2)
            send_dh3.wait_recv()
            r.dhx[...] = add(dh[2][...], r.rdh[1]).astype(BF)
            send_dhx.start()

        def tile0():
            back_tile(0)
            r.cbuf[...] = r.acc[...].astype(BF)
            send_cols.start()
            total = jnp.sum(r.gn[...], axis=0, keepdims=True)
            wide = tsum.shape[2]
            row = lax.broadcasted_iota(jnp.int32, (tsum.shape[1], wide), 0) == 16
            for k in range(2):
                part = total[:, k * wide : (k + 1) * wide]
                r.tbuf[k] = jnp.where(row, part, r.tiny[k]).astype(BF)
            send_tiny.start()

        def sum_out():
            send_out[0].wait_recv()
            r.osend[...] = add(r.gout_in[:, far_cols], r.rout[0]).astype(BF)
            send_outx.start()

        def tiny_y():
            send_tiny.wait_recv()
            tsum[0] = add(r.tbuf[f], r.rtiny[...]).astype(BF)
            tiny_x()

        def sum_cols():
            send_cols.wait_recv()
            v = add(r.cbuf[mine_rows, :], r.rcol[...]).astype(BF)
            for i in range(4):
                mine[n_out + i] = v[i * piece : (i + 1) * piece]

        def sum_outx():
            send_out[1].wait_recv()
            send_outx.wait_recv()
            v = add(r.gout_in[:, near_cols], r.rout[1]) + r.rox[...].astype(F32)
            v = v.astype(BF)
            for i in range(4):
                r.eo[i // 2, i % 2] = v[i * piece : (i + 1) * piece]
            for i in range(2):
                eo_core[i].start()
                mine[n_moe + i] = r.eo[core, i]

        def inputs_back():
            send_dh1.wait_recv()
            send_dhx.wait_recv()
            up_grad = add(dh[0][...], r.rdh[0]) + r.rdx[...].astype(F32)
            normed, factor = rms_parts(r.tok_in[:tile].astype(F32))
            d_n = up_grad * r.small[16:17, :].astype(F32)
            r.dtok[...] = r.dmid_in[...] + factor * (
                d_n - normed * jnp.mean(d_n * normed, axis=-1, keepdims=True)
            )

        def arrive():
            for copy in loads:
                copy.wait()

        first_step = 1
        done = first_step + n_steps
        order = [
            send_keys, None, None, sum_outx, None, sum_dkv, tile3, tile1, tile2, tile0, None, None,
            tiny_y, sum_cols, None, inputs_back, tiny_core, None, tiny_spread,
        ]
        steps = {done + i: fn for i, fn in enumerate(order) if fn is not None}
        steps.update({0: arrive, OUT_STEP: sum_out})
    else:
        tsum[0] = r.tiny[...].astype(BF)
        tiny_x()
        steps = {1: tiny_core, 2: tiny_spread}

    @pl.loop(0, items + ahead + (last + 1) * lag)
    def _(i):
        for fn, b, cond in (
            (begin, i, True),
            (prefix, i - ahead - lag * z, z > 0),
            (suffix, i - ahead - lag * (last - z), z < last),
            (forward, i - ahead - lag * (last + 1), True),
        ):
            @pl.when(within(b, cond))
            def _():
                fn(b)

        if fused:
            @pl.when((i >= first_step) & (i < done))
            def _():
                attention(i - first_step)

        for k, fn in steps.items():
            pl.when(i == k)(fn)

    tiny_end()

    @pl.loop(0, items)
    def _(b):
        one = rc.at[b]

        @pl.when(b < n_out)
        def _():
            remote(one, one, r.s_rc, b, peer_core).wait_send()

        @pl.when(z < last)
        def _():
            hop(pre, r.s_pre, b, peer_x).wait_send()

        @pl.when(z > 0)
        def _():
            hop(suf, r.s_suf, b, peer_x).wait_send()

        remote(one, one, r.s_far, b, peer_x).wait_send()

    remote(rc, rc, r.s_oth, 0, peer_core).wait()
    remote(rc, rc, r.s_faro, 0, peer_core).wait()
    pltpu.make_async_copy(rc, rc, r.s_out.at[0]).wait()
    tiny_swap(0, peer_x).wait_send()
    tiny_swap(1, peer_core).wait_send()
    for k in range(1, slots):
        remote(tsum.at[2], trecv.at[1 + k], s_tiny, 1 + k, other_z(k)).wait_send()
    if fused:
        for copy in (send_dkv, *send_out, send_dh3, send_dh1, send_dhx, send_cols, send_outx, send_tiny):
            copy.wait_send()
        for copy in moe_back:
            copy.wait()


def reduce_grads(gm, tiny, slots, shards, eo=None, cols=None, fused=None, small=None, tables=None, moes=None):
    count, _, ff, _ = gm.shape
    width = 2 * ff
    nb = 6 * count
    piece = ff // 4
    items = 2 * nb + 6
    hbm = pl.BlockSpec(memory_space=pl.ANY)
    vmem = pl.BlockSpec(memory_space=pltpu.VMEM)
    dma = pltpu.SemaphoreType.DMA
    args = dict(gm=(gm.reshape(nb, 2, 2, piece, ff), hbm), tiny=(tiny, vmem))
    outs = dict(
        gate=(jax.ShapeDtypeStruct((2 * count, width, ff), BF), hbm),
        up=(jax.ShapeDtypeStruct((2 * count, width, ff), BF), hbm),
        down=(jax.ShapeDtypeStruct((2 * count, ff, width), BF), hbm),
        out=(jax.ShapeDtypeStruct((ff, width), BF), hbm),
        qkv=(jax.ShapeDtypeStruct((ff, 2 * width), BF), hbm),
        tiny_out=(jax.ShapeDtypeStruct(tiny.shape[-2:], F32), vmem),
    )
    buf = pltpu.VMEM((items, piece, ff), BF)
    scratch = dict(
        mine=buf, rc=buf, pre=buf, suf=buf,
        tsum=pltpu.VMEM((3,) + tiny.shape[-2:], BF),
        trecv=pltpu.VMEM((slots + 1,) + tiny.shape[-2:], BF),
        s_tiny=dma((2, slots + 1)), s_mine=dma((items,)), s_out=dma((1,)),
    )
    each = dma((2, items))
    scratch.update(s_rc=each, s_pre=each, s_suf=each, s_far=each)
    scratch.update(s_oth=dma((2, 1)), s_faro=dma((2, 1)))
    if fused is None:
        args.update(
            eo=(eo.reshape(2, 2, piece, ff), hbm), cols=(cols.reshape(4, piece, ff), hbm)
        )
    else:
        inner = {}
        for k, v in fused.items():
            args[k] = (v, hbm)
            inner[k + "_in"] = pltpu.VMEM(v.shape, v.dtype)
        smem = pl.BlockSpec(memory_space=pltpu.SMEM)
        order, limit = tables
        args.update(
            small=(small, vmem), order=(order, smem), limit=(limit, smem),
            moe1=(moes[0], hbm), moe3=(moes[1], hbm),
        )
        outs.update({k: (jax.ShapeDtypeStruct(moes[0].shape, BF), hbm) for k in ("got1", "got3")})
        rows = args["dmid"][0].shape[0]
        keys = args["kv"][0].shape[0] // 2
        inner.update(gout_in=pltpu.VMEM((ff, width), BF))
        scratch.update(inner)
        outs.update(dtok=(jax.ShapeDtypeStruct((rows, width), F32), vmem))
        scratch.update(
            rdkv=pltpu.VMEM((keys, 256), BF), dkvs=pltpu.VMEM((keys, 256), BF),
            rout=pltpu.VMEM((2, ff, ff), BF),
            osend=pltpu.VMEM((ff, ff), BF), rox=pltpu.VMEM((ff, ff), BF),
            eo=pltpu.VMEM((2, 2, piece, ff), BF),
            dq_in=pltpu.VMEM((keys, 256), BF),
            dk=pltpu.VMEM((2 * keys, 128), F32), dv=pltpu.VMEM((2 * keys, 128), F32),
            qs=pltpu.VMEM((2 * rows, 128), BF), dos=pltpu.VMEM((2 * rows, 128), BF),
            delta=pltpu.VMEM((8, 2 * rows), F32), dqa=pltpu.VMEM((2 * rows, 128), F32),
            kpos=pltpu.VMEM((2 * keys, 1), jnp.int32), last=pltpu.VMEM((8, 8, 2 * rows), jnp.int32),
            s_in=dma((len(fused),)), s_moe=dma((2, 2)),
            rdh=pltpu.VMEM((2, rows, width), BF),
            dhx=pltpu.VMEM((rows, width), BF), rdx=pltpu.VMEM((rows, width), BF),
            acc=pltpu.VMEM((width, ff), F32), gn=pltpu.VMEM((8, width), F32),
            cbuf=pltpu.VMEM((width, ff), BF), rcol=pltpu.VMEM((ff, ff), BF),
            tbuf=pltpu.VMEM(tiny.shape, BF), rtiny=pltpu.VMEM(tiny.shape[-2:], BF),
            s_fg=dma((2, 9)),
        )
    names = tuple(args) + tuple(outs) + tuple(scratch)
    got = pl.pallas_call(
        functools.partial(
            reduce_kernel, names=names, slots=slots, shards=shards, fused=fused is not None
        ),
        in_specs=[v[1] for v in args.values()],
        out_specs=[v[1] for v in outs.values()],
        out_shape=[v[0] for v in outs.values()],
        scratch_shapes=list(scratch.values()),
        compiler_params=pltpu.CompilerParams(
            vmem_limit_bytes=67043328, collective_id=1, has_side_effects=True
        ),
        name="reduce_grads",
    )(*[v[0] for v in args.values()])
    return types.SimpleNamespace(**dict(zip(outs, got)))


def gather_rows(x):
    return lax.all_gather(x, "fsdp", axis=0, tiled=True)


def local(
    tokens, cotangent, lengths, order, routes, norm1, query_key_value_weight, w_out, norm2, router,
    w_gate, w_up, w_down,
):
    groups = lax.axis_size("seq")
    shards = lax.axis_size("fsdp")
    slots = lax.axis_size("dp")
    assert groups == 4
    seq, fsdp = lax.axis_index("seq"), lax.axis_index("fsdp")
    core, far = seq % 2, seq // 2
    rows, width = tokens.shape[1:]
    span = rows // 2
    x = tokens[0]
    limit = lengths[:1]
    n_experts = router.shape[1]
    owned = w_gate.shape[0]
    count = owned // 2

    own = lax.dynamic_slice_in_dim(order, (seq * shards + fsdp) * 2, 2)
    own_pos = (own[:, None] * span + jnp.arange(span, dtype=jnp.int32)[None, :]).reshape(-1)

    heads = QUERY_HEADS // groups
    qw, kw = heads * HEAD_WIDTH, KEY_VALUE_HEADS // groups * HEAD_WIDTH
    w3 = query_key_value_weight
    if shards == 2:
        tok, wcols, small, hidden_one, q, kv, cos, sin = front(order, x, w3, norm1, norm2, router)
        tok, kv = tok.reshape(groups * rows, width), kv.reshape(-1, 256)
        w_out, cotangent, kv = lax.optimization_barrier((w_out, cotangent, kv))
    else:
        table = order.reshape(groups, shards, 2)
        relative = jnp.arange(groups, dtype=jnp.int32) ^ seq
        table = jnp.take(table, relative, axis=0)
        qtab = jnp.take(table, fsdp, axis=1).reshape(-1)
        ktab = jnp.transpose(table, (1, 0, 2)).reshape(-1)
        qpos = (qtab[:, None] * span + jnp.arange(span, dtype=jnp.int32)[None, :]).reshape(-1)
        small = jnp.concatenate(
            [jnp.transpose(router), norm1[None], norm2[None], jnp.zeros((14, norm1.shape[0]), BF)]
        )
        half = HEAD_WIDTH // 2
        freqs = jnp.exp(jnp.arange(half, dtype=F32) * (-2.0 * math.log(ROPE_BASE) / HEAD_WIDTH))
        angles = qpos.astype(F32)[:, None] * freqs[None, :]
        cos, sin = jnp.tile(jnp.cos(angles), (1, 4)), jnp.tile(jnp.sin(angles), (1, 4))
        wq = lax.dynamic_slice_in_dim(w3, seq * qw, qw, 1)
        wk = lax.dynamic_slice_in_dim(w3, QUERY_HEADS * HEAD_WIDTH + seq * kw, kw, 1)
        wv = lax.dynamic_slice_in_dim(
            w3, (QUERY_HEADS + KEY_VALUE_HEADS) * HEAD_WIDTH + seq * kw, kw, 1
        )
        wcols = gather_rows(jnp.concatenate([wq, wk, wv], axis=1))
        small = lax.all_gather(small, "fsdp", axis=1, tiled=True)
        tok = gather_seq(x).reshape(groups * rows, width)
        hidden_one, q, kv_own = project(tok, small[16:17].astype(F32), wcols, cos, sin, rows)
        kv = gather_fsdp(kv_own)
    gain_one, gain_two = small[16].astype(F32), small[17].astype(F32)
    route_rows = small[:n_experts]

    kb = 4 * span
    own_valid = (own_pos < limit[0])[:, None]
    masked_cot = jnp.where(own_valid, cotangent[0], jnp.zeros_like(cotangent[0]))
    if shards == 2:
        shared = w_out.shape[0] // 2
        wo_near = flip_y(lax.dynamic_slice_in_dim(w_out, core * shared, shared, 0))
        cot_y, cot_x = flip_y(masked_cot), flip_x(masked_cot)
    if shards == 2:
        body, tables = attend_short_kernel, (order, limit)
    else:
        body, tables = attend_kernel, (qtab, ktab, limit)
    attended, low, lse = attend(body, tables, q, kv, span, kb)
    inputs = x.astype(F32)
    if shards == 2:
        out = moe_layer(
            low, x, w_out, wo_near, small, routes[0], masked_cot, cot_y, cot_x, w_gate, w_up, w_down
        )
        moes = (out.moe1, out.moe3)
        d_heads = out.do.reshape(groups * rows, qw)
        middle, d_middle, grad_out, tiny = out.middle, out.dmid, out.gout, out.tiny
        weight_grads = out.grads.reshape(count, 6, w_gate.shape[2], -1)
    else:
        sent = low.reshape(groups, rows, qw)
        got = jnp.stack(swap_seq([sent[m] for m in range(groups)]))
        got = jnp.take(got, relative, axis=0)
        token_out = jnp.transpose(got, (1, 0, 2)).reshape(rows, groups * qw)
        out_full = gather_rows(w_out)

        middle = inputs + mm(token_out, out_full)
        normed_two, factor_two = rms_parts(middle)
        hidden_two = (normed_two * gain_two).astype(BF)
        logits = mm_nt(hidden_two, route_rows)
        chosen = jnp.any(
            routes[0][:, :, None] == jnp.arange(n_experts, dtype=jnp.int32)[None, None, :], axis=1
        )
        top = jnp.max(jnp.where(chosen, logits, NEG), axis=-1, keepdims=True)
        raised = jnp.where(chosen, jnp.exp(logits - top), 0.0)
        gates = raised / jnp.sum(raised, axis=-1, keepdims=True)

        def share(v):
            near = gather_rows(v)
            return jnp.concatenate([near, flip_x(near)])

        cot_all = share(masked_cot)
        extended = jnp.concatenate(
            [hidden_two, gates.astype(BF), jnp.zeros((rows, 128 - n_experts), BF)], axis=1
        )
        hid_all = share(extended)
        base = jnp.stack([far * count, fsdp * owned + far * count]).astype(jnp.int32)
        part = rows * 4
        moe_parts, dh_parts, weight_grads = [], [], None
        for i in range(hid_all.shape[0] // part):
            got = experts(
                base, count, hid_all[i * part : (i + 1) * part], cot_all[i * part : (i + 1) * part],
                w_gate, w_up, w_down, rows,
            )
            moe_parts.append(got[0])
            dh_parts.append(got[1])
            if weight_grads is None:
                weight_grads = got[2]
            else:
                weight_grads = (weight_grads.astype(F32) + got[2].astype(F32)).astype(BF)

        def give_back(parts):
            v = jnp.concatenate(parts) if len(parts) > 1 else parts[0]
            n = v.shape[0] // 2
            near = v[:n].astype(F32) + flip_x(v[n:]).astype(F32)
            return lax.psum_scatter(near.astype(BF), "fsdp", scatter_dimension=0, tiled=True).astype(F32)

        d_ext = give_back(dh_parts)
        d_gates = d_ext[:, width : width + n_experts]
        d_logits = (gates * (d_gates - jnp.sum(gates * d_gates, axis=-1, keepdims=True))).astype(BF)
        grad_router = mm_tn(hidden_two, d_logits)
        d_hidden = d_ext[:, :width] + mm(d_logits, route_rows)
        grad_norm2 = jnp.sum(d_hidden * normed_two, axis=0)
        d_n = d_hidden * gain_two
        d_middle = masked_cot.astype(F32) + factor_two * (
            d_n - normed_two * jnp.mean(d_n * normed_two, axis=-1, keepdims=True)
        )
        d_attn = d_middle.astype(BF)
        grad_out = mm_tn(token_out, d_attn).astype(BF)
        d_token_out = mm_nt(d_attn, out_full).astype(BF)
        d_heads = jnp.transpose(d_token_out.reshape(rows, groups, qw), (1, 0, 2))
        d_heads = jnp.take(d_heads, relative, axis=0)
        d_heads = jnp.concatenate(swap_seq([d_heads[m] for m in range(groups)]))
    block = w_gate.shape[2]
    shard_rows = width // shards

    def tiny_rows(first):
        return jnp.concatenate(
            [jnp.transpose(grad_router), first[None], grad_norm2[None], jnp.zeros((14, width), F32)]
        ).reshape(32, shards, shard_rows).transpose(1, 0, 2)

    if shards == 2:
        got = reduce_grads(
            weight_grads, tiny, slots, shards,
            fused=dict(
                q=q, kv=kv, do=d_heads, o=attended, lse=lse,
                tok=tok, h=hidden_one, wc=wcols, cos=cos, sin=sin, dmid=d_middle, gout=grad_out,
            ),
            small=small, tables=(order, limit), moes=moes,
        )
        d_inputs = got.dtok
    else:
        dq, dkv = attend_back(qtab, ktab, limit, q, kv, d_heads, attended, lse, span, kb)
        dh_one, grad_cols, grad_norm1 = project_back(
            tok, hidden_one, dq, scatter_fsdp(dkv), wcols, cos, sin, rows
        )
        dh_one = dh_one.reshape(groups, rows, width)
        near = dh_one[0::2].astype(F32) + flip_core(dh_one[1::2]).astype(F32)
        d_hidden_one = near[0] + flip_x(near[1].astype(BF)).astype(F32)
        normed_one, factor_one = rms_parts(inputs)
        d_n = d_hidden_one * gain_one
        d_inputs = d_middle + factor_one * (
            d_n - normed_one * jnp.mean(d_n * normed_one, axis=-1, keepdims=True)
        )

        def to_owner(g):
            part = lax.psum_scatter(g, "fsdp", scatter_dimension=0, tiled=True)
            return jnp.pad(part, ((0, block - part.shape[0]), (0, 0)))

        cols = to_owner(grad_cols)
        mine = to_owner(grad_out).reshape(block, 2, block)
        kept = lax.dynamic_index_in_dim(mine, far, 1, keepdims=False)
        sent = lax.dynamic_index_in_dim(mine, 1 - far, 1, keepdims=False)
        outs = (kept.astype(F32) + flip_x(sent).astype(F32)).astype(BF)
        tiny = tiny_rows(jnp.sum(grad_norm1, axis=0))
        tiny = lax.psum_scatter(tiny, "fsdp", scatter_dimension=0, tiled=True)[0]
        got = reduce_grads(weight_grads, tiny, slots, shards, eo=outs, cols=cols)
    parts = (middle, out.moe0, got.got1, out.got2, got.got3) if shards == 2 else ()
    wide, sums, tiny = widen(
        [got.gate, got.up, got.down, got.out, got.qkv, d_inputs], parts, got.tiny_out, n_experts
    )
    grad_gate, grad_up, grad_down, shard_out, shard_qkv, d_inputs = wide
    shard_out, shard_qkv = shard_out[:shard_rows], shard_qkv[:shard_rows]
    if shards == 2:
        layer_out = sums[0]
    else:
        layer_out = (middle + give_back(moe_parts)).astype(BF)
    return (
        layer_out[None], d_inputs[None], tiny[0], shard_qkv, shard_out, tiny[1], tiny[2],
        grad_gate, grad_up, grad_down,
    )


def solution(mesh):
    placed = (
        P("dp", ("seq", "fsdp"), None),
        P("dp", ("seq", "fsdp"), None),
        P("dp"),
        P(),
        P("dp", ("seq", "fsdp"), None),
        P("fsdp"),
        P("fsdp", None),
        P("fsdp", None),
        P("fsdp"),
        P("fsdp", None),
        P("fsdp", None, None),
        P("fsdp", None, None),
        P("fsdp", None, None),
    )
    return jax.shard_map(
        local,
        mesh=mesh,
        in_specs=placed,
        out_specs=(
            P("dp", ("seq", "fsdp"), None),
            P("dp", ("seq", "fsdp"), None),
            P("fsdp"),
            P("fsdp", None),
            P("fsdp", None),
            P("fsdp"),
            P("fsdp", None),
            P("fsdp", None, None),
            P("fsdp", None, None),
            P("fsdp", None, None),
        ),
        check_vma=False,
    )
```

```python
import functools
import math
import types

import jax
import jax.numpy as jnp
import numpy as np
from jax import lax
from jax.experimental import pallas as pl
from jax.experimental.pallas import tpu as pltpu
from jax.sharding import PartitionSpec as P

QUERY_HEADS = 16
KEY_VALUE_HEADS = 8
HEAD_WIDTH = 64
TOPK = 8

EPS = 1e-06
ROPE_BASE = 10000.0
LOG2E = math.log2(math.e)
NEG = -1e30
BF = jnp.bfloat16
F32 = jnp.float32
VMEM_LIMIT = 60 * 1024 * 1024
OUT_STEP = 6

NT_DIMS = (((1,), (1,)), ((), ()))
TN_DIMS = (((0,), (0,)), ((), ()))


def mm(a, b):
    return jnp.dot(a, b, preferred_element_type=F32)


def mm_nt(a, b):
    return lax.dot_general(a, b, NT_DIMS, preferred_element_type=F32)


def mm_tn(a, b):
    return lax.dot_general(a, b, TN_DIMS, preferred_element_type=F32)


def params(**kw):
    return pltpu.CompilerParams(vmem_limit_bytes=VMEM_LIMIT, **kw)


def whole(shape):
    return pl.BlockSpec(shape, lambda *_: (0,) * len(shape))


def rms_parts(x):
    factor = lax.rsqrt(jnp.mean(x * x, axis=-1, keepdims=True) + EPS)
    return x * factor, factor


def qkv_kernel(tok_ref, gain_ref, w_ref, cos_ref, sin_ref, h_ref, q_ref, kv_ref):
    normed, _ = rms_parts(tok_ref[...].astype(F32))
    h = (normed * gain_ref[...]).astype(BF)
    h_ref[...] = h
    proj = mm(h, w_ref[...])
    cos, sin = cos_ref[...], sin_ref[...]
    low_half = lax.broadcasted_iota(jnp.int32, cos.shape, 1) % HEAD_WIDTH < HEAD_WIDTH // 2
    half = HEAD_WIDTH // 2
    for t in range(3):
        w = proj[:, t * 128 : (t + 1) * 128]
        rot = jnp.where(low_half, -pltpu.roll(w, 128 - half, 1), pltpu.roll(w, half, 1))
        out = (w * cos + rot * sin).astype(BF)
        if t < 2:
            q_ref[:, t * 128 : (t + 1) * 128] = out
        else:
            kv_ref[:, :128] = out
    kv_ref[:, 128:] = proj[:, 384:].astype(BF)


def project(tok, gain, w, cos, sin, tile):
    rows, width = tok.shape
    return pl.pallas_call(
        qkv_kernel,
        grid=(rows // tile,),
        in_specs=[
            pl.BlockSpec((tile, width), lambda i: (i, 0)),
            whole((1, width)),
            whole(w.shape),
            pl.BlockSpec((tile, 128), lambda i: (i, 0)),
            pl.BlockSpec((tile, 128), lambda i: (i, 0)),
        ],
        out_specs=[
            pl.BlockSpec((tile, width), lambda i: (i, 0)),
            pl.BlockSpec((tile, 256), lambda i: (i, 0)),
            pl.BlockSpec((tile, 256), lambda i: (i, 0)),
        ],
        out_shape=[
            jax.ShapeDtypeStruct((rows, width), BF),
            jax.ShapeDtypeStruct((rows, 256), BF),
            jax.ShapeDtypeStruct((rows, 256), BF),
        ],
        compiler_params=params(),
        name="project",
    )(tok, gain, w, cos, sin)


MESH = pl.DeviceIdType.MESH


def rope_rows(w, cos, sin):
    half = HEAD_WIDTH // 2
    low_half = lax.broadcasted_iota(jnp.int32, w.shape, 1) % HEAD_WIDTH < half
    rot = jnp.where(low_half, -pltpu.roll(w, 128 - half, 1), pltpu.roll(w, half, 1))
    return w * cos + rot * sin


def span_at(order, j):
    s, f = lax.axis_index("seq"), lax.axis_index("fsdp")
    x, c = s // 2, s % 2
    a, b, away = j % 8 // 4, j % 4 // 2, j // 8
    q = (x + a - 2 * x * a) * 2 + c + b - 2 * c * b
    return order[(q * 2 + f + away - 2 * f * away) * 2 + j % 2]


def front_kernel(
    order, tok, w3, norm1, norm2, router, rtab, stab, tok_out, wc_out, small_all, h_out, q, kv, cos_out, sin_out,
    small, tok_all, wc, h, cos, sin, s_tok, s_w, s_own, s_kv, s_end
):
    z, s, f = lax.axis_index("dp"), lax.axis_index("seq"), lax.axis_index("fsdp")
    core = s % 2
    peer_core = (z, s + 1 - 2 * core, f)
    peer_x = (z, (s + 2) % 4, f)
    peer_y = (z, s, 1 - f)
    rows, width = tok.shape
    part = small.shape[1]

    barrier = pltpu.get_barrier_semaphore()
    for dev in (peer_core, peer_x, peer_y):
        pl.semaphore_signal(barrier, inc=1, device_id=dev, device_id_type=MESH)

    def remote(src, dst, sems, b, dev):
        return pltpu.make_async_remote_copy(
            src_ref=src, dst_ref=dst, send_sem=sems.at[0, b], recv_sem=sems.at[1, b],
            device_id=dev, device_id_type=MESH,
        )

    own_rows = pl.ds(pl.multiple_of(f * part, part), part)
    pieces = []
    for first, n, to in ((width, 128, 256), (width + width // 2, 128, 384), (0, 256, 0)):
        src = w3.at[:, pl.ds(pl.multiple_of(first + s * n, 128), n)]
        pieces.append((src, wc.at[own_rows, pl.ds(to, n)]))
    local = [pltpu.make_async_copy(a, b, s_own.at[i]) for i, (a, b) in enumerate(pieces)]
    for copy in local:
        copy.start()
    n_exp = router.shape[0]
    row = lax.broadcasted_iota(jnp.int32, (small.shape[0] - n_exp, part), 0)
    gains = [v[...].astype(F32).reshape(1, part) for v in (norm1, norm2)]
    small[:n_exp, :] = router[...]
    small[n_exp:, :] = jnp.where(row == 0, gains[0], jnp.where(row == 1, gains[1], 0.0)).astype(BF)
    small_all[:, own_rows] = small[...]
    tok_all[0] = tok[...]
    pl.semaphore_wait(barrier, 3)
    over = remote(tok, tok_all.at[2], s_tok, 1, peer_x)
    near = remote(tok, tok_all.at[1], s_tok, 0, peer_core)
    onward = remote(tok_all.at[2], tok_all.at[3], s_tok, 2, peer_core)
    weights = [remote(a, b, s_w, i, peer_y) for i, (a, b) in enumerate(pieces)]
    weights.insert(0, remote(small, small_all.at[:, own_rows], s_w, 3, peer_y))
    over.start()
    for copy in weights:
        copy.start()
    near.start()
    for copy in local:
        copy.wait()
    for copy in weights[:3]:
        copy.wait_recv()
    gain = small_all[16:17, :].astype(F32)

    def kv_copy(t):
        at = pl.ds(pl.multiple_of(t * rows, rows), rows)
        return remote(kv.at[0, at], kv.at[1, at], s_kv, t, peer_y)

    ends = []
    span = rows // 2
    for k in range(8):
        at = pl.ds(k * span, span)
        row = pl.ds(span_at(order, k), 1)
        c, n = stab[0, row, :], stab[1, row, :]
        cos[at, :] = rtab[0] * c - rtab[1] * n
        sin[at, :] = rtab[1] * c + rtab[0] * n
    for i, (src, dst) in enumerate(((cos, cos_out), (sin, sin_out))):
        ends.append(pltpu.make_async_copy(src, dst, s_end.at[1 + i]))
        ends[-1].start()

    def end(t):
        at = pl.ds(pl.multiple_of(t * rows, rows), rows)
        return [
            pltpu.make_async_copy(tok_all.at[t], tok_out.at[t], s_end.at[3 + t]),
            pltpu.make_async_copy(h.at[at], h_out.at[at], s_end.at[7 + t]),
        ]

    @pl.loop(0, 4)
    def _(t):
        pl.when(t == 1)(near.wait_recv)

        @pl.when(t == 2)
        def _():
            over.wait_recv()
            onward.start()

        pl.when(t == 3)(onward.wait_recv)
        at = pl.ds(pl.multiple_of(t * rows, rows), rows)
        normed, _ = rms_parts(tok_all[t].astype(F32))
        hidden = (normed * gain).astype(BF)
        h[at, :] = hidden
        proj = mm(hidden, wc[:, 256:])
        kv[0, at, :128] = rope_rows(proj[:, :128], cos[at, :], sin[at, :]).astype(BF)
        kv[0, at, 128:] = proj[:, 128:].astype(BF)
        kv_copy(t).start()
        for copy in end(t):
            copy.start()

    weights[3].wait_recv()
    ends.append(pltpu.make_async_copy(wc, wc_out, s_end.at[0]))
    ends[-1].start()

    @pl.loop(0, 4)
    def _(t):
        at = pl.ds(pl.multiple_of(t * rows, rows), rows)
        proj = mm(h[at, :], wc[:, :256])
        for k in range(2):
            w = proj[:, k * 128 : (k + 1) * 128]
            q[at, k * 128 : (k + 1) * 128] = rope_rows(w, cos[at, :], sin[at, :]).astype(BF)

    for t in range(4):
        ends.extend(end(t))
    for t in range(4):
        kv_copy(t).wait()
    for copy in ends:
        copy.wait()
    for copy in (over, near, onward, *weights):
        copy.wait_send()


def front(order, tok, w3, norm1, norm2, router):
    rows, width = tok.shape
    n_spans = order.shape[0]
    span, half = rows // 2, HEAD_WIDTH // 2
    freqs = np.exp(np.arange(half) * (-2.0 * math.log(ROPE_BASE) / HEAD_WIDTH)).astype(np.float32)

    def table(positions):
        angles = np.tile(positions[:, None].astype(np.float64) * freqs[None, :], (1, 4))
        return jnp.asarray(np.stack([np.cos(angles), np.sin(angles)]), F32)

    rtab, stab = table(np.arange(span)), table(np.arange(n_spans) * span)
    vmem = pl.BlockSpec(memory_space=pltpu.VMEM)
    hbm = pl.BlockSpec(memory_space=pl.ANY)
    dma = pltpu.SemaphoreType.DMA
    shape = jax.ShapeDtypeStruct
    return pl.pallas_call(
        front_kernel,
        in_specs=[pl.BlockSpec(memory_space=pltpu.SMEM), vmem, hbm, vmem, vmem, vmem, vmem, vmem],
        out_specs=[hbm, hbm, vmem, hbm, vmem, vmem, hbm, hbm],
        out_shape=[
            shape((4, rows, width), BF),
            shape((width, 512), BF),
            shape((32, width), BF),
            shape((4 * rows, width), BF),
            shape((4 * rows, 256), BF),
            shape((2, 4 * rows, 256), BF),
            shape((4 * rows, 128), F32),
            shape((4 * rows, 128), F32),
        ],
        scratch_shapes=[
            pltpu.VMEM((32, norm1.shape[0]), BF),
            pltpu.VMEM((4, rows, width), BF), pltpu.VMEM((width, 512), BF),
            pltpu.VMEM((4 * rows, width), BF),
            pltpu.VMEM((4 * rows, 128), F32), pltpu.VMEM((4 * rows, 128), F32),
            dma((2, 3)), dma((2, 4)), dma((3,)), dma((2, 4)), dma((11,)),
        ],
        compiler_params=params(collective_id=2, has_side_effects=True),
        name="front",
    )(order, tok, w3, norm1, norm2, router, rtab, stab)


def widen_kernel(*refs, wide, parts):
    n = wide + parts + 1
    ins, outs = refs[:n], refs[n:]
    for a, b in zip(ins[:wide], outs[:wide]):
        b[...] = a[...].astype(F32)
    if parts:
        total = ins[wide][...].astype(F32)
        for part in ins[wide + 1 : wide + parts]:
            total = total + part[...].astype(F32)
        outs[wide][...] = total.astype(BF)
    tiny, (one, two, router) = ins[-1], outs[-3:]

    @pl.when(pl.program_id(0) == 0)
    def _():
        one[...] = tiny[16:17, :]
        two[...] = tiny[17:18, :]
        router[...] = tiny[: router.shape[0], :]


def widen(arrays, parts, tiny, n_experts):
    flat = [a.reshape(-1, a.shape[-1]) for a in arrays]
    steps = 4
    cols = tiny.shape[1]
    block = lambda a: pl.BlockSpec((a.shape[0] // steps, a.shape[1]), lambda i: (i, 0))
    shape = jax.ShapeDtypeStruct
    smalls = [(1, cols), (1, cols), (n_experts, cols)]
    sums = [shape(p.shape, BF) for p in parts[:1]]
    got = pl.pallas_call(
        functools.partial(widen_kernel, wide=len(flat), parts=len(parts)),
        grid=(steps,),
        in_specs=[block(a) for a in (*flat, *parts)] + [whole(tiny.shape)],
        out_specs=[block(a) for a in (*flat, *sums)] + [whole(v) for v in smalls],
        out_shape=[shape(a.shape, F32) for a in flat] + sums + [shape(v, F32) for v in smalls],
        compiler_params=params(),
        name="widen",
    )(*flat, *parts, tiny)
    n = len(arrays)
    wide = [g.reshape(a.shape) for g, a in zip(got, arrays)]
    return wide, got[n : n + len(sums)], [got[-3][0], got[-2][0], jnp.transpose(got[-1])]


def project_back_kernel(
    tok_ref, h_ref, dq_ref, dkv_ref, w_ref, cos_ref, sin_ref, dh_ref, gw_ref, gn_ref, acc
):
    step = pl.program_id(0)

    @pl.when(step == 0)
    def _():
        acc[...] = jnp.zeros_like(acc)
        gn_ref[...] = jnp.zeros_like(gn_ref)

    cos, sin = cos_ref[...], sin_ref[...]
    half = HEAD_WIDTH // 2
    low_half = lax.broadcasted_iota(jnp.int32, cos.shape, 1) % HEAD_WIDTH < half
    parts = []
    for t in range(3):
        w = dq_ref[:, t * 128 : (t + 1) * 128] if t < 2 else dkv_ref[:, :128]
        w = w.astype(F32)
        y = w * sin
        rot = jnp.where(low_half, pltpu.roll(y, 128 - half, 1), -pltpu.roll(y, half, 1))
        parts.append((w * cos + rot).astype(BF))
    parts.append(dkv_ref[:, 128:].astype(BF))
    dproj = jnp.concatenate(parts, axis=1)
    acc[...] += mm_tn(h_ref[...], dproj)
    dh = mm_nt(dproj, w_ref[...])
    dh_ref[...] = dh.astype(BF)
    normed, _ = rms_parts(tok_ref[...].astype(F32))
    gn_ref[...] += jnp.sum((dh * normed).reshape(-1, 8, dh.shape[1]), axis=0)

    @pl.when(step == pl.num_programs(0) - 1)
    def _():
        gw_ref[...] = acc[...].astype(BF)


def project_back(tok, h, dq, dkv, w, cos, sin, tile):
    rows, width = tok.shape
    row = lambda n: pl.BlockSpec((tile, n), lambda i: (i, 0))
    return pl.pallas_call(
        project_back_kernel,
        grid=(rows // tile,),
        in_specs=[row(width), row(width), row(256), row(256), whole(w.shape), row(128), row(128)],
        out_specs=[row(width), whole(w.shape), whole((8, width))],
        out_shape=[
            jax.ShapeDtypeStruct((rows, width), BF),
            jax.ShapeDtypeStruct(w.shape, BF),
            jax.ShapeDtypeStruct((8, width), F32),
        ],
        scratch_shapes=[pltpu.VMEM(w.shape, F32)],
        compiler_params=params(),
        name="project_back",
    )(tok, h, dq, dkv, w, cos, sin)


def stack_heads(a, b, dtype=BF):
    a, b = a.astype(F32), b.astype(F32)
    low = lax.broadcasted_iota(jnp.int32, a.shape, 1) < HEAD_WIDTH
    turn = lambda v: pltpu.roll(v, HEAD_WIDTH, 1)
    rows = [
        jnp.where(low, a, 0.0), jnp.where(low, turn(a), 0.0),
        jnp.where(low, 0.0, turn(b)), jnp.where(low, 0.0, b),
    ]
    return jnp.concatenate(rows, axis=0).astype(dtype)


def unstack_heads(x):
    n = x.shape[0] // 4
    low = lax.broadcasted_iota(jnp.int32, (n, 128), 1) < HEAD_WIDTH
    turn = lambda v: pltpu.roll(v, HEAD_WIDTH, 1)
    return (
        jnp.where(low, x[:n], turn(x[n : 2 * n])),
        jnp.where(low, turn(x[2 * n : 3 * n]), x[3 * n :]),
    )


def block_counts(span_id, limit, span, kb):
    first = span_id * span
    seen = (first + span - 1) // kb + 1
    blocks = jnp.minimum(seen, (limit + kb - 1) // kb)
    full = jnp.minimum(first + 1, limit) // kb
    return jnp.minimum(full, blocks), blocks


def sort_spans(ktab_ref, src, dst, lanes, span, count):
    @pl.loop(0, count)
    def _(j):
        to = pl.multiple_of(ktab_ref[j] * span, span)
        dst[pl.ds(to, span), :] = src[pl.ds(pl.multiple_of(j * span, span), span), lanes]


def attend_kernel(
    qtab_ref, ktab_ref, len_ref, q_ref, kv_ref, o_ref, low_ref, lse_ref, ks, vs, *, span, kb
):
    step = pl.program_id(0)
    count = ks.shape[0] // span

    @pl.when(step == 0)
    def _():
        sort_spans(ktab_ref, kv_ref, ks, slice(0, 128), span, count)
        sort_spans(ktab_ref, kv_ref, vs, slice(128, 256), span, count)

    q = stack_heads(q_ref[:, :128], q_ref[:, 128:])
    rows = 4 * span
    limit = len_ref[0]
    span_id = qtab_ref[step]
    full, blocks = block_counts(span_id, limit, span, kb)
    qpos = span_id * span + lax.broadcasted_iota(jnp.int32, (rows, kb), 0) % span
    col = lax.broadcasted_iota(jnp.int32, (rows, kb), 1)
    last = jnp.minimum(qpos, limit - 1)

    def body(masked, i, carry):
        top, total, acc = carry
        at = pl.multiple_of(i * kb, kb)
        s = mm_nt(q, ks[pl.ds(at, kb), :]) * (HEAD_WIDTH**-0.5 * LOG2E)
        if masked:
            s = jnp.where(col + i * kb <= last, s, NEG)
        new = jnp.maximum(top, jnp.max(s, axis=1, keepdims=True))
        fade = jnp.exp2(top - new)
        p = jnp.exp2(s - new)
        total = total * fade + jnp.sum(p, axis=1, keepdims=True)
        acc = acc * fade + mm(p.astype(BF), vs[pl.ds(at, kb), :])
        return new, total, acc

    carry = (
        jnp.full((rows, 1), NEG, F32),
        jnp.zeros((rows, 1), F32),
        jnp.zeros((rows, 128), F32),
    )
    carry = lax.fori_loop(0, full, functools.partial(body, False), carry)
    top, total, acc = lax.fori_loop(full, blocks, functools.partial(body, True), carry)
    a, b = unstack_heads(acc / total)
    o_ref[:, :128] = a
    o_ref[:, 128:] = b
    low_ref[:, :128] = a.astype(BF)
    low_ref[:, 128:] = b.astype(BF)
    lse = jnp.broadcast_to(top + jnp.log2(total), (rows, 128))
    lse_ref[0] = jnp.transpose(lse)[:8]


def attend_short_kernel(
    order_ref, len_ref, q_ref, kv_ref, o_ref, low_ref, lse_ref, ks, vs, *, span, kb
):
    step = pl.program_id(0)
    count = ks.shape[0] // span

    @pl.when(step == 0)
    def _():
        @pl.loop(0, count)
        def _(j):
            to = pl.ds(pl.multiple_of(span_at(order_ref, j) * span, span), span)
            at = pl.ds(pl.multiple_of(j * span, span), span)
            ks[to, :] = kv_ref[at, :128]
            vs[to, :] = kv_ref[at, 128:]

    q = stack_heads(q_ref[:, :128], q_ref[:, 128:])
    rows = 2 * span
    limit = len_ref[0]
    span_id = span_at(order_ref, step)
    _, blocks = block_counts(span_id, limit, span, kb)
    qpos = span_id * span + lax.broadcasted_iota(jnp.int32, (rows, kb), 0) % span
    last = jnp.minimum(qpos, limit - 1)
    col = lax.broadcasted_iota(jnp.int32, (rows, kb), 1)

    def run(n):
        outs, sums = [], []
        for g in range(2):
            part = q[g * rows : (g + 1) * rows]
            scores = []
            for i in range(n):
                v = mm_nt(part, ks[i * kb : (i + 1) * kb, :]) * (HEAD_WIDTH**-0.5 * LOG2E)
                if i == n - 1:
                    v = jnp.where(col + i * kb <= last, v, NEG)
                scores.append(v)
            tops = [jnp.max(v, axis=1, keepdims=True) for v in scores]
            top = functools.reduce(jnp.maximum, tops)
            total = jnp.zeros((rows, 1), F32)
            acc = jnp.zeros((rows, 128), F32)
            for i in range(n):
                p = jnp.exp2(scores[i] - top)
                total = total + jnp.sum(p, axis=1, keepdims=True)
                acc = acc + mm(p.astype(BF), vs[i * kb : (i + 1) * kb, :])
            outs.append(acc / total)
            sums.append(top + jnp.log2(total))
        a, b = unstack_heads(jnp.concatenate(outs, axis=0))
        o_ref[:, :128] = a
        o_ref[:, 128:] = b
        low_ref[:, :128] = a.astype(BF)
        low_ref[:, 128:] = b.astype(BF)
        lse = jnp.broadcast_to(jnp.concatenate(sums, axis=0), (2 * rows, 128))
        lse_ref[0] = jnp.transpose(lse)[:8]

    for n in range(1, ks.shape[0] // kb + 1):
        pl.when(blocks == n)(functools.partial(run, n))


def attend(body, tables, q, kv, span, kb):
    steps, keys = q.shape[0] // span, kv.shape[0]
    return pl.pallas_call(
        functools.partial(body, span=span, kb=kb),
        grid_spec=pltpu.PrefetchScalarGridSpec(
            num_scalar_prefetch=len(tables),
            grid=(steps,),
            in_specs=[pl.BlockSpec((span, 256), lambda i, *_: (i, 0)), whole(kv.shape)],
            out_specs=[
                pl.BlockSpec((span, 256), lambda i, *_: (i, 0)),
                pl.BlockSpec((span, 256), lambda i, *_: (i, 0)),
                pl.BlockSpec((1, 8, 4 * span), lambda i, *_: (i, 0, 0)),
            ],
            scratch_shapes=[pltpu.VMEM((keys, 128), BF), pltpu.VMEM((keys, 128), BF)],
        ),
        out_shape=[
            jax.ShapeDtypeStruct((q.shape[0], 256), F32),
            jax.ShapeDtypeStruct((q.shape[0], 256), BF),
            jax.ShapeDtypeStruct((steps, 8, 4 * span), F32),
        ],
        compiler_params=params(),
        name="attend",
    )(*tables, q, kv)


def attend_back_kernel(
    qtab_ref, ktab_ref, len_ref, q_ref, kv_ref, do_ref, o_ref, lse_ref, dq_ref, dkv_ref,
    ks, vs, dk, dv, *, span, kb,
):
    step = pl.program_id(0)
    count = ks.shape[0] // span
    scale = HEAD_WIDTH**-0.5

    @pl.when(step == 0)
    def _():
        sort_spans(ktab_ref, kv_ref, ks, slice(0, 128), span, count)
        sort_spans(ktab_ref, kv_ref, vs, slice(128, 256), span, count)
        dk[...] = jnp.zeros_like(dk)
        dv[...] = jnp.zeros_like(dv)

    q = stack_heads(q_ref[:, :128], q_ref[:, 128:])
    do = stack_heads(do_ref[:, :128], do_ref[:, 128:])
    rows = 4 * span
    inner = do.astype(F32) * stack_heads(o_ref[:, :128], o_ref[:, 128:], F32)
    delta = jnp.sum(jnp.transpose(inner), axis=0, keepdims=True)
    lse = lse_ref[0, :1]
    limit = len_ref[0]
    span_id = qtab_ref[step]
    full, blocks = block_counts(span_id, limit, span, kb)
    blocks = jnp.where(span_id * span < limit, blocks, 0)
    full = jnp.minimum(full, blocks)
    qpos = span_id * span + lax.broadcasted_iota(jnp.int32, (kb, rows), 1) % span
    key = lax.broadcasted_iota(jnp.int32, (kb, rows), 0)
    last = jnp.minimum(qpos, limit - 1)

    def body(masked, i, dq):
        at = pl.ds(pl.multiple_of(i * kb, kb), kb)
        k, v = ks[at, :], vs[at, :]
        s = mm_nt(k, q) * (scale * LOG2E)
        p = jnp.exp2(s - lse)
        if masked:
            p = jnp.where(key + i * kb <= last, p, 0.0)
        dp = mm_nt(v, do)
        ds = (p * (dp - delta)).astype(BF)
        dk[at, :] += mm(ds, q)
        dv[at, :] += mm(p.astype(BF), do)
        return dq + mm_tn(ds, k)

    dq = jnp.zeros((rows, 128), F32)
    dq = lax.fori_loop(0, full, functools.partial(body, False), dq)
    dq = lax.fori_loop(full, blocks, functools.partial(body, True), dq)
    a, b = unstack_heads(dq * scale)
    dq_ref[:, :128] = a.astype(BF)
    dq_ref[:, 128:] = b.astype(BF)

    @pl.when(step == pl.num_programs(0) - 1)
    def _():
        @pl.loop(0, count)
        def _(j):
            at = pl.ds(pl.multiple_of(ktab_ref[j] * span, span), span)
            to = pl.ds(pl.multiple_of(j * span, span), span)
            dkv_ref[to, :128] = (dk[at, :] * scale).astype(BF)
            dkv_ref[to, 128:] = dv[at, :].astype(BF)


def attend_back(qtab, ktab, limit, q, kv, do, o, lse, span, kb):
    steps, keys = q.shape[0] // span, kv.shape[0]
    row = pl.BlockSpec((span, 256), lambda i, *_: (i, 0))
    return pl.pallas_call(
        functools.partial(attend_back_kernel, span=span, kb=kb),
        grid_spec=pltpu.PrefetchScalarGridSpec(
            num_scalar_prefetch=3,
            grid=(steps,),
            in_specs=[
                row, whole(kv.shape), row, row,
                pl.BlockSpec((1, 8, 4 * span), lambda i, *_: (i, 0, 0)),
            ],
            out_specs=[row, whole(kv.shape)],
            scratch_shapes=[
                pltpu.VMEM((keys, 128), BF), pltpu.VMEM((keys, 128), BF),
                pltpu.VMEM((keys, 128), F32), pltpu.VMEM((keys, 128), F32),
            ],
        ),
        out_shape=[
            jax.ShapeDtypeStruct((q.shape[0], 256), BF),
            jax.ShapeDtypeStruct(kv.shape, BF),
        ],
        compiler_params=params(),
        name="attend_back",
    )(qtab, ktab, limit, q, kv, do, o, lse)


def experts_kernel(
    base_ref, h_ref, c_ref, wg_ref, wu_ref, wd_ref, moe_ref, dh_ref, grad_ref,
    moe, dh, dgates, s_act, s_gate, s_up, *, tile,
):
    step = pl.program_id(0)
    width = c_ref.shape[1]
    expert = base_ref[1] + step
    wg, wu, wd = wg_ref[0], wu_ref[0], wd_ref[0]

    @pl.when(step == 0)
    def _():
        moe[...] = jnp.zeros_like(moe)
        dh[...] = jnp.zeros_like(dh)
        dgates[...] = jnp.zeros_like(dgates)

    @pl.loop(0, moe.shape[0] // tile)
    def _(t):
        at = pl.ds(pl.multiple_of(t * tile, tile), tile)
        h, c = h_ref[at, :width], c_ref[at, :]
        lane = lax.broadcasted_iota(jnp.int32, (tile, 128), 1)
        mine = lane == expert
        gate = jnp.sum(
            jnp.where(mine, h_ref[at, width:].astype(F32), 0.0), axis=1, keepdims=True
        )
        g, u, z = mm(h, wg), mm(h, wu), mm_nt(c, wd)
        sig = jax.nn.sigmoid(g)
        silu = g * sig
        act = silu * u
        dgates[at, :] += jnp.where(mine, jnp.sum(act * z, axis=1, keepdims=True), 0.0)
        act = (act * gate).astype(BF)
        dact = z * gate
        dgate = (dact * u * sig * (1.0 + g * (1.0 - sig))).astype(BF)
        dup = (dact * silu).astype(BF)
        s_act[at, :] = act
        s_gate[at, :] = dgate
        s_up[at, :] = dup
        moe[at, :] += mm(act, wd)
        dh[at, :] += mm_nt(dgate, wg) + mm_nt(dup, wu)

    block = grad_ref.shape[2]
    for i in range(2):
        at = slice(i * block, (i + 1) * block)
        grad_ref[0, i] = mm_tn(h_ref[:, at], s_gate[...]).astype(BF)
        grad_ref[0, 2 + i] = mm_tn(h_ref[:, at], s_up[...]).astype(BF)
        grad_ref[0, 4 + i] = mm_tn(s_act[...], c_ref[:, at]).astype(BF)

    @pl.when(step == pl.num_programs(0) - 1)
    def _():
        moe_ref[...] = moe[...].astype(BF)
        dh_ref[:, :width] = dh[...].astype(BF)
        dh_ref[:, width:] = dgates[...].astype(BF)


def experts(base, count, h, c, wg, wu, wd, tile):
    rows, width = c.shape
    ff = wg.shape[2]
    pick = lambda shape: pl.BlockSpec((1,) + shape, lambda e, s: (s[0] + e, 0, 0))
    return pl.pallas_call(
        functools.partial(experts_kernel, tile=tile),
        grid_spec=pltpu.PrefetchScalarGridSpec(
            num_scalar_prefetch=1,
            grid=(count,),
            in_specs=[
                whole(h.shape), whole(c.shape),
                pick((width, ff)), pick((width, ff)), pick((ff, width)),
            ],
            out_specs=[
                whole(c.shape), whole(h.shape),
                pl.BlockSpec((1, 6, ff, ff), lambda e, s: (e, 0, 0, 0)),
            ],
            scratch_shapes=[
                pltpu.VMEM((rows, width), F32), pltpu.VMEM((rows, width), F32),
                pltpu.VMEM((rows, 128), F32),
                pltpu.VMEM((rows, ff), BF), pltpu.VMEM((rows, ff), BF), pltpu.VMEM((rows, ff), BF),
            ],
        ),
        out_shape=[
            jax.ShapeDtypeStruct(c.shape, BF),
            jax.ShapeDtypeStruct(h.shape, BF),
            jax.ShapeDtypeStruct((count, 6, ff, ff), BF),
        ],
        compiler_params=params(),
        name="experts",
    )(base, h, c, wg, wu, wd)


def moe_kernel(*refs, names, topk, count):
    r = types.SimpleNamespace(**dict(zip(names, refs)))
    z, s, f = lax.axis_index("dp"), lax.axis_index("seq"), lax.axis_index("fsdp")
    core, x = s % 2, s // 2
    flip = 1 - 2 * core
    seqs = (s, s + flip, (s + 2) % 4, (s + 2) % 4 + flip)
    peers = [(z, q, f) for q in seqs]
    peer_x, peer_y = peers[2], (z, s, 1 - f)
    att, att_in, tout, hx, cots = r.att, r.att_in, r.tout, r.hx, r.cots
    rows, width = tout.shape
    n = rows // 2
    ext = hx.shape[1]
    ff = r.wgs.shape[2]
    owned = r.wg.shape[0]

    barrier = pltpu.get_barrier_semaphore()
    for dev in (*peers[1:], peer_y):
        pl.semaphore_signal(barrier, inc=1, device_id=dev, device_id_type=MESH)

    def remote(src, dst, sems, b, dev):
        return pltpu.make_async_remote_copy(
            src_ref=src, dst_ref=dst, send_sem=sems.at[0, b], recv_sem=sems.at[1, b],
            device_id=dev, device_id_type=MESH,
        )

    def block(t):
        return pl.ds(pl.multiple_of(t * rows, rows), rows)

    def rows_x(i):
        return pl.ds(pl.multiple_of(rows + 2 * i * rows, n), n)

    def rows_y(i):
        return pl.ds(pl.multiple_of(rows + n + 2 * i * rows, n), n)

    load_cots = [pltpu.make_async_copy(r.cot, cots.at[block(0)], r.s_cot.at[0])]
    for i in range(2):
        at = pl.ds(i * n, n)
        load_cots += [
            pltpu.make_async_copy(r.cot_x.at[at], cots.at[rows_x(i)], r.s_cot.at[1 + i]),
            pltpu.make_async_copy(r.cot_y.at[at], cots.at[rows_y(i)], r.s_cot.at[3 + i]),
        ]
    for copy in load_cots:
        copy.start()

    def load_weights(e, act):
        for i, (src, dst) in enumerate(((r.wg, r.wgs), (r.wu, r.wus), (r.wd, r.wds))):
            act(pltpu.make_async_copy(src.at[x * count + e], dst.at[e], r.s_w.at[i, e]))

    @pl.loop(0, count)
    def _(e):
        load_weights(e, lambda copy: copy.start())

    pl.semaphore_wait(barrier, 4)
    def head(m, i):
        at = pl.ds(pl.multiple_of(i * n, n), n)
        return remote(att.at[m, at], att_in.at[m, at], r.s_att, 2 * m + i, peers[m])

    heads = [head(m, i) for i in range(2) for m in (3, 2, 1)]
    for copy in heads:
        copy.start()
    diag = [
        remote(r.cot_x.at[pl.ds(0, n)], cots.at[pl.ds(2 * rows, n)], r.s_diag, 0, peer_y),
        remote(r.cot_x.at[pl.ds(n, n)], cots.at[pl.ds(2 * rows + n, n)], r.s_diag, 1, peer_y),
    ]
    wo_rows = pl.ds(pl.multiple_of(core * (ff // 2), ff // 2), ff // 2)
    wo_there = r.wo_there
    wo_copy = pltpu.make_async_copy(r.wo_near, wo_there.at[wo_rows], r.s_wo.at[0])
    wo_share = remote(r.wo_near, wo_there.at[wo_rows], r.s_diag, 2, peers[1])
    wo_copy.start()
    wo_share.start()
    diag[0].start()

    small = r.small
    table = r.table
    table[...] = jnp.zeros_like(table)
    table[: small.shape[0], :] = small[...]
    n_exp = r.gates.shape[1]
    gain = small[17:18, :].astype(F32)
    own_cols = pl.ds(pl.multiple_of(f * ff, ff), ff)
    away_cols = pl.ds(pl.multiple_of((1 - f) * ff, ff), ff)

    def head_cols(m):
        return pl.ds(pl.multiple_of(seqs[m] * 256, 256), 256)

    wo_copy.wait()
    wo_share.wait_recv()
    def share(i, j, dev):
        at = pl.ds(pl.multiple_of(i * n, n), n)
        to = rows_x(i) if j else rows_y(i)
        return remote(hx.at[at], hx.at[to], r.s_h, 2 * j + i, dev)

    @pl.loop(0, 2)
    def _(i):
        at = pl.ds(pl.multiple_of(i * n, n), n)
        tout[at, head_cols(0)] = att[0, at, :]
        for m in range(1, 4):
            head(m, i).wait_recv()
            tout[at, head_cols(m)] = att_in[m, at, :]
        middle = (
            r.tok[at, :].astype(F32)
            + mm(tout[at, own_cols], r.wo_own[...])
            + mm(tout[at, away_cols], wo_there[...])
        )
        r.middle[at, :] = middle
        normed, _ = rms_parts(middle)
        hidden = (normed * gain).astype(BF)
        logits = mm_nt(hidden, table[...])
        lane = lax.broadcasted_iota(jnp.int32, logits.shape, 1)
        chosen = lane == r.routes[at, 0:1]
        for k in range(1, topk):
            chosen = chosen | (lane == r.routes[at, k : k + 1])
        top = jnp.max(jnp.where(chosen, logits, NEG), axis=-1, keepdims=True)
        raised = jnp.where(chosen, jnp.exp(logits - top), 0.0)
        gates = raised / jnp.sum(raised, axis=-1, keepdims=True)
        r.gates[at, :] = gates
        hx[at, :width] = hidden
        hx[at, width:] = gates.astype(BF)
        share(i, 0, peer_y).start()
        share(i, 1, peer_x).start()

    shares = [share(i, j, dev) for i in range(2) for j, dev in ((0, peer_y), (1, peer_x))]
    second = remote(hx.at[rows_y(1)], hx.at[pl.ds(2 * rows + n, n)], r.s_h, 4, peer_x)
    first = remote(hx.at[rows_x(0)], hx.at[pl.ds(2 * rows, n)], r.s_h, 5, peer_y)

    dhs, moe, dh, dgates = r.dhs, r.moe_acc, r.dh_acc, r.dg_acc
    back_x = [
        remote(dhs.at[rows_x(i)], r.rdh.at[1, pl.ds(i * n, n)], r.s_d, i, peer_x) for i in range(2)
    ]
    back_y = [
        remote(dhs.at[rows_y(i)], r.rdh.at[0, pl.ds(i * n, n)], r.s_d, 2 + i, peer_y) for i in range(2)
    ]

    def two_hops(i, sem, first_dev, second_dev):
        at = pl.ds(i * n, n)
        return (
            remote(dhs.at[pl.ds(2 * rows + i * n, n)], r.via.at[at], r.s_d, sem, first_dev),
            remote(r.via.at[at], r.rdd.at[at], r.s_d, sem + 1, second_dev),
        )

    hop_y, end_x = two_hops(0, 4, peer_y, peer_x)
    hop_x, end_y = two_hops(1, 6, peer_x, peer_y)
    moe_x = remote(r.moe2, r.got2, r.s_d, 8, peer_x)

    def moe_out(turn):
        src = r.mstage.at[turn % 2]
        if turn % 2 == 0:
            return [pltpu.make_async_copy(src, (r.moe0, r.moe3)[turn // 2], r.s_m.at[turn])]
        to = pl.ds(turn // 2 * n, n)
        return [
            pltpu.make_async_copy(src.at[pl.ds(0, n)], r.moe2.at[to], r.s_m.at[turn]),
            pltpu.make_async_copy(src.at[pl.ds(n, n)], r.moe1.at[to], r.s_m.at[turn + 3]),
        ]

    def forward():
        hop_y.wait_recv()
        end_x.start()
        hop_x.wait_recv()
        end_y.start()

    @pl.loop(0, 4 * count)
    def _(k):
        t, e = k // count, k % count

        @pl.when(k < count)
        def _():
            load_weights(e, lambda copy: copy.wait())

        @pl.when(k == 0)
        def _():
            load_cots[0].wait()

        @pl.when(k == count)
        def _():
            for copy in shares:
                copy.wait_recv()
            second.start()
            first.start()
            diag[1].start()
            for copy in load_cots[1:]:
                copy.wait()

        @pl.when(k == 2 * count)
        def _():
            first.wait_recv()
            second.wait_recv()
            for copy in diag:
                copy.wait_recv()

        pl.when(k == 4 * count - 1)(forward)
        at = block(t)
        h, c = hx[at, :width], cots[at, :]
        wg, wu, wd = r.wgs[e], r.wus[e], r.wds[e]
        expert = f * owned + x * count + e
        mine = lax.broadcasted_iota(jnp.int32, (rows, ext - width), 1) == expert
        gate = jnp.sum(jnp.where(mine, hx[at, width:].astype(F32), 0.0), axis=1, keepdims=True)
        g, u, zz = mm(h, wg), mm(h, wu), mm_nt(c, wd)
        sig = jax.nn.sigmoid(g)
        silu = g * sig
        act = silu * u
        dgate_col = jnp.where(mine, jnp.sum(act * zz, axis=1, keepdims=True), 0.0)
        act = (act * gate).astype(BF)
        dact = zz * gate
        dgate = (dact * u * sig * (1.0 + g * (1.0 - sig))).astype(BF)
        dup = (dact * silu).astype(BF)
        r.s_act[e, at, :] = act
        r.s_gate[e, at, :] = dgate
        r.s_up[e, at, :] = dup

        @pl.when(e == 0)
        def _():
            moe[...] = mm(act, wd)
            dh[...] = mm_nt(dgate, wg) + mm_nt(dup, wu)
            dgates[...] = dgate_col

        @pl.when(e > 0)
        def _():
            moe[...] += mm(act, wd)
            dh[...] += mm_nt(dgate, wg) + mm_nt(dup, wu)
            dgates[...] += dgate_col

        @pl.when(e == count - 1)
        def _():
            dhs[at, :width] = dh[...].astype(BF)
            dhs[at, width:] = dgates[...].astype(BF)
            for i in range(4):
                @pl.when(t == i)
                def _():
                    if i == 2:
                        hop_y.start()
                        hop_x.start()
                    elif i > 0:
                        back_x[i // 2].start()
                        back_y[i // 2].start()
                    for copy in moe_out(i - 2) if i >= 2 else ():
                        copy.wait()
                    r.mstage[i % 2] = moe[...].astype(BF)
                    for copy in moe_out(i):
                        copy.start()

    stage = r.stage

    def grad_copy(b, slot):
        return pltpu.make_async_copy(stage.at[slot], r.grads.at[b], r.s_g.at[slot])

    dattn, dto, dsend = r.dattn, r.dto, r.dsend
    returns = [
        [
            remote(dsend.at[m, pl.ds(i * n, n)], r.do.at[m, pl.ds(i * n, n)], r.s_back, 2 * m + i, peers[m])
            for m in (3, 2, 1)
        ]
        for i in range(2)
    ]

    def middle_back(i):
        at = pl.ds(i * n, n)
        total = (
            dhs[at, :].astype(F32) + r.rdh[0, at, :].astype(F32)
            + r.rdh[1, at, :].astype(F32) + r.rdd[at, :].astype(F32)
        )
        dg, gates = total[:, width:], r.gates[at, :]
        dl = (gates * (dg - jnp.sum(gates * dg, axis=-1, keepdims=True))).astype(BF)
        rg = mm_tn(dl, hx[at, :width])[:32]
        d_hidden = total[:, :width] + mm(dl, table[...])
        normed, factor = rms_parts(r.middle[at, :])
        gn = jnp.sum(d_hidden * normed, axis=0, keepdims=True)
        d_n = d_hidden * gain
        d_mid = cots[at, :].astype(F32) + factor * (
            d_n - normed * jnp.mean(d_n * normed, axis=-1, keepdims=True)
        )
        r.dmid[at, :] = d_mid
        low = d_mid.astype(BF)
        dattn[at, :] = low
        dto[at, own_cols] = mm_nt(low, r.wo_own[...]).astype(BF)
        dto[at, away_cols] = mm_nt(low, wo_there[...]).astype(BF)
        for m in range(1, 4):
            dsend[m, at, :] = dto[at, head_cols(m)]
        for copy in returns[i]:
            copy.start()
        r.do[0, at, :] = dto[at, head_cols(0)]
        if i == 0:
            r.rg[...] = rg
            r.gn[:1, :] = gn
            return
        rg, gn = r.rg[...] + rg, r.gn[:1, :] + gn
        row = lax.broadcasted_iota(jnp.int32, rg.shape, 0)
        top = jnp.where(row == 17, gn, jnp.where(row < 16, rg, 0.0))
        r.tiny[0] = top[:, : width // 2]
        r.tiny[1] = top[:, width // 2 :]
        for k in range(4):
            cols = slice(k * 256, (k + 1) * 256)
            r.gout[cols, :] = mm_tn(tout[:, cols], dattn[...]).astype(BF)

    def send_moe():
        for copy in moe_out(3):
            copy.wait()
        moe_x.start()

    def back0():
        for copy in (back_x[0], back_y[0], end_x):
            copy.wait_recv()
        middle_back(0)

    def back1():
        for copy in (back_x[1], back_y[1], end_y):
            copy.wait_recv()
        middle_back(1)

    @pl.loop(0, 3 * count)
    def _(k):
        e, j = k // 3, k % 3
        pl.when(k == 1)(send_moe)
        pl.when(k == 3 * count - 7)(back0)
        pl.when(k == 3 * count - 4)(back1)

        @pl.when(k > 0)
        def _():
            grad_copy(0, 0).wait()
            grad_copy(0, 1).wait()

        for which, left, right in ((0, hx, r.s_gate), (1, hx, r.s_up), (2, cots, r.s_act)):
            @pl.when(j == which)
            def _():
                for i in range(2):
                    at = slice(i * ff, (i + 1) * ff)
                    if which < 2:
                        v = mm_tn(left[:, at], right[e])
                    else:
                        v = mm_tn(right[e], left[:, at])
                    stage[i] = v.astype(BF)

        for i in range(2):
            grad_copy(6 * e + 2 * j + i, i).start()

    grad_copy(0, 0).wait()
    grad_copy(0, 1).wait()
    for copy in moe_out(2):
        copy.wait()
    for copy in (*returns[0], *returns[1], moe_x):
        copy.wait()
    for copy in (*heads, *diag, wo_share, *shares, first, second, *back_y, *back_x, hop_x, hop_y, end_y, end_x):
        copy.wait_send()


def moe_layer(att, tok, wo_own, wo_near, small, routes, cot, cot_y, cot_x, wg, wu, wd):
    rows, width = tok.shape
    owned, _, ff = wg.shape
    count = owned // 2
    ext = width + 128
    hbm = pl.BlockSpec(memory_space=pl.ANY)
    vmem = pl.BlockSpec(memory_space=pltpu.VMEM)
    dma = pltpu.SemaphoreType.DMA
    args = dict(
        att=(att.reshape(4, rows, 256), vmem), tok=(tok, vmem), wo_own=(wo_own, vmem),
        wo_near=(wo_near, hbm), small=(small, vmem), routes=(routes, vmem),
        cot=(cot, hbm), cot_y=(cot_y, hbm), cot_x=(cot_x, hbm),
        wg=(wg, hbm), wu=(wu, hbm), wd=(wd, hbm),
    )
    shape = jax.ShapeDtypeStruct
    outs = dict(
        middle=(shape((rows, width), F32), vmem),
        moe0=(shape((rows, width), BF), hbm), moe1=(shape((rows, width), BF), hbm),
        moe2=(shape((rows, width), BF), hbm), moe3=(shape((rows, width), BF), hbm),
        got2=(shape((rows, width), BF), hbm),
        dmid=(shape((rows, width), F32), vmem),
        do=(shape((4, rows, 256), BF), vmem),
        grads=(shape((6 * count, ff, ff), BF), hbm),
        gout=(shape((width, width), BF), vmem),
        tiny=(shape((2, 32, width // 2), F32), vmem),
    )
    stash = pltpu.VMEM((count, 4 * rows, ff), BF)
    scratch = dict(
        att_in=pltpu.VMEM((4, rows, 256), BF), tout=pltpu.VMEM((rows, width), BF),
        hx=pltpu.VMEM((4 * rows, ext), BF), cots=pltpu.VMEM((4 * rows, width), BF),
        wo_there=pltpu.VMEM((ff, width), BF), rg=pltpu.VMEM((32, width), F32),
        gn=pltpu.VMEM((8, width), F32), table=pltpu.VMEM((128, width), BF), gates=pltpu.VMEM((rows, 128), F32),
        wgs=pltpu.VMEM((count, width, ff), BF), wus=pltpu.VMEM((count, width, ff), BF),
        wds=pltpu.VMEM((count, ff, width), BF),
        s_act=stash, s_gate=stash, s_up=stash,
        moe_acc=pltpu.VMEM((rows, width), F32), dh_acc=pltpu.VMEM((rows, width), F32),
        dg_acc=pltpu.VMEM((rows, 128), F32), mstage=pltpu.VMEM((2, rows, width), BF),
        dhs=pltpu.VMEM((4 * rows, ext), BF), rdh=pltpu.VMEM((2, rows, ext), BF),
        via=pltpu.VMEM((rows, ext), BF), rdd=pltpu.VMEM((rows, ext), BF),
        dattn=pltpu.VMEM((rows, width), BF), dto=pltpu.VMEM((rows, width), BF),
        dsend=pltpu.VMEM((4, rows, 256), BF), stage=pltpu.VMEM((2, ff, ff), BF),
        s_att=dma((2, 8)), s_diag=dma((2, 3)), s_h=dma((2, 6)), s_d=dma((2, 9)), s_back=dma((2, 8)),
        s_cot=dma((5,)), s_wo=dma((1,)), s_w=dma((3, count)), s_m=dma((7,)), s_g=dma((2,)),
    )
    names = tuple(args) + tuple(outs) + tuple(scratch)
    got = pl.pallas_call(
        functools.partial(moe_kernel, names=names, topk=routes.shape[1], count=count),
        in_specs=[v[1] for v in args.values()],
        out_specs=[v[1] for v in outs.values()],
        out_shape=[v[0] for v in outs.values()],
        scratch_shapes=list(scratch.values()),
        compiler_params=pltpu.CompilerParams(
            vmem_limit_bytes=67043328, collective_id=3, has_side_effects=True
        ),
        name="moe_layer",
    )(*[v[0] for v in args.values()])
    return types.SimpleNamespace(**dict(zip(outs, got)))


def flip_core(x):
    return lax.ppermute(x, "seq", [(0, 1), (1, 0), (2, 3), (3, 2)])


def flip_x(x):
    return lax.ppermute(x, "seq", [(0, 2), (2, 0), (1, 3), (3, 1)])


def flip_both(x):
    return lax.ppermute(x, "seq", [(0, 3), (3, 0), (1, 2), (2, 1)])


def flip_y(x):
    return lax.ppermute(x, "fsdp", [(0, 1), (1, 0)])


def gather_seq(x):
    own = jnp.stack([x, flip_core(x)])
    far = flip_x(x)
    return jnp.concatenate([own, far[None], flip_core(far)[None]])


def swap_seq(blocks):
    return [blocks[0], flip_core(blocks[1]), flip_x(blocks[2]), flip_both(blocks[3])]


def gather_fsdp(x, axis=0):
    if lax.axis_size("fsdp") == 2:
        return jnp.concatenate([x, lax.ppermute(x, "fsdp", [(0, 1), (1, 0)])], axis=axis)
    return lax.all_gather(x, "fsdp", axis=axis, tiled=True)


def scatter_fsdp(x):
    if lax.axis_size("fsdp") == 2:
        n = x.shape[0] // 2
        other = lax.ppermute(x[n:], "fsdp", [(0, 1), (1, 0)])
        return x[:n].astype(F32) + other.astype(F32)
    return lax.psum_scatter(x, "fsdp", scatter_dimension=0, tiled=True).astype(F32)


def rope_back(w, cos, sin, low_half):
    half = HEAD_WIDTH // 2
    y = w * sin
    return w * cos + jnp.where(low_half, pltpu.roll(y, 128 - half, 1), -pltpu.roll(y, half, 1))


def reduce_kernel(*refs, names, slots, shards, fused):
    r = types.SimpleNamespace(**dict(zip(names, refs)))
    gm, mine, rc, pre, suf = r.gm, r.mine, r.rc, r.pre, r.suf
    gate, up, down, out, qkv = r.gate, r.up, r.down, r.out, r.qkv
    z, s, f = lax.axis_index("dp"), lax.axis_index("seq"), lax.axis_index("fsdp")
    core, x = s % 2, s // 2
    peer_core = (z, s + 1 - 2 * core, f)
    peer_x = (z, (s + 2) % 4, f)
    peer_y = (z, s, 1 - f)
    right, left = (z + 1, s, f), (z - 1, s, f)
    nb = gm.shape[0]
    n_moe, n_out, items = 2 * nb, 2 * nb + 2, 2 * nb + 6
    count = nb // 6
    piece = mine.shape[1]
    half, block = 2 * piece, 4 * piece
    last = slots - 1

    def other_z(k):
        return ((z + k) % slots, s, f)

    barrier = pltpu.get_barrier_semaphore()
    peer_xy = (z, (s + 2) % 4, 1 - f)
    peers = [other_z(k) for k in range(1, slots)] + [peer_core, peer_x] + [peer_y, peer_xy] * fused
    for dev in peers:
        pl.semaphore_signal(barrier, inc=1, device_id=dev, device_id_type=MESH)

    def remote(src, dst, sems, b, dev):
        return pltpu.make_async_remote_copy(
            src_ref=src, dst_ref=dst, send_sem=sems.at[0, b], recv_sem=sems.at[1, b],
            device_id=dev, device_id_type=MESH,
        )

    def load(src, b):
        return pltpu.make_async_copy(src, mine.at[b], r.s_mine.at[b])

    @pl.loop(0, n_moe)
    def _(b):
        load(gm.at[b // 2, core, b % 2], b).start()

    if fused:
        loads = [
            pltpu.make_async_copy(a, b, r.s_in.at[i])
            for i, (a, b) in enumerate((
                (r.q, r.q_in), (r.kv, r.kv_in), (r.do, r.do_in), (r.o, r.o_in), (r.lse, r.lse_in),
                (r.wc, r.wc_in),
                (r.cos, r.cos_in), (r.sin, r.sin_in), (r.h, r.h_in), (r.tok, r.tok_in),
                (r.gout.at[pl.ds(pl.multiple_of(f * block, block), block)], r.gout_in),
                (r.dmid, r.dmid_in),
            ))
        ]
        for copy in loads:
            copy.start()
    else:
        for i in range(2):
            load(r.eo.at[core, i], n_moe + i).start()
        for i in range(4):
            load(r.cols.at[i], n_out + i).start()
    pl.semaphore_wait(barrier, len(peers))

    @pl.loop(0, n_moe)
    def _(b):
        remote(gm.at[b // 2, 1 - core, b % 2], rc.at[b], r.s_rc, b, peer_core).start()

    if not fused:
        for i in range(2):
            remote(r.eo.at[1 - core, i], rc.at[n_moe + i], r.s_rc, n_moe + i, peer_core).start()

    def place(b, which, part, act):
        first_row = part * half + b % 2 * piece
        rows = pl.ds(pl.multiple_of(first_row, piece), piece)
        e, j = which * count + b // 12, b // 2 % 6
        jj = j % 2
        wide = pl.ds(pl.multiple_of(jj * block, block), block)
        at = pl.ds(pl.multiple_of(jj * block + first_row, piece), piece)
        for m, o in enumerate((gate, up)):
            @pl.when((b < n_moe) & (j // 2 == m))
            def _():
                act(o.at[e, at, :])

        @pl.when((b < n_moe) & (j // 2 == 2))
        def _():
            act(down.at[e, rows, wide])

        @pl.when((b >= n_moe) & (b < n_out))
        def _():
            act(out.at[rows, pl.ds(pl.multiple_of(which * block, block), block)])

        @pl.when(b >= n_out)
        def _():
            at = pl.ds(pl.multiple_of((b - n_out) * piece, piece), piece)
            wide = 2 * block
            for first, n, to in ((0, 256, 0), (wide, 128, 256), (wide + wide // 2, 128, 384)):
                col = pl.multiple_of(first + (2 * which + part) * n, 128)
                act(qkv.at[at, pl.ds(col, n)], pl.ds(to, n))

    def add(a, b):
        return a.astype(F32) + b.astype(F32)

    def hop(buf, sems, b, dev):
        return remote(buf.at[b], buf.at[b], sems, b, dev)

    def spread(b):
        def act(dst, cut=None):
            src = rc.at[b] if cut is None else rc.at[b, :, cut]
            remote(src, dst, r.s_oth, 0, peer_core).start()
            pltpu.make_async_copy(src, dst, r.s_out.at[0]).start()
            remote(src, dst, r.s_far, b, peer_x).start()

        place(b, x, core, act)

    lag = 2
    ahead = 4

    def begin(b):
        @pl.when(b < (n_moe if fused else items))
        def _():
            load(gm.at[0, 0, 0], b).wait()

        @pl.when(b < n_out)
        def _():
            remote(gm.at[0, 0, 0], rc.at[b], r.s_rc, b, peer_core).wait_recv()
            mine[b] = add(mine[b], rc[b]).astype(BF)

        @pl.when(z == 0)
        def _():
            remote(mine.at[b], pre.at[b], r.s_pre, b, right).start()

        @pl.when(z == last)
        def _():
            remote(mine.at[b], suf.at[b], r.s_suf, b, left).start()

    def prefix(b):
        hop(pre, r.s_pre, b, peer_x).wait_recv()
        got = pre[b].astype(F32)
        own = got + mine[b].astype(F32)

        @pl.when(z == last)
        def _():
            rc[b] = own.astype(BF)

        @pl.when(z < last)
        def _():
            @pl.when(2 * z >= slots)
            def _():
                rc[b] = (got + suf[b].astype(F32)).astype(BF)

            pre[b] = own.astype(BF)
            hop(pre, r.s_pre, b, right).start()

        @pl.when(2 * z >= slots)
        def _():
            spread(b)

    def suffix(b):
        hop(suf, r.s_suf, b, peer_x).wait_recv()
        got = suf[b].astype(F32)
        own = got + mine[b].astype(F32)

        @pl.when(z == 0)
        def _():
            rc[b] = own.astype(BF)

        @pl.when(z > 0)
        def _():
            @pl.when(2 * z < slots)
            def _():
                rc[b] = (got + pre[b].astype(F32)).astype(BF)

            suf[b] = own.astype(BF)
            hop(suf, r.s_suf, b, left).start()

        @pl.when(2 * z < slots)
        def _():
            spread(b)

    def forward(b):
        remote(rc.at[b], rc.at[b], r.s_far, b, peer_x).wait_recv()

        def act(dst, cut=None):
            remote(dst, dst, r.s_faro, 0, peer_core).start()

        place(b, 1 - x, core, act)

    def within(b, cond=True):
        return (b >= 0) & (b < items) & cond

    tsum, trecv, s_tiny = r.tsum, r.trecv, r.s_tiny

    def tiny_swap(k, dev):
        return remote(tsum.at[k], trecv.at[k], s_tiny, k, dev)

    def tiny_add(k):
        tiny_swap(k, peer_x).wait_recv()
        tsum[k + 1] = add(tsum[k], trecv[k]).astype(BF)

    def tiny_x():
        tiny_swap(0, peer_x).start()

    def tiny_core():
        tiny_add(0)
        tiny_swap(1, peer_core).start()

    def tiny_spread():
        tiny_add(1)
        for k in range(1, slots):
            remote(tsum.at[2], trecv.at[1 + k], s_tiny, 1 + k, other_z(k)).start()

    def tiny_end():
        total = tsum[2].astype(F32)
        for k in range(1, slots):
            remote(tsum.at[2], trecv.at[1 + k], s_tiny, 1 + k, other_z(k)).wait_recv()
            total = total + trecv[1 + k].astype(F32)
        r.tiny_out[...] = total

    steps = {}
    if fused:
        s_fg = r.s_fg
        keys = r.dkvs.shape[0]
        tile = r.dhx.shape[0]
        dh = [r.h_in.at[pl.ds(t * tile, tile)] for t in range(4)]
        owner = pl.multiple_of(f * block, block)
        away = pl.multiple_of((1 - f) * block, block)
        mine_rows, away_rows = pl.ds(owner, block), pl.ds(away, block)
        near_cols = pl.ds(pl.multiple_of(x * block, block), block)
        far_cols = pl.ds(pl.multiple_of((1 - x) * block, block), block)

        send_dkv = remote(r.kv_in.at[pl.ds(keys, keys)], r.rdkv, s_fg, 0, peer_y)
        send_out = [
            remote(r.gout.at[away_rows, cols], r.rout.at[i], s_fg, (1, 8)[i], peer_y)
            for i, cols in enumerate((far_cols, near_cols))
        ]
        send_dh3 = remote(dh[3], r.rdh.at[1], s_fg, 2, peer_core)
        send_dh1 = remote(dh[1], r.rdh.at[0], s_fg, 3, peer_core)
        send_dhx = remote(r.dhx, r.rdx, s_fg, 4, peer_x)
        send_cols = remote(r.cbuf.at[away_rows], r.rcol, s_fg, 5, peer_y)
        send_outx = remote(r.osend, r.rox, s_fg, 6, peer_x)
        send_tiny = remote(r.tbuf.at[1 - f], r.rtiny, s_fg, 7, peer_y)
        eo_core = [
            remote(r.eo.at[1 - core, i], rc.at[n_moe + i], r.s_rc, n_moe + i, peer_core)
            for i in range(2)
        ]
        moe_back = [
            remote(r.moe3, r.got3, r.s_moe, 1, peer_xy), remote(r.moe1, r.got1, r.s_moe, 0, peer_y),
        ]
        moe_back[0].start()
        for copy in send_out:
            copy.start()
        moe_back[1].start()

        span, kb = tile // 2, 2 * tile
        parts = 2 * keys // kb
        n_steps = 8 * parts
        scale = HEAD_WIDTH**-0.5

        def attention(n):
            j, m = n // parts, n % parts
            at = pl.ds(pl.multiple_of(j * span, span), span)

            @pl.when(n == 0)
            def _():
                r.dk[...] = jnp.zeros_like(r.dk)
                r.dv[...] = jnp.zeros_like(r.dv)
                inside = lax.broadcasted_iota(jnp.int32, (span, 1), 0)
                for k in range(2 * keys // span):
                    r.kpos[k * span : (k + 1) * span, :] = span_at(r.order, k) * span + inside
                across = lax.broadcasted_iota(jnp.int32, (8, 4 * span), 1) % span
                for k in range(8):
                    r.last[k] = jnp.minimum(span_at(r.order, k) * span + across, r.limit[0] - 1)

            @pl.when(m == 0)
            def _():
                r.qs[...] = stack_heads(r.q_in[at, :128], r.q_in[at, 128:])
                do = stack_heads(r.do_in[at, :128], r.do_in[at, 128:])
                r.dos[...] = do
                inner = do.astype(F32) * stack_heads(r.o_in[at, :128], r.o_in[at, 128:], F32)
                delta = jnp.sum(jnp.transpose(inner), axis=0, keepdims=True)
                r.delta[...] = jnp.broadcast_to(delta, r.delta.shape)

            key = pl.ds(pl.multiple_of(m * kb, kb), kb)
            k, v = r.kv_in[key, :128], r.kv_in[key, 128:]
            q, do = r.qs[...], r.dos[...]
            p = jnp.exp2(mm_nt(k, q) * (scale * LOG2E) - r.lse_in[j, :1])
            p = jnp.where(r.kpos[key, :] <= r.last[j, :1], p, 0.0)
            ds = (p * (mm_nt(v, do) - r.delta[:1])).astype(BF)
            r.dk[key, :] += mm(ds, q)
            r.dv[key, :] += mm(p.astype(BF), do)
            dq = mm_tn(ds, k)

            @pl.when(m == 0)
            def _():
                r.dqa[...] = dq

            @pl.when(m > 0)
            def _():
                r.dqa[...] += dq

            @pl.when(m == parts - 1)
            def _():
                a, b = unstack_heads(r.dqa[...] * scale)
                r.dq_in[at, :128] = a.astype(BF)
                r.dq_in[at, 128:] = b.astype(BF)

        def send_keys():
            r.kv_in[:, :128] = (r.dk[...] * scale).astype(BF)
            r.kv_in[:, 128:] = r.dv[...].astype(BF)
            send_dkv.start()

        def sum_dkv():
            send_dkv.wait_recv()
            r.dkvs[...] = add(r.kv_in[:keys], r.rdkv[...]).astype(BF)

        def back_tile(t, first=False):
            at = pl.ds(t * tile, tile)
            cos, sin = r.cos_in[at, :], r.sin_in[at, :]
            low_half = lax.broadcasted_iota(jnp.int32, cos.shape, 1) % HEAD_WIDTH < HEAD_WIDTH // 2
            parts = []
            for k in range(3):
                w = r.dq_in[at, k * 128 : (k + 1) * 128] if k < 2 else r.dkvs[at, :128]
                parts.append(rope_back(w.astype(F32), cos, sin, low_half).astype(BF))
            parts.append(r.dkvs[at, 128:])
            dproj = jnp.concatenate(parts, axis=1)
            grad = mm_tn(r.h_in[at, :], dproj)
            back = mm_nt(dproj, r.wc_in[...])
            dh[t][...] = back.astype(BF)
            normed, _ = rms_parts(r.tok_in[at, :].astype(F32))
            gain = jnp.sum((back * normed).reshape(-1, 8, back.shape[1]), axis=0)
            if first:
                r.acc[...] = grad
                r.gn[...] = gain
            else:
                r.acc[...] += grad
                r.gn[...] += gain

        def tile3():
            back_tile(3, True)
            send_dh3.start()

        def tile1():
            back_tile(1)
            send_dh1.start()

        def tile2():
            back_tile(2)
            send_dh3.wait_recv()
            r.dhx[...] = add(dh[2][...], r.rdh[1]).astype(BF)
            send_dhx.start()

        def tile0():
            back_tile(0)
            r.cbuf[...] = r.acc[...].astype(BF)
            send_cols.start()
            total = jnp.sum(r.gn[...], axis=0, keepdims=True)
            wide = tsum.shape[2]
            row = lax.broadcasted_iota(jnp.int32, (tsum.shape[1], wide), 0) == 16
            for k in range(2):
                part = total[:, k * wide : (k + 1) * wide]
                r.tbuf[k] = jnp.where(row, part, r.tiny[k]).astype(BF)
            send_tiny.start()

        def sum_out():
            send_out[0].wait_recv()
            r.osend[...] = add(r.gout_in[:, far_cols], r.rout[0]).astype(BF)
            send_outx.start()

        def tiny_y():
            send_tiny.wait_recv()
            tsum[0] = add(r.tbuf[f], r.rtiny[...]).astype(BF)
            tiny_x()

        def sum_cols():
            send_cols.wait_recv()
            v = add(r.cbuf[mine_rows, :], r.rcol[...]).astype(BF)
            for i in range(4):
                mine[n_out + i] = v[i * piece : (i + 1) * piece]

        def sum_outx():
            send_out[1].wait_recv()
            send_outx.wait_recv()
            v = add(r.gout_in[:, near_cols], r.rout[1]) + r.rox[...].astype(F32)
            v = v.astype(BF)
            for i in range(4):
                r.eo[i // 2, i % 2] = v[i * piece : (i + 1) * piece]
            for i in range(2):
                eo_core[i].start()
                mine[n_moe + i] = r.eo[core, i]

        def inputs_back():
            send_dh1.wait_recv()
            send_dhx.wait_recv()
            up_grad = add(dh[0][...], r.rdh[0]) + r.rdx[...].astype(F32)
            normed, factor = rms_parts(r.tok_in[:tile].astype(F32))
            d_n = up_grad * r.small[16:17, :].astype(F32)
            r.dtok[...] = r.dmid_in[...] + factor * (
                d_n - normed * jnp.mean(d_n * normed, axis=-1, keepdims=True)
            )

        def arrive():
            for copy in loads:
                copy.wait()

        first_step = 1
        done = first_step + n_steps
        order = [
            send_keys, None, None, sum_outx, None, sum_dkv, tile3, tile1, tile2, tile0, None, None,
            tiny_y, sum_cols, None, inputs_back, tiny_core, None, tiny_spread,
        ]
        steps = {done + i: fn for i, fn in enumerate(order) if fn is not None}
        steps.update({0: arrive, OUT_STEP: sum_out})
    else:
        tsum[0] = r.tiny[...].astype(BF)
        tiny_x()
        steps = {1: tiny_core, 2: tiny_spread}

    @pl.loop(0, items + ahead + (last + 1) * lag)
    def _(i):
        for fn, b, cond in (
            (begin, i, True),
            (prefix, i - ahead - lag * z, z > 0),
            (suffix, i - ahead - lag * (last - z), z < last),
            (forward, i - ahead - lag * (last + 1), True),
        ):
            @pl.when(within(b, cond))
            def _():
                fn(b)

        if fused:
            @pl.when((i >= first_step) & (i < done))
            def _():
                attention(i - first_step)

        for k, fn in steps.items():
            pl.when(i == k)(fn)

    tiny_end()

    @pl.loop(0, items)
    def _(b):
        one = rc.at[b]

        @pl.when(b < n_out)
        def _():
            remote(one, one, r.s_rc, b, peer_core).wait_send()

        @pl.when(z < last)
        def _():
            hop(pre, r.s_pre, b, peer_x).wait_send()

        @pl.when(z > 0)
        def _():
            hop(suf, r.s_suf, b, peer_x).wait_send()

        remote(one, one, r.s_far, b, peer_x).wait_send()

    remote(rc, rc, r.s_oth, 0, peer_core).wait()
    remote(rc, rc, r.s_faro, 0, peer_core).wait()
    pltpu.make_async_copy(rc, rc, r.s_out.at[0]).wait()
    tiny_swap(0, peer_x).wait_send()
    tiny_swap(1, peer_core).wait_send()
    for k in range(1, slots):
        remote(tsum.at[2], trecv.at[1 + k], s_tiny, 1 + k, other_z(k)).wait_send()
    if fused:
        for copy in (send_dkv, *send_out, send_dh3, send_dh1, send_dhx, send_cols, send_outx, send_tiny):
            copy.wait_send()
        for copy in moe_back:
            copy.wait()


def reduce_grads(gm, tiny, slots, shards, eo=None, cols=None, fused=None, small=None, tables=None, moes=None):
    count, _, ff, _ = gm.shape
    width = 2 * ff
    nb = 6 * count
    piece = ff // 4
    items = 2 * nb + 6
    hbm = pl.BlockSpec(memory_space=pl.ANY)
    vmem = pl.BlockSpec(memory_space=pltpu.VMEM)
    dma = pltpu.SemaphoreType.DMA
    args = dict(gm=(gm.reshape(nb, 2, 2, piece, ff), hbm), tiny=(tiny, vmem))
    outs = dict(
        gate=(jax.ShapeDtypeStruct((2 * count, width, ff), BF), hbm),
        up=(jax.ShapeDtypeStruct((2 * count, width, ff), BF), hbm),
        down=(jax.ShapeDtypeStruct((2 * count, ff, width), BF), hbm),
        out=(jax.ShapeDtypeStruct((ff, width), BF), hbm),
        qkv=(jax.ShapeDtypeStruct((ff, 2 * width), BF), hbm),
        tiny_out=(jax.ShapeDtypeStruct(tiny.shape[-2:], F32), vmem),
    )
    buf = pltpu.VMEM((items, piece, ff), BF)
    scratch = dict(
        mine=buf, rc=buf, pre=buf, suf=buf,
        tsum=pltpu.VMEM((3,) + tiny.shape[-2:], BF),
        trecv=pltpu.VMEM((slots + 1,) + tiny.shape[-2:], BF),
        s_tiny=dma((2, slots + 1)), s_mine=dma((items,)), s_out=dma((1,)),
    )
    each = dma((2, items))
    scratch.update(s_rc=each, s_pre=each, s_suf=each, s_far=each)
    scratch.update(s_oth=dma((2, 1)), s_faro=dma((2, 1)))
    if fused is None:
        args.update(
            eo=(eo.reshape(2, 2, piece, ff), hbm), cols=(cols.reshape(4, piece, ff), hbm)
        )
    else:
        inner = {}
        for k, v in fused.items():
            args[k] = (v, hbm)
            inner[k + "_in"] = pltpu.VMEM(v.shape, v.dtype)
        smem = pl.BlockSpec(memory_space=pltpu.SMEM)
        order, limit = tables
        args.update(
            small=(small, vmem), order=(order, smem), limit=(limit, smem),
            moe1=(moes[0], hbm), moe3=(moes[1], hbm),
        )
        outs.update({k: (jax.ShapeDtypeStruct(moes[0].shape, BF), hbm) for k in ("got1", "got3")})
        rows = args["dmid"][0].shape[0]
        keys = args["kv"][0].shape[0] // 2
        inner.update(gout_in=pltpu.VMEM((ff, width), BF))
        scratch.update(inner)
        outs.update(dtok=(jax.ShapeDtypeStruct((rows, width), F32), vmem))
        scratch.update(
            rdkv=pltpu.VMEM((keys, 256), BF), dkvs=pltpu.VMEM((keys, 256), BF),
            rout=pltpu.VMEM((2, ff, ff), BF),
            osend=pltpu.VMEM((ff, ff), BF), rox=pltpu.VMEM((ff, ff), BF),
            eo=pltpu.VMEM((2, 2, piece, ff), BF),
            dq_in=pltpu.VMEM((keys, 256), BF),
            dk=pltpu.VMEM((2 * keys, 128), F32), dv=pltpu.VMEM((2 * keys, 128), F32),
            qs=pltpu.VMEM((2 * rows, 128), BF), dos=pltpu.VMEM((2 * rows, 128), BF),
            delta=pltpu.VMEM((8, 2 * rows), F32), dqa=pltpu.VMEM((2 * rows, 128), F32),
            kpos=pltpu.VMEM((2 * keys, 1), jnp.int32), last=pltpu.VMEM((8, 8, 2 * rows), jnp.int32),
            s_in=dma((len(fused),)), s_moe=dma((2, 2)),
            rdh=pltpu.VMEM((2, rows, width), BF),
            dhx=pltpu.VMEM((rows, width), BF), rdx=pltpu.VMEM((rows, width), BF),
            acc=pltpu.VMEM((width, ff), F32), gn=pltpu.VMEM((8, width), F32),
            cbuf=pltpu.VMEM((width, ff), BF), rcol=pltpu.VMEM((ff, ff), BF),
            tbuf=pltpu.VMEM(tiny.shape, BF), rtiny=pltpu.VMEM(tiny.shape[-2:], BF),
            s_fg=dma((2, 9)),
        )
    names = tuple(args) + tuple(outs) + tuple(scratch)
    got = pl.pallas_call(
        functools.partial(
            reduce_kernel, names=names, slots=slots, shards=shards, fused=fused is not None
        ),
        in_specs=[v[1] for v in args.values()],
        out_specs=[v[1] for v in outs.values()],
        out_shape=[v[0] for v in outs.values()],
        scratch_shapes=list(scratch.values()),
        compiler_params=pltpu.CompilerParams(
            vmem_limit_bytes=67043328, collective_id=1, has_side_effects=True
        ),
        name="reduce_grads",
    )(*[v[0] for v in args.values()])
    return types.SimpleNamespace(**dict(zip(outs, got)))


def gather_rows(x):
    return lax.all_gather(x, "fsdp", axis=0, tiled=True)


def local(
    tokens, cotangent, lengths, order, routes, norm1, query_key_value_weight, w_out, norm2, router,
    w_gate, w_up, w_down,
):
    groups = lax.axis_size("seq")
    shards = lax.axis_size("fsdp")
    slots = lax.axis_size("dp")
    assert groups == 4
    seq, fsdp = lax.axis_index("seq"), lax.axis_index("fsdp")
    core, far = seq % 2, seq // 2
    rows, width = tokens.shape[1:]
    span = rows // 2
    x = tokens[0]
    limit = lengths[:1]
    n_experts = router.shape[1]
    owned = w_gate.shape[0]
    count = owned // 2

    own = lax.dynamic_slice_in_dim(order, (seq * shards + fsdp) * 2, 2)
    own_pos = (own[:, None] * span + jnp.arange(span, dtype=jnp.int32)[None, :]).reshape(-1)

    heads = QUERY_HEADS // groups
    qw, kw = heads * HEAD_WIDTH, KEY_VALUE_HEADS // groups * HEAD_WIDTH
    w3 = query_key_value_weight
    if shards == 2:
        tok, wcols, small, hidden_one, q, kv, cos, sin = front(
            order, x, w3, norm1, norm2, jnp.transpose(router)
        )
        tok, kv = tok.reshape(groups * rows, width), kv.reshape(-1, 256)
        w_out, cotangent, kv = lax.optimization_barrier((w_out, cotangent, kv))
    else:
        table = order.reshape(groups, shards, 2)
        relative = jnp.arange(groups, dtype=jnp.int32) ^ seq
        table = jnp.take(table, relative, axis=0)
        qtab = jnp.take(table, fsdp, axis=1).reshape(-1)
        ktab = jnp.transpose(table, (1, 0, 2)).reshape(-1)
        qpos = (qtab[:, None] * span + jnp.arange(span, dtype=jnp.int32)[None, :]).reshape(-1)
        small = jnp.concatenate(
            [jnp.transpose(router), norm1[None], norm2[None], jnp.zeros((14, norm1.shape[0]), BF)]
        )
        half = HEAD_WIDTH // 2
        freqs = jnp.exp(jnp.arange(half, dtype=F32) * (-2.0 * math.log(ROPE_BASE) / HEAD_WIDTH))
        angles = qpos.astype(F32)[:, None] * freqs[None, :]
        cos, sin = jnp.tile(jnp.cos(angles), (1, 4)), jnp.tile(jnp.sin(angles), (1, 4))
        wq = lax.dynamic_slice_in_dim(w3, seq * qw, qw, 1)
        wk = lax.dynamic_slice_in_dim(w3, QUERY_HEADS * HEAD_WIDTH + seq * kw, kw, 1)
        wv = lax.dynamic_slice_in_dim(
            w3, (QUERY_HEADS + KEY_VALUE_HEADS) * HEAD_WIDTH + seq * kw, kw, 1
        )
        wcols = gather_rows(jnp.concatenate([wq, wk, wv], axis=1))
        small = lax.all_gather(small, "fsdp", axis=1, tiled=True)
        tok = gather_seq(x).reshape(groups * rows, width)
        hidden_one, q, kv_own = project(tok, small[16:17].astype(F32), wcols, cos, sin, rows)
        kv = gather_fsdp(kv_own)
    gain_one, gain_two = small[16].astype(F32), small[17].astype(F32)
    route_rows = small[:n_experts]

    kb = 4 * span
    own_valid = (own_pos < limit[0])[:, None]
    masked_cot = jnp.where(own_valid, cotangent[0], jnp.zeros_like(cotangent[0]))
    if shards == 2:
        shared = w_out.shape[0] // 2
        wo_near = flip_y(lax.dynamic_slice_in_dim(w_out, core * shared, shared, 0))
        cot_y, cot_x = flip_y(masked_cot), flip_x(masked_cot)
    if shards == 2:
        body, tables = attend_short_kernel, (order, limit)
    else:
        body, tables = attend_kernel, (qtab, ktab, limit)
    attended, low, lse = attend(body, tables, q, kv, span, kb)
    inputs = x.astype(F32)
    if shards == 2:
        out = moe_layer(
            low, x, w_out, wo_near, small, routes[0], masked_cot, cot_y, cot_x, w_gate, w_up, w_down
        )
        moes = (out.moe1, out.moe3)
        d_heads = out.do.reshape(groups * rows, qw)
        middle, d_middle, grad_out, tiny = out.middle, out.dmid, out.gout, out.tiny
        weight_grads = out.grads.reshape(count, 6, w_gate.shape[2], -1)
    else:
        sent = low.reshape(groups, rows, qw)
        got = jnp.stack(swap_seq([sent[m] for m in range(groups)]))
        got = jnp.take(got, relative, axis=0)
        token_out = jnp.transpose(got, (1, 0, 2)).reshape(rows, groups * qw)
        out_full = gather_rows(w_out)

        middle = inputs + mm(token_out, out_full)
        normed_two, factor_two = rms_parts(middle)
        hidden_two = (normed_two * gain_two).astype(BF)
        logits = mm_nt(hidden_two, route_rows)
        chosen = jnp.any(
            routes[0][:, :, None] == jnp.arange(n_experts, dtype=jnp.int32)[None, None, :], axis=1
        )
        top = jnp.max(jnp.where(chosen, logits, NEG), axis=-1, keepdims=True)
        raised = jnp.where(chosen, jnp.exp(logits - top), 0.0)
        gates = raised / jnp.sum(raised, axis=-1, keepdims=True)

        def share(v):
            near = gather_rows(v)
            return jnp.concatenate([near, flip_x(near)])

        cot_all = share(masked_cot)
        extended = jnp.concatenate(
            [hidden_two, gates.astype(BF), jnp.zeros((rows, 128 - n_experts), BF)], axis=1
        )
        hid_all = share(extended)
        base = jnp.stack([far * count, fsdp * owned + far * count]).astype(jnp.int32)
        part = rows * 4
        moe_parts, dh_parts, weight_grads = [], [], None
        for i in range(hid_all.shape[0] // part):
            got = experts(
                base, count, hid_all[i * part : (i + 1) * part], cot_all[i * part : (i + 1) * part],
                w_gate, w_up, w_down, rows,
            )
            moe_parts.append(got[0])
            dh_parts.append(got[1])
            if weight_grads is None:
                weight_grads = got[2]
            else:
                weight_grads = (weight_grads.astype(F32) + got[2].astype(F32)).astype(BF)

        def give_back(parts):
            v = jnp.concatenate(parts) if len(parts) > 1 else parts[0]
            n = v.shape[0] // 2
            near = v[:n].astype(F32) + flip_x(v[n:]).astype(F32)
            return lax.psum_scatter(near.astype(BF), "fsdp", scatter_dimension=0, tiled=True).astype(F32)

        d_ext = give_back(dh_parts)
        d_gates = d_ext[:, width : width + n_experts]
        d_logits = (gates * (d_gates - jnp.sum(gates * d_gates, axis=-1, keepdims=True))).astype(BF)
        grad_router = mm_tn(hidden_two, d_logits)
        d_hidden = d_ext[:, :width] + mm(d_logits, route_rows)
        grad_norm2 = jnp.sum(d_hidden * normed_two, axis=0)
        d_n = d_hidden * gain_two
        d_middle = masked_cot.astype(F32) + factor_two * (
            d_n - normed_two * jnp.mean(d_n * normed_two, axis=-1, keepdims=True)
        )
        d_attn = d_middle.astype(BF)
        grad_out = mm_tn(token_out, d_attn).astype(BF)
        d_token_out = mm_nt(d_attn, out_full).astype(BF)
        d_heads = jnp.transpose(d_token_out.reshape(rows, groups, qw), (1, 0, 2))
        d_heads = jnp.take(d_heads, relative, axis=0)
        d_heads = jnp.concatenate(swap_seq([d_heads[m] for m in range(groups)]))
    block = w_gate.shape[2]
    shard_rows = width // shards

    def tiny_rows(first):
        return jnp.concatenate(
            [jnp.transpose(grad_router), first[None], grad_norm2[None], jnp.zeros((14, width), F32)]
        ).reshape(32, shards, shard_rows).transpose(1, 0, 2)

    if shards == 2:
        got = reduce_grads(
            weight_grads, tiny, slots, shards,
            fused=dict(
                q=q, kv=kv, do=d_heads, o=attended, lse=lse,
                tok=tok, h=hidden_one, wc=wcols, cos=cos, sin=sin, dmid=d_middle, gout=grad_out,
            ),
            small=small, tables=(order, limit), moes=moes,
        )
        d_inputs = got.dtok
    else:
        dq, dkv = attend_back(qtab, ktab, limit, q, kv, d_heads, attended, lse, span, kb)
        dh_one, grad_cols, grad_norm1 = project_back(
            tok, hidden_one, dq, scatter_fsdp(dkv), wcols, cos, sin, rows
        )
        dh_one = dh_one.reshape(groups, rows, width)
        near = dh_one[0::2].astype(F32) + flip_core(dh_one[1::2]).astype(F32)
        d_hidden_one = near[0] + flip_x(near[1].astype(BF)).astype(F32)
        normed_one, factor_one = rms_parts(inputs)
        d_n = d_hidden_one * gain_one
        d_inputs = d_middle + factor_one * (
            d_n - normed_one * jnp.mean(d_n * normed_one, axis=-1, keepdims=True)
        )

        def to_owner(g):
            part = lax.psum_scatter(g, "fsdp", scatter_dimension=0, tiled=True)
            return jnp.pad(part, ((0, block - part.shape[0]), (0, 0)))

        cols = to_owner(grad_cols)
        mine = to_owner(grad_out).reshape(block, 2, block)
        kept = lax.dynamic_index_in_dim(mine, far, 1, keepdims=False)
        sent = lax.dynamic_index_in_dim(mine, 1 - far, 1, keepdims=False)
        outs = (kept.astype(F32) + flip_x(sent).astype(F32)).astype(BF)
        tiny = tiny_rows(jnp.sum(grad_norm1, axis=0))
        tiny = lax.psum_scatter(tiny, "fsdp", scatter_dimension=0, tiled=True)[0]
        got = reduce_grads(weight_grads, tiny, slots, shards, eo=outs, cols=cols)
    parts = (middle, out.moe0, got.got1, out.got2, got.got3) if shards == 2 else ()
    wide, sums, tiny = widen(
        [got.gate, got.up, got.down, got.out, got.qkv, d_inputs], parts, got.tiny_out, n_experts
    )
    grad_gate, grad_up, grad_down, shard_out, shard_qkv, d_inputs = wide
    shard_out, shard_qkv = shard_out[:shard_rows], shard_qkv[:shard_rows]
    if shards == 2:
        layer_out = sums[0]
    else:
        layer_out = (middle + give_back(moe_parts)).astype(BF)
    return (
        layer_out[None], d_inputs[None], tiny[0], shard_qkv, shard_out, tiny[1], tiny[2],
        grad_gate, grad_up, grad_down,
    )


def solution(mesh):
    placed = (
        P("dp", ("seq", "fsdp"), None),
        P("dp", ("seq", "fsdp"), None),
        P("dp"),
        P(),
        P("dp", ("seq", "fsdp"), None),
        P("fsdp"),
        P("fsdp", None),
        P("fsdp", None),
        P("fsdp"),
        P("fsdp", None),
        P("fsdp", None, None),
        P("fsdp", None, None),
        P("fsdp", None, None),
    )
    return jax.shard_map(
        local,
        mesh=mesh,
        in_specs=placed,
        out_specs=(
            P("dp", ("seq", "fsdp"), None),
            P("dp", ("seq", "fsdp"), None),
            P("fsdp"),
            P("fsdp", None),
            P("fsdp", None),
            P("fsdp"),
            P("fsdp", None),
            P("fsdp", None, None),
            P("fsdp", None, None),
            P("fsdp", None, None),
        ),
        check_vma=False,
    )
```

```python
import functools
import math
import types

import jax
import jax.numpy as jnp
import numpy as np
from jax import lax
from jax.experimental import pallas as pl
from jax.experimental.pallas import tpu as pltpu
from jax.sharding import PartitionSpec as P

QUERY_HEADS = 16
KEY_VALUE_HEADS = 8
HEAD_WIDTH = 64
TOPK = 8

EPS = 1e-06
ROPE_BASE = 10000.0
LOG2E = math.log2(math.e)
NEG = -1e30
BF = jnp.bfloat16
F32 = jnp.float32
VMEM_LIMIT = 60 * 1024 * 1024
OUT_STEP = 6

NT_DIMS = (((1,), (1,)), ((), ()))
TN_DIMS = (((0,), (0,)), ((), ()))


def mm(a, b):
    return jnp.dot(a, b, preferred_element_type=F32)


def mm_nt(a, b):
    return lax.dot_general(a, b, NT_DIMS, preferred_element_type=F32)


def mm_tn(a, b):
    return lax.dot_general(a, b, TN_DIMS, preferred_element_type=F32)


def params(**kw):
    return pltpu.CompilerParams(vmem_limit_bytes=VMEM_LIMIT, **kw)


def whole(shape):
    return pl.BlockSpec(shape, lambda *_: (0,) * len(shape))


def rms_parts(x):
    factor = lax.rsqrt(jnp.mean(x * x, axis=-1, keepdims=True) + EPS)
    return x * factor, factor


def qkv_kernel(tok_ref, gain_ref, w_ref, cos_ref, sin_ref, h_ref, q_ref, kv_ref):
    normed, _ = rms_parts(tok_ref[...].astype(F32))
    h = (normed * gain_ref[...]).astype(BF)
    h_ref[...] = h
    proj = mm(h, w_ref[...])
    cos, sin = cos_ref[...], sin_ref[...]
    low_half = lax.broadcasted_iota(jnp.int32, cos.shape, 1) % HEAD_WIDTH < HEAD_WIDTH // 2
    half = HEAD_WIDTH // 2
    for t in range(3):
        w = proj[:, t * 128 : (t + 1) * 128]
        rot = jnp.where(low_half, -pltpu.roll(w, 128 - half, 1), pltpu.roll(w, half, 1))
        out = (w * cos + rot * sin).astype(BF)
        if t < 2:
            q_ref[:, t * 128 : (t + 1) * 128] = out
        else:
            kv_ref[:, :128] = out
    kv_ref[:, 128:] = proj[:, 384:].astype(BF)


def project(tok, gain, w, cos, sin, tile):
    rows, width = tok.shape
    return pl.pallas_call(
        qkv_kernel,
        grid=(rows // tile,),
        in_specs=[
            pl.BlockSpec((tile, width), lambda i: (i, 0)),
            whole((1, width)),
            whole(w.shape),
            pl.BlockSpec((tile, 128), lambda i: (i, 0)),
            pl.BlockSpec((tile, 128), lambda i: (i, 0)),
        ],
        out_specs=[
            pl.BlockSpec((tile, width), lambda i: (i, 0)),
            pl.BlockSpec((tile, 256), lambda i: (i, 0)),
            pl.BlockSpec((tile, 256), lambda i: (i, 0)),
        ],
        out_shape=[
            jax.ShapeDtypeStruct((rows, width), BF),
            jax.ShapeDtypeStruct((rows, 256), BF),
            jax.ShapeDtypeStruct((rows, 256), BF),
        ],
        compiler_params=params(),
        name="project",
    )(tok, gain, w, cos, sin)


MESH = pl.DeviceIdType.MESH


def rope_rows(w, cos, sin):
    half = HEAD_WIDTH // 2
    low_half = lax.broadcasted_iota(jnp.int32, w.shape, 1) % HEAD_WIDTH < half
    rot = jnp.where(low_half, -pltpu.roll(w, 128 - half, 1), pltpu.roll(w, half, 1))
    return w * cos + rot * sin


def span_at(order, j):
    s, f = lax.axis_index("seq"), lax.axis_index("fsdp")
    x, c = s // 2, s % 2
    a, b, away = j % 8 // 4, j % 4 // 2, j // 8
    q = (x + a - 2 * x * a) * 2 + c + b - 2 * c * b
    return order[(q * 2 + f + away - 2 * f * away) * 2 + j % 2]


def front_kernel(
    order, tok, w3, norm1, norm2, router, rtab, stab, tok_out, wc_out, small_all, h_out, q, kv, cos_out, sin_out,
    small, tok_all, wc, h, cos, sin, s_tok, s_w, s_own, s_kv, s_end
):
    z, s, f = lax.axis_index("dp"), lax.axis_index("seq"), lax.axis_index("fsdp")
    core = s % 2
    peer_core = (z, s + 1 - 2 * core, f)
    peer_x = (z, (s + 2) % 4, f)
    peer_y = (z, s, 1 - f)
    rows, width = tok.shape
    part = small.shape[1]

    barrier = pltpu.get_barrier_semaphore()
    for dev in (peer_core, peer_x, peer_y):
        pl.semaphore_signal(barrier, inc=1, device_id=dev, device_id_type=MESH)

    def remote(src, dst, sems, b, dev):
        return pltpu.make_async_remote_copy(
            src_ref=src, dst_ref=dst, send_sem=sems.at[0, b], recv_sem=sems.at[1, b],
            device_id=dev, device_id_type=MESH,
        )

    own_rows = pl.ds(pl.multiple_of(f * part, part), part)
    pieces = []
    for first, n, to in ((width, 128, 256), (width + width // 2, 128, 384), (0, 256, 0)):
        src = w3.at[:, pl.ds(pl.multiple_of(first + s * n, 128), n)]
        pieces.append((src, wc.at[own_rows, pl.ds(to, n)]))
    local = [pltpu.make_async_copy(a, b, s_own.at[i]) for i, (a, b) in enumerate(pieces)]
    for copy in local:
        copy.start()
    n_exp = router.shape[0]
    row = lax.broadcasted_iota(jnp.int32, (small.shape[0] - n_exp, part), 0)
    gains = [v[...].astype(F32).reshape(1, part) for v in (norm1, norm2)]
    small[:n_exp, :] = router[...]
    small[n_exp:, :] = jnp.where(row == 0, gains[0], jnp.where(row == 1, gains[1], 0.0)).astype(BF)
    small_all[:, own_rows] = small[...]
    tok_all[0] = tok[...]
    pl.semaphore_wait(barrier, 3)
    over = remote(tok, tok_all.at[2], s_tok, 1, peer_x)
    near = remote(tok, tok_all.at[1], s_tok, 0, peer_core)
    onward = remote(tok_all.at[2], tok_all.at[3], s_tok, 2, peer_core)
    weights = [remote(a, b, s_w, i, peer_y) for i, (a, b) in enumerate(pieces)]
    weights.insert(0, remote(small, small_all.at[:, own_rows], s_w, 3, peer_y))
    over.start()
    for copy in weights:
        copy.start()
    near.start()
    for copy in local:
        copy.wait()
    for copy in weights[:3]:
        copy.wait_recv()
    gain = small_all[16:17, :].astype(F32)

    def kv_copy(t):
        at = pl.ds(pl.multiple_of(t * rows, rows), rows)
        return remote(kv.at[0, at], kv.at[1, at], s_kv, t, peer_y)

    ends = []
    span = rows // 2
    for k in range(8):
        at = pl.ds(k * span, span)
        row = pl.ds(span_at(order, k), 1)
        c, n = stab[0, row, :], stab[1, row, :]
        cos[at, :] = rtab[0] * c - rtab[1] * n
        sin[at, :] = rtab[1] * c + rtab[0] * n
    for i, (src, dst) in enumerate(((cos, cos_out), (sin, sin_out))):
        ends.append(pltpu.make_async_copy(src, dst, s_end.at[1 + i]))
        ends[-1].start()

    def end(t):
        at = pl.ds(pl.multiple_of(t * rows, rows), rows)
        return [
            pltpu.make_async_copy(tok_all.at[t], tok_out.at[t], s_end.at[3 + t]),
            pltpu.make_async_copy(h.at[at], h_out.at[at], s_end.at[7 + t]),
        ]

    @pl.loop(0, 4)
    def _(t):
        pl.when(t == 1)(near.wait_recv)

        @pl.when(t == 2)
        def _():
            over.wait_recv()
            onward.start()

        pl.when(t == 3)(onward.wait_recv)
        at = pl.ds(pl.multiple_of(t * rows, rows), rows)
        normed, _ = rms_parts(tok_all[t].astype(F32))
        hidden = (normed * gain).astype(BF)
        h[at, :] = hidden
        proj = mm(hidden, wc[:, 256:])
        kv[0, at, :128] = rope_rows(proj[:, :128], cos[at, :], sin[at, :]).astype(BF)
        kv[0, at, 128:] = proj[:, 128:].astype(BF)
        kv_copy(t).start()
        for copy in end(t):
            copy.start()

    weights[3].wait_recv()
    ends.append(pltpu.make_async_copy(wc, wc_out, s_end.at[0]))
    ends[-1].start()

    @pl.loop(0, 4)
    def _(t):
        at = pl.ds(pl.multiple_of(t * rows, rows), rows)
        proj = mm(h[at, :], wc[:, :256])
        for k in range(2):
            w = proj[:, k * 128 : (k + 1) * 128]
            q[at, k * 128 : (k + 1) * 128] = rope_rows(w, cos[at, :], sin[at, :]).astype(BF)

    for t in range(4):
        ends.extend(end(t))
    for t in range(4):
        kv_copy(t).wait()
    for copy in ends:
        copy.wait()
    for copy in (over, near, onward, *weights):
        copy.wait_send()


def front(order, tok, w3, norm1, norm2, router):
    rows, width = tok.shape
    n_spans = order.shape[0]
    span, half = rows // 2, HEAD_WIDTH // 2
    freqs = np.exp(np.arange(half) * (-2.0 * math.log(ROPE_BASE) / HEAD_WIDTH)).astype(np.float32)

    def table(positions):
        angles = np.tile(positions[:, None].astype(np.float64) * freqs[None, :], (1, 4))
        return jnp.asarray(np.stack([np.cos(angles), np.sin(angles)]), F32)

    rtab, stab = table(np.arange(span)), table(np.arange(n_spans) * span)
    vmem = pl.BlockSpec(memory_space=pltpu.VMEM)
    hbm = pl.BlockSpec(memory_space=pl.ANY)
    dma = pltpu.SemaphoreType.DMA
    shape = jax.ShapeDtypeStruct
    return pl.pallas_call(
        front_kernel,
        in_specs=[pl.BlockSpec(memory_space=pltpu.SMEM), vmem, hbm, vmem, vmem, vmem, vmem, vmem],
        out_specs=[hbm, hbm, vmem, hbm, vmem, vmem, hbm, hbm],
        out_shape=[
            shape((4, rows, width), BF),
            shape((width, 512), BF),
            shape((32, width), BF),
            shape((4 * rows, width), BF),
            shape((4 * rows, 256), BF),
            shape((2, 4 * rows, 256), BF),
            shape((4 * rows, 128), F32),
            shape((4 * rows, 128), F32),
        ],
        scratch_shapes=[
            pltpu.VMEM((32, norm1.shape[0]), BF),
            pltpu.VMEM((4, rows, width), BF), pltpu.VMEM((width, 512), BF),
            pltpu.VMEM((4 * rows, width), BF),
            pltpu.VMEM((4 * rows, 128), F32), pltpu.VMEM((4 * rows, 128), F32),
            dma((2, 3)), dma((2, 4)), dma((3,)), dma((2, 4)), dma((11,)),
        ],
        compiler_params=params(collective_id=2, has_side_effects=True),
        name="front",
    )(order, tok, w3, norm1, norm2, router, rtab, stab)


def widen_kernel(*refs, wide, parts):
    n = wide + parts + 1
    ins, outs = refs[:n], refs[n:]
    for a, b in zip(ins[:wide], outs[:wide]):
        b[...] = a[...].astype(F32)
    if parts:
        total = ins[wide][...].astype(F32)
        for part in ins[wide + 1 : wide + parts]:
            total = total + part[...].astype(F32)
        outs[wide][...] = total.astype(BF)
    tiny, (one, two, router) = ins[-1], outs[-3:]

    @pl.when(pl.program_id(0) == 0)
    def _():
        one[...] = tiny[16:17, :]
        two[...] = tiny[17:18, :]
        router[...] = tiny[: router.shape[0], :]


def widen(arrays, parts, tiny, n_experts):
    flat = [a.reshape(-1, a.shape[-1]) for a in arrays]
    steps = 4
    cols = tiny.shape[1]
    block = lambda a: pl.BlockSpec((a.shape[0] // steps, a.shape[1]), lambda i: (i, 0))
    shape = jax.ShapeDtypeStruct
    smalls = [(1, cols), (1, cols), (n_experts, cols)]
    sums = [shape(p.shape, BF) for p in parts[:1]]
    got = pl.pallas_call(
        functools.partial(widen_kernel, wide=len(flat), parts=len(parts)),
        grid=(steps,),
        in_specs=[block(a) for a in (*flat, *parts)] + [whole(tiny.shape)],
        out_specs=[block(a) for a in (*flat, *sums)] + [whole(v) for v in smalls],
        out_shape=[shape(a.shape, F32) for a in flat] + sums + [shape(v, F32) for v in smalls],
        compiler_params=params(),
        name="widen",
    )(*flat, *parts, tiny)
    n = len(arrays)
    wide = [g.reshape(a.shape) for g, a in zip(got, arrays)]
    return wide, got[n : n + len(sums)], [got[-3][0], got[-2][0], jnp.transpose(got[-1])]


def project_back_kernel(
    tok_ref, h_ref, dq_ref, dkv_ref, w_ref, cos_ref, sin_ref, dh_ref, gw_ref, gn_ref, acc
):
    step = pl.program_id(0)

    @pl.when(step == 0)
    def _():
        acc[...] = jnp.zeros_like(acc)
        gn_ref[...] = jnp.zeros_like(gn_ref)

    cos, sin = cos_ref[...], sin_ref[...]
    half = HEAD_WIDTH // 2
    low_half = lax.broadcasted_iota(jnp.int32, cos.shape, 1) % HEAD_WIDTH < half
    parts = []
    for t in range(3):
        w = dq_ref[:, t * 128 : (t + 1) * 128] if t < 2 else dkv_ref[:, :128]
        w = w.astype(F32)
        y = w * sin
        rot = jnp.where(low_half, pltpu.roll(y, 128 - half, 1), -pltpu.roll(y, half, 1))
        parts.append((w * cos + rot).astype(BF))
    parts.append(dkv_ref[:, 128:].astype(BF))
    dproj = jnp.concatenate(parts, axis=1)
    acc[...] += mm_tn(h_ref[...], dproj)
    dh = mm_nt(dproj, w_ref[...])
    dh_ref[...] = dh.astype(BF)
    normed, _ = rms_parts(tok_ref[...].astype(F32))
    gn_ref[...] += jnp.sum((dh * normed).reshape(-1, 8, dh.shape[1]), axis=0)

    @pl.when(step == pl.num_programs(0) - 1)
    def _():
        gw_ref[...] = acc[...].astype(BF)


def project_back(tok, h, dq, dkv, w, cos, sin, tile):
    rows, width = tok.shape
    row = lambda n: pl.BlockSpec((tile, n), lambda i: (i, 0))
    return pl.pallas_call(
        project_back_kernel,
        grid=(rows // tile,),
        in_specs=[row(width), row(width), row(256), row(256), whole(w.shape), row(128), row(128)],
        out_specs=[row(width), whole(w.shape), whole((8, width))],
        out_shape=[
            jax.ShapeDtypeStruct((rows, width), BF),
            jax.ShapeDtypeStruct(w.shape, BF),
            jax.ShapeDtypeStruct((8, width), F32),
        ],
        scratch_shapes=[pltpu.VMEM(w.shape, F32)],
        compiler_params=params(),
        name="project_back",
    )(tok, h, dq, dkv, w, cos, sin)


def stack_heads(a, b, dtype=BF):
    a, b = a.astype(F32), b.astype(F32)
    low = lax.broadcasted_iota(jnp.int32, a.shape, 1) < HEAD_WIDTH
    turn = lambda v: pltpu.roll(v, HEAD_WIDTH, 1)
    rows = [
        jnp.where(low, a, 0.0), jnp.where(low, turn(a), 0.0),
        jnp.where(low, 0.0, turn(b)), jnp.where(low, 0.0, b),
    ]
    return jnp.concatenate(rows, axis=0).astype(dtype)


def unstack_heads(x):
    n = x.shape[0] // 4
    low = lax.broadcasted_iota(jnp.int32, (n, 128), 1) < HEAD_WIDTH
    turn = lambda v: pltpu.roll(v, HEAD_WIDTH, 1)
    return (
        jnp.where(low, x[:n], turn(x[n : 2 * n])),
        jnp.where(low, turn(x[2 * n : 3 * n]), x[3 * n :]),
    )


def block_counts(span_id, limit, span, kb):
    first = span_id * span
    seen = (first + span - 1) // kb + 1
    blocks = jnp.minimum(seen, (limit + kb - 1) // kb)
    full = jnp.minimum(first + 1, limit) // kb
    return jnp.minimum(full, blocks), blocks


def sort_spans(ktab_ref, src, dst, lanes, span, count):
    @pl.loop(0, count)
    def _(j):
        to = pl.multiple_of(ktab_ref[j] * span, span)
        dst[pl.ds(to, span), :] = src[pl.ds(pl.multiple_of(j * span, span), span), lanes]


def attend_kernel(
    qtab_ref, ktab_ref, len_ref, q_ref, kv_ref, o_ref, low_ref, lse_ref, ks, vs, *, span, kb
):
    step = pl.program_id(0)
    count = ks.shape[0] // span

    @pl.when(step == 0)
    def _():
        sort_spans(ktab_ref, kv_ref, ks, slice(0, 128), span, count)
        sort_spans(ktab_ref, kv_ref, vs, slice(128, 256), span, count)

    q = stack_heads(q_ref[:, :128], q_ref[:, 128:])
    rows = 4 * span
    limit = len_ref[0]
    span_id = qtab_ref[step]
    full, blocks = block_counts(span_id, limit, span, kb)
    qpos = span_id * span + lax.broadcasted_iota(jnp.int32, (rows, kb), 0) % span
    col = lax.broadcasted_iota(jnp.int32, (rows, kb), 1)
    last = jnp.minimum(qpos, limit - 1)

    def body(masked, i, carry):
        top, total, acc = carry
        at = pl.multiple_of(i * kb, kb)
        s = mm_nt(q, ks[pl.ds(at, kb), :]) * (HEAD_WIDTH**-0.5 * LOG2E)
        if masked:
            s = jnp.where(col + i * kb <= last, s, NEG)
        new = jnp.maximum(top, jnp.max(s, axis=1, keepdims=True))
        fade = jnp.exp2(top - new)
        p = jnp.exp2(s - new)
        total = total * fade + jnp.sum(p, axis=1, keepdims=True)
        acc = acc * fade + mm(p.astype(BF), vs[pl.ds(at, kb), :])
        return new, total, acc

    carry = (
        jnp.full((rows, 1), NEG, F32),
        jnp.zeros((rows, 1), F32),
        jnp.zeros((rows, 128), F32),
    )
    carry = lax.fori_loop(0, full, functools.partial(body, False), carry)
    top, total, acc = lax.fori_loop(full, blocks, functools.partial(body, True), carry)
    a, b = unstack_heads(acc / total)
    o_ref[:, :128] = a
    o_ref[:, 128:] = b
    low_ref[:, :128] = a.astype(BF)
    low_ref[:, 128:] = b.astype(BF)
    lse = jnp.broadcast_to(top + jnp.log2(total), (rows, 128))
    lse_ref[0] = jnp.transpose(lse)[:8]


def attend_short_kernel(
    order_ref, len_ref, q_ref, kv_ref, o_ref, low_ref, lse_ref, ks, vs, *, span, kb
):
    step = pl.program_id(0)
    count = ks.shape[0] // span

    @pl.when(step == 0)
    def _():
        @pl.loop(0, count)
        def _(j):
            to = pl.ds(pl.multiple_of(span_at(order_ref, j) * span, span), span)
            at = pl.ds(pl.multiple_of(j * span, span), span)
            ks[to, :] = kv_ref[at, :128]
            vs[to, :] = kv_ref[at, 128:]

    q = stack_heads(q_ref[:, :128], q_ref[:, 128:])
    rows = 2 * span
    limit = len_ref[0]
    span_id = span_at(order_ref, step)
    _, blocks = block_counts(span_id, limit, span, kb)
    qpos = span_id * span + lax.broadcasted_iota(jnp.int32, (rows, kb), 0) % span
    last = jnp.minimum(qpos, limit - 1)
    col = lax.broadcasted_iota(jnp.int32, (rows, kb), 1)

    def run(n):
        outs, sums = [], []
        for g in range(2):
            part = q[g * rows : (g + 1) * rows]
            scores = []
            for i in range(n):
                v = mm_nt(part, ks[i * kb : (i + 1) * kb, :]) * (HEAD_WIDTH**-0.5 * LOG2E)
                if i == n - 1:
                    v = jnp.where(col + i * kb <= last, v, NEG)
                scores.append(v)
            tops = [jnp.max(v, axis=1, keepdims=True) for v in scores]
            top = functools.reduce(jnp.maximum, tops)
            total = jnp.zeros((rows, 1), F32)
            acc = jnp.zeros((rows, 128), F32)
            for i in range(n):
                p = jnp.exp2(scores[i] - top)
                total = total + jnp.sum(p, axis=1, keepdims=True)
                acc = acc + mm(p.astype(BF), vs[i * kb : (i + 1) * kb, :])
            outs.append(acc / total)
            sums.append(top + jnp.log2(total))
        a, b = unstack_heads(jnp.concatenate(outs, axis=0))
        o_ref[:, :128] = a
        o_ref[:, 128:] = b
        low_ref[:, :128] = a.astype(BF)
        low_ref[:, 128:] = b.astype(BF)
        lse = jnp.broadcast_to(jnp.concatenate(sums, axis=0), (2 * rows, 128))
        lse_ref[0] = jnp.transpose(lse)[:8]

    for n in range(1, ks.shape[0] // kb + 1):
        pl.when(blocks == n)(functools.partial(run, n))


def attend(body, tables, q, kv, span, kb):
    steps, keys = q.shape[0] // span, kv.shape[0]
    return pl.pallas_call(
        functools.partial(body, span=span, kb=kb),
        grid_spec=pltpu.PrefetchScalarGridSpec(
            num_scalar_prefetch=len(tables),
            grid=(steps,),
            in_specs=[pl.BlockSpec((span, 256), lambda i, *_: (i, 0)), whole(kv.shape)],
            out_specs=[
                pl.BlockSpec((span, 256), lambda i, *_: (i, 0)),
                pl.BlockSpec((span, 256), lambda i, *_: (i, 0)),
                pl.BlockSpec((1, 8, 4 * span), lambda i, *_: (i, 0, 0)),
            ],
            scratch_shapes=[pltpu.VMEM((keys, 128), BF), pltpu.VMEM((keys, 128), BF)],
        ),
        out_shape=[
            jax.ShapeDtypeStruct((q.shape[0], 256), F32),
            jax.ShapeDtypeStruct((q.shape[0], 256), BF),
            jax.ShapeDtypeStruct((steps, 8, 4 * span), F32),
        ],
        compiler_params=pltpu.CompilerParams(vmem_limit_bytes=67043328),
        name="attend",
    )(*tables, q, kv)


def attend_back_kernel(
    qtab_ref, ktab_ref, len_ref, q_ref, kv_ref, do_ref, o_ref, lse_ref, dq_ref, dkv_ref,
    ks, vs, dk, dv, *, span, kb,
):
    step = pl.program_id(0)
    count = ks.shape[0] // span
    scale = HEAD_WIDTH**-0.5

    @pl.when(step == 0)
    def _():
        sort_spans(ktab_ref, kv_ref, ks, slice(0, 128), span, count)
        sort_spans(ktab_ref, kv_ref, vs, slice(128, 256), span, count)
        dk[...] = jnp.zeros_like(dk)
        dv[...] = jnp.zeros_like(dv)

    q = stack_heads(q_ref[:, :128], q_ref[:, 128:])
    do = stack_heads(do_ref[:, :128], do_ref[:, 128:])
    rows = 4 * span
    inner = do.astype(F32) * stack_heads(o_ref[:, :128], o_ref[:, 128:], F32)
    delta = jnp.sum(jnp.transpose(inner), axis=0, keepdims=True)
    lse = lse_ref[0, :1]
    limit = len_ref[0]
    span_id = qtab_ref[step]
    full, blocks = block_counts(span_id, limit, span, kb)
    blocks = jnp.where(span_id * span < limit, blocks, 0)
    full = jnp.minimum(full, blocks)
    qpos = span_id * span + lax.broadcasted_iota(jnp.int32, (kb, rows), 1) % span
    key = lax.broadcasted_iota(jnp.int32, (kb, rows), 0)
    last = jnp.minimum(qpos, limit - 1)

    def body(masked, i, dq):
        at = pl.ds(pl.multiple_of(i * kb, kb), kb)
        k, v = ks[at, :], vs[at, :]
        s = mm_nt(k, q) * (scale * LOG2E)
        p = jnp.exp2(s - lse)
        if masked:
            p = jnp.where(key + i * kb <= last, p, 0.0)
        dp = mm_nt(v, do)
        ds = (p * (dp - delta)).astype(BF)
        dk[at, :] += mm(ds, q)
        dv[at, :] += mm(p.astype(BF), do)
        return dq + mm_tn(ds, k)

    dq = jnp.zeros((rows, 128), F32)
    dq = lax.fori_loop(0, full, functools.partial(body, False), dq)
    dq = lax.fori_loop(full, blocks, functools.partial(body, True), dq)
    a, b = unstack_heads(dq * scale)
    dq_ref[:, :128] = a.astype(BF)
    dq_ref[:, 128:] = b.astype(BF)

    @pl.when(step == pl.num_programs(0) - 1)
    def _():
        @pl.loop(0, count)
        def _(j):
            at = pl.ds(pl.multiple_of(ktab_ref[j] * span, span), span)
            to = pl.ds(pl.multiple_of(j * span, span), span)
            dkv_ref[to, :128] = (dk[at, :] * scale).astype(BF)
            dkv_ref[to, 128:] = dv[at, :].astype(BF)


def attend_back(qtab, ktab, limit, q, kv, do, o, lse, span, kb):
    steps, keys = q.shape[0] // span, kv.shape[0]
    row = pl.BlockSpec((span, 256), lambda i, *_: (i, 0))
    return pl.pallas_call(
        functools.partial(attend_back_kernel, span=span, kb=kb),
        grid_spec=pltpu.PrefetchScalarGridSpec(
            num_scalar_prefetch=3,
            grid=(steps,),
            in_specs=[
                row, whole(kv.shape), row, row,
                pl.BlockSpec((1, 8, 4 * span), lambda i, *_: (i, 0, 0)),
            ],
            out_specs=[row, whole(kv.shape)],
            scratch_shapes=[
                pltpu.VMEM((keys, 128), BF), pltpu.VMEM((keys, 128), BF),
                pltpu.VMEM((keys, 128), F32), pltpu.VMEM((keys, 128), F32),
            ],
        ),
        out_shape=[
            jax.ShapeDtypeStruct((q.shape[0], 256), BF),
            jax.ShapeDtypeStruct(kv.shape, BF),
        ],
        compiler_params=params(),
        name="attend_back",
    )(qtab, ktab, limit, q, kv, do, o, lse)


def experts_kernel(
    base_ref, h_ref, c_ref, wg_ref, wu_ref, wd_ref, moe_ref, dh_ref, grad_ref,
    moe, dh, dgates, s_act, s_gate, s_up, *, tile,
):
    step = pl.program_id(0)
    width = c_ref.shape[1]
    expert = base_ref[1] + step
    wg, wu, wd = wg_ref[0], wu_ref[0], wd_ref[0]

    @pl.when(step == 0)
    def _():
        moe[...] = jnp.zeros_like(moe)
        dh[...] = jnp.zeros_like(dh)
        dgates[...] = jnp.zeros_like(dgates)

    @pl.loop(0, moe.shape[0] // tile)
    def _(t):
        at = pl.ds(pl.multiple_of(t * tile, tile), tile)
        h, c = h_ref[at, :width], c_ref[at, :]
        lane = lax.broadcasted_iota(jnp.int32, (tile, 128), 1)
        mine = lane == expert
        gate = jnp.sum(
            jnp.where(mine, h_ref[at, width:].astype(F32), 0.0), axis=1, keepdims=True
        )
        g, u, z = mm(h, wg), mm(h, wu), mm_nt(c, wd)
        sig = jax.nn.sigmoid(g)
        silu = g * sig
        act = silu * u
        dgates[at, :] += jnp.where(mine, jnp.sum(act * z, axis=1, keepdims=True), 0.0)
        act = (act * gate).astype(BF)
        dact = z * gate
        dgate = (dact * u * sig * (1.0 + g * (1.0 - sig))).astype(BF)
        dup = (dact * silu).astype(BF)
        s_act[at, :] = act
        s_gate[at, :] = dgate
        s_up[at, :] = dup
        moe[at, :] += mm(act, wd)
        dh[at, :] += mm_nt(dgate, wg) + mm_nt(dup, wu)

    block = grad_ref.shape[2]
    for i in range(2):
        at = slice(i * block, (i + 1) * block)
        grad_ref[0, i] = mm_tn(h_ref[:, at], s_gate[...]).astype(BF)
        grad_ref[0, 2 + i] = mm_tn(h_ref[:, at], s_up[...]).astype(BF)
        grad_ref[0, 4 + i] = mm_tn(s_act[...], c_ref[:, at]).astype(BF)

    @pl.when(step == pl.num_programs(0) - 1)
    def _():
        moe_ref[...] = moe[...].astype(BF)
        dh_ref[:, :width] = dh[...].astype(BF)
        dh_ref[:, width:] = dgates[...].astype(BF)


def experts(base, count, h, c, wg, wu, wd, tile):
    rows, width = c.shape
    ff = wg.shape[2]
    pick = lambda shape: pl.BlockSpec((1,) + shape, lambda e, s: (s[0] + e, 0, 0))
    return pl.pallas_call(
        functools.partial(experts_kernel, tile=tile),
        grid_spec=pltpu.PrefetchScalarGridSpec(
            num_scalar_prefetch=1,
            grid=(count,),
            in_specs=[
                whole(h.shape), whole(c.shape),
                pick((width, ff)), pick((width, ff)), pick((ff, width)),
            ],
            out_specs=[
                whole(c.shape), whole(h.shape),
                pl.BlockSpec((1, 6, ff, ff), lambda e, s: (e, 0, 0, 0)),
            ],
            scratch_shapes=[
                pltpu.VMEM((rows, width), F32), pltpu.VMEM((rows, width), F32),
                pltpu.VMEM((rows, 128), F32),
                pltpu.VMEM((rows, ff), BF), pltpu.VMEM((rows, ff), BF), pltpu.VMEM((rows, ff), BF),
            ],
        ),
        out_shape=[
            jax.ShapeDtypeStruct(c.shape, BF),
            jax.ShapeDtypeStruct(h.shape, BF),
            jax.ShapeDtypeStruct((count, 6, ff, ff), BF),
        ],
        compiler_params=params(),
        name="experts",
    )(base, h, c, wg, wu, wd)


def moe_kernel(*refs, names, topk, count):
    r = types.SimpleNamespace(**dict(zip(names, refs)))
    z, s, f = lax.axis_index("dp"), lax.axis_index("seq"), lax.axis_index("fsdp")
    core, x = s % 2, s // 2
    flip = 1 - 2 * core
    seqs = (s, s + flip, (s + 2) % 4, (s + 2) % 4 + flip)
    peers = [(z, q, f) for q in seqs]
    peer_x, peer_y = peers[2], (z, s, 1 - f)
    att, att_in, tout, hx, cots = r.att, r.att_in, r.tout, r.hx, r.cots
    rows, width = tout.shape
    n = rows // 2
    ext = hx.shape[1]
    ff = r.wgs.shape[2]
    owned = r.wg.shape[0]

    barrier = pltpu.get_barrier_semaphore()
    for dev in (*peers[1:], peer_y):
        pl.semaphore_signal(barrier, inc=1, device_id=dev, device_id_type=MESH)

    def remote(src, dst, sems, b, dev):
        return pltpu.make_async_remote_copy(
            src_ref=src, dst_ref=dst, send_sem=sems.at[0, b], recv_sem=sems.at[1, b],
            device_id=dev, device_id_type=MESH,
        )

    def block(t):
        return pl.ds(pl.multiple_of(t * rows, rows), rows)

    def rows_x(i):
        return pl.ds(pl.multiple_of(rows + 2 * i * rows, n), n)

    def rows_y(i):
        return pl.ds(pl.multiple_of(rows + n + 2 * i * rows, n), n)

    load_cots = [pltpu.make_async_copy(r.cot, cots.at[block(0)], r.s_cot.at[0])]
    for i in range(2):
        at = pl.ds(i * n, n)
        load_cots += [
            pltpu.make_async_copy(r.cot_x.at[at], cots.at[rows_x(i)], r.s_cot.at[1 + i]),
            pltpu.make_async_copy(r.cot_y.at[at], cots.at[rows_y(i)], r.s_cot.at[3 + i]),
        ]
    for copy in load_cots:
        copy.start()

    def load_weights(e, act):
        for i, (src, dst) in enumerate(((r.wg, r.wgs), (r.wu, r.wus), (r.wd, r.wds))):
            act(pltpu.make_async_copy(src.at[x * count + e], dst.at[e], r.s_w.at[i, e]))

    @pl.loop(0, count)
    def _(e):
        load_weights(e, lambda copy: copy.start())

    pl.semaphore_wait(barrier, 4)
    def head(m, i):
        at = pl.ds(pl.multiple_of(i * n, n), n)
        return remote(att.at[m, at], att_in.at[m, at], r.s_att, 2 * m + i, peers[m])

    heads = [head(m, i) for i in range(2) for m in (3, 2, 1)]
    for copy in heads:
        copy.start()
    diag = [
        remote(r.cot_x.at[pl.ds(0, n)], cots.at[pl.ds(2 * rows, n)], r.s_diag, 0, peer_y),
        remote(r.cot_x.at[pl.ds(n, n)], cots.at[pl.ds(2 * rows + n, n)], r.s_diag, 1, peer_y),
    ]
    wo_rows = pl.ds(pl.multiple_of(core * (ff // 2), ff // 2), ff // 2)
    wo_there = r.wo_there
    wo_copy = pltpu.make_async_copy(r.wo_near, wo_there.at[wo_rows], r.s_wo.at[0])
    wo_share = remote(r.wo_near, wo_there.at[wo_rows], r.s_diag, 2, peers[1])
    wo_copy.start()
    wo_share.start()
    diag[0].start()

    small = r.small
    table = r.table
    table[...] = jnp.zeros_like(table)
    table[: small.shape[0], :] = small[...]
    n_exp = r.gates.shape[1]
    gain = small[17:18, :].astype(F32)
    own_cols = pl.ds(pl.multiple_of(f * ff, ff), ff)
    away_cols = pl.ds(pl.multiple_of((1 - f) * ff, ff), ff)

    def head_cols(m):
        return pl.ds(pl.multiple_of(seqs[m] * 256, 256), 256)

    wo_copy.wait()
    wo_share.wait_recv()
    def share(i, j, dev):
        at = pl.ds(pl.multiple_of(i * n, n), n)
        to = rows_x(i) if j else rows_y(i)
        return remote(hx.at[at], hx.at[to], r.s_h, 2 * j + i, dev)

    @pl.loop(0, 2)
    def _(i):
        at = pl.ds(pl.multiple_of(i * n, n), n)
        tout[at, head_cols(0)] = att[0, at, :]
        for m in range(1, 4):
            head(m, i).wait_recv()
            tout[at, head_cols(m)] = att_in[m, at, :]
        middle = (
            r.tok[at, :].astype(F32)
            + mm(tout[at, own_cols], r.wo_own[...])
            + mm(tout[at, away_cols], wo_there[...])
        )
        r.middle[at, :] = middle
        normed, _ = rms_parts(middle)
        hidden = (normed * gain).astype(BF)
        logits = mm_nt(hidden, table[...])
        lane = lax.broadcasted_iota(jnp.int32, logits.shape, 1)
        chosen = lane == r.routes[at, 0:1]
        for k in range(1, topk):
            chosen = chosen | (lane == r.routes[at, k : k + 1])
        top = jnp.max(jnp.where(chosen, logits, NEG), axis=-1, keepdims=True)
        raised = jnp.where(chosen, jnp.exp(logits - top), 0.0)
        gates = raised / jnp.sum(raised, axis=-1, keepdims=True)
        r.gates[at, :] = gates
        hx[at, :width] = hidden
        hx[at, width:] = gates.astype(BF)
        share(i, 0, peer_y).start()
        share(i, 1, peer_x).start()

    shares = [share(i, j, dev) for i in range(2) for j, dev in ((0, peer_y), (1, peer_x))]
    second = remote(hx.at[rows_y(1)], hx.at[pl.ds(2 * rows + n, n)], r.s_h, 4, peer_x)
    first = remote(hx.at[rows_x(0)], hx.at[pl.ds(2 * rows, n)], r.s_h, 5, peer_y)

    dhs, moe, dh, dgates = r.dhs, r.moe_acc, r.dh_acc, r.dg_acc
    back_x = [
        remote(dhs.at[rows_x(i)], r.rdh.at[1, pl.ds(i * n, n)], r.s_d, i, peer_x) for i in range(2)
    ]
    back_y = [
        remote(dhs.at[rows_y(i)], r.rdh.at[0, pl.ds(i * n, n)], r.s_d, 2 + i, peer_y) for i in range(2)
    ]

    def two_hops(i, sem, first_dev, second_dev):
        at = pl.ds(i * n, n)
        return (
            remote(dhs.at[pl.ds(2 * rows + i * n, n)], r.via.at[at], r.s_d, sem, first_dev),
            remote(r.via.at[at], r.rdd.at[at], r.s_d, sem + 1, second_dev),
        )

    hop_y, end_x = two_hops(0, 4, peer_y, peer_x)
    hop_x, end_y = two_hops(1, 6, peer_x, peer_y)
    moe_x = remote(r.moe2, r.got2, r.s_d, 8, peer_x)

    def moe_out(turn):
        src = r.mstage.at[turn % 2]
        if turn % 2 == 0:
            return [pltpu.make_async_copy(src, (r.moe0, r.moe3)[turn // 2], r.s_m.at[turn])]
        to = pl.ds(turn // 2 * n, n)
        return [
            pltpu.make_async_copy(src.at[pl.ds(0, n)], r.moe2.at[to], r.s_m.at[turn]),
            pltpu.make_async_copy(src.at[pl.ds(n, n)], r.moe1.at[to], r.s_m.at[turn + 3]),
        ]

    def forward():
        hop_y.wait_recv()
        end_x.start()
        hop_x.wait_recv()
        end_y.start()

    @pl.loop(0, 4 * count)
    def _(k):
        t, e = k // count, k % count

        @pl.when(k < count)
        def _():
            load_weights(e, lambda copy: copy.wait())

        @pl.when(k == 0)
        def _():
            load_cots[0].wait()

        @pl.when(k == count)
        def _():
            for copy in shares:
                copy.wait_recv()
            second.start()
            first.start()
            diag[1].start()
            for copy in load_cots[1:]:
                copy.wait()

        @pl.when(k == 2 * count)
        def _():
            first.wait_recv()
            second.wait_recv()
            for copy in diag:
                copy.wait_recv()

        pl.when(k == 4 * count - 1)(forward)
        at = block(t)
        h, c = hx[at, :width], cots[at, :]
        wg, wu, wd = r.wgs[e], r.wus[e], r.wds[e]
        expert = f * owned + x * count + e
        mine = lax.broadcasted_iota(jnp.int32, (rows, ext - width), 1) == expert
        gate = jnp.sum(jnp.where(mine, hx[at, width:].astype(F32), 0.0), axis=1, keepdims=True)
        g, u, zz = mm(h, wg), mm(h, wu), mm_nt(c, wd)
        sig = jax.nn.sigmoid(g)
        silu = g * sig
        act = silu * u
        dgate_col = jnp.where(mine, jnp.sum(act * zz, axis=1, keepdims=True), 0.0)
        act = (act * gate).astype(BF)
        dact = zz * gate
        dgate = (dact * u * sig * (1.0 + g * (1.0 - sig))).astype(BF)
        dup = (dact * silu).astype(BF)
        r.s_act[e, at, :] = act
        r.s_gate[e, at, :] = dgate
        r.s_up[e, at, :] = dup

        @pl.when(e == 0)
        def _():
            moe[...] = mm(act, wd)
            dh[...] = mm_nt(dgate, wg) + mm_nt(dup, wu)
            dgates[...] = dgate_col

        @pl.when(e > 0)
        def _():
            moe[...] += mm(act, wd)
            dh[...] += mm_nt(dgate, wg) + mm_nt(dup, wu)
            dgates[...] += dgate_col

        @pl.when(e == count - 1)
        def _():
            dhs[at, :width] = dh[...].astype(BF)
            dhs[at, width:] = dgates[...].astype(BF)
            for i in range(4):
                @pl.when(t == i)
                def _():
                    if i == 2:
                        hop_y.start()
                        hop_x.start()
                    elif i > 0:
                        back_x[i // 2].start()
                        back_y[i // 2].start()
                    for copy in moe_out(i - 2) if i >= 2 else ():
                        copy.wait()
                    r.mstage[i % 2] = moe[...].astype(BF)
                    for copy in moe_out(i):
                        copy.start()

    stage = r.stage

    def grad_copy(b, slot):
        return pltpu.make_async_copy(stage.at[slot], r.grads.at[b], r.s_g.at[slot])

    dattn, dto, dsend = r.dattn, r.dto, r.dsend
    returns = [
        [
            remote(dsend.at[m, pl.ds(i * n, n)], r.do.at[m, pl.ds(i * n, n)], r.s_back, 2 * m + i, peers[m])
            for m in (3, 2, 1)
        ]
        for i in range(2)
    ]

    def middle_back(i):
        at = pl.ds(i * n, n)
        total = (
            dhs[at, :].astype(F32) + r.rdh[0, at, :].astype(F32)
            + r.rdh[1, at, :].astype(F32) + r.rdd[at, :].astype(F32)
        )
        dg, gates = total[:, width:], r.gates[at, :]
        dl = (gates * (dg - jnp.sum(gates * dg, axis=-1, keepdims=True))).astype(BF)
        rg = mm_tn(dl, hx[at, :width])[:32]
        d_hidden = total[:, :width] + mm(dl, table[...])
        normed, factor = rms_parts(r.middle[at, :])
        gn = jnp.sum(d_hidden * normed, axis=0, keepdims=True)
        d_n = d_hidden * gain
        d_mid = cots[at, :].astype(F32) + factor * (
            d_n - normed * jnp.mean(d_n * normed, axis=-1, keepdims=True)
        )
        r.dmid[at, :] = d_mid
        low = d_mid.astype(BF)
        dattn[at, :] = low
        dto[at, own_cols] = mm_nt(low, r.wo_own[...]).astype(BF)
        dto[at, away_cols] = mm_nt(low, wo_there[...]).astype(BF)
        for m in range(1, 4):
            dsend[m, at, :] = dto[at, head_cols(m)]
        for copy in returns[i]:
            copy.start()
        r.do[0, at, :] = dto[at, head_cols(0)]
        if i == 0:
            r.rg[...] = rg
            r.gn[:1, :] = gn
            return
        rg, gn = r.rg[...] + rg, r.gn[:1, :] + gn
        row = lax.broadcasted_iota(jnp.int32, rg.shape, 0)
        top = jnp.where(row == 17, gn, jnp.where(row < 16, rg, 0.0))
        r.tiny[0] = top[:, : width // 2]
        r.tiny[1] = top[:, width // 2 :]
        for k in range(4):
            cols = slice(k * 256, (k + 1) * 256)
            r.gout[cols, :] = mm_tn(tout[:, cols], dattn[...]).astype(BF)

    def send_moe():
        for copy in moe_out(3):
            copy.wait()
        moe_x.start()

    def back0():
        for copy in (back_x[0], back_y[0], end_x):
            copy.wait_recv()
        middle_back(0)

    def back1():
        for copy in (back_x[1], back_y[1], end_y):
            copy.wait_recv()
        middle_back(1)

    @pl.loop(0, 3 * count)
    def _(k):
        e, j = k // 3, k % 3
        pl.when(k == 1)(send_moe)
        pl.when(k == 3 * count - 7)(back0)
        pl.when(k == 3 * count - 4)(back1)

        @pl.when(k > 0)
        def _():
            grad_copy(0, 0).wait()
            grad_copy(0, 1).wait()

        for which, left, right in ((0, hx, r.s_gate), (1, hx, r.s_up), (2, cots, r.s_act)):
            @pl.when(j == which)
            def _():
                for i in range(2):
                    at = slice(i * ff, (i + 1) * ff)
                    if which < 2:
                        v = mm_tn(left[:, at], right[e])
                    else:
                        v = mm_tn(right[e], left[:, at])
                    stage[i] = v.astype(BF)

        for i in range(2):
            grad_copy(6 * e + 2 * j + i, i).start()

    grad_copy(0, 0).wait()
    grad_copy(0, 1).wait()
    for copy in moe_out(2):
        copy.wait()
    for copy in (*returns[0], *returns[1], moe_x):
        copy.wait()
    for copy in (*heads, *diag, wo_share, *shares, first, second, *back_y, *back_x, hop_x, hop_y, end_y, end_x):
        copy.wait_send()


def moe_layer(att, tok, wo_own, wo_near, small, routes, cot, cot_y, cot_x, wg, wu, wd):
    rows, width = tok.shape
    owned, _, ff = wg.shape
    count = owned // 2
    ext = width + 128
    hbm = pl.BlockSpec(memory_space=pl.ANY)
    vmem = pl.BlockSpec(memory_space=pltpu.VMEM)
    dma = pltpu.SemaphoreType.DMA
    args = dict(
        att=(att.reshape(4, rows, 256), vmem), tok=(tok, vmem), wo_own=(wo_own, vmem),
        wo_near=(wo_near, hbm), small=(small, vmem), routes=(routes, vmem),
        cot=(cot, hbm), cot_y=(cot_y, hbm), cot_x=(cot_x, hbm),
        wg=(wg, hbm), wu=(wu, hbm), wd=(wd, hbm),
    )
    shape = jax.ShapeDtypeStruct
    outs = dict(
        middle=(shape((rows, width), F32), vmem),
        moe0=(shape((rows, width), BF), hbm), moe1=(shape((rows, width), BF), hbm),
        moe2=(shape((rows, width), BF), hbm), moe3=(shape((rows, width), BF), hbm),
        got2=(shape((rows, width), BF), hbm),
        dmid=(shape((rows, width), F32), vmem),
        do=(shape((4, rows, 256), BF), vmem),
        grads=(shape((6 * count, ff, ff), BF), hbm),
        gout=(shape((width, width), BF), vmem),
        tiny=(shape((2, 32, width // 2), F32), vmem),
    )
    stash = pltpu.VMEM((count, 4 * rows, ff), BF)
    scratch = dict(
        att_in=pltpu.VMEM((4, rows, 256), BF), tout=pltpu.VMEM((rows, width), BF),
        hx=pltpu.VMEM((4 * rows, ext), BF), cots=pltpu.VMEM((4 * rows, width), BF),
        wo_there=pltpu.VMEM((ff, width), BF), rg=pltpu.VMEM((32, width), F32),
        gn=pltpu.VMEM((8, width), F32), table=pltpu.VMEM((128, width), BF), gates=pltpu.VMEM((rows, 128), F32),
        wgs=pltpu.VMEM((count, width, ff), BF), wus=pltpu.VMEM((count, width, ff), BF),
        wds=pltpu.VMEM((count, ff, width), BF),
        s_act=stash, s_gate=stash, s_up=stash,
        moe_acc=pltpu.VMEM((rows, width), F32), dh_acc=pltpu.VMEM((rows, width), F32),
        dg_acc=pltpu.VMEM((rows, 128), F32), mstage=pltpu.VMEM((2, rows, width), BF),
        dhs=pltpu.VMEM((4 * rows, ext), BF), rdh=pltpu.VMEM((2, rows, ext), BF),
        via=pltpu.VMEM((rows, ext), BF), rdd=pltpu.VMEM((rows, ext), BF),
        dattn=pltpu.VMEM((rows, width), BF), dto=pltpu.VMEM((rows, width), BF),
        dsend=pltpu.VMEM((4, rows, 256), BF), stage=pltpu.VMEM((2, ff, ff), BF),
        s_att=dma((2, 8)), s_diag=dma((2, 3)), s_h=dma((2, 6)), s_d=dma((2, 9)), s_back=dma((2, 8)),
        s_cot=dma((5,)), s_wo=dma((1,)), s_w=dma((3, count)), s_m=dma((7,)), s_g=dma((2,)),
    )
    names = tuple(args) + tuple(outs) + tuple(scratch)
    got = pl.pallas_call(
        functools.partial(moe_kernel, names=names, topk=routes.shape[1], count=count),
        in_specs=[v[1] for v in args.values()],
        out_specs=[v[1] for v in outs.values()],
        out_shape=[v[0] for v in outs.values()],
        scratch_shapes=list(scratch.values()),
        compiler_params=pltpu.CompilerParams(
            vmem_limit_bytes=67043328, collective_id=3, has_side_effects=True
        ),
        name="moe_layer",
    )(*[v[0] for v in args.values()])
    return types.SimpleNamespace(**dict(zip(outs, got)))


def flip_core(x):
    return lax.ppermute(x, "seq", [(0, 1), (1, 0), (2, 3), (3, 2)])


def flip_x(x):
    return lax.ppermute(x, "seq", [(0, 2), (2, 0), (1, 3), (3, 1)])


def flip_both(x):
    return lax.ppermute(x, "seq", [(0, 3), (3, 0), (1, 2), (2, 1)])


def flip_y(x):
    return lax.ppermute(x, "fsdp", [(0, 1), (1, 0)])


def gather_seq(x):
    own = jnp.stack([x, flip_core(x)])
    far = flip_x(x)
    return jnp.concatenate([own, far[None], flip_core(far)[None]])


def swap_seq(blocks):
    return [blocks[0], flip_core(blocks[1]), flip_x(blocks[2]), flip_both(blocks[3])]


def gather_fsdp(x, axis=0):
    if lax.axis_size("fsdp") == 2:
        return jnp.concatenate([x, lax.ppermute(x, "fsdp", [(0, 1), (1, 0)])], axis=axis)
    return lax.all_gather(x, "fsdp", axis=axis, tiled=True)


def scatter_fsdp(x):
    if lax.axis_size("fsdp") == 2:
        n = x.shape[0] // 2
        other = lax.ppermute(x[n:], "fsdp", [(0, 1), (1, 0)])
        return x[:n].astype(F32) + other.astype(F32)
    return lax.psum_scatter(x, "fsdp", scatter_dimension=0, tiled=True).astype(F32)


def rope_back(w, cos, sin, low_half):
    half = HEAD_WIDTH // 2
    y = w * sin
    return w * cos + jnp.where(low_half, pltpu.roll(y, 128 - half, 1), -pltpu.roll(y, half, 1))


def reduce_kernel(*refs, names, slots, shards, fused):
    r = types.SimpleNamespace(**dict(zip(names, refs)))
    gm, mine, rc, pre, suf = r.gm, r.mine, r.rc, r.pre, r.suf
    gate, up, down, out, qkv = r.gate, r.up, r.down, r.out, r.qkv
    z, s, f = lax.axis_index("dp"), lax.axis_index("seq"), lax.axis_index("fsdp")
    core, x = s % 2, s // 2
    peer_core = (z, s + 1 - 2 * core, f)
    peer_x = (z, (s + 2) % 4, f)
    peer_y = (z, s, 1 - f)
    right, left = (z + 1, s, f), (z - 1, s, f)
    nb = gm.shape[0]
    n_moe, n_out, items = 2 * nb, 2 * nb + 2, 2 * nb + 6
    count = nb // 6
    piece = mine.shape[1]
    half, block = 2 * piece, 4 * piece
    last = slots - 1

    def other_z(k):
        return ((z + k) % slots, s, f)

    barrier = pltpu.get_barrier_semaphore()
    peer_xy = (z, (s + 2) % 4, 1 - f)
    peers = [other_z(k) for k in range(1, slots)] + [peer_core, peer_x] + [peer_y, peer_xy] * fused
    for dev in peers:
        pl.semaphore_signal(barrier, inc=1, device_id=dev, device_id_type=MESH)

    def remote(src, dst, sems, b, dev):
        return pltpu.make_async_remote_copy(
            src_ref=src, dst_ref=dst, send_sem=sems.at[0, b], recv_sem=sems.at[1, b],
            device_id=dev, device_id_type=MESH,
        )

    def load(src, b):
        return pltpu.make_async_copy(src, mine.at[b], r.s_mine.at[b])

    @pl.loop(0, n_moe)
    def _(b):
        load(gm.at[b // 2, core, b % 2], b).start()

    if fused:
        loads = [
            pltpu.make_async_copy(a, b, r.s_in.at[i])
            for i, (a, b) in enumerate((
                (r.q, r.q_in), (r.kv, r.kv_in), (r.do, r.do_in), (r.o, r.o_in), (r.lse, r.lse_in),
                (r.wc, r.wc_in),
                (r.cos, r.cos_in), (r.sin, r.sin_in), (r.h, r.h_in), (r.tok, r.tok_in),
                (r.gout.at[pl.ds(pl.multiple_of(f * block, block), block)], r.gout_in),
                (r.dmid, r.dmid_in),
            ))
        ]
        for copy in loads:
            copy.start()
    else:
        for i in range(2):
            load(r.eo.at[core, i], n_moe + i).start()
        for i in range(4):
            load(r.cols.at[i], n_out + i).start()
    pl.semaphore_wait(barrier, len(peers))

    @pl.loop(0, n_moe)
    def _(b):
        remote(gm.at[b // 2, 1 - core, b % 2], rc.at[b], r.s_rc, b, peer_core).start()

    if not fused:
        for i in range(2):
            remote(r.eo.at[1 - core, i], rc.at[n_moe + i], r.s_rc, n_moe + i, peer_core).start()

    def place(b, which, part, act):
        first_row = part * half + b % 2 * piece
        rows = pl.ds(pl.multiple_of(first_row, piece), piece)
        e, j = which * count + b // 12, b // 2 % 6
        jj = j % 2
        wide = pl.ds(pl.multiple_of(jj * block, block), block)
        at = pl.ds(pl.multiple_of(jj * block + first_row, piece), piece)
        for m, o in enumerate((gate, up)):
            @pl.when((b < n_moe) & (j // 2 == m))
            def _():
                act(o.at[e, at, :])

        @pl.when((b < n_moe) & (j // 2 == 2))
        def _():
            act(down.at[e, rows, wide])

        @pl.when((b >= n_moe) & (b < n_out))
        def _():
            act(out.at[rows, pl.ds(pl.multiple_of(which * block, block), block)])

        @pl.when(b >= n_out)
        def _():
            at = pl.ds(pl.multiple_of((b - n_out) * piece, piece), piece)
            wide = 2 * block
            for first, n, to in ((0, 256, 0), (wide, 128, 256), (wide + wide // 2, 128, 384)):
                col = pl.multiple_of(first + (2 * which + part) * n, 128)
                act(qkv.at[at, pl.ds(col, n)], pl.ds(to, n))

    def add(a, b):
        return a.astype(F32) + b.astype(F32)

    def hop(buf, sems, b, dev):
        return remote(buf.at[b], buf.at[b], sems, b, dev)

    def spread(b):
        def act(dst, cut=None):
            src = rc.at[b] if cut is None else rc.at[b, :, cut]
            remote(src, dst, r.s_oth, 0, peer_core).start()
            pltpu.make_async_copy(src, dst, r.s_out.at[0]).start()
            remote(src, dst, r.s_far, b, peer_x).start()

        place(b, x, core, act)

    lag = 2
    ahead = 4

    def begin(b):
        @pl.when(b < (n_moe if fused else items))
        def _():
            load(gm.at[0, 0, 0], b).wait()

        @pl.when(b < n_out)
        def _():
            remote(gm.at[0, 0, 0], rc.at[b], r.s_rc, b, peer_core).wait_recv()
            mine[b] = add(mine[b], rc[b]).astype(BF)

        @pl.when(z == 0)
        def _():
            remote(mine.at[b], pre.at[b], r.s_pre, b, right).start()

        @pl.when(z == last)
        def _():
            remote(mine.at[b], suf.at[b], r.s_suf, b, left).start()

    def prefix(b):
        hop(pre, r.s_pre, b, peer_x).wait_recv()
        got = pre[b].astype(F32)
        own = got + mine[b].astype(F32)

        @pl.when(z == last)
        def _():
            rc[b] = own.astype(BF)

        @pl.when(z < last)
        def _():
            @pl.when(2 * z >= slots)
            def _():
                rc[b] = (got + suf[b].astype(F32)).astype(BF)

            pre[b] = own.astype(BF)
            hop(pre, r.s_pre, b, right).start()

        @pl.when(2 * z >= slots)
        def _():
            spread(b)

    def suffix(b):
        hop(suf, r.s_suf, b, peer_x).wait_recv()
        got = suf[b].astype(F32)
        own = got + mine[b].astype(F32)

        @pl.when(z == 0)
        def _():
            rc[b] = own.astype(BF)

        @pl.when(z > 0)
        def _():
            @pl.when(2 * z < slots)
            def _():
                rc[b] = (got + pre[b].astype(F32)).astype(BF)

            suf[b] = own.astype(BF)
            hop(suf, r.s_suf, b, left).start()

        @pl.when(2 * z < slots)
        def _():
            spread(b)

    def forward(b):
        remote(rc.at[b], rc.at[b], r.s_far, b, peer_x).wait_recv()

        def act(dst, cut=None):
            remote(dst, dst, r.s_faro, 0, peer_core).start()

        place(b, 1 - x, core, act)

    def within(b, cond=True):
        return (b >= 0) & (b < items) & cond

    tsum, trecv, s_tiny = r.tsum, r.trecv, r.s_tiny

    def tiny_swap(k, dev):
        return remote(tsum.at[k], trecv.at[k], s_tiny, k, dev)

    def tiny_add(k):
        tiny_swap(k, peer_x).wait_recv()
        tsum[k + 1] = add(tsum[k], trecv[k]).astype(BF)

    def tiny_x():
        tiny_swap(0, peer_x).start()

    def tiny_core():
        tiny_add(0)
        tiny_swap(1, peer_core).start()

    def tiny_spread():
        tiny_add(1)
        for k in range(1, slots):
            remote(tsum.at[2], trecv.at[1 + k], s_tiny, 1 + k, other_z(k)).start()

    def tiny_end():
        total = tsum[2].astype(F32)
        for k in range(1, slots):
            remote(tsum.at[2], trecv.at[1 + k], s_tiny, 1 + k, other_z(k)).wait_recv()
            total = total + trecv[1 + k].astype(F32)
        r.tiny_out[...] = total

    steps = {}
    if fused:
        s_fg = r.s_fg
        keys = r.dkvs.shape[0]
        tile = r.dhx.shape[0]
        dh = [r.h_in.at[pl.ds(t * tile, tile)] for t in range(4)]
        owner = pl.multiple_of(f * block, block)
        away = pl.multiple_of((1 - f) * block, block)
        mine_rows, away_rows = pl.ds(owner, block), pl.ds(away, block)
        near_cols = pl.ds(pl.multiple_of(x * block, block), block)
        far_cols = pl.ds(pl.multiple_of((1 - x) * block, block), block)

        send_dkv = remote(r.kv_in.at[pl.ds(keys, keys)], r.rdkv, s_fg, 0, peer_y)
        send_out = [
            remote(r.gout.at[away_rows, cols], r.rout.at[i], s_fg, (1, 8)[i], peer_y)
            for i, cols in enumerate((far_cols, near_cols))
        ]
        send_dh3 = remote(dh[3], r.rdh.at[1], s_fg, 2, peer_core)
        send_dh1 = remote(dh[1], r.rdh.at[0], s_fg, 3, peer_core)
        send_dhx = remote(r.dhx, r.rdx, s_fg, 4, peer_x)
        send_cols = remote(r.cbuf.at[away_rows], r.rcol, s_fg, 5, peer_y)
        send_outx = remote(r.osend, r.rox, s_fg, 6, peer_x)
        send_tiny = remote(r.tbuf.at[1 - f], r.rtiny, s_fg, 7, peer_y)
        eo_core = [
            remote(r.eo.at[1 - core, i], rc.at[n_moe + i], r.s_rc, n_moe + i, peer_core)
            for i in range(2)
        ]
        moe_back = [
            remote(r.moe3, r.got3, r.s_moe, 1, peer_xy), remote(r.moe1, r.got1, r.s_moe, 0, peer_y),
        ]
        moe_back[0].start()
        for copy in send_out:
            copy.start()
        moe_back[1].start()

        span, kb = tile // 2, 2 * tile
        parts = 2 * keys // kb
        n_steps = 8 * parts
        scale = HEAD_WIDTH**-0.5

        def attention(n):
            j, m = n // parts, n % parts
            at = pl.ds(pl.multiple_of(j * span, span), span)

            @pl.when(n == 0)
            def _():
                r.dk[...] = jnp.zeros_like(r.dk)
                r.dv[...] = jnp.zeros_like(r.dv)
                inside = lax.broadcasted_iota(jnp.int32, (span, 1), 0)
                for k in range(2 * keys // span):
                    r.kpos[k * span : (k + 1) * span, :] = span_at(r.order, k) * span + inside
                across = lax.broadcasted_iota(jnp.int32, (8, 4 * span), 1) % span
                for k in range(8):
                    r.last[k] = jnp.minimum(span_at(r.order, k) * span + across, r.limit[0] - 1)

            @pl.when(m == 0)
            def _():
                r.qs[...] = stack_heads(r.q_in[at, :128], r.q_in[at, 128:])
                do = stack_heads(r.do_in[at, :128], r.do_in[at, 128:])
                r.dos[...] = do
                inner = do.astype(F32) * stack_heads(r.o_in[at, :128], r.o_in[at, 128:], F32)
                delta = jnp.sum(jnp.transpose(inner), axis=0, keepdims=True)
                r.delta[...] = jnp.broadcast_to(delta, r.delta.shape)

            key = pl.ds(pl.multiple_of(m * kb, kb), kb)
            k, v = r.kv_in[key, :128], r.kv_in[key, 128:]
            q, do = r.qs[...], r.dos[...]
            p = jnp.exp2(mm_nt(k, q) * (scale * LOG2E) - r.lse_in[j, :1])
            p = jnp.where(r.kpos[key, :] <= r.last[j, :1], p, 0.0)
            ds = (p * (mm_nt(v, do) - r.delta[:1])).astype(BF)
            r.dk[key, :] += mm(ds, q)
            r.dv[key, :] += mm(p.astype(BF), do)
            dq = mm_tn(ds, k)

            @pl.when(m == 0)
            def _():
                r.dqa[...] = dq

            @pl.when(m > 0)
            def _():
                r.dqa[...] += dq

            @pl.when(m == parts - 1)
            def _():
                a, b = unstack_heads(r.dqa[...] * scale)
                r.dq_in[at, :128] = a.astype(BF)
                r.dq_in[at, 128:] = b.astype(BF)

        def send_keys():
            r.kv_in[:, :128] = (r.dk[...] * scale).astype(BF)
            r.kv_in[:, 128:] = r.dv[...].astype(BF)
            send_dkv.start()

        def sum_dkv():
            send_dkv.wait_recv()
            r.dkvs[...] = add(r.kv_in[:keys], r.rdkv[...]).astype(BF)

        def back_tile(t, first=False):
            at = pl.ds(t * tile, tile)
            cos, sin = r.cos_in[at, :], r.sin_in[at, :]
            low_half = lax.broadcasted_iota(jnp.int32, cos.shape, 1) % HEAD_WIDTH < HEAD_WIDTH // 2
            parts = []
            for k in range(3):
                w = r.dq_in[at, k * 128 : (k + 1) * 128] if k < 2 else r.dkvs[at, :128]
                parts.append(rope_back(w.astype(F32), cos, sin, low_half).astype(BF))
            parts.append(r.dkvs[at, 128:])
            dproj = jnp.concatenate(parts, axis=1)
            grad = mm_tn(r.h_in[at, :], dproj)
            back = mm_nt(dproj, r.wc_in[...])
            dh[t][...] = back.astype(BF)
            normed, _ = rms_parts(r.tok_in[at, :].astype(F32))
            gain = jnp.sum((back * normed).reshape(-1, 8, back.shape[1]), axis=0)
            if first:
                r.acc[...] = grad
                r.gn[...] = gain
            else:
                r.acc[...] += grad
                r.gn[...] += gain

        def tile3():
            back_tile(3, True)
            send_dh3.start()

        def tile1():
            back_tile(1)
            send_dh1.start()

        def tile2():
            back_tile(2)
            send_dh3.wait_recv()
            r.dhx[...] = add(dh[2][...], r.rdh[1]).astype(BF)
            send_dhx.start()

        def tile0():
            back_tile(0)
            r.cbuf[...] = r.acc[...].astype(BF)
            send_cols.start()
            total = jnp.sum(r.gn[...], axis=0, keepdims=True)
            wide = tsum.shape[2]
            row = lax.broadcasted_iota(jnp.int32, (tsum.shape[1], wide), 0) == 16
            for k in range(2):
                part = total[:, k * wide : (k + 1) * wide]
                r.tbuf[k] = jnp.where(row, part, r.tiny[k]).astype(BF)
            send_tiny.start()

        def sum_out():
            send_out[0].wait_recv()
            r.osend[...] = add(r.gout_in[:, far_cols], r.rout[0]).astype(BF)
            send_outx.start()

        def tiny_y():
            send_tiny.wait_recv()
            tsum[0] = add(r.tbuf[f], r.rtiny[...]).astype(BF)
            tiny_x()

        def sum_cols():
            send_cols.wait_recv()
            v = add(r.cbuf[mine_rows, :], r.rcol[...]).astype(BF)
            for i in range(4):
                mine[n_out + i] = v[i * piece : (i + 1) * piece]

        def sum_outx():
            send_out[1].wait_recv()
            send_outx.wait_recv()
            v = add(r.gout_in[:, near_cols], r.rout[1]) + r.rox[...].astype(F32)
            v = v.astype(BF)
            for i in range(4):
                r.eo[i // 2, i % 2] = v[i * piece : (i + 1) * piece]
            for i in range(2):
                eo_core[i].start()
                mine[n_moe + i] = r.eo[core, i]

        def inputs_back():
            send_dh1.wait_recv()
            send_dhx.wait_recv()
            up_grad = add(dh[0][...], r.rdh[0]) + r.rdx[...].astype(F32)
            normed, factor = rms_parts(r.tok_in[:tile].astype(F32))
            d_n = up_grad * r.small[16:17, :].astype(F32)
            r.dtok[...] = r.dmid_in[...] + factor * (
                d_n - normed * jnp.mean(d_n * normed, axis=-1, keepdims=True)
            )

        def arrive():
            for copy in loads:
                copy.wait()

        first_step = 1
        done = first_step + n_steps
        order = [
            send_keys, None, None, sum_outx, None, sum_dkv, tile3, tile1, tile2, tile0, None, None,
            tiny_y, sum_cols, None, inputs_back, tiny_core, None, tiny_spread,
        ]
        steps = {done + i: fn for i, fn in enumerate(order) if fn is not None}
        steps.update({0: arrive, OUT_STEP: sum_out})
    else:
        tsum[0] = r.tiny[...].astype(BF)
        tiny_x()
        steps = {1: tiny_core, 2: tiny_spread}

    @pl.loop(0, items + ahead + (last + 1) * lag)
    def _(i):
        for fn, b, cond in (
            (begin, i, True),
            (prefix, i - ahead - lag * z, z > 0),
            (suffix, i - ahead - lag * (last - z), z < last),
            (forward, i - ahead - lag * (last + 1), True),
        ):
            @pl.when(within(b, cond))
            def _():
                fn(b)

        if fused:
            @pl.when((i >= first_step) & (i < done))
            def _():
                attention(i - first_step)

        for k, fn in steps.items():
            pl.when(i == k)(fn)

    tiny_end()

    @pl.loop(0, items)
    def _(b):
        one = rc.at[b]

        @pl.when(b < n_out)
        def _():
            remote(one, one, r.s_rc, b, peer_core).wait_send()

        @pl.when(z < last)
        def _():
            hop(pre, r.s_pre, b, peer_x).wait_send()

        @pl.when(z > 0)
        def _():
            hop(suf, r.s_suf, b, peer_x).wait_send()

        remote(one, one, r.s_far, b, peer_x).wait_send()

    remote(rc, rc, r.s_oth, 0, peer_core).wait()
    remote(rc, rc, r.s_faro, 0, peer_core).wait()
    pltpu.make_async_copy(rc, rc, r.s_out.at[0]).wait()
    tiny_swap(0, peer_x).wait_send()
    tiny_swap(1, peer_core).wait_send()
    for k in range(1, slots):
        remote(tsum.at[2], trecv.at[1 + k], s_tiny, 1 + k, other_z(k)).wait_send()
    if fused:
        for copy in (send_dkv, *send_out, send_dh3, send_dh1, send_dhx, send_cols, send_outx, send_tiny):
            copy.wait_send()
        for copy in moe_back:
            copy.wait()


def reduce_grads(gm, tiny, slots, shards, eo=None, cols=None, fused=None, small=None, tables=None, moes=None):
    count, _, ff, _ = gm.shape
    width = 2 * ff
    nb = 6 * count
    piece = ff // 4
    items = 2 * nb + 6
    hbm = pl.BlockSpec(memory_space=pl.ANY)
    vmem = pl.BlockSpec(memory_space=pltpu.VMEM)
    dma = pltpu.SemaphoreType.DMA
    args = dict(gm=(gm.reshape(nb, 2, 2, piece, ff), hbm), tiny=(tiny, vmem))
    outs = dict(
        gate=(jax.ShapeDtypeStruct((2 * count, width, ff), BF), hbm),
        up=(jax.ShapeDtypeStruct((2 * count, width, ff), BF), hbm),
        down=(jax.ShapeDtypeStruct((2 * count, ff, width), BF), hbm),
        out=(jax.ShapeDtypeStruct((ff, width), BF), hbm),
        qkv=(jax.ShapeDtypeStruct((ff, 2 * width), BF), hbm),
        tiny_out=(jax.ShapeDtypeStruct(tiny.shape[-2:], F32), vmem),
    )
    buf = pltpu.VMEM((items, piece, ff), BF)
    scratch = dict(
        mine=buf, rc=buf, pre=buf, suf=buf,
        tsum=pltpu.VMEM((3,) + tiny.shape[-2:], BF),
        trecv=pltpu.VMEM((slots + 1,) + tiny.shape[-2:], BF),
        s_tiny=dma((2, slots + 1)), s_mine=dma((items,)), s_out=dma((1,)),
    )
    each = dma((2, items))
    scratch.update(s_rc=each, s_pre=each, s_suf=each, s_far=each)
    scratch.update(s_oth=dma((2, 1)), s_faro=dma((2, 1)))
    if fused is None:
        args.update(
            eo=(eo.reshape(2, 2, piece, ff), hbm), cols=(cols.reshape(4, piece, ff), hbm)
        )
    else:
        inner = {}
        for k, v in fused.items():
            args[k] = (v, hbm)
            inner[k + "_in"] = pltpu.VMEM(v.shape, v.dtype)
        smem = pl.BlockSpec(memory_space=pltpu.SMEM)
        order, limit = tables
        args.update(
            small=(small, vmem), order=(order, smem), limit=(limit, smem),
            moe1=(moes[0], hbm), moe3=(moes[1], hbm),
        )
        outs.update({k: (jax.ShapeDtypeStruct(moes[0].shape, BF), hbm) for k in ("got1", "got3")})
        rows = args["dmid"][0].shape[0]
        keys = args["kv"][0].shape[0] // 2
        inner.update(gout_in=pltpu.VMEM((ff, width), BF))
        scratch.update(inner)
        outs.update(dtok=(jax.ShapeDtypeStruct((rows, width), F32), vmem))
        scratch.update(
            rdkv=pltpu.VMEM((keys, 256), BF), dkvs=pltpu.VMEM((keys, 256), BF),
            rout=pltpu.VMEM((2, ff, ff), BF),
            osend=pltpu.VMEM((ff, ff), BF), rox=pltpu.VMEM((ff, ff), BF),
            eo=pltpu.VMEM((2, 2, piece, ff), BF),
            dq_in=pltpu.VMEM((keys, 256), BF),
            dk=pltpu.VMEM((2 * keys, 128), F32), dv=pltpu.VMEM((2 * keys, 128), F32),
            qs=pltpu.VMEM((2 * rows, 128), BF), dos=pltpu.VMEM((2 * rows, 128), BF),
            delta=pltpu.VMEM((8, 2 * rows), F32), dqa=pltpu.VMEM((2 * rows, 128), F32),
            kpos=pltpu.VMEM((2 * keys, 1), jnp.int32), last=pltpu.VMEM((8, 8, 2 * rows), jnp.int32),
            s_in=dma((len(fused),)), s_moe=dma((2, 2)),
            rdh=pltpu.VMEM((2, rows, width), BF),
            dhx=pltpu.VMEM((rows, width), BF), rdx=pltpu.VMEM((rows, width), BF),
            acc=pltpu.VMEM((width, ff), F32), gn=pltpu.VMEM((8, width), F32),
            cbuf=pltpu.VMEM((width, ff), BF), rcol=pltpu.VMEM((ff, ff), BF),
            tbuf=pltpu.VMEM(tiny.shape, BF), rtiny=pltpu.VMEM(tiny.shape[-2:], BF),
            s_fg=dma((2, 9)),
        )
    names = tuple(args) + tuple(outs) + tuple(scratch)
    got = pl.pallas_call(
        functools.partial(
            reduce_kernel, names=names, slots=slots, shards=shards, fused=fused is not None
        ),
        in_specs=[v[1] for v in args.values()],
        out_specs=[v[1] for v in outs.values()],
        out_shape=[v[0] for v in outs.values()],
        scratch_shapes=list(scratch.values()),
        compiler_params=pltpu.CompilerParams(
            vmem_limit_bytes=67043328, collective_id=1, has_side_effects=True
        ),
        name="reduce_grads",
    )(*[v[0] for v in args.values()])
    return types.SimpleNamespace(**dict(zip(outs, got)))


def gather_rows(x):
    return lax.all_gather(x, "fsdp", axis=0, tiled=True)


def local(
    tokens, cotangent, lengths, order, routes, norm1, query_key_value_weight, w_out, norm2, router,
    w_gate, w_up, w_down,
):
    groups = lax.axis_size("seq")
    shards = lax.axis_size("fsdp")
    slots = lax.axis_size("dp")
    assert groups == 4
    seq, fsdp = lax.axis_index("seq"), lax.axis_index("fsdp")
    core, far = seq % 2, seq // 2
    rows, width = tokens.shape[1:]
    span = rows // 2
    x = tokens[0]
    limit = lengths[:1]
    n_experts = router.shape[1]
    owned = w_gate.shape[0]
    count = owned // 2

    own = lax.dynamic_slice_in_dim(order, (seq * shards + fsdp) * 2, 2)
    own_pos = (own[:, None] * span + jnp.arange(span, dtype=jnp.int32)[None, :]).reshape(-1)

    heads = QUERY_HEADS // groups
    qw, kw = heads * HEAD_WIDTH, KEY_VALUE_HEADS // groups * HEAD_WIDTH
    w3 = query_key_value_weight
    if shards == 2:
        tok, wcols, small, hidden_one, q, kv, cos, sin = front(
            order, x, w3, norm1, norm2, jnp.transpose(router)
        )
        tok, kv = tok.reshape(groups * rows, width), kv.reshape(-1, 256)
        w_out, cotangent, kv = lax.optimization_barrier((w_out, cotangent, kv))
    else:
        table = order.reshape(groups, shards, 2)
        relative = jnp.arange(groups, dtype=jnp.int32) ^ seq
        table = jnp.take(table, relative, axis=0)
        qtab = jnp.take(table, fsdp, axis=1).reshape(-1)
        ktab = jnp.transpose(table, (1, 0, 2)).reshape(-1)
        qpos = (qtab[:, None] * span + jnp.arange(span, dtype=jnp.int32)[None, :]).reshape(-1)
        small = jnp.concatenate(
            [jnp.transpose(router), norm1[None], norm2[None], jnp.zeros((14, norm1.shape[0]), BF)]
        )
        half = HEAD_WIDTH // 2
        freqs = jnp.exp(jnp.arange(half, dtype=F32) * (-2.0 * math.log(ROPE_BASE) / HEAD_WIDTH))
        angles = qpos.astype(F32)[:, None] * freqs[None, :]
        cos, sin = jnp.tile(jnp.cos(angles), (1, 4)), jnp.tile(jnp.sin(angles), (1, 4))
        wq = lax.dynamic_slice_in_dim(w3, seq * qw, qw, 1)
        wk = lax.dynamic_slice_in_dim(w3, QUERY_HEADS * HEAD_WIDTH + seq * kw, kw, 1)
        wv = lax.dynamic_slice_in_dim(
            w3, (QUERY_HEADS + KEY_VALUE_HEADS) * HEAD_WIDTH + seq * kw, kw, 1
        )
        wcols = gather_rows(jnp.concatenate([wq, wk, wv], axis=1))
        small = lax.all_gather(small, "fsdp", axis=1, tiled=True)
        tok = gather_seq(x).reshape(groups * rows, width)
        hidden_one, q, kv_own = project(tok, small[16:17].astype(F32), wcols, cos, sin, rows)
        kv = gather_fsdp(kv_own)
    gain_one, gain_two = small[16].astype(F32), small[17].astype(F32)
    route_rows = small[:n_experts]

    kb = 4 * span
    own_valid = (own_pos < limit[0])[:, None]
    masked_cot = jnp.where(own_valid, cotangent[0], jnp.zeros_like(cotangent[0]))
    if shards == 2:
        shared = w_out.shape[0] // 2
        wo_near = flip_y(lax.dynamic_slice_in_dim(w_out, core * shared, shared, 0))
        cot_y, cot_x = flip_y(masked_cot), flip_x(masked_cot)
    if shards == 2:
        body, tables = attend_short_kernel, (order, limit)
    else:
        body, tables = attend_kernel, (qtab, ktab, limit)
    attended, low, lse = attend(body, tables, q, kv, span, kb)
    inputs = x.astype(F32)
    if shards == 2:
        out = moe_layer(
            low, x, w_out, wo_near, small, routes[0], masked_cot, cot_y, cot_x, w_gate, w_up, w_down
        )
        moes = (out.moe1, out.moe3)
        d_heads = out.do.reshape(groups * rows, qw)
        middle, d_middle, grad_out, tiny = out.middle, out.dmid, out.gout, out.tiny
        weight_grads = out.grads.reshape(count, 6, w_gate.shape[2], -1)
    else:
        sent = low.reshape(groups, rows, qw)
        got = jnp.stack(swap_seq([sent[m] for m in range(groups)]))
        got = jnp.take(got, relative, axis=0)
        token_out = jnp.transpose(got, (1, 0, 2)).reshape(rows, groups * qw)
        out_full = gather_rows(w_out)

        middle = inputs + mm(token_out, out_full)
        normed_two, factor_two = rms_parts(middle)
        hidden_two = (normed_two * gain_two).astype(BF)
        logits = mm_nt(hidden_two, route_rows)
        chosen = jnp.any(
            routes[0][:, :, None] == jnp.arange(n_experts, dtype=jnp.int32)[None, None, :], axis=1
        )
        top = jnp.max(jnp.where(chosen, logits, NEG), axis=-1, keepdims=True)
        raised = jnp.where(chosen, jnp.exp(logits - top), 0.0)
        gates = raised / jnp.sum(raised, axis=-1, keepdims=True)

        def share(v):
            near = gather_rows(v)
            return jnp.concatenate([near, flip_x(near)])

        cot_all = share(masked_cot)
        extended = jnp.concatenate(
            [hidden_two, gates.astype(BF), jnp.zeros((rows, 128 - n_experts), BF)], axis=1
        )
        hid_all = share(extended)
        base = jnp.stack([far * count, fsdp * owned + far * count]).astype(jnp.int32)
        part = rows * 4
        moe_parts, dh_parts, weight_grads = [], [], None
        for i in range(hid_all.shape[0] // part):
            got = experts(
                base, count, hid_all[i * part : (i + 1) * part], cot_all[i * part : (i + 1) * part],
                w_gate, w_up, w_down, rows,
            )
            moe_parts.append(got[0])
            dh_parts.append(got[1])
            if weight_grads is None:
                weight_grads = got[2]
            else:
                weight_grads = (weight_grads.astype(F32) + got[2].astype(F32)).astype(BF)

        def give_back(parts):
            v = jnp.concatenate(parts) if len(parts) > 1 else parts[0]
            n = v.shape[0] // 2
            near = v[:n].astype(F32) + flip_x(v[n:]).astype(F32)
            return lax.psum_scatter(near.astype(BF), "fsdp", scatter_dimension=0, tiled=True).astype(F32)

        d_ext = give_back(dh_parts)
        d_gates = d_ext[:, width : width + n_experts]
        d_logits = (gates * (d_gates - jnp.sum(gates * d_gates, axis=-1, keepdims=True))).astype(BF)
        grad_router = mm_tn(hidden_two, d_logits)
        d_hidden = d_ext[:, :width] + mm(d_logits, route_rows)
        grad_norm2 = jnp.sum(d_hidden * normed_two, axis=0)
        d_n = d_hidden * gain_two
        d_middle = masked_cot.astype(F32) + factor_two * (
            d_n - normed_two * jnp.mean(d_n * normed_two, axis=-1, keepdims=True)
        )
        d_attn = d_middle.astype(BF)
        grad_out = mm_tn(token_out, d_attn).astype(BF)
        d_token_out = mm_nt(d_attn, out_full).astype(BF)
        d_heads = jnp.transpose(d_token_out.reshape(rows, groups, qw), (1, 0, 2))
        d_heads = jnp.take(d_heads, relative, axis=0)
        d_heads = jnp.concatenate(swap_seq([d_heads[m] for m in range(groups)]))
    block = w_gate.shape[2]
    shard_rows = width // shards

    def tiny_rows(first):
        return jnp.concatenate(
            [jnp.transpose(grad_router), first[None], grad_norm2[None], jnp.zeros((14, width), F32)]
        ).reshape(32, shards, shard_rows).transpose(1, 0, 2)

    if shards == 2:
        got = reduce_grads(
            weight_grads, tiny, slots, shards,
            fused=dict(
                q=q, kv=kv, do=d_heads, o=attended, lse=lse,
                tok=tok, h=hidden_one, wc=wcols, cos=cos, sin=sin, dmid=d_middle, gout=grad_out,
            ),
            small=small, tables=(order, limit), moes=moes,
        )
        d_inputs = got.dtok
    else:
        dq, dkv = attend_back(qtab, ktab, limit, q, kv, d_heads, attended, lse, span, kb)
        dh_one, grad_cols, grad_norm1 = project_back(
            tok, hidden_one, dq, scatter_fsdp(dkv), wcols, cos, sin, rows
        )
        dh_one = dh_one.reshape(groups, rows, width)
        near = dh_one[0::2].astype(F32) + flip_core(dh_one[1::2]).astype(F32)
        d_hidden_one = near[0] + flip_x(near[1].astype(BF)).astype(F32)
        normed_one, factor_one = rms_parts(inputs)
        d_n = d_hidden_one * gain_one
        d_inputs = d_middle + factor_one * (
            d_n - normed_one * jnp.mean(d_n * normed_one, axis=-1, keepdims=True)
        )

        def to_owner(g):
            part = lax.psum_scatter(g, "fsdp", scatter_dimension=0, tiled=True)
            return jnp.pad(part, ((0, block - part.shape[0]), (0, 0)))

        cols = to_owner(grad_cols)
        mine = to_owner(grad_out).reshape(block, 2, block)
        kept = lax.dynamic_index_in_dim(mine, far, 1, keepdims=False)
        sent = lax.dynamic_index_in_dim(mine, 1 - far, 1, keepdims=False)
        outs = (kept.astype(F32) + flip_x(sent).astype(F32)).astype(BF)
        tiny = tiny_rows(jnp.sum(grad_norm1, axis=0))
        tiny = lax.psum_scatter(tiny, "fsdp", scatter_dimension=0, tiled=True)[0]
        got = reduce_grads(weight_grads, tiny, slots, shards, eo=outs, cols=cols)
    parts = (middle, out.moe0, got.got1, out.got2, got.got3) if shards == 2 else ()
    wide, sums, tiny = widen(
        [got.gate, got.up, got.down, got.out, got.qkv, d_inputs], parts, got.tiny_out, n_experts
    )
    grad_gate, grad_up, grad_down, shard_out, shard_qkv, d_inputs = wide
    shard_out, shard_qkv = shard_out[:shard_rows], shard_qkv[:shard_rows]
    if shards == 2:
        layer_out = sums[0]
    else:
        layer_out = (middle + give_back(moe_parts)).astype(BF)
    return (
        layer_out[None], d_inputs[None], tiny[0], shard_qkv, shard_out, tiny[1], tiny[2],
        grad_gate, grad_up, grad_down,
    )


def solution(mesh):
    placed = (
        P("dp", ("seq", "fsdp"), None),
        P("dp", ("seq", "fsdp"), None),
        P("dp"),
        P(),
        P("dp", ("seq", "fsdp"), None),
        P("fsdp"),
        P("fsdp", None),
        P("fsdp", None),
        P("fsdp"),
        P("fsdp", None),
        P("fsdp", None, None),
        P("fsdp", None, None),
        P("fsdp", None, None),
    )
    return jax.shard_map(
        local,
        mesh=mesh,
        in_specs=placed,
        out_specs=(
            P("dp", ("seq", "fsdp"), None),
            P("dp", ("seq", "fsdp"), None),
            P("fsdp"),
            P("fsdp", None),
            P("fsdp", None),
            P("fsdp"),
            P("fsdp", None),
            P("fsdp", None, None),
            P("fsdp", None, None),
            P("fsdp", None, None),
        ),
        check_vma=False,
    )
```
